32 devices in a mesh: dp: 8 (over z, y), tp: 4 (over x, core).
Axes of the slice: x: 2, y: 2, z: 4, core: 2. Of those that a mesh axis runs over, the one named last changes fastest.
Arguments:
- tokens: bfloat16 [32768, 768], P(('dp', 'tp')), may hold values from -6 to 6
- w_qkv: bfloat16 [3, 768, 768], P(None, None, 'tp'), may hold values from -0.21875 to 0.21875
- qv_bias: float32 [2, 768], P(None, 'tp'), may hold values from -1.75 to 1.75
- w_out: bfloat16 [768, 768], P('tp'), may hold values from -1.25 to 1.25
- out_bias: float32 [768], replicated, may hold values from -1.75 to 1.75
- w_in: bfloat16 [768, 3072], P(None, 'tp'), may hold values from -0.21875 to 0.21875
- in_bias: float32 [3072], P('tp'), may hold values from -1.75 to 1.75
- w_down: bfloat16 [3072, 768], P('tp'), may hold values from -0.109375 to 0.109375
- down_bias: float32 [768], replicated, may hold values from -1.75 to 1.75
- norm_gain: float32 [2, 768], replicated, may hold values from 0.5 to 1.5
- norm_shift: float32 [2, 768], replicated, may hold values from -1.75 to 1.75
- valid_len: int32 [64], P('dp'), may hold values from 256 to 512, as said below
- picked: int32 [64, 128], P('dp'), may hold values from 0 to 512, as said below
- d_out: bfloat16 [32768, 768], P(('dp', 'tp')), may hold values from -6 to 6
Outputs:
- out: bfloat16 [32768, 768], P(('dp', 'tp'))
- d_tokens: bfloat16 [32768, 768], P(('dp', 'tp'))
- g_qkv: float32 [3, 768, 768], P(None, None, 'tp')
- g_qv_bias: float32 [2, 768], P(None, 'tp')
- g_out: float32 [768, 768], P('tp')
- g_out_bias: float32 [768], replicated
- g_in: float32 [768, 3072], P(None, 'tp')
- g_in_bias: float32 [3072], P('tp')
- g_down: float32 [3072, 768], P('tp')
- g_down_bias: float32 [768], replicated
- g_norm_gain: float32 [2, 768], replicated
- g_norm_shift: float32 [2, 768], replicated
The draws below stay inside these ranges and needn't reach their ends.
Inputs may be any that keep to these rules, and one draw needn't show every extreme that they name: One sequence of every draw has valid_len 512. `picked`: the value 512 marks an unused slot; the other entries of a row are distinct positions below that sequence's valid_len.
All inputs are finite; a program needn't handle non-finite values.
Results may differ from the reference program's by a relative error of at most 0.014.
The reference program's roundings to bfloat16 on the way count: a program that leaves them out, or rounds other values in their place, can miss the bound.
Values may be sent and summed in bfloat16 or wider, within the bound.
No kernel may reach another device: no remote copies, remote signals or barrier semaphores. Data moves between devices by JAX's collectives and lax.ppermute only.
A program may use at most 192 MiB of HBM per device.

```python
import jax
import jax.numpy as jnp
from jax import lax

D = 768
H = 12
HD = 64
FF = 3072
LEN = 512
PICK = 128
SEQS = 64
TOKENS = 32768


def draw_common(key):
    base_key = jax.random.fold_in(key, 11)
    len_key, class_key, count_key, perm_key = jax.random.split(base_key, 4)
    lengths = jax.random.randint(len_key, (SEQS,), LEN // 2, LEN + 1)
    lengths = lengths.at[0].set(LEN)
    tail_class = jax.random.randint(class_key, (SEQS,), 0, 4)
    count_cap = jnp.minimum(jnp.left_shift(jnp.full((SEQS,), PICK, jnp.int32), tail_class) // 4, PICK)
    floor_count = jnp.maximum(count_cap // 2, 1)
    fraction = jax.random.randint(count_key, (SEQS,), 0, 1 << 20)
    counts = floor_count + jnp.right_shift(fraction * (count_cap - floor_count + 1), 20)
    seq_keys = jax.random.split(perm_key, SEQS)
    orders = jax.vmap(lambda seq_key: jax.random.permutation(seq_key, LEN))(seq_keys).astype(jnp.int32)
    outside = (orders >= lengths[:, None]).astype(jnp.int32)
    rank_order = jnp.argsort(outside, axis=1, stable=True)
    chosen = jnp.take_along_axis(orders, rank_order, axis=1)[:, :PICK]
    slot_index = jnp.arange(PICK)[None, :]
    picked = jnp.where(slot_index < counts[:, None], chosen, LEN).astype(jnp.int32)
    return (lengths.astype(jnp.int32), picked)


def draw_valid_len(key, part):
    return draw_common(key)[0]


def draw_picked(key, part):
    return draw_common(key)[1]


def steps_of(key, extent, cuts, least, high):
    factor_of, own = 1.0, jax.random.fold_in(key, 6)
    for dim, parts in cuts:
        draws = jnp.exp(jax.random.uniform(jax.random.fold_in(own, dim), (parts,), jnp.float32, least / len(cuts), high / len(cuts)))
        factor_of = factor_of * jnp.repeat(draws, extent[dim] // parts).reshape([-1 if axis == dim else 1 for axis in range(len(extent))])
    return factor_of


def bell_draw(rng, shape, width, most, pieces=(), kind=jnp.bfloat16):
    factor_of = steps_of(rng, shape, pieces, -0.22, 0.18) if pieces else 1.0
    values = jax.random.normal(rng, shape, jnp.float32) * width * factor_of
    return jnp.minimum(jnp.maximum(values, -most), most).astype(kind)


def setup_inputs(seed: int = 0) -> dict:
    key_list = jax.random.split(jax.random.key(seed), 15)
    return {
        "tokens": bell_draw(key_list[0], (TOKENS, D), 1.0, 6.0, ((0, 32),)),
        "w_qkv": bell_draw(key_list[1], (3, D, D), D ** -0.5, 0.21875, ((2, 4),)),
        "qv_bias": bell_draw(key_list[2], (2, D), 0.3, 1.75, ((1, 4),), jnp.float32),
        "w_out": bell_draw(key_list[3], (D, D), (D // 32) ** -0.5, 1.25, ((0, 4),)),
        "out_bias": bell_draw(key_list[4], (D,), 0.3, 1.75, (), jnp.float32),
        "w_in": bell_draw(key_list[5], (D, FF), D ** -0.5, 0.21875, ((1, 4),)),
        "in_bias": bell_draw(key_list[6], (FF,), 0.3, 1.75, ((0, 4),), jnp.float32),
        "w_down": bell_draw(key_list[7], (FF, D), FF ** -0.5, 0.109375, ((0, 4),)),
        "down_bias": bell_draw(key_list[8], (D,), 0.3, 1.75, (), jnp.float32),
        "norm_gain": jnp.clip(1.0 + 0.1 * jax.random.normal(key_list[9], (2, D), jnp.float32), 0.5, 1.5),
        "norm_shift": bell_draw(key_list[10], (2, D), 0.3, 1.75, (), jnp.float32),
        "valid_len": draw_valid_len(jax.random.fold_in(key_list[14], 71), 0),
        "picked": draw_picked(jax.random.fold_in(key_list[14], 71), 0),
        "d_out": bell_draw(key_list[13], (TOKENS, D), 1.0, 6.0, ((0, 32),)),
    }


@jax.custom_vjp
def low(v):
    return lax.optimization_barrier(v.astype(jnp.bfloat16)).astype(jnp.float32)

@jax.custom_vjp
def low_back(v):
    return v

def low_keep(v):
    return (low(v), None)

def low_pass(kept, grad):
    return (grad,)

def back_keep(v):
    return (v, None)

def back_low(kept, grad):
    return (low(grad),)
low.defvjp(low_keep, low_pass)
low_back.defvjp(back_keep, back_low)
norm_eps = 1e-06

def product(left, right):
    return jnp.dot(left, right, precision=lax.Precision.HIGHEST)

def norm_rows(values, gain, shift):
    average = lax.optimization_barrier(jnp.mean(values, axis=-1, keepdims=True))
    centered = values - average
    variance = lax.optimization_barrier(jnp.mean(centered * centered, axis=-1, keepdims=True))
    return centered * lax.rsqrt(variance + norm_eps) * gain + shift

def attend_one(item):
    queries, key_rows, values, length = item
    raw = low_back(jnp.einsum('qhd,khd->hqk', queries, key_rows, precision=lax.Precision.HIGHEST))
    keep = jnp.arange(LEN) < length
    logits = jnp.where(keep[None, None, :], raw * HD ** (-0.5), -1e+30)
    probs = low(jax.nn.softmax(logits, axis=-1))
    return jnp.einsum('hqk,khd->qhd', probs, values, precision=lax.Precision.HIGHEST)

def forward(tokens_f, w_qkv, qv_bias, w_out, out_bias, w_in, in_bias, w_down, down_bias, norm_gain, norm_shift, valid_len):
    projected = jnp.einsum('td,cde->cte', tokens_f, w_qkv, precision=lax.Precision.HIGHEST)
    bias_rows = jnp.stack([qv_bias[0], jnp.zeros_like(qv_bias[0]), qv_bias[1]])
    projected = low(low_back(projected + bias_rows[:, None, :]))
    shaped = projected.reshape(3, SEQS, LEN, H, HD)
    attended = lax.map(jax.checkpoint(attend_one), (shaped[0], shaped[1], shaped[2], valid_len))
    context = low(low_back(attended.reshape(TOKENS, D)))
    attn_sum = low_back(product(context, w_out)) + out_bias + tokens_f
    hidden = norm_rows(attn_sum, norm_gain[0], norm_shift[0])
    pre_act = low_back(product(low(hidden), w_in) + in_bias)
    activated = low(jax.nn.gelu(pre_act, approximate=False))
    ffn_sum = low_back(product(activated, w_down)) + down_bias + hidden
    return norm_rows(ffn_sum, norm_gain[1], norm_shift[1])

def reference(tokens, w_qkv, qv_bias, w_out, out_bias, w_in, in_bias, w_down, down_bias, norm_gain, norm_shift, valid_len, picked, d_out):
    positions = jnp.arange(LEN)
    hits = jnp.any(picked[:, None, :] == positions[None, :, None], axis=2)
    selected = hits.reshape(TOKENS).astype(jnp.float32)

    def layer(tokens_f, w_qkv_f, qv_bias_f, w_out_f, out_bias_f, w_in_f, in_bias_f, w_down_f, down_bias_f, gain_f, shift_f):
        return forward(tokens_f, w_qkv_f, qv_bias_f, w_out_f, out_bias_f, w_in_f, in_bias_f, w_down_f, down_bias_f, gain_f, shift_f, valid_len)
    result, pullback = jax.vjp(layer, tokens.astype(jnp.float32), w_qkv.astype(jnp.float32), qv_bias, w_out.astype(jnp.float32), out_bias, w_in.astype(jnp.float32), in_bias, w_down.astype(jnp.float32), down_bias, norm_gain, norm_shift)
    cotangent = d_out.astype(jnp.float32) * selected[:, None]
    grads = pullback(cotangent)
    return (result.astype(jnp.bfloat16), grads[0].astype(jnp.bfloat16), grads[1], grads[2], grads[3], grads[4], grads[5], grads[6], grads[7], grads[8], grads[9], grads[10])
```

```python
import jax
import jax.numpy as jnp
from jax import lax
from jax.experimental import pallas as pl
from jax.experimental.pallas import tpu as pltpu
from jax.sharding import PartitionSpec as P

HD = 64
SCALE = HD ** (-0.5)
NORM_EPS = 1e-06
MASKED = -1e30
HALF_ROOT = 0.5 ** 0.5
DENSITY = 0.3989422804014327
BF = jnp.bfloat16
F32 = jnp.float32


def nn(left, right):
    return lax.dot_general(left, right, (((1,), (0,)), ((), ())), preferred_element_type=F32)


def nt(left, right):
    return lax.dot_general(left, right, (((1,), (1,)), ((), ())), preferred_element_type=F32)


def tn(left, right):
    return lax.dot_general(left, right, (((0,), (0,)), ((), ())), preferred_element_type=F32)


def head_masks(width, dtype=BF):
    lane = lax.broadcasted_iota(jnp.int32, (1, width), 1) // HD
    return [(lane == head).astype(dtype) for head in range(width // HD)]


def one_hot_rows(column, length):
    slots = column.shape[0]
    return (lax.broadcasted_iota(jnp.int32, (slots, length), 1) == column).astype(F32).astype(BF)


def whole(shape):
    zeros = (0,) * len(shape)
    return pl.BlockSpec(shape, lambda *_: zeros)


def norm_forward(values, gain, shift):
    average = jnp.mean(values, axis=1, keepdims=True)
    centered = values - average
    inv_std = lax.rsqrt(jnp.mean(centered * centered, axis=1, keepdims=True) + NORM_EPS)
    normed = centered * inv_std
    return normed * gain + shift, normed, inv_std


def norm_backward(grad, normed, inv_std, gain):
    scaled = grad * gain
    first = jnp.mean(scaled, axis=1, keepdims=True)
    second = jnp.mean(scaled * normed, axis=1, keepdims=True)
    return inv_std * (scaled - first - normed * second)


def col_sum(values):
    return jnp.sum(values, axis=0, keepdims=True)


def attend_body(len_ref, x_ref, w_ref, b_ref, pick_ref, q_sel_ref, k_ref, v_ref, ctx_ref, ctx_sel_ref, ext_ref):
    rows, width = k_ref.shape
    length = len_ref[pl.program_id(0)]
    x = x_ref[...]
    queries = (nn(x, w_ref[0]) + b_ref[0:1, :]).astype(BF)
    key_rows = nn(x, w_ref[1]).astype(BF)
    values = (nn(x, w_ref[2]) + b_ref[1:2, :]).astype(BF)
    k_ref[...] = key_rows
    v_ref[...] = values
    ext_ref[:, :width] = values
    ext_ref[:, width:] = jnp.ones((rows, ext_ref.shape[1] - width), BF)
    picks = one_hot_rows(pick_ref[0], rows)
    q_sel_ref[...] = nn(picks, queries).astype(BF)
    scaled = queries * jnp.asarray(SCALE, BF)
    masks = head_masks(width)
    tile = min(256, rows)
    keep = lax.broadcasted_iota(jnp.int32, (tile, rows), 1) < length
    for start in range(0, rows, tile):
        total = jnp.zeros((tile, width), F32)
        for mask in masks:
            logits = nt(scaled[start : start + tile] * mask, key_rows)
            logits = jnp.where(keep, logits, MASKED)
            peak = jnp.max(logits, axis=1, keepdims=True)
            probs = jnp.exp(logits - peak).astype(BF)
            mixed = nn(probs, ext_ref[...])
            share = mixed[:, :width] / mixed[:, width : width + 1]
            total = jnp.where(mask.astype(F32) > 0.5, share, total)
        ctx_ref[start : start + tile, :] = total.astype(BF)
    ctx_sel_ref[...] = nn(picks, ctx_ref[...]).astype(BF)


def attend_forward(lengths, x, w, bias, pick_col):
    seqs, slots, _ = pick_col.shape
    rows = x.shape[0] // seqs
    depth = x.shape[1]
    width = w.shape[2]
    ext = -(-(width + 1) // 128) * 128
    row_spec = pl.BlockSpec((rows, width), lambda s, _: (s, 0))
    sel_spec = pl.BlockSpec((slots, width), lambda s, _: (s, 0))
    heads = width // HD
    return pl.pallas_call(
        attend_body,
        grid_spec=pltpu.PrefetchScalarGridSpec(
            num_scalar_prefetch=1,
            grid=(seqs,),
            in_specs=[
                pl.BlockSpec((rows, depth), lambda s, _: (s, 0)),
                whole(w.shape),
                whole(bias.shape),
                pl.BlockSpec((1, slots, 1), lambda s, _: (s, 0, 0)),
            ],
            out_specs=[sel_spec, row_spec, row_spec, row_spec, sel_spec],
            scratch_shapes=[pltpu.VMEM((rows, ext), BF)],
        ),
        out_shape=[
            jax.ShapeDtypeStruct((seqs * slots, width), BF),
            jax.ShapeDtypeStruct((seqs * rows, width), BF),
            jax.ShapeDtypeStruct((seqs * rows, width), BF),
            jax.ShapeDtypeStruct((seqs * rows, width), BF),
            jax.ShapeDtypeStruct((seqs * slots, width), BF),
        ],
        cost_estimate=pl.CostEstimate(
            flops=2 * seqs * rows * (3 * depth * width + heads * rows * 512),
            transcendentals=seqs * heads * rows * rows,
            bytes_accessed=2 * (x.size + w.size + 4 * seqs * rows * width),
        ),
        name="attend_forward",
    )(lengths, x, w, bias, pick_col)


def attend_back_body(len_ref, q_ref, k_ref, v_ref, d_ctx_ref, dq_ref, dk_ref, dv_ref, sums_ref):
    rows, width = k_ref.shape
    slots = q_ref.shape[0]
    length = len_ref[pl.program_id(0)]
    masks = head_masks(width)
    queries, d_ctx = q_ref[...], d_ctx_ref[...]
    key_rows, values = k_ref[...], v_ref[...]
    q_stack = jnp.concatenate([queries * mask for mask in masks], axis=0)
    d_stack = jnp.concatenate([d_ctx * mask for mask in masks], axis=0)
    logits = nt(key_rows, q_stack * jnp.asarray(SCALE, BF))
    keep = lax.broadcasted_iota(jnp.int32, logits.shape, 0) < length
    logits = jnp.where(keep, logits, MASKED)
    grown = jnp.exp(logits - jnp.max(logits, axis=0, keepdims=True))
    probs = grown * (1.0 / jnp.sum(grown, axis=0, keepdims=True))
    d_probs = nt(values, d_stack)
    inner = jnp.sum(probs * d_probs, axis=0, keepdims=True)
    d_raw = (probs * (d_probs - inner) * SCALE).astype(BF)
    dk_ref[...] = nn(d_raw, q_stack).astype(BF)
    d_values = nn(probs.astype(BF), d_stack).astype(BF)
    dv_ref[...] = d_values
    dq_stack = tn(d_raw, key_rows)
    dq = jnp.zeros((slots, width), F32)
    for head, mask in enumerate(masks):
        dq = jnp.where(mask.astype(F32) > 0.5, dq_stack[head * slots : (head + 1) * slots], dq)
    dq = dq.astype(BF)
    dq_ref[...] = dq
    sums_ref[0] = jnp.zeros(sums_ref.shape[1:], F32)
    sums_ref[0, 0:1, :] = col_sum(dq.astype(F32))
    sums_ref[0, 1:2, :] = col_sum(d_values.astype(F32))


def attend_backward(lengths, q_sel, k, v, d_ctx):
    seqs = lengths.shape[0]
    rows, slots, width = k.shape[0] // seqs, q_sel.shape[0] // seqs, k.shape[1]
    row_spec = pl.BlockSpec((rows, width), lambda s, _: (s, 0))
    sel_spec = pl.BlockSpec((slots, width), lambda s, _: (s, 0))
    heads = width // HD
    return pl.pallas_call(
        attend_back_body,
        grid_spec=pltpu.PrefetchScalarGridSpec(
            num_scalar_prefetch=1,
            grid=(seqs,),
            in_specs=[sel_spec, row_spec, row_spec, sel_spec],
            out_specs=[sel_spec, row_spec, row_spec, pl.BlockSpec((1, 8, width), lambda s, _: (s, 0, 0))],
        ),
        out_shape=[
            jax.ShapeDtypeStruct(q_sel.shape, BF),
            jax.ShapeDtypeStruct(k.shape, BF),
            jax.ShapeDtypeStruct(k.shape, BF),
            jax.ShapeDtypeStruct((seqs, 8, width), F32),
        ],
        cost_estimate=pl.CostEstimate(
            flops=2 * seqs * rows * slots * heads * 5 * 256,
            transcendentals=seqs * heads * rows * slots,
            bytes_accessed=2 * (4 * k.size + 3 * q_sel.size),
        ),
        name="attend_backward",
    )(lengths, q_sel, k, v, d_ctx)


def erf_gelu(values):
    return 0.5 * (1.0 + lax.erf(values * HALF_ROOT))


def ffn_picked_body(*refs, parts, seqs):
    it = iter(refs)
    pick_ref, x_ref, d_out_ref = next(it), next(it), next(it)
    ctx_refs = [next(it) for _ in range(parts)]
    wo_refs = [next(it) for _ in range(parts)]
    wi_refs = [next(it) for _ in range(parts)]
    wd_refs = [next(it) for _ in range(parts)]
    ib_refs = [next(it) for _ in range(parts)]
    ob_ref, db_ref, gain_ref, shift_ref = next(it), next(it), next(it), next(it)
    act_ref, d_pre_ref, x_sel_ref, low_ref, g2_ref, g1_ref, grad1_ref = (next(it) for _ in range(7))
    d_ctx_refs = [next(it) for _ in range(parts)]
    vec_ref = next(it)
    slope_ref = next(it)
    rows = x_ref.shape[0] // seqs
    slots = pick_ref.shape[1]
    d_rows = []
    for seq in range(seqs):
        picks = one_hot_rows(pick_ref[seq], rows)
        x_sel_ref[seq * slots : (seq + 1) * slots, :] = nn(picks, x_ref[seq * rows : (seq + 1) * rows, :]).astype(BF)
        d_rows.append(nn(picks, d_out_ref[seq * rows : (seq + 1) * rows, :]))
    cotangent = jnp.concatenate(d_rows, axis=0)
    attn_sum = x_sel_ref[...].astype(F32) + ob_ref[...]
    for part in range(parts):
        attn_sum = attn_sum + nn(ctx_refs[part][...], wo_refs[part][...])
    hidden, normed1, inv1 = norm_forward(attn_sum, gain_ref[0:1, :], shift_ref[0:1, :])
    low = hidden.astype(BF)
    low_ref[...] = low
    ffn_sum = hidden + db_ref[...]
    for part in range(parts):
        pre = nn(low, wi_refs[part][...]) + ib_refs[part][...]
        chance = erf_gelu(pre)
        slope_ref[part] = chance + pre * (DENSITY * jnp.exp(-0.5 * pre * pre))
        act = (pre * chance).astype(BF)
        act_ref[part] = act
        ffn_sum = ffn_sum + nn(act, wd_refs[part][...])
    _, normed2, inv2 = norm_forward(ffn_sum, gain_ref[1:2, :], shift_ref[1:2, :])
    grad2 = norm_backward(cotangent, normed2, inv2, gain_ref[1:2, :])
    vec_ref[...] = jnp.zeros(vec_ref.shape, F32)
    vec_ref[0:1, :] = col_sum(grad2)
    vec_ref[1:2, :] = col_sum(cotangent * normed2)
    vec_ref[2:3, :] = col_sum(cotangent)
    g2 = grad2.astype(BF)
    g2_ref[...] = g2
    d_hidden = grad2
    for part in range(parts):
        d_pre = (nt(g2, wd_refs[part][...]) * slope_ref[part]).astype(BF)
        d_pre_ref[part] = d_pre
        vec_ref[8 + part : 9 + part, :] = col_sum(d_pre.astype(F32))
        d_hidden = d_hidden + nt(d_pre, wi_refs[part][...])
    grad1 = norm_backward(d_hidden, normed1, inv1, gain_ref[0:1, :])
    vec_ref[3:4, :] = col_sum(grad1)
    vec_ref[4:5, :] = col_sum(d_hidden * normed1)
    vec_ref[5:6, :] = col_sum(d_hidden)
    grad1_ref[...] = grad1
    g1 = grad1.astype(BF)
    g1_ref[...] = g1
    for part in range(parts):
        d_ctx_refs[part][...] = nt(g1, wo_refs[part][...]).astype(BF)


def ffn_picked(pick_col, x, d_out, ctx_sel, w_out, w_in, w_down, in_bias, out_bias, down_bias, gain, shift):
    parts = len(w_out)
    seqs, slots, _ = pick_col.shape
    picked, depth = seqs * slots, x.shape[1]
    units, width = w_in[0].shape[1], ctx_sel[0].shape[1]
    operands = [pick_col, x, d_out, *ctx_sel, *w_out, *w_in, *w_down, *in_bias, out_bias, down_bias, gain, shift]
    shapes = [
        jax.ShapeDtypeStruct((parts, picked, units), BF),
        jax.ShapeDtypeStruct((parts, picked, units), BF),
        jax.ShapeDtypeStruct((picked, depth), BF),
        jax.ShapeDtypeStruct((picked, depth), BF),
        jax.ShapeDtypeStruct((picked, depth), BF),
        jax.ShapeDtypeStruct((picked, depth), BF),
        jax.ShapeDtypeStruct((picked, depth), F32),
        *[jax.ShapeDtypeStruct((picked, width), BF)] * parts,
        jax.ShapeDtypeStruct((8 + 8 * (-(-parts // 8)), depth), F32),
    ]
    vmem = pl.BlockSpec(memory_space=pltpu.VMEM)
    return pl.pallas_call(
        lambda *refs: ffn_picked_body(*refs, parts=parts, seqs=seqs),
        in_specs=[vmem] * len(operands),
        out_specs=[vmem] * len(shapes),
        out_shape=shapes,
        scratch_shapes=[pltpu.VMEM((parts, picked, units), F32)],
        cost_estimate=pl.CostEstimate(
            flops=8 * picked * depth * units * parts, transcendentals=picked * units * parts, bytes_accessed=4 * parts * depth * units
        ),
        name="ffn_picked",
    )(*operands)


def ffn_rows_body(*refs, parts):
    it = iter(refs)
    x_ref = next(it)
    ctx_refs = [next(it) for _ in range(parts)]
    wo_refs = [next(it) for _ in range(parts)]
    wi_refs = [next(it) for _ in range(parts)]
    wd_refs = [next(it) for _ in range(parts)]
    ib_refs = [next(it) for _ in range(parts)]
    ob_ref, db_ref, gain_ref, shift_ref, out_ref = (next(it) for _ in range(5))
    attn_sum = x_ref[...].astype(F32) + ob_ref[...]
    for part in range(parts):
        attn_sum = attn_sum + nn(ctx_refs[part][...], wo_refs[part][...])
    hidden, _, _ = norm_forward(attn_sum, gain_ref[0:1, :], shift_ref[0:1, :])
    low = hidden.astype(BF)
    ffn_sum = hidden + db_ref[...]
    for part in range(parts):
        pre = nn(low, wi_refs[part][...]) + ib_refs[part][...]
        act = (pre * erf_gelu(pre)).astype(BF)
        ffn_sum = ffn_sum + nn(act, wd_refs[part][...])
    out_ref[...] = norm_forward(ffn_sum, gain_ref[1:2, :], shift_ref[1:2, :])[0].astype(BF)


def ffn_rows(x, ctx, w_out, w_in, w_down, in_bias, out_bias, down_bias, gain, shift):
    parts = len(w_out)
    rows, depth = x.shape
    units, width = w_in[0].shape[1], ctx[0].shape[1]
    tile = min(256, rows)
    fixed = [*w_out, *w_in, *w_down, *in_bias, out_bias, down_bias, gain, shift]
    return pl.pallas_call(
        lambda *refs: ffn_rows_body(*refs, parts=parts),
        grid=(rows // tile,),
        in_specs=[
            pl.BlockSpec((tile, depth), lambda i: (i, 0)),
            *[pl.BlockSpec((tile, width), lambda i: (i, 0))] * parts,
            *[pl.BlockSpec(a.shape, lambda i: (0, 0), pipeline_mode=pl.Buffered(1)) for a in fixed],
        ],
        out_specs=pl.BlockSpec((tile, depth), lambda i: (i, 0)),
        out_shape=jax.ShapeDtypeStruct((rows, depth), BF),
        cost_estimate=pl.CostEstimate(
            flops=4 * rows * depth * units * parts, transcendentals=rows * units * parts, bytes_accessed=4 * parts * depth * units
        ),
        name="ffn_rows",
    )(x, *ctx, *fixed)


def d_tokens_body(*refs, parts):
    it = iter(refs)
    pick_ref, grad1_ref = next(it), next(it)
    dq_refs = [next(it) for _ in range(parts)]
    dk_refs = [next(it) for _ in range(parts)]
    dv_refs = [next(it) for _ in range(parts)]
    w_refs = [next(it) for _ in range(parts)]
    out_ref = next(it)
    rows = out_ref.shape[0]
    slots = grad1_ref.shape[0]
    chosen = grad1_ref[...]
    for part in range(parts):
        chosen = chosen + nt(dq_refs[part][...], w_refs[part][0])
    high = chosen.astype(BF)
    rest = (chosen - high.astype(F32)).astype(BF)
    spread = (lax.broadcasted_iota(jnp.int32, (rows, slots), 0) == pick_ref[0]).astype(F32).astype(BF)
    total = nn(spread, high) + nn(spread, rest)
    for part in range(parts):
        total = total + nt(dk_refs[part][...], w_refs[part][1])
        total = total + nt(dv_refs[part][...], w_refs[part][2])
    out_ref[...] = total.astype(BF)


def input_gradient(pick_row, grad1, dq, dk, dv, w_qkv):
    parts = len(dq)
    seqs, _, slots = pick_row.shape
    depth = grad1.shape[1]
    rows, width = dk[0].shape[0] // seqs, dk[0].shape[1]
    row_spec = pl.BlockSpec((rows, width), lambda s: (s, 0))
    return pl.pallas_call(
        lambda *refs: d_tokens_body(*refs, parts=parts),
        grid=(seqs,),
        in_specs=[
            pl.BlockSpec((1, 1, slots), lambda s: (s, 0, 0)),
            pl.BlockSpec((slots, depth), lambda s: (s, 0)),
            *[pl.BlockSpec((slots, width), lambda s: (s, 0))] * parts,
            *[row_spec] * (2 * parts),
            *[whole(w.shape) for w in w_qkv],
        ],
        out_specs=pl.BlockSpec((rows, depth), lambda s: (s, 0)),
        out_shape=jax.ShapeDtypeStruct((seqs * rows, depth), BF),
        cost_estimate=pl.CostEstimate(
            flops=4 * seqs * rows * depth * width * parts, transcendentals=0, bytes_accessed=4 * seqs * rows * width * parts
        ),
        name="input_gradient",
    )(pick_row, grad1, *dq, *dk, *dv, *w_qkv)


def bits_of(count):
    return [1 << b for b in range(count.bit_length() - 1)]


def swap(value, axis, bit):
    count = lax.axis_size(axis)
    return lax.ppermute(value, axis, [(i, i ^ bit) for i in range(count)])


def gather_parts(value):
    parts = {0: value}
    for bit in reversed(bits_of(lax.axis_size("tp"))):
        for j in list(parts):
            parts[j | bit] = swap(parts[j], "tp", bit)
    return [parts[j] for j in range(len(parts))]


def scatter_parts(parts):
    parts = dict(enumerate(parts))
    for bit in bits_of(lax.axis_size("tp")):
        for j in [j for j in parts if not j & bit]:
            parts[j] = parts[j] + swap(parts.pop(j | bit), "tp", bit)
    return parts[0]


def all_sum_dp(value):
    index = lax.axis_index("dp")
    bits = bits_of(lax.axis_size("dp"))
    for bit in bits:
        half = value.shape[0] // 2
        upper = (index & bit) != 0
        mine, other = jnp.where(upper, half, 0), jnp.where(upper, 0, half)
        sent = swap(lax.dynamic_slice_in_dim(value, other, half, 0), "dp", bit)
        value = lax.dynamic_slice_in_dim(value, mine, half, 0) + sent
    for bit in reversed(bits):
        got = swap(value, "dp", bit)
        upper = (index & bit) != 0
        value = jnp.concatenate([jnp.where(upper, got, value), jnp.where(upper, value, got)], axis=0)
    return value


def all_sum_small(own, common):
    parts = dict(enumerate(own))
    size = own[0].shape[0]
    for bit in bits_of(lax.axis_size("tp")):
        keep = [j for j in parts if not j & bit]
        got = swap(jnp.concatenate([parts[j | bit] for j in keep] + [common]), "tp", bit)
        parts = {j: parts[j] + got[n * size : (n + 1) * size] for n, j in enumerate(keep)}
        common = common + got[len(keep) * size :]
    joined = jnp.concatenate([parts[0], common])
    for bit in bits_of(lax.axis_size("dp")):
        joined = joined + swap(joined, "dp", bit)
    return joined[:size], joined[size:]


def on_device(
    tokens, w_qkv, qv_bias, w_out, out_bias, w_in, in_bias, w_down, down_bias, norm_gain, norm_shift, valid_len, picked, d_out
):
    parts = lax.axis_size("tp")
    rank = lax.axis_index("tp")
    seqs = valid_len.shape[0] // parts
    depth = tokens.shape[1]
    width = w_qkv.shape[2]
    units = w_in.shape[1]

    lengths = lax.dynamic_slice_in_dim(valid_len, rank * seqs, seqs, 0)
    picks = lax.dynamic_slice_in_dim(picked, rank * seqs, seqs, 0)
    pick_col, pick_row = picks[:, :, None], picks[:, None, :]

    small = gather_parts(jnp.concatenate([qv_bias.reshape(-1), in_bias]))
    qv_parts = [s[: 2 * width].reshape(2, width) for s in small]
    ib_parts = [s[2 * width :].reshape(1, units) for s in small]
    wq_parts = gather_parts(w_qkv)
    wo_parts = gather_parts(w_out)
    wi_parts = gather_parts(w_in)
    wd_parts = gather_parts(w_down)
    ob_row, db_row = out_bias.reshape(1, depth), down_bias.reshape(1, depth)

    q_sel, k, v, ctx, ctx_sel = zip(
        *[attend_forward(lengths, tokens, wq_parts[j], qv_parts[j], pick_col) for j in range(parts)]
    )
    act, d_pre, x_sel, low, g2, g1, grad1, *rest = ffn_picked(
        pick_col, tokens, d_out, ctx_sel, wo_parts, wi_parts, wd_parts, ib_parts, ob_row, db_row, norm_gain, norm_shift
    )
    d_ctx, vec = rest[:parts], rest[parts]
    g_down = all_sum_dp(scatter_parts([tn(act[j], g2).astype(BF) for j in range(parts)]))
    g_in = all_sum_dp(scatter_parts([tn(low, d_pre[j]).astype(BF) for j in range(parts)]))
    dq, dk, dv, sums = zip(*[attend_backward(lengths, q_sel[j], k[j], v[j], d_ctx[j]) for j in range(parts)])
    g_out = all_sum_dp(scatter_parts([tn(ctx_sel[j], g1).astype(BF) for j in range(parts)]))
    g_qkv = all_sum_dp(
        scatter_parts(
            [
                jnp.concatenate([tn(x_sel, dq[j]), tn(tokens, dk[j]), tn(tokens, dv[j])], axis=1).astype(BF)
                for j in range(parts)
            ]
        )
    )
    out = ffn_rows(tokens, ctx, wo_parts, wi_parts, wd_parts, ib_parts, ob_row, db_row, norm_gain, norm_shift)
    d_tokens = input_gradient(pick_row, grad1, dq, dk, dv, wq_parts)

    own = [jnp.concatenate([vec[8 + j], jnp.sum(sums[j], axis=0)[:2].reshape(-1)]) for j in range(parts)]
    own, common = all_sum_small(own, vec[:6].reshape(-1))
    common = common.reshape(6, depth)
    return (
        out,
        d_tokens,
        g_qkv.astype(F32).reshape(depth, 3, width).transpose(1, 0, 2),
        own[units:].reshape(2, width),
        g_out.astype(F32),
        common[3],
        g_in.astype(F32),
        own[:units],
        g_down.astype(F32),
        common[0],
        jnp.stack([common[4], common[1]]),
        jnp.stack([common[5], common[2]]),
    )


def solution(mesh):
    placed = (
        P(("dp", "tp"), None),
        P(None, None, "tp"),
        P(None, "tp"),
        P("tp", None),
        P(),
        P(None, "tp"),
        P("tp"),
        P("tp", None),
        P(),
        P(),
        P(),
        P("dp"),
        P("dp", None),
        P(("dp", "tp"), None),
    )
    return jax.shard_map(
        on_device,
        mesh=mesh,
        in_specs=placed,
        out_specs=(
            P(("dp", "tp"), None),
            P(("dp", "tp"), None),
            P(None, None, "tp"),
            P(None, "tp"),
            P("tp", None),
            P(),
            P(None, "tp"),
            P("tp"),
            P("tp", None),
            P(),
            P(),
            P(),
        ),
        check_vma=False,
    )
```

```python
import jax
import jax.numpy as jnp
from jax import lax
from jax.experimental import pallas as pl
from jax.experimental.pallas import tpu as pltpu
from jax.sharding import PartitionSpec as P

HD = 64
SCALE = HD ** (-0.5)
NORM_EPS = 1e-06
MASKED = -1e30
HALF_ROOT = 0.5 ** 0.5
DENSITY = 0.3989422804014327
BF = jnp.bfloat16
F32 = jnp.float32


def nn(left, right):
    return lax.dot_general(left, right, (((1,), (0,)), ((), ())), preferred_element_type=F32)


def nt(left, right):
    return lax.dot_general(left, right, (((1,), (1,)), ((), ())), preferred_element_type=F32)


def tn(left, right):
    return lax.dot_general(left, right, (((0,), (0,)), ((), ())), preferred_element_type=F32)


def head_masks(width, dtype=BF):
    lane = lax.broadcasted_iota(jnp.int32, (1, width), 1) // HD
    return [(lane == head).astype(dtype) for head in range(width // HD)]


def one_hot_rows(column, length):
    slots = column.shape[0]
    return (lax.broadcasted_iota(jnp.int32, (slots, length), 1) == column).astype(F32).astype(BF)


def whole(shape):
    zeros = (0,) * len(shape)
    return pl.BlockSpec(shape, lambda *_: zeros)


def norm_forward(values, gain, shift):
    average = jnp.mean(values, axis=1, keepdims=True)
    centered = values - average
    inv_std = lax.rsqrt(jnp.mean(centered * centered, axis=1, keepdims=True) + NORM_EPS)
    normed = centered * inv_std
    return normed * gain + shift, normed, inv_std


def norm_backward(grad, normed, inv_std, gain):
    scaled = grad * gain
    first = jnp.mean(scaled, axis=1, keepdims=True)
    second = jnp.mean(scaled * normed, axis=1, keepdims=True)
    return inv_std * (scaled - first - normed * second)


def tie(value, *others):
    return lax.optimization_barrier((value, others))[0]


SMALL = pl.CostEstimate(flops=1024, transcendentals=0, bytes_accessed=1024)


def col_sum(values):
    return jnp.sum(values, axis=0, keepdims=True)


def attend_body(len_ref, x_ref, w_ref, b_ref, pick_ref, q_sel_ref, k_ref, v_ref, ctx_ref, ctx_sel_ref, ext_ref):
    rows, width = k_ref.shape
    length = len_ref[pl.program_id(0)]
    x = x_ref[...]
    queries = (nt(x, w_ref[0:width, :]) + b_ref[0:1, :]).astype(BF)
    key_rows = nt(x, w_ref[width : 2 * width, :]).astype(BF)
    values = (nt(x, w_ref[2 * width : 3 * width, :]) + b_ref[1:2, :]).astype(BF)
    k_ref[...] = key_rows
    v_ref[...] = values
    ext_ref[:, :width] = values
    ext_ref[:, width:] = jnp.ones((rows, ext_ref.shape[1] - width), BF)
    picks = one_hot_rows(pick_ref[0], rows)
    q_sel_ref[...] = nn(picks, queries).astype(BF)
    scaled = queries * jnp.asarray(SCALE, BF)
    masks = head_masks(width)
    tile = min(256, rows)
    keep = lax.broadcasted_iota(jnp.int32, (tile, rows), 1) < length
    for start in range(0, rows, tile):
        total = jnp.zeros((tile, width), F32)
        for mask in masks:
            logits = nt(scaled[start : start + tile] * mask, key_rows)
            logits = jnp.where(keep, logits, MASKED)
            peak = jnp.max(logits, axis=1, keepdims=True)
            probs = jnp.exp(logits - peak).astype(BF)
            mixed = nn(probs, ext_ref[...])
            share = mixed[:, :width] / mixed[:, width : width + 1]
            total = jnp.where(mask.astype(F32) > 0.5, share, total)
        ctx_ref[start : start + tile, :] = total.astype(BF)
    ctx_sel_ref[...] = nn(picks, ctx_ref[...]).astype(BF)


def attend_forward(lengths, x, proj, bias, pick_col):
    seqs, slots, _ = pick_col.shape
    rows = x.shape[0] // seqs
    depth = x.shape[1]
    width = bias.shape[1]
    ext = -(-(width + 1) // 128) * 128
    row_spec = pl.BlockSpec((rows, width), lambda s, _: (s, 0))
    sel_spec = pl.BlockSpec((slots, width), lambda s, _: (s, 0))
    return pl.pallas_call(
        attend_body,
        grid_spec=pltpu.PrefetchScalarGridSpec(
            num_scalar_prefetch=1,
            grid=(seqs,),
            in_specs=[
                pl.BlockSpec((rows, depth), lambda s, _: (s, 0)),
                whole(proj.shape),
                whole(bias.shape),
                pl.BlockSpec((1, slots, 1), lambda s, _: (s, 0, 0)),
            ],
            out_specs=[sel_spec, row_spec, row_spec, row_spec, sel_spec],
            scratch_shapes=[pltpu.VMEM((rows, ext), BF)],
        ),
        out_shape=[
            jax.ShapeDtypeStruct((seqs * slots, width), BF),
            jax.ShapeDtypeStruct((seqs * rows, width), BF),
            jax.ShapeDtypeStruct((seqs * rows, width), BF),
            jax.ShapeDtypeStruct((seqs * rows, width), BF),
            jax.ShapeDtypeStruct((seqs * slots, width), BF),
        ],
        cost_estimate=SMALL,
        name="attend_forward",
    )(lengths, x, proj, bias, pick_col)


def attend_back_body(
    len_ref, q_ref, k_ref, v_ref, d_ctx_ref, x_ref, x_sel_ref, ctx_sel_ref, g1_ref, dq_ref, dk_ref, dv_ref, sums_ref, grad_ref, acc_ref
):
    rows, width = k_ref.shape
    slots = q_ref.shape[0]
    seq = pl.program_id(0)
    length = len_ref[seq]
    masks = head_masks(width)
    queries, d_ctx = q_ref[...], d_ctx_ref[...]
    key_rows, values = k_ref[...], v_ref[...]
    q_stack = jnp.concatenate([queries * mask for mask in masks], axis=0)
    d_stack = jnp.concatenate([d_ctx * mask for mask in masks], axis=0)
    logits = nt(key_rows, q_stack * jnp.asarray(SCALE, BF))
    keep = lax.broadcasted_iota(jnp.int32, logits.shape, 0) < length
    logits = jnp.where(keep, logits, MASKED)
    grown = jnp.exp(logits - jnp.max(logits, axis=0, keepdims=True))
    probs = grown * (1.0 / jnp.sum(grown, axis=0, keepdims=True))
    d_probs = nt(values, d_stack)
    inner = jnp.sum(probs * d_probs, axis=0, keepdims=True)
    d_raw = (probs * (d_probs - inner) * SCALE).astype(BF)
    d_keys = nn(d_raw, q_stack).astype(BF)
    dk_ref[...] = d_keys
    d_values = nn(probs.astype(BF), d_stack).astype(BF)
    dv_ref[...] = d_values
    dq_stack = tn(d_raw, key_rows)
    dq = jnp.zeros((slots, width), F32)
    for head, mask in enumerate(masks):
        dq = jnp.where(mask.astype(F32) > 0.5, dq_stack[head * slots : (head + 1) * slots], dq)
    dq = dq.astype(BF)
    dq_ref[...] = dq
    sums_ref[0] = jnp.zeros(sums_ref.shape[1:], F32)
    sums_ref[0, 0:1, :] = col_sum(dq.astype(F32))
    sums_ref[0, 1:2, :] = col_sum(d_values.astype(F32))

    @pl.when(seq == 0)
    def _():
        acc_ref[...] = jnp.zeros(acc_ref.shape, F32)

    acc_ref[0:width, :] += tn(dq, x_sel_ref[...])
    acc_ref[width : 2 * width, :] += tn(d_keys, x_ref[...])
    acc_ref[2 * width : 3 * width, :] += tn(d_values, x_ref[...])
    acc_ref[3 * width : 4 * width, :] += tn(ctx_sel_ref[...], g1_ref[...])

    @pl.when(seq == pl.num_programs(0) - 1)
    def _():
        grad_ref[...] = acc_ref[...].astype(BF)


def attend_backward(lengths, q_sel, k, v, d_ctx, x, x_sel, ctx_sel, g1):
    seqs = lengths.shape[0]
    rows, slots, width = k.shape[0] // seqs, q_sel.shape[0] // seqs, k.shape[1]
    depth = x.shape[1]
    row_spec = pl.BlockSpec((rows, width), lambda s, _: (s, 0))
    sel_spec = pl.BlockSpec((slots, width), lambda s, _: (s, 0))
    wide_spec = pl.BlockSpec((slots, depth), lambda s, _: (s, 0))
    return pl.pallas_call(
        attend_back_body,
        grid_spec=pltpu.PrefetchScalarGridSpec(
            num_scalar_prefetch=1,
            grid=(seqs,),
            in_specs=[
                sel_spec,
                row_spec,
                row_spec,
                sel_spec,
                pl.BlockSpec((rows, depth), lambda s, _: (s, 0)),
                wide_spec,
                sel_spec,
                wide_spec,
            ],
            out_specs=[
                sel_spec,
                row_spec,
                row_spec,
                pl.BlockSpec((1, 8, width), lambda s, _: (s, 0, 0)),
                pl.BlockSpec((4 * width, depth), lambda s, _: (0, 0)),
            ],
            scratch_shapes=[pltpu.VMEM((4 * width, depth), F32)],
        ),
        out_shape=[
            jax.ShapeDtypeStruct(q_sel.shape, BF),
            jax.ShapeDtypeStruct(k.shape, BF),
            jax.ShapeDtypeStruct(k.shape, BF),
            jax.ShapeDtypeStruct((seqs, 8, width), F32),
            jax.ShapeDtypeStruct((4 * width, depth), BF),
        ],
        cost_estimate=SMALL,
        name="attend_backward",
    )(lengths, q_sel, k, v, d_ctx, x, x_sel, ctx_sel, g1)


def erf_gelu(values):
    return 0.5 * (1.0 + lax.erf(values * HALF_ROOT))


def piece_copies(pieces, target, sems, first, bit):
    half = target.shape[1] // 2
    own = ((lax.axis_index("dp") // bit) % 2) * half
    copies, sem = [], first
    for part, refs in enumerate(pieces):
        if len(refs) == 1:
            copies.append([pltpu.make_async_copy(refs[0], target.at[part], sems.at[sem])])
        else:
            copies.append(
                [
                    pltpu.make_async_copy(refs[0], target.at[part, pl.ds(pl.multiple_of(own, half), half), :], sems.at[sem]),
                    pltpu.make_async_copy(refs[1], target.at[part, pl.ds(pl.multiple_of(half - own, half), half), :], sems.at[sem + 1]),
                ]
            )
        sem += len(refs)
    return copies


def take(it, pieces):
    return [[next(it) for _ in piece] for piece in pieces]


def flat(pieces):
    return [p for piece in pieces for p in piece]


def wait_all(copies):
    for copy in copies:
        copy.wait()


def ffn_front_body(*refs, parts, seqs, wi, wd):
    it = iter(refs)
    pick_ref, x_ref, d_out_ref = next(it), next(it), next(it)
    ctx_refs = [next(it) for _ in range(parts)]
    wo_refs = [next(it) for _ in range(parts)]
    wi_refs, wd_refs = take(it, wi), take(it, wd)
    ib_refs = [next(it) for _ in range(parts)]
    ob_ref, db_ref, gain_ref, shift_ref = next(it), next(it), next(it), next(it)
    gd_refs = [next(it) for _ in range(parts)]
    slope_ref, x_sel_ref, low_ref, grad2_ref, g2_ref, normed1_ref, inv1_ref, vec_ref = (next(it) for _ in range(8))
    wi_v, wd_v, act_ref, gd_v, in_sems, out_sems = (next(it) for _ in range(6))
    in_copies = piece_copies(wi_refs, wi_v, in_sems, 0, 1)
    down_copies = piece_copies(wd_refs, wd_v, in_sems, len(flat(wi_refs)), 2)
    for part in range(parts):
        for copy in in_copies[part] + down_copies[part]:
            copy.start()
    rows = x_ref.shape[0] // seqs
    slots = pick_ref.shape[1]
    d_rows = []
    for seq in range(seqs):
        picks = one_hot_rows(pick_ref[seq], rows)
        x_sel_ref[seq * slots : (seq + 1) * slots, :] = nn(picks, x_ref[seq * rows : (seq + 1) * rows, :]).astype(BF)
        d_rows.append(nn(picks, d_out_ref[seq * rows : (seq + 1) * rows, :]))
    cotangent = jnp.concatenate(d_rows, axis=0)
    attn_sum = x_sel_ref[...].astype(F32) + ob_ref[...]
    for part in range(parts):
        attn_sum = attn_sum + nn(ctx_refs[part][...], wo_refs[part][...])
    hidden, normed1, inv1 = norm_forward(attn_sum, gain_ref[0:1, :], shift_ref[0:1, :])
    low = hidden.astype(BF)
    low_ref[...] = low
    normed1_ref[...] = normed1
    inv1_ref[...] = inv1
    ffn_sum = hidden + db_ref[...]
    for part in range(parts):
        wait_all(in_copies[part])
        pre = nn(low, wi_v[part]) + ib_refs[part][...]
        chance = erf_gelu(pre)
        slope_ref[part] = chance + pre * (DENSITY * jnp.exp(-0.5 * pre * pre))
        act = (pre * chance).astype(BF)
        act_ref[part] = act
        wait_all(down_copies[part])
        ffn_sum = ffn_sum + nn(act, wd_v[part])
    _, normed2, inv2 = norm_forward(ffn_sum, gain_ref[1:2, :], shift_ref[1:2, :])
    grad2 = norm_backward(cotangent, normed2, inv2, gain_ref[1:2, :])
    g2 = grad2.astype(BF)
    out_copies = []
    for part in reversed(range(parts)):
        gd_v[part] = tn(act_ref[part], g2).astype(BF)
        out_copies.append(pltpu.make_async_copy(gd_v.at[part], gd_refs[part], out_sems.at[part]))
        out_copies[-1].start()
    vec_ref[...] = jnp.zeros(vec_ref.shape, F32)
    vec_ref[0:1, :] = col_sum(grad2)
    vec_ref[1:2, :] = col_sum(cotangent * normed2)
    vec_ref[2:3, :] = col_sum(cotangent)
    grad2_ref[...] = grad2
    g2_ref[...] = g2
    wait_all(out_copies)


VMEM_SPEC = pl.BlockSpec(memory_space=pltpu.VMEM)
ANY_SPEC = pl.BlockSpec(memory_space=pl.ANY)


def out_weights(proj, width):
    return pl.BlockSpec((width, proj.shape[1]), lambda *_: (3, 0))


def shaped(shape):
    return pl.BlockSpec(shape, lambda *_: (0,) * len(shape))


def ffn_front(pick_col, x, d_out, ctx_sel, proj, wi, wd, in_bias, out_bias, down_bias, gain, shift):
    parts = len(proj)
    seqs, slots, _ = pick_col.shape
    picked, depth = seqs * slots, x.shape[1]
    units, width = in_bias[0].shape[1], ctx_sel[0].shape[1]
    plain = [pick_col, x, d_out, *ctx_sel]
    rest = [*in_bias, out_bias, down_bias, gain, shift]
    pieces = flat(wi) + flat(wd)
    shapes = [
        *[jax.ShapeDtypeStruct((units, depth), BF)] * parts,
        jax.ShapeDtypeStruct((parts, picked, units), F32),
        jax.ShapeDtypeStruct((picked, depth), BF),
        jax.ShapeDtypeStruct((picked, depth), BF),
        jax.ShapeDtypeStruct((picked, depth), F32),
        jax.ShapeDtypeStruct((picked, depth), BF),
        jax.ShapeDtypeStruct((picked, depth), F32),
        jax.ShapeDtypeStruct((picked, 1), F32),
        jax.ShapeDtypeStruct((8, depth), F32),
    ]
    return pl.pallas_call(
        lambda *refs: ffn_front_body(*refs, parts=parts, seqs=seqs, wi=wi, wd=wd),
        grid=(1,),
        in_specs=[
            *[shaped(a.shape) for a in plain],
            *[out_weights(p, width) for p in proj],
            *[ANY_SPEC] * len(pieces),
            *[shaped(a.shape) for a in rest],
        ],
        out_specs=[*[ANY_SPEC] * parts, *[shaped(a.shape) for a in shapes[parts:]]],
        out_shape=shapes,
        scratch_shapes=[
            pltpu.VMEM((parts, depth, units), BF),
            pltpu.VMEM((parts, units, depth), BF),
            pltpu.VMEM((parts, picked, units), BF),
            pltpu.VMEM((parts, units, depth), BF),
            pltpu.SemaphoreType.DMA((len(pieces),)),
            pltpu.SemaphoreType.DMA((parts,)),
        ],
        cost_estimate=SMALL,
        name="ffn_front",
    )(*plain, *proj, *pieces, *rest)


def ffn_back_body(*refs, parts, wi, wd):
    it = iter(refs)
    g2_ref, grad2_ref, low_ref, normed1_ref, inv1_ref, gain_ref = (next(it) for _ in range(6))
    wo_refs = [next(it) for _ in range(parts)]
    slope_hbm = next(it)
    wi_refs, wd_refs = take(it, wi), take(it, wd)
    gi_refs = [next(it) for _ in range(parts)]
    g1_ref, grad1_ref = next(it), next(it)
    d_ctx_refs = [next(it) for _ in range(parts)]
    vec_ref = next(it)
    wi_v, wd_v, slope_v, gi_v, in_sems, out_sems = (next(it) for _ in range(6))
    count = len(flat(wi_refs)) + len(flat(wd_refs))
    in_copies = piece_copies(wi_refs, wi_v, in_sems, 0, 1)
    down_copies = piece_copies(wd_refs, wd_v, in_sems, len(flat(wi_refs)), 2)
    slope_copies = [pltpu.make_async_copy(slope_hbm.at[part], slope_v.at[part], in_sems.at[count + part]) for part in range(parts)]
    order = list(reversed(range(parts)))
    for part in order:
        for copy in down_copies[part] + [slope_copies[part]] + in_copies[part]:
            copy.start()
    vec_ref[...] = jnp.zeros(vec_ref.shape, F32)
    g2, low = g2_ref[...], low_ref[...]
    d_hidden = grad2_ref[...]
    out_copies = []
    for part in order:
        wait_all(down_copies[part] + [slope_copies[part]])
        d_pre = (nt(g2, wd_v[part]) * slope_v[part]).astype(BF)
        gi_v[part] = tn(low, d_pre).astype(BF)
        out_copies.append(pltpu.make_async_copy(gi_v.at[part], gi_refs[part], out_sems.at[part]))
        out_copies[-1].start()
        vec_ref[8 + part : 9 + part, :] = col_sum(d_pre.astype(F32))
        wait_all(in_copies[part])
        d_hidden = d_hidden + nt(d_pre, wi_v[part])
    normed1 = normed1_ref[...]
    grad1 = norm_backward(d_hidden, normed1, inv1_ref[...], gain_ref[0:1, :])
    vec_ref[3:4, :] = col_sum(grad1)
    vec_ref[4:5, :] = col_sum(d_hidden * normed1)
    vec_ref[5:6, :] = col_sum(d_hidden)
    grad1_ref[...] = grad1
    g1 = grad1.astype(BF)
    g1_ref[...] = g1
    for part in range(parts):
        d_ctx_refs[part][...] = nt(g1, wo_refs[part][...]).astype(BF)
    wait_all(out_copies)


def ffn_back(g2, grad2, low, normed1, inv1, gain, proj, slope, wi, wd, width):
    parts = len(proj)
    picked, depth = g2.shape
    units = slope.shape[2]
    plain = [g2, grad2, low, normed1, inv1, gain]
    pieces = flat(wi) + flat(wd)
    shapes = [
        *[jax.ShapeDtypeStruct((depth, units), BF)] * parts,
        jax.ShapeDtypeStruct((picked, depth), BF),
        jax.ShapeDtypeStruct((picked, depth), F32),
        *[jax.ShapeDtypeStruct((picked, width), BF)] * parts,
        jax.ShapeDtypeStruct((8 + 8 * (-(-parts // 8)), depth), F32),
    ]
    return pl.pallas_call(
        lambda *refs: ffn_back_body(*refs, parts=parts, wi=wi, wd=wd),
        grid=(1,),
        in_specs=[
            *[shaped(a.shape) for a in plain],
            *[out_weights(p, width) for p in proj],
            ANY_SPEC,
            *[ANY_SPEC] * len(pieces),
        ],
        out_specs=[*[ANY_SPEC] * parts, *[shaped(a.shape) for a in shapes[parts:]]],
        out_shape=shapes,
        scratch_shapes=[
            pltpu.VMEM((parts, depth, units), BF),
            pltpu.VMEM((parts, units, depth), BF),
            pltpu.VMEM((parts, picked, units), F32),
            pltpu.VMEM((parts, depth, units), BF),
            pltpu.SemaphoreType.DMA((len(pieces) + parts,)),
            pltpu.SemaphoreType.DMA((parts,)),
        ],
        cost_estimate=SMALL,
        name="ffn_back",
    )(*plain, *proj, slope, *pieces)


def ffn_rows_body(*refs, parts, wi, wd):
    it = iter(refs)
    x_ref = next(it)
    ctx_refs = [next(it) for _ in range(parts)]
    wo_refs = [next(it) for _ in range(parts)]
    ib_refs = [next(it) for _ in range(parts)]
    ob_ref, db_ref, gain_ref, shift_ref = (next(it) for _ in range(4))
    wi_refs, wd_refs = take(it, wi), take(it, wd)
    out_ref = next(it)
    wi_v, wd_v, sems = (next(it) for _ in range(3))
    in_copies = piece_copies(wi_refs, wi_v, sems, 0, 1)
    down_copies = piece_copies(wd_refs, wd_v, sems, len(flat(wi_refs)), 2)
    first = pl.program_id(0) == 0

    @pl.when(first)
    def _():
        for part in range(parts):
            for copy in in_copies[part] + down_copies[part]:
                copy.start()

    attn_sum = x_ref[...].astype(F32) + ob_ref[...]
    for part in range(parts):
        attn_sum = attn_sum + nn(ctx_refs[part][...], wo_refs[part][...])
    hidden, _, _ = norm_forward(attn_sum, gain_ref[0:1, :], shift_ref[0:1, :])
    low = hidden.astype(BF)
    ffn_sum = hidden + db_ref[...]

    @pl.when(first)
    def _():
        for part in range(parts):
            wait_all(in_copies[part] + down_copies[part])

    for part in range(parts):
        pre = nn(low, wi_v[part]) + ib_refs[part][...]
        act = (pre * erf_gelu(pre)).astype(BF)
        ffn_sum = ffn_sum + nn(act, wd_v[part])
    out_ref[...] = norm_forward(ffn_sum, gain_ref[1:2, :], shift_ref[1:2, :])[0].astype(BF)


def ffn_rows(x, ctx, proj, wi, wd, in_bias, out_bias, down_bias, gain, shift):
    parts = len(proj)
    rows, depth = x.shape
    units, width = in_bias[0].shape[1], ctx[0].shape[1]
    tile = min(256, rows)
    fixed = [*in_bias, out_bias, down_bias, gain, shift]
    pieces = flat(wi) + flat(wd)
    return pl.pallas_call(
        lambda *refs: ffn_rows_body(*refs, parts=parts, wi=wi, wd=wd),
        grid=(rows // tile,),
        in_specs=[
            pl.BlockSpec((tile, depth), lambda i: (i, 0)),
            *[pl.BlockSpec((tile, width), lambda i: (i, 0))] * parts,
            *[out_weights(p, width) for p in proj],
            *[shaped(a.shape) for a in fixed],
            *[ANY_SPEC] * len(pieces),
        ],
        out_specs=pl.BlockSpec((tile, depth), lambda i: (i, 0)),
        out_shape=jax.ShapeDtypeStruct((rows, depth), BF),
        scratch_shapes=[
            pltpu.VMEM((parts, depth, units), BF),
            pltpu.VMEM((parts, units, depth), BF),
            pltpu.SemaphoreType.DMA((len(pieces),)),
        ],
        cost_estimate=SMALL,
        name="ffn_rows",
    )(x, *ctx, *proj, *fixed, *pieces)


def d_tokens_body(*refs, parts):
    it = iter(refs)
    pick_ref, grad1_ref = next(it), next(it)
    dq_refs = [next(it) for _ in range(parts)]
    dk_refs = [next(it) for _ in range(parts)]
    dv_refs = [next(it) for _ in range(parts)]
    w_refs = [next(it) for _ in range(parts)]
    out_ref = next(it)
    rows = out_ref.shape[0]
    slots = grad1_ref.shape[0]
    width = dk_refs[0].shape[1]
    chosen = grad1_ref[...]
    for part in range(parts):
        chosen = chosen + nn(dq_refs[part][...], w_refs[part][0:width, :])
    high = chosen.astype(BF)
    rest = (chosen - high.astype(F32)).astype(BF)
    spread = (lax.broadcasted_iota(jnp.int32, (rows, slots), 0) == pick_ref[0]).astype(F32).astype(BF)
    total = nn(spread, high) + nn(spread, rest)
    for part in range(parts):
        total = total + nn(dk_refs[part][...], w_refs[part][width : 2 * width, :])
        total = total + nn(dv_refs[part][...], w_refs[part][2 * width : 3 * width, :])
    out_ref[...] = total.astype(BF)


def input_gradient(pick_row, grad1, dq, dk, dv, proj):
    parts = len(dq)
    seqs, _, slots = pick_row.shape
    depth = grad1.shape[1]
    rows, width = dk[0].shape[0] // seqs, dk[0].shape[1]
    row_spec = pl.BlockSpec((rows, width), lambda s: (s, 0))
    return pl.pallas_call(
        lambda *refs: d_tokens_body(*refs, parts=parts),
        grid=(seqs,),
        in_specs=[
            pl.BlockSpec((1, 1, slots), lambda s: (s, 0, 0)),
            pl.BlockSpec((slots, depth), lambda s: (s, 0)),
            *[pl.BlockSpec((slots, width), lambda s: (s, 0))] * parts,
            *[row_spec] * (2 * parts),
            *[whole(w.shape) for w in proj],
        ],
        out_specs=pl.BlockSpec((rows, depth), lambda s: (s, 0)),
        out_shape=jax.ShapeDtypeStruct((seqs * rows, depth), BF),
        cost_estimate=SMALL,
        name="input_gradient",
    )(pick_row, grad1, *dq, *dk, *dv, *proj)


def bits_of(count):
    return [1 << b for b in range(count.bit_length() - 1)]


def swap(value, axis, bit):
    count = lax.axis_size(axis)
    return lax.ppermute(value, axis, [(i, i ^ bit) for i in range(count)])


def half_of(value, bit, own):
    half = value.shape[0] // 2
    side = (lax.axis_index("dp") // bit) % 2
    return lax.dynamic_slice_in_dim(value, jnp.where(side == 0, 0, half) if own else jnp.where(side == 0, half, 0), half, 0)


def joined(own, got, bit):
    side = (lax.axis_index("dp") // bit) % 2
    return jnp.concatenate([jnp.where(side == 0, own, got), jnp.where(side == 0, got, own)], axis=0)


def add(*values):
    total = values[0].astype(F32)
    for value in values[1:]:
        total = total + value.astype(F32)
    return total.astype(BF)


def on_device(
    tokens, w_qkv, qv_bias, w_out, out_bias, w_in, in_bias, w_down, down_bias, norm_gain, norm_shift, valid_len, picked, d_out
):
    parts = lax.axis_size("tp")
    rank = lax.axis_index("tp")
    seqs = valid_len.shape[0] // parts
    depth = tokens.shape[1]
    width = w_qkv.shape[2]
    units = w_in.shape[1]
    core, far = 1, 2
    dp_bits = bits_of(lax.axis_size("dp"))

    lengths = lax.dynamic_slice_in_dim(valid_len, rank * seqs, seqs, 0)
    picks = lax.dynamic_slice_in_dim(picked, rank * seqs, seqs, 0)
    pick_col, pick_row = picks[:, :, None], picks[:, None, :]

    small = [jnp.concatenate([qv_bias.reshape(-1), in_bias])]
    proj = [jnp.concatenate([w_qkv.transpose(0, 2, 1).reshape(3 * width, depth), w_out], axis=0)]
    small += [swap(small[0], "tp", core), swap(small[0], "tp", far)]
    small += [swap(small[2], "tp", core)]
    proj_far = swap(half_of(proj[0], 1, True), "tp", far)
    proj += [swap(proj[0], "tp", core)]
    in_far = swap(tie(half_of(w_in, 1, True), small[1]), "tp", far)
    down_far = swap(tie(half_of(w_down, 2, True), small[3]), "tp", far)
    in_near, down_near = swap(w_in, "tp", core), swap(w_down, "tp", core)

    qv_parts = [s[: 2 * width].reshape(2, width) for s in small]
    ib_parts = [s[2 * width :].reshape(1, units) for s in small]
    ob_row, db_row = out_bias.reshape(1, depth), down_bias.reshape(1, depth)

    def forward(j, x):
        return attend_forward(lengths, x, proj[j], qv_parts[j], pick_col)

    parts_out = [forward(0, tie(tokens, small[1]))]
    parts_out += [forward(1, tie(tokens, parts_out[0][0]))]
    proj_far = tie(proj_far, parts_out[1][0])
    proj_far_core = swap(proj_far, "tp", core)
    proj_rest = swap(proj_far, "dp", 1)
    in_far = tie(in_far, proj_rest)
    in_far_core = swap(in_far, "tp", core)
    in_rest = swap(in_far, "dp", 1)
    proj += [joined(proj_far, proj_rest, 1)]
    proj += [joined(proj_far_core, swap(proj_rest, "tp", core), 1)]
    parts_out += [forward(2, tie(tokens, parts_out[1][0], in_far))]
    down_far = tie(down_far, parts_out[2][0])
    down_far_core = swap(down_far, "tp", core)
    down_rest = swap(down_far, "dp", 2)
    parts_out += [forward(3, tie(tokens, parts_out[2][0], down_far))]
    in_rest_core = swap(tie(in_rest, parts_out[3][0]), "tp", core)
    down_rest_core = swap(tie(down_rest, parts_out[3][0]), "tp", core)
    wi = [[w_in], [in_near], [in_far, in_rest], [in_far_core, in_rest_core]]
    wd = [[w_down], [down_near], [down_far, down_rest], [down_far_core, down_rest_core]]
    q_sel, k, v, ctx, ctx_sel = zip(*parts_out)

    front = ffn_front(pick_col, tokens, d_out, ctx_sel, proj, wi, wd, ib_parts, ob_row, db_row, norm_gain, norm_shift)
    g_down = front[:parts]
    slope, x_sel, low, grad2, g2, normed1, inv1, vec = front[parts:]
    back = ffn_back(g2, grad2, low, normed1, inv1, norm_gain, proj, slope, wi, wd, width)
    g_in = back[:parts]
    g1, grad1, *rest = back[parts:]
    d_ctx, vec2 = rest[:parts], rest[parts]

    def near_sums(grads):
        far_sum = add(grads[2], swap(grads[3], "tp", core))
        return far_sum, (grads[0], swap(grads[1], "tp", core))

    def far_step(grads_sum):
        far_sum, near = grads_sum
        return add(*near, swap(far_sum, "tp", far))

    def backward(j, x):
        return attend_backward(lengths, q_sel[j], k[j], v[j], d_ctx[j], x, x_sel, ctx_sel[j], g1)

    sum_a = near_sums(g_down)
    sum_b = near_sums(g_in)
    out3 = backward(3, tie(tokens, sum_a[0]))
    out2 = backward(2, tie(tokens, out3[0], sum_b[0]))
    far_c = add(out2[4], swap(out3[4], "tp", core))
    out1 = backward(1, tie(tokens, out2[0], far_c))
    out0 = backward(0, tie(tokens, out1[0]))
    dq, dk, dv, sums, g_heads = zip(out0, out1, out2, out3)
    sum_c = far_c, (g_heads[0], swap(g_heads[1], "tp", core))

    def scatter(value, bit, order=None):
        sent, kept = half_of(value, bit, False), half_of(value, bit, True)
        return add(kept, swap(sent, "dp", bit))

    def gather(value, bit):
        return joined(value, swap(value, "dp", bit), bit)

    total_a = far_step(sum_a)
    total_a = tie(total_a, out0[0])
    sent_a = half_of(total_a, dp_bits[0], False)
    half_rows = tokens.shape[0] // 2

    def rows_of(first, x):
        return ffn_rows(
            x[first : first + half_rows],
            [c[first : first + half_rows] for c in ctx],
            proj, wi, wd, ib_parts, ob_row, db_row, norm_gain, norm_shift,
        )

    out_first = rows_of(0, tie(tokens, sent_a))
    total_a = add(half_of(total_a, dp_bits[0], True), tie(swap(sent_a, "dp", dp_bits[0]), out_first))
    out_second = rows_of(half_rows, tie(tokens, total_a, out_first))
    for bit in dp_bits[1:2]:
        total_a = scatter(total_a, bit)
    total_b = far_step(sum_b)
    d_tokens = input_gradient(tie(pick_row, out_second, total_a), grad1, dq, dk, dv, proj)
    for bit in dp_bits[2:]:
        total_a = scatter(total_a, bit)
    for bit in reversed(dp_bits):
        total_a = gather(total_a, bit)
    for bit in dp_bits:
        total_b = scatter(total_b, bit)
    for bit in reversed(dp_bits):
        total_b = gather(total_b, bit)
    total_c = far_step(sum_c)
    own = [jnp.concatenate([vec2[8 + j], jnp.sum(sums[j], axis=0)[:2].reshape(-1)]) for j in range(parts)]
    common = jnp.concatenate([vec[:3].reshape(-1), vec2[3:6].reshape(-1)])
    size = own[0].shape[0]
    got = swap(jnp.concatenate([own[1], own[3], common]), "tp", core)
    own = [own[0] + got[:size], own[2] + got[size : 2 * size]]
    common = common + got[2 * size :]
    got = swap(tie(jnp.concatenate([own[1], common]), total_c), "tp", far)
    line = jnp.concatenate([own[0] + got[:size], common + got[size:]])
    for bit in dp_bits:
        total_c = scatter(total_c, bit)
        line = line + swap(line, "dp", bit)
    for bit in reversed(dp_bits):
        total_c = gather(total_c, bit)
    own, common = line[:size], line[size:].reshape(6, depth)
    total_c = total_c.astype(F32)
    return (
        jnp.concatenate([out_first, out_second], axis=0),
        d_tokens,
        total_c[: 3 * width].reshape(3, width, depth).transpose(0, 2, 1),
        own[units:].reshape(2, width),
        total_c[3 * width :],
        common[3],
        total_b.astype(F32),
        own[:units],
        total_a.astype(F32),
        common[0],
        jnp.stack([common[4], common[1]]),
        jnp.stack([common[5], common[2]]),
    )


def solution(mesh):
    placed = (
        P(("dp", "tp"), None),
        P(None, None, "tp"),
        P(None, "tp"),
        P("tp", None),
        P(),
        P(None, "tp"),
        P("tp"),
        P("tp", None),
        P(),
        P(),
        P(),
        P("dp"),
        P("dp", None),
        P(("dp", "tp"), None),
    )
    return jax.shard_map(
        on_device,
        mesh=mesh,
        in_specs=placed,
        out_specs=(
            P(("dp", "tp"), None),
            P(("dp", "tp"), None),
            P(None, None, "tp"),
            P(None, "tp"),
            P("tp", None),
            P(),
            P(None, "tp"),
            P("tp"),
            P("tp", None),
            P(),
            P(),
            P(),
        ),
        check_vma=False,
    )
```

```python
import jax
import jax.numpy as jnp
from jax import lax
from jax.experimental import pallas as pl
from jax.experimental.pallas import tpu as pltpu
from jax.sharding import PartitionSpec as P

HD = 64
SCALE = HD ** (-0.5)
NORM_EPS = 1e-06
MASKED = -1e30
HALF_ROOT = 0.5 ** 0.5
DENSITY = 0.3989422804014327
PARTS = 4
BF = jnp.bfloat16
F32 = jnp.float32


def nn(left, right):
    return lax.dot_general(left, right, (((1,), (0,)), ((), ())), preferred_element_type=F32)


def nt(left, right):
    return lax.dot_general(left, right, (((1,), (1,)), ((), ())), preferred_element_type=F32)


def tn(left, right):
    return lax.dot_general(left, right, (((0,), (0,)), ((), ())), preferred_element_type=F32)


def head_masks(width, dtype=BF):
    lane = lax.broadcasted_iota(jnp.int32, (1, width), 1) // HD
    return [(lane == head).astype(dtype) for head in range(width // HD)]


def spread_of(picks, length):
    slots = picks.shape[1]
    return (lax.broadcasted_iota(jnp.int32, (length, slots), 0) == picks).astype(F32).astype(BF)


def whole(shape):
    zeros = (0,) * len(shape)
    return pl.BlockSpec(shape, lambda *_: zeros)


def norm_forward(values, gain, shift):
    average = jnp.mean(values, axis=1, keepdims=True)
    centered = values - average
    inv_std = lax.rsqrt(jnp.mean(centered * centered, axis=1, keepdims=True) + NORM_EPS)
    normed = centered * inv_std
    return normed * gain + shift, normed, inv_std


def norm_backward(grad, normed, inv_std, gain):
    scaled = grad * gain
    first = jnp.mean(scaled, axis=1, keepdims=True)
    second = jnp.mean(scaled * normed, axis=1, keepdims=True)
    return inv_std * (scaled - first - normed * second)


def tie(value, *others):
    return lax.optimization_barrier((value, others))[0]


LARGE = pl.CostEstimate(flops=20_000_000_000, transcendentals=0, bytes_accessed=1024)
SMALL = pl.CostEstimate(flops=1024, transcendentals=0, bytes_accessed=1024)


def col_sum(values):
    return jnp.sum(values, axis=0, keepdims=True)


def piece_copies(pieces, target, sems, first, bit):
    rows = target.shape[0]
    if len(pieces) == 1:
        return [pltpu.make_async_copy(pieces[0][0], target, sems.at[first])]
    half, step = rows // 2, rows // len(pieces)
    own = ((lax.axis_index("dp") // bit) % 2) * half
    copies = []
    for n, (ref, skip) in enumerate(pieces):
        base = own if n * step < half else half - own
        start = pl.multiple_of(base + (n * step) % half, step)
        copies.append(pltpu.make_async_copy(ref.at[pl.ds(skip, step), :], target.at[pl.ds(start, step), :], sems.at[first + n]))
    return copies


def stacked_copies(pieces, target, sems, first, bit):
    copies = []
    for part, refs in enumerate(pieces):
        copies.append(piece_copies(refs, target.at[part], sems, first, bit))
        first += len(refs)
    return copies


def take(it, pieces):
    return [[(next(it), skip) for _, skip in piece] for piece in pieces]


def flat(pieces):
    return [p for piece in pieces for p in piece]


def arrays(pieces):
    return [array for array, _ in flat(pieces)]


def start_all(copies):
    for copy in copies:
        copy.start()


def wait_all(copies):
    for copy in copies:
        copy.wait()


ANY_SPEC = pl.BlockSpec(memory_space=pl.ANY)


def shaped(shape):
    return pl.BlockSpec(shape, lambda *_: (0,) * len(shape))


def attend_body(len_ref, x_ref, small_ref, pick_ref, *rest, count):
    w_refs = [(ref, 0) for ref in rest[:count]]
    q_sel_ref, k_ref, v_ref, ctx_ref, ctx_sel_ref, ext_ref, w_ref, sems = rest[count:]
    rows, width = k_ref.shape
    seq = pl.program_id(0)
    row = lax.axis_index("tp") * pl.num_programs(0) + seq
    length = len_ref[row]
    copies = piece_copies(w_refs, w_ref, sems, 0, 1)

    @pl.when(seq == 0)
    def _():
        start_all(copies)
        wait_all(copies)

    x = x_ref[...]
    queries = (nt(x, w_ref[0:width, :]) + small_ref[1:2, :width]).astype(BF)
    key_rows = nt(x, w_ref[width : 2 * width, :]).astype(BF)
    values = (nt(x, w_ref[2 * width : 3 * width, :]) + small_ref[2:3, :width]).astype(BF)
    k_ref[...] = key_rows
    v_ref[...] = values
    ext_ref[:, :width] = values
    ext_ref[:, width:] = jnp.ones((rows, ext_ref.shape[1] - width), BF)
    spread = spread_of(pick_ref[pl.ds(row, 1), :], rows)
    q_sel_ref[...] = tn(spread, queries).astype(BF)
    scaled = queries * jnp.asarray(SCALE, BF)
    masks = head_masks(width)
    tile = min(256, rows)
    keep = lax.broadcasted_iota(jnp.int32, (tile, rows), 1) < length
    for start in range(0, rows, tile):
        total = jnp.zeros((tile, width), F32)
        for mask in masks:
            logits = nt(scaled[start : start + tile] * mask, key_rows)
            logits = jnp.where(keep, logits, MASKED)
            peak = jnp.max(logits, axis=1, keepdims=True)
            probs = jnp.exp(logits - peak).astype(BF)
            mixed = nn(probs, ext_ref[...])
            share = mixed[:, :width] / mixed[:, width : width + 1]
            total = jnp.where(mask.astype(F32) > 0.5, share, total)
        ctx_ref[start : start + tile, :] = total.astype(BF)
    ctx_sel_ref[...] = tn(spread, ctx_ref[...]).astype(BF)


def attend_forward(lengths, x, pieces, width, small, picked, seqs):
    slots = picked.shape[1]
    rows = x.shape[0] // seqs
    depth = x.shape[1]
    ext = -(-(width + 1) // 128) * 128
    row_spec = pl.BlockSpec((rows, width), lambda s, _: (s, 0))
    sel_spec = pl.BlockSpec((slots, width), lambda s, _: (s, 0))
    return pl.pallas_call(
        lambda *refs: attend_body(*refs, count=len(pieces)),
        grid_spec=pltpu.PrefetchScalarGridSpec(
            num_scalar_prefetch=1,
            grid=(seqs,),
            in_specs=[
                pl.BlockSpec((rows, depth), lambda s, _: (s, 0)),
                whole(small.shape),
                whole(picked.shape),
                *[ANY_SPEC] * len(pieces),
            ],
            out_specs=[sel_spec, row_spec, row_spec, row_spec, sel_spec],
            scratch_shapes=[
                pltpu.VMEM((rows, ext), BF),
                pltpu.VMEM((3 * width, depth), BF),
                pltpu.SemaphoreType.DMA((len(pieces),)),
            ],
        ),
        out_shape=[
            jax.ShapeDtypeStruct((seqs * slots, width), BF),
            jax.ShapeDtypeStruct((seqs * rows, width), BF),
            jax.ShapeDtypeStruct((seqs * rows, width), BF),
            jax.ShapeDtypeStruct((seqs * rows, width), BF),
            jax.ShapeDtypeStruct((seqs * slots, width), BF),
        ],
        cost_estimate=SMALL,
        name="attend_forward",
    )(lengths, x, small, picked, *pieces)


def attend_back_body(
    len_ref, q_ref, k_ref, v_ref, d_ctx_ref, x_ref, x_sel_ref, ctx_sel_ref, g1_ref, dq_ref, dk_ref, dv_ref, sums_ref, grad_ref, acc_ref, *, part
):
    rows, width = k_ref.shape
    slots = q_ref.shape[0]
    seq = pl.program_id(0)
    rank = lax.axis_index("tp")
    length = len_ref[rank * pl.num_programs(0) + seq]
    masks = head_masks(width)
    queries, d_ctx = q_ref[...], d_ctx_ref[...]
    key_rows, values = k_ref[...], v_ref[...]
    q_stack = jnp.concatenate([queries * mask for mask in masks], axis=0)
    d_stack = jnp.concatenate([d_ctx * mask for mask in masks], axis=0)
    logits = nt(key_rows, q_stack * jnp.asarray(SCALE, BF))
    keep = lax.broadcasted_iota(jnp.int32, logits.shape, 0) < length
    logits = jnp.where(keep, logits, MASKED)
    grown = jnp.exp(logits - jnp.max(logits, axis=0, keepdims=True))
    probs = grown * (1.0 / jnp.sum(grown, axis=0, keepdims=True))
    d_probs = nt(values, d_stack)
    inner = jnp.sum(probs * d_probs, axis=0, keepdims=True)
    d_raw = (probs * (d_probs - inner) * SCALE).astype(BF)
    d_keys = nn(d_raw, q_stack).astype(BF)
    dk_ref[...] = d_keys
    d_values = nn(probs.astype(BF), d_stack).astype(BF)
    dv_ref[...] = d_values
    dq_stack = tn(d_raw, key_rows)
    dq = jnp.zeros((slots, width), F32)
    for head, mask in enumerate(masks):
        dq = jnp.where(mask.astype(F32) > 0.5, dq_stack[head * slots : (head + 1) * slots], dq)
    dq = dq.astype(BF)
    dq_ref[...] = dq

    @pl.when(seq == 0)
    def _():
        acc_ref[...] = jnp.zeros(acc_ref.shape, F32)
        sums_ref[...] = jnp.zeros(sums_ref.shape, F32)

    at = rank ^ part
    sums_ref[pl.ds(at, 1), 0:width] += col_sum(dq.astype(F32))
    sums_ref[pl.ds(PARTS + at, 1), 0:width] += col_sum(d_values.astype(F32))
    acc_ref[0:width, :] += tn(dq, x_sel_ref[...])
    acc_ref[width : 2 * width, :] += tn(d_keys, x_ref[...])
    acc_ref[2 * width : 3 * width, :] += tn(d_values, x_ref[...])
    acc_ref[3 * width : 4 * width, :] += tn(ctx_sel_ref[...], g1_ref[...])

    @pl.when(seq == pl.num_programs(0) - 1)
    def _():
        grad_ref[...] = acc_ref[...].astype(BF)


def attend_backward(part, lengths, q_sel, k, v, d_ctx, x, x_sel, ctx_sel, g1, seqs):
    rows, slots, width = k.shape[0] // seqs, q_sel.shape[0] // seqs, k.shape[1]
    depth = x.shape[1]
    row_spec = pl.BlockSpec((rows, width), lambda s, _: (s, 0))
    sel_spec = pl.BlockSpec((slots, width), lambda s, _: (s, 0))
    wide_spec = pl.BlockSpec((slots, depth), lambda s, _: (s, 0))
    return pl.pallas_call(
        lambda *refs: attend_back_body(*refs, part=part),
        grid_spec=pltpu.PrefetchScalarGridSpec(
            num_scalar_prefetch=1,
            grid=(seqs,),
            in_specs=[
                sel_spec,
                row_spec,
                row_spec,
                sel_spec,
                pl.BlockSpec((rows, depth), lambda s, _: (s, 0)),
                wide_spec,
                sel_spec,
                wide_spec,
            ],
            out_specs=[sel_spec, row_spec, row_spec, whole((2 * PARTS, depth)), whole((4 * width, depth))],
            scratch_shapes=[pltpu.VMEM((4 * width, depth), F32)],
        ),
        out_shape=[
            jax.ShapeDtypeStruct(q_sel.shape, BF),
            jax.ShapeDtypeStruct(k.shape, BF),
            jax.ShapeDtypeStruct(k.shape, BF),
            jax.ShapeDtypeStruct((2 * PARTS, depth), F32),
            jax.ShapeDtypeStruct((4 * width, depth), BF),
        ],
        cost_estimate=SMALL,
        name="attend_backward",
    )(lengths, q_sel, k, v, d_ctx, x, x_sel, ctx_sel, g1)


def erf_gelu(values):
    return 0.5 * (1.0 + lax.erf(values * HALF_ROOT))


def run(body, plain, hbm, outs, hbm_outs, scratch, name):
    return pl.pallas_call(
        body,
        grid=(1,),
        in_specs=[*[shaped(a.shape) for a in plain], *[ANY_SPEC] * len(hbm)],
        out_specs=[*[shaped(a.shape) for a in outs], *[ANY_SPEC] * len(hbm_outs)],
        out_shape=[*outs, *hbm_outs],
        scratch_shapes=scratch,
        cost_estimate=SMALL,
        name=name,
    )(*plain, *hbm)


def struct(dtype, *shape):
    return jax.ShapeDtypeStruct(shape, dtype)


def unit_part(low, wi, bias, act_ref, slope_ref, n):
    pre = nn(low, wi) + bias
    chance = erf_gelu(pre)
    slope_ref[n] = chance + pre * (DENSITY * jnp.exp(-0.5 * pre * pre))
    act = (pre * chance).astype(BF)
    act_ref[n] = act
    return act


def ffn_prep(picked, x, d_out, ctx_sel, wo, wi, wd, small, shared, seqs):
    parts, near = len(wo), len(wi)
    slots = picked.shape[1]
    count, depth, units, width = seqs * slots, x.shape[1], wi[0][0][0].shape[1], ctx_sel[0].shape[1]
    plain = [picked, x, d_out, shared, *ctx_sel, *small]
    hbm = arrays(wo) + arrays(wi) + arrays(wd)

    def body(*refs):
        it = iter(refs)
        pick_ref, x_ref, d_out_ref, shared_ref = (next(it) for _ in range(4))
        ctx_refs = [next(it) for _ in range(parts)]
        small_refs = [next(it) for _ in range(near)]
        wo_refs, wi_refs, wd_refs = take(it, wo), take(it, wi), take(it, wd)
        act_ref, slope_ref, x_sel_ref, cot_ref, low_ref, sum_ref, normed1_ref, inv1_ref = (next(it) for _ in range(8))
        wo_v, wi_v, wd_v, sems = (next(it) for _ in range(4))
        out_copies = stacked_copies(wo_refs, wo_v, sems, 0, 1)
        first = len(flat(wo))
        in_copies = stacked_copies(wi_refs, wi_v, sems, first, 1)
        down_copies = stacked_copies(wd_refs, wd_v, sems, first + len(flat(wi)), 2)
        start_all(flat(out_copies) + flat(in_copies) + flat(down_copies))
        rows = x_ref.shape[0] // seqs
        for seq in range(seqs):
            at = lax.axis_index("tp") * seqs + seq
            spread = spread_of(pick_ref[pl.ds(at, 1), :], rows)
            x_sel_ref[seq * slots : (seq + 1) * slots, :] = tn(spread, x_ref[seq * rows : (seq + 1) * rows, :]).astype(BF)
            cot_ref[seq * slots : (seq + 1) * slots, :] = tn(spread, d_out_ref[seq * rows : (seq + 1) * rows, :]).astype(BF)
        attn_sum = x_sel_ref[...].astype(F32) + shared_ref[0:1, :]
        wait_all(flat(out_copies))
        for part in range(parts):
            attn_sum = attn_sum + nn(ctx_refs[part][...], wo_v[part])
        hidden, normed1, inv1 = norm_forward(attn_sum, shared_ref[2:3, :], shared_ref[4:5, :])
        low = hidden.astype(BF)
        low_ref[...] = low
        normed1_ref[...] = normed1
        inv1_ref[...] = inv1
        total = hidden + shared_ref[1:2, :]
        wait_all(flat(in_copies) + flat(down_copies))
        for n in range(near):
            act = unit_part(low, wi_v[n], small_refs[n][0:1, :], act_ref, slope_ref, n)
            total = total + nn(act, wd_v[n])
        sum_ref[...] = total

    outs = [
        struct(BF, near, count, units),
        struct(F32, near, count, units),
        struct(BF, count, depth),
        struct(BF, count, depth),
        struct(BF, count, depth),
        struct(F32, count, depth),
        struct(F32, count, depth),
        struct(F32, count, 1),
    ]
    scratch = [
        pltpu.VMEM((parts, width, depth), BF),
        pltpu.VMEM((near, depth, units), BF),
        pltpu.VMEM((near, units, depth), BF),
        pltpu.SemaphoreType.DMA((len(hbm),)),
    ]
    return run(body, plain, hbm, outs, [], scratch, "ffn_prep")


def ffn_front(low, total, cot, act, wi, wd, small, shared):
    far, near = len(wi), act.shape[0]
    parts = near + far
    count, depth = low.shape
    units = act.shape[2]
    plain = [low, total, cot, shared, act, *small]
    hbm = arrays(wi) + arrays(wd)

    def body(*refs):
        it = iter(refs)
        low_ref, sum_ref, cot_ref, shared_ref, act_ref = (next(it) for _ in range(5))
        small_refs = [next(it) for _ in range(far)]
        wi_refs, wd_refs = take(it, wi), take(it, wd)
        slope_ref, grad2_ref, g2_ref, vec_ref = (next(it) for _ in range(4))
        gd_refs = [next(it) for _ in range(parts)]
        wi_v, wd_v, far_act, gd_v, sems, out_sems = (next(it) for _ in range(6))
        in_copies = stacked_copies(wi_refs, wi_v, sems, 0, 1)
        down_copies = stacked_copies(wd_refs, wd_v, sems, len(flat(wi)), 2)
        for n in range(far):
            start_all(in_copies[n] + down_copies[n])
        low = low_ref[...]
        total = sum_ref[...]
        for n in range(far):
            wait_all(in_copies[n])
            act = unit_part(low, wi_v[n], small_refs[n][0:1, :], far_act, slope_ref, n)
            wait_all(down_copies[n])
            total = total + nn(act, wd_v[n])
        _, normed2, inv2 = norm_forward(total, shared_ref[3:4, :], shared_ref[5:6, :])
        cotangent = cot_ref[...].astype(F32)
        grad2 = norm_backward(cotangent, normed2, inv2, shared_ref[3:4, :])
        g2 = grad2.astype(BF)
        copies = []
        for part in reversed(range(parts)):
            rows = act_ref[part] if part < near else far_act[part - near]
            gd_v[part] = tn(rows, g2).astype(BF)
            copies.append(pltpu.make_async_copy(gd_v.at[part], gd_refs[part], out_sems.at[part]))
            copies[-1].start()
        vec_ref[...] = jnp.zeros(vec_ref.shape, F32)
        vec_ref[0:1, :] = col_sum(grad2)
        vec_ref[1:2, :] = col_sum(cotangent * normed2)
        vec_ref[2:3, :] = col_sum(cotangent)
        grad2_ref[...] = grad2
        g2_ref[...] = g2
        wait_all(copies)

    outs = [struct(F32, far, count, units), struct(F32, count, depth), struct(BF, count, depth), struct(F32, 16, depth)]
    scratch = [
        pltpu.VMEM((far, depth, units), BF),
        pltpu.VMEM((far, units, depth), BF),
        pltpu.VMEM((far, count, units), BF),
        pltpu.VMEM((parts, units, depth), BF),
        pltpu.SemaphoreType.DMA((len(hbm),)),
        pltpu.SemaphoreType.DMA((parts,)),
    ]
    return run(body, plain, hbm, outs, [struct(BF, units, depth)] * parts, scratch, "ffn_front")


def ffn_mid(g2, low, slopes, wd):
    parts = len(wd)
    count, depth = g2.shape
    units = slopes[0].shape[2]
    hbm = [*slopes, *arrays(wd)]

    def body(*refs):
        it = iter(refs)
        g2_ref, low_ref = next(it), next(it)
        slope_hbm = [next(it) for _ in slopes]
        wd_refs = take(it, wd)
        d_pre_ref, vec_ref = next(it), next(it)
        gi_refs = [next(it) for _ in range(parts)]
        wd_v, slope_v, gi_v, sems, slope_sems, out_sems = (next(it) for _ in range(6))
        down_copies = stacked_copies(wd_refs, wd_v, sems, 0, 2)
        sources = [ref.at[n] for ref in slope_hbm for n in range(ref.shape[0])]
        slope_copies = [pltpu.make_async_copy(sources[part], slope_v.at[part], slope_sems.at[part]) for part in range(parts)]
        order = list(reversed(range(parts)))
        for part in order:
            start_all(down_copies[part] + [slope_copies[part]])
        vec_ref[...] = jnp.zeros(vec_ref.shape, F32)
        g2, low = g2_ref[...], low_ref[...]
        copies = []
        for part in order:
            wait_all(down_copies[part] + [slope_copies[part]])
            d_pre = (nt(g2, wd_v[part]) * slope_v[part]).astype(BF)
            d_pre_ref[part] = d_pre
            gi_v[part] = tn(low, d_pre).astype(BF)
            copies.append(pltpu.make_async_copy(gi_v.at[part], gi_refs[part], out_sems.at[part]))
            copies[-1].start()
            at = 8 + (lax.axis_index("tp") ^ part)
            vec_ref[pl.ds(at, 1), :] = col_sum(d_pre.astype(F32))
        wait_all(copies)

    outs = [struct(BF, parts, count, units), struct(F32, 16, depth)]
    scratch = [
        pltpu.VMEM((parts, units, depth), BF),
        pltpu.VMEM((parts, count, units), F32),
        pltpu.VMEM((parts, depth, units), BF),
        pltpu.SemaphoreType.DMA((len(flat(wd)),)),
        pltpu.SemaphoreType.DMA((parts,)),
        pltpu.SemaphoreType.DMA((parts,)),
    ]
    return run(body, [g2, low], hbm, outs, [struct(BF, depth, units)] * parts, scratch, "ffn_mid")


def ffn_back(grad2, d_pre, normed1, inv1, shared, wi, wo, width):
    parts = len(wi)
    count, depth = grad2.shape
    units = d_pre.shape[2]
    hbm = arrays(wi) + arrays(wo)

    def body(*refs):
        it = iter(refs)
        grad2_ref, d_pre_ref, normed1_ref, inv1_ref, shared_ref = (next(it) for _ in range(5))
        wi_refs, wo_refs = take(it, wi), take(it, wo)
        g1_ref, grad1_ref, vec_ref = next(it), next(it), next(it)
        d_ctx_refs = [next(it) for _ in range(parts)]
        wi_v, wo_v, sems = (next(it) for _ in range(3))
        in_copies = stacked_copies(wi_refs, wi_v, sems, 0, 1)
        out_copies = stacked_copies(wo_refs, wo_v, sems, len(flat(wi)), 1)
        start_all(flat(in_copies) + flat(out_copies))
        d_hidden = grad2_ref[...]
        for part in range(parts):
            wait_all(in_copies[part])
            d_hidden = d_hidden + nt(d_pre_ref[part], wi_v[part])
        normed1 = normed1_ref[...]
        grad1 = norm_backward(d_hidden, normed1, inv1_ref[...], shared_ref[2:3, :])
        vec_ref[...] = jnp.zeros(vec_ref.shape, F32)
        vec_ref[3:4, :] = col_sum(grad1)
        vec_ref[4:5, :] = col_sum(d_hidden * normed1)
        vec_ref[5:6, :] = col_sum(d_hidden)
        grad1_ref[...] = grad1
        g1 = grad1.astype(BF)
        g1_ref[...] = g1
        wait_all(flat(out_copies))
        for part in range(parts):
            d_ctx_refs[part][...] = nt(g1, wo_v[part]).astype(BF)

    outs = [struct(BF, count, depth), struct(F32, count, depth), struct(F32, 16, depth), *[struct(BF, count, width)] * parts]
    scratch = [
        pltpu.VMEM((parts, depth, units), BF),
        pltpu.VMEM((parts, width, depth), BF),
        pltpu.SemaphoreType.DMA((len(hbm),)),
    ]
    return run(body, [grad2, d_pre, normed1, inv1, shared], hbm, outs, [], scratch, "ffn_back")


def ffn_rows(x, ctx, wo, wi, wd, small, shared, first, count):
    parts = len(wo)
    depth = x.shape[1]
    units, width = wi[0][0][0].shape[1], ctx[0].shape[1]
    tile = min(256, count)
    start = first // tile
    hbm = arrays(wo) + arrays(wi) + arrays(wd)

    def body(*refs):
        it = iter(refs)
        x_ref = next(it)
        ctx_refs = [next(it) for _ in range(parts)]
        small_refs = [next(it) for _ in range(parts)]
        shared_ref = next(it)
        wo_refs, wi_refs, wd_refs = take(it, wo), take(it, wi), take(it, wd)
        out_ref, wo_v, wi_v, wd_v, sems = (next(it) for _ in range(5))
        out_copies = flat(stacked_copies(wo_refs, wo_v, sems, 0, 1))
        near = len(flat(wo))
        in_copies = stacked_copies(wi_refs, wi_v, sems, near, 1)
        down_copies = stacked_copies(wd_refs, wd_v, sems, near + len(flat(wi)), 2)
        opening = pl.program_id(0) == 0

        @pl.when(opening)
        def _():
            start_all(out_copies)
            for part in range(parts):
                start_all(in_copies[part] + down_copies[part])
            wait_all(out_copies)

        attn_sum = x_ref[...].astype(F32) + shared_ref[0:1, :]
        for part in range(parts):
            attn_sum = attn_sum + nn(ctx_refs[part][...], wo_v[part])
        hidden, _, _ = norm_forward(attn_sum, shared_ref[2:3, :], shared_ref[4:5, :])
        low = hidden.astype(BF)
        total = hidden + shared_ref[1:2, :]
        for part in range(parts):

            @pl.when(opening)
            def _():
                wait_all(in_copies[part] + down_copies[part])

            pre = nn(low, wi_v[part]) + small_refs[part][0:1, :]
            act = (pre * erf_gelu(pre)).astype(BF)
            total = total + nn(act, wd_v[part])
        out_ref[...] = norm_forward(total, shared_ref[3:4, :], shared_ref[5:6, :])[0].astype(BF)

    return pl.pallas_call(
        body,
        grid=(count // tile,),
        in_specs=[
            pl.BlockSpec((tile, depth), lambda i: (i + start, 0)),
            *[pl.BlockSpec((tile, width), lambda i: (i + start, 0))] * parts,
            *[shaped(a.shape) for a in small],
            shaped(shared.shape),
            *[ANY_SPEC] * len(hbm),
        ],
        out_specs=pl.BlockSpec((tile, depth), lambda i: (i, 0)),
        out_shape=jax.ShapeDtypeStruct((count, depth), BF),
        scratch_shapes=[
            pltpu.VMEM((parts, width, depth), BF),
            pltpu.VMEM((parts, depth, units), BF),
            pltpu.VMEM((parts, units, depth), BF),
            pltpu.SemaphoreType.DMA((len(hbm),)),
        ],
        cost_estimate=LARGE,
        name="ffn_rows",
    )(x, *ctx, *small, shared, *hbm)


def input_gradient(picked, grad1, dq, dk, dv, wq, seqs):
    parts = len(dq)
    slots = picked.shape[1]
    depth = grad1.shape[1]
    rows, width = dk[0].shape[0] // seqs, dk[0].shape[1]
    hbm = arrays(wq)

    def body(*refs):
        it = iter(refs)
        pick_ref, grad1_ref = next(it), next(it)
        dq_refs = [next(it) for _ in range(parts)]
        dk_refs = [next(it) for _ in range(parts)]
        dv_refs = [next(it) for _ in range(parts)]
        wq_refs = take(it, wq)
        out_ref, wq_v, sems = next(it), next(it), next(it)
        copies = flat(stacked_copies(wq_refs, wq_v, sems, 0, 1))
        seq = pl.program_id(0)

        @pl.when(seq == 0)
        def _():
            start_all(copies)
            wait_all(copies)

        chosen = grad1_ref[...]
        for part in range(parts):
            chosen = chosen + nn(dq_refs[part][...], wq_v[part, 0:width, :])
        high = chosen.astype(BF)
        rest = (chosen - high.astype(F32)).astype(BF)
        spread = spread_of(pick_ref[pl.ds(lax.axis_index("tp") * seqs + seq, 1), :], rows)
        total = nn(spread, high) + nn(spread, rest)
        for part in range(parts):
            total = total + nn(dk_refs[part][...], wq_v[part, width : 2 * width, :])
            total = total + nn(dv_refs[part][...], wq_v[part, 2 * width : 3 * width, :])
        out_ref[...] = total.astype(BF)

    row_spec = pl.BlockSpec((rows, width), lambda s: (s, 0))
    return pl.pallas_call(
        body,
        grid=(seqs,),
        in_specs=[
            whole(picked.shape),
            pl.BlockSpec((slots, depth), lambda s: (s, 0)),
            *[pl.BlockSpec((slots, width), lambda s: (s, 0))] * parts,
            *[row_spec] * (2 * parts),
            *[ANY_SPEC] * len(hbm),
        ],
        out_specs=pl.BlockSpec((rows, depth), lambda s: (s, 0)),
        out_shape=jax.ShapeDtypeStruct((seqs * rows, depth), BF),
        scratch_shapes=[pltpu.VMEM((parts, 3 * width, depth), BF), pltpu.SemaphoreType.DMA((len(hbm),))],
        cost_estimate=LARGE,
        name="input_gradient",
    )(picked, grad1, *dq, *dk, *dv, *hbm)


def bits_of(count):
    return [1 << b for b in range(count.bit_length() - 1)]


def swap(value, axis, bit):
    count = lax.axis_size(axis)
    return lax.ppermute(value, axis, [(i, i ^ bit) for i in range(count)])


def half_of(value, bit, own):
    half = value.shape[0] // 2
    side = (lax.axis_index("dp") // bit) % 2
    return lax.dynamic_slice_in_dim(value, jnp.where(side == 0, 0, half) if own else jnp.where(side == 0, half, 0), half, 0)


def joined(own, got, bit):
    side = (lax.axis_index("dp") // bit) % 2
    return jnp.concatenate([jnp.where(side == 0, own, got), jnp.where(side == 0, got, own)], axis=0)


def add(*values):
    total = values[0].astype(F32)
    for value in values[1:]:
        total = total + value.astype(F32)
    return total.astype(BF)


def scatter(value, bit, *after):
    sent, kept = half_of(value, bit, False), half_of(value, bit, True)
    return add(tie(kept, *after), swap(sent, "dp", bit))


def gather(value, bit):
    return joined(value, swap(value, "dp", bit), bit)


def on_device(
    tokens, w_qkv, qv_bias, w_out, out_bias, w_in, in_bias, w_down, down_bias, norm_gain, norm_shift, valid_len, picked, d_out
):
    parts = lax.axis_size("tp")
    rank = lax.axis_index("tp")
    seqs = valid_len.shape[0] // parts
    depth = tokens.shape[1]
    width = w_qkv.shape[2]
    core, far = 1, 2
    dp_bits = bits_of(lax.axis_size("dp"))

    shared = jnp.concatenate([out_bias[None], down_bias[None], norm_gain, norm_shift, jnp.zeros((2, depth), F32)], axis=0)
    small = [jnp.concatenate([in_bias[None], jnp.pad(qv_bias, ((0, 5), (0, depth - width)))], axis=0)]
    small += [swap(small[0], "tp", core)]
    wq = w_qkv.transpose(0, 2, 1).reshape(3 * width, depth)
    qo_far = swap(jnp.concatenate([half_of(wq, 1, True), half_of(w_out, 1, True)], axis=0), "tp", far)
    wq_near = swap(wq, "tp", core)
    ready = small[1]
    ff_far = swap(tie(jnp.concatenate([half_of(w_in, 1, True), half_of(w_down, 2, True)], axis=0), ready), "tp", far)
    small_far = swap(jnp.concatenate(small, axis=0), "tp", far)
    small += [small_far[:8], small_far[8:]]

    def forward(j, x, pieces):
        return attend_forward(valid_len, x, pieces, width, small[j], picked, seqs)

    out0 = forward(0, tie(tokens, ready), [wq])
    qo_far = tie(qo_far, out0[0])
    qo_rest, qo_far_core = swap(qo_far, "dp", 1), swap(qo_far, "tp", core)
    out1 = forward(1, tie(tokens, qo_far), [wq_near])
    qo_rest = tie(qo_rest, out1[0])
    qo_rest_core = swap(qo_rest, "tp", core)
    wo_near = swap(tie(w_out, qo_rest), "tp", core)
    out2 = forward(2, tie(tokens, qo_rest), [qo_far, qo_rest])
    wi_near, wd_near = swap(tie(w_in, out2[0]), "tp", core), swap(tie(w_down, out2[0]), "tp", core)
    out3 = forward(3, tie(tokens, out2[0]), [qo_far_core, qo_rest_core])
    ff_far = tie(ff_far, out3[0])
    rows_in = ff_far.shape[0] // 2
    wi_rest, wd_rest = swap(ff_far[:rows_in], "dp", 1), swap(ff_far[rows_in:], "dp", 2)
    ff_far_core = swap(ff_far, "tp", core)
    q_sel, k, v, ctx, ctx_sel = zip(out0, out1, out2, out3)
    rows_q = 3 * width // 2

    def pieces(own, near, far_pieces, core_pieces):
        return [[(own, 0)], [(near, 0)], far_pieces, core_pieces]

    wq = pieces(wq, wq_near, [(qo_far, 0), (qo_rest, 0)], [(qo_far_core, 0), (qo_rest_core, 0)])
    wo = pieces(w_out, wo_near, [(qo_far, rows_q), (qo_rest, rows_q)], [(qo_far_core, rows_q), (qo_rest_core, rows_q)])
    near_in, near_down = [[(w_in, 0)], [(wi_near, 0)]], [[(w_down, 0)], [(wd_near, 0)]]
    prep = ffn_prep(picked, tie(tokens, ff_far), d_out, ctx_sel, wo, near_in, near_down, small[:2], shared, seqs)
    act, slope_near, x_sel, cot, low, ffn_sum, normed1, inv1 = prep
    wi_rest, wd_rest = tie((wi_rest, wd_rest), low)
    wi_rest_core, wd_rest_core = swap(wi_rest, "tp", core), swap(wd_rest, "tp", core)
    wi = near_in + [[(ff_far, 0), (wi_rest, 0)], [(ff_far_core, 0), (wi_rest_core, 0)]]
    wd = near_down + [[(ff_far, rows_in), (wd_rest, 0)], [(ff_far_core, rows_in), (wd_rest_core, 0)]]

    slope_far, grad2, g2, vec, *g_down = ffn_front(low, ffn_sum, cot, act, wi[2:], wd[2:], small[2:], shared)

    def near_sums(grads):
        far_sum = add(grads[2], swap(grads[3], "tp", core))
        return far_sum, (grads[0], swap(grads[1], "tp", core))

    def far_step(grads_sum, after):
        far_sum, near = grads_sum
        return add(*tie(near, after), swap(far_sum, "tp", far))

    def backward(j, x):
        return attend_backward(j, valid_len, q_sel[j], k[j], v[j], d_ctx[j], x, x_sel, ctx_sel[j], g1, seqs)

    d_pre, vec_mid, *g_in = ffn_mid(g2, low, [slope_near, slope_far], wd)
    sum_a = near_sums((*g_down[:3], tie(g_down[3], g2)))
    far_a = sum_a[0]
    g1, grad1, vec_back, *d_ctx = ffn_back(tie(grad2, far_a), d_pre, normed1, inv1, shared, wi, wo, width)
    sum_b = near_sums(g_in)
    out3 = backward(3, tie(tokens, sum_b[0]))
    out2 = backward(2, tie(tokens, out3[0]))
    out1 = backward(1, tie(tokens, out2[0]))
    far_c = add(out2[4], swap(tie(out3[4], out1[0]), "tp", core))
    total_a = far_step(sum_a, out1[0])
    sent_a = half_of(total_a, dp_bits[0], False)
    out0 = backward(0, tie(tokens, out1[0], sent_a))
    dq, dk, dv, sums, g_heads = zip(out0, out1, out2, out3)
    sum_c = far_c, (g_heads[0], swap(g_heads[1], "tp", core))
    line = jnp.concatenate([vec + vec_mid + vec_back, sums[0] + sums[1] + sums[2] + sums[3]], axis=0)
    d_tokens = input_gradient(tie(picked, line, far_c), grad1, dq, dk, dv, wq, seqs)
    got_a, line = tie((swap(sent_a, "dp", dp_bits[0]), line + swap(line, "dp", dp_bits[0])), d_tokens)
    total_a = add(half_of(total_a, dp_bits[0], True), got_a)
    half_rows = tokens.shape[0] // 2
    out_first = ffn_rows(tie(tokens, total_a, line), ctx, wo, wi, wd, small, shared, 0, half_rows)
    total_b = far_step(sum_b, out_first)
    total_a = tie(total_a, out_first)
    sent_b = half_of(total_b, dp_bits[0], False)
    out_second = ffn_rows(tie(tokens, sent_b), ctx, wo, wi, wd, small, shared, half_rows, half_rows)
    for bit in dp_bits[1:2]:
        total_a, line = scatter(total_a, bit, out_second), tie(line, out_second) + swap(line, "dp", bit)
    for bit in dp_bits[2:]:
        total_a, line = scatter(total_a, bit), line + swap(line, "dp", bit)
    total_a, line, got_b = tie((total_a, line, swap(sent_b, "dp", dp_bits[0])), out_second)
    total_b = add(half_of(total_b, dp_bits[0], True), got_b)
    for bit in reversed(dp_bits):
        total_a = gather(total_a, bit)
    for bit in dp_bits[1:]:
        total_b = scatter(total_b, bit)
    for bit in reversed(dp_bits):
        total_b = gather(total_b, bit)
    line = line + swap(line, "tp", core)
    total_c = far_step(sum_c, out_second)
    line = tie(line, total_c)
    line = line + swap(line, "tp", far)
    for bit in dp_bits:
        total_c = scatter(total_c, bit)
    for bit in reversed(dp_bits):
        total_c = gather(total_c, bit)
    total_c = total_c.astype(F32)
    own = lax.dynamic_slice_in_dim(line, 8 + rank, 1, 0)[0]
    own_q = lax.dynamic_slice(line, (16 + rank, 0), (1, width))
    own_v = lax.dynamic_slice(line, (16 + PARTS + rank, 0), (1, width))
    return (
        jnp.concatenate([out_first, out_second], axis=0),
        d_tokens,
        total_c[: 3 * width].reshape(3, width, depth).transpose(0, 2, 1),
        jnp.concatenate([own_q, own_v], axis=0),
        total_c[3 * width :],
        line[3],
        total_b.astype(F32),
        own,
        total_a.astype(F32),
        line[0],
        jnp.stack([line[4], line[1]]),
        jnp.stack([line[5], line[2]]),
    )


def solution(mesh):
    placed = (
        P(("dp", "tp"), None),
        P(None, None, "tp"),
        P(None, "tp"),
        P("tp", None),
        P(),
        P(None, "tp"),
        P("tp"),
        P("tp", None),
        P(),
        P(),
        P(),
        P("dp"),
        P("dp", None),
        P(("dp", "tp"), None),
    )
    return jax.shard_map(
        on_device,
        mesh=mesh,
        in_specs=placed,
        out_specs=(
            P(("dp", "tp"), None),
            P(("dp", "tp"), None),
            P(None, None, "tp"),
            P(None, "tp"),
            P("tp", None),
            P(),
            P(None, "tp"),
            P("tp"),
            P("tp", None),
            P(),
            P(),
            P(),
        ),
        check_vma=False,
    )
```

```python
import jax
import jax.numpy as jnp
from jax import lax
from jax.experimental import pallas as pl
from jax.experimental.pallas import tpu as pltpu
from jax.sharding import PartitionSpec as P

HD = 64
SCALE = HD ** (-0.5)
NORM_EPS = 1e-06
MASKED = -1e30
HALF_ROOT = 0.5 ** 0.5
DENSITY = 0.3989422804014327
PARTS = 4
BF = jnp.bfloat16
F32 = jnp.float32


def nn(left, right):
    return lax.dot_general(left, right, (((1,), (0,)), ((), ())), preferred_element_type=F32)


def nt(left, right):
    return lax.dot_general(left, right, (((1,), (1,)), ((), ())), preferred_element_type=F32)


def tn(left, right):
    return lax.dot_general(left, right, (((0,), (0,)), ((), ())), preferred_element_type=F32)


def head_masks(width, dtype=BF):
    lane = lax.broadcasted_iota(jnp.int32, (1, width), 1) // HD
    return [(lane == head).astype(dtype) for head in range(width // HD)]


def spread_of(picks, length):
    slots = picks.shape[1]
    return (lax.broadcasted_iota(jnp.int32, (length, slots), 0) == picks).astype(F32).astype(BF)


def whole(shape):
    zeros = (0,) * len(shape)
    return pl.BlockSpec(shape, lambda *_: zeros)


def norm_forward(values, gain, shift):
    average = jnp.mean(values, axis=1, keepdims=True)
    centered = values - average
    inv_std = lax.rsqrt(jnp.mean(centered * centered, axis=1, keepdims=True) + NORM_EPS)
    normed = centered * inv_std
    return normed * gain + shift, normed, inv_std


def norm_backward(grad, normed, inv_std, gain):
    scaled = grad * gain
    first = jnp.mean(scaled, axis=1, keepdims=True)
    second = jnp.mean(scaled * normed, axis=1, keepdims=True)
    return inv_std * (scaled - first - normed * second)


def tie(value, *others):
    return lax.optimization_barrier((value, others))[0]


SMALL = pl.CostEstimate(flops=1024, transcendentals=0, bytes_accessed=1024)


def col_sum(values):
    return jnp.sum(values, axis=0, keepdims=True)


def piece_copies(pieces, target, sems, first, bit):
    rows = target.shape[0]
    if len(pieces) == 1:
        return [pltpu.make_async_copy(pieces[0][0], target, sems.at[first])]
    half, step = rows // 2, rows // len(pieces)
    own = ((lax.axis_index("dp") // bit) % 2) * half
    copies = []
    for n, (ref, skip) in enumerate(pieces):
        base = own if n * step < half else half - own
        start = pl.multiple_of(base + (n * step) % half, step)
        copies.append(pltpu.make_async_copy(ref.at[pl.ds(skip, step), :], target.at[pl.ds(start, step), :], sems.at[first + n]))
    return copies


def stacked_copies(pieces, target, sems, first, bit):
    copies = []
    for part, refs in enumerate(pieces):
        copies.append(piece_copies(refs, target.at[part], sems, first, bit))
        first += len(refs)
    return copies


def take(it, pieces):
    return [[(next(it), skip) for _, skip in piece] for piece in pieces]


def flat(pieces):
    return [p for piece in pieces for p in piece]


def arrays(pieces):
    return [array for array, _ in flat(pieces)]


def start_all(copies):
    for copy in copies:
        copy.start()


def wait_all(copies):
    for copy in copies:
        copy.wait()


ANY_SPEC = pl.BlockSpec(memory_space=pl.ANY)


def shaped(shape):
    return pl.BlockSpec(shape, lambda *_: (0,) * len(shape))


def attend_body(len_ref, x_ref, small_ref, pick_ref, *rest, count):
    w_refs = [(ref, 0) for ref in rest[:count]]
    q_sel_ref, k_ref, v_ref, ctx_ref, ctx_sel_ref, ext_ref, w_ref, sems = rest[count:]
    rows, width = k_ref.shape
    seq = pl.program_id(0)
    row = lax.axis_index("tp") * pl.num_programs(0) + seq
    length = len_ref[row]
    copies = piece_copies(w_refs, w_ref, sems, 0, 1)

    @pl.when(seq == 0)
    def _():
        start_all(copies)
        wait_all(copies)

    x = x_ref[...]
    queries = (nt(x, w_ref[0:width, :]) + small_ref[1:2, :width]).astype(BF)
    key_rows = nt(x, w_ref[width : 2 * width, :]).astype(BF)
    values = (nt(x, w_ref[2 * width : 3 * width, :]) + small_ref[2:3, :width]).astype(BF)
    k_ref[...] = key_rows
    v_ref[...] = values
    ext_ref[:, :width] = values
    ext_ref[:, width:] = jnp.ones((rows, ext_ref.shape[1] - width), BF)
    spread = spread_of(pick_ref[pl.ds(row, 1), :], rows)
    q_sel_ref[...] = tn(spread, queries).astype(BF)
    scaled = queries * jnp.asarray(SCALE, BF)
    masks = head_masks(width)
    tile = min(256, rows)
    keep = lax.broadcasted_iota(jnp.int32, (tile, rows), 1) < length
    for start in range(0, rows, tile):
        total = jnp.zeros((tile, width), F32)
        for mask in masks:
            logits = nt(scaled[start : start + tile] * mask, key_rows)
            logits = jnp.where(keep, logits, MASKED)
            peak = jnp.max(logits, axis=1, keepdims=True)
            probs = jnp.exp(logits - peak).astype(BF)
            mixed = nn(probs, ext_ref[...])
            share = mixed[:, :width] / mixed[:, width : width + 1]
            total = jnp.where(mask.astype(F32) > 0.5, share, total)
        ctx_ref[start : start + tile, :] = total.astype(BF)
    ctx_sel_ref[...] = tn(spread, ctx_ref[...]).astype(BF)


def attend_forward(lengths, x, pieces, width, small, picked, seqs):
    slots = picked.shape[1]
    rows = x.shape[0] // seqs
    depth = x.shape[1]
    ext = -(-(width + 1) // 128) * 128
    row_spec = pl.BlockSpec((rows, width), lambda s, _: (s, 0))
    sel_spec = pl.BlockSpec((slots, width), lambda s, _: (s, 0))
    return pl.pallas_call(
        lambda *refs: attend_body(*refs, count=len(pieces)),
        grid_spec=pltpu.PrefetchScalarGridSpec(
            num_scalar_prefetch=1,
            grid=(seqs,),
            in_specs=[
                pl.BlockSpec((rows, depth), lambda s, _: (s, 0)),
                whole(small.shape),
                whole(picked.shape),
                *[ANY_SPEC] * len(pieces),
            ],
            out_specs=[sel_spec, row_spec, row_spec, row_spec, sel_spec],
            scratch_shapes=[
                pltpu.VMEM((rows, ext), BF),
                pltpu.VMEM((3 * width, depth), BF),
                pltpu.SemaphoreType.DMA((len(pieces),)),
            ],
        ),
        out_shape=[
            jax.ShapeDtypeStruct((seqs * slots, width), BF),
            jax.ShapeDtypeStruct((seqs * rows, width), BF),
            jax.ShapeDtypeStruct((seqs * rows, width), BF),
            jax.ShapeDtypeStruct((seqs * rows, width), BF),
            jax.ShapeDtypeStruct((seqs * slots, width), BF),
        ],
        cost_estimate=SMALL,
        name="attend_forward",
    )(lengths, x, small, picked, *pieces)


def attend_back_body(
    len_ref, q_ref, k_ref, v_ref, d_ctx_ref, x_ref, x_sel_ref, ctx_sel_ref, g1_ref, dq_ref, dk_ref, dv_ref, sums_ref, grad_ref, acc_ref, *, part
):
    rows, width = k_ref.shape
    slots = q_ref.shape[0]
    seq = pl.program_id(0)
    rank = lax.axis_index("tp")
    length = len_ref[rank * pl.num_programs(0) + seq]
    masks = head_masks(width)
    queries, d_ctx = q_ref[...], d_ctx_ref[...]
    key_rows, values = k_ref[...], v_ref[...]
    q_stack = jnp.concatenate([queries * mask for mask in masks], axis=0)
    d_stack = jnp.concatenate([d_ctx * mask for mask in masks], axis=0)
    logits = nt(key_rows, q_stack * jnp.asarray(SCALE, BF))
    keep = lax.broadcasted_iota(jnp.int32, logits.shape, 0) < length
    logits = jnp.where(keep, logits, MASKED)
    grown = jnp.exp(logits - jnp.max(logits, axis=0, keepdims=True))
    probs = grown * (1.0 / jnp.sum(grown, axis=0, keepdims=True))
    d_probs = nt(values, d_stack)
    inner = jnp.sum(probs * d_probs, axis=0, keepdims=True)
    d_raw = (probs * (d_probs - inner) * SCALE).astype(BF)
    d_keys = nn(d_raw, q_stack).astype(BF)
    dk_ref[...] = d_keys
    d_values = nn(probs.astype(BF), d_stack).astype(BF)
    dv_ref[...] = d_values
    dq_stack = tn(d_raw, key_rows)
    dq = jnp.zeros((slots, width), F32)
    for head, mask in enumerate(masks):
        dq = jnp.where(mask.astype(F32) > 0.5, dq_stack[head * slots : (head + 1) * slots], dq)
    dq = dq.astype(BF)
    dq_ref[...] = dq

    @pl.when(seq == 0)
    def _():
        acc_ref[...] = jnp.zeros(acc_ref.shape, F32)
        sums_ref[...] = jnp.zeros(sums_ref.shape, F32)

    at = rank ^ part
    sums_ref[pl.ds(at, 1), 0:width] += col_sum(dq.astype(F32))
    sums_ref[pl.ds(PARTS + at, 1), 0:width] += col_sum(d_values.astype(F32))
    acc_ref[0:width, :] += tn(dq, x_sel_ref[...])
    acc_ref[width : 2 * width, :] += tn(d_keys, x_ref[...])
    acc_ref[2 * width : 3 * width, :] += tn(d_values, x_ref[...])
    acc_ref[3 * width : 4 * width, :] += tn(ctx_sel_ref[...], g1_ref[...])

    @pl.when(seq == pl.num_programs(0) - 1)
    def _():
        grad_ref[...] = acc_ref[...].astype(BF)


def attend_backward(part, lengths, q_sel, k, v, d_ctx, x, x_sel, ctx_sel, g1, seqs):
    rows, slots, width = k.shape[0] // seqs, q_sel.shape[0] // seqs, k.shape[1]
    depth = x.shape[1]
    row_spec = pl.BlockSpec((rows, width), lambda s, _: (s, 0))
    sel_spec = pl.BlockSpec((slots, width), lambda s, _: (s, 0))
    wide_spec = pl.BlockSpec((slots, depth), lambda s, _: (s, 0))
    return pl.pallas_call(
        lambda *refs: attend_back_body(*refs, part=part),
        grid_spec=pltpu.PrefetchScalarGridSpec(
            num_scalar_prefetch=1,
            grid=(seqs,),
            in_specs=[
                sel_spec,
                row_spec,
                row_spec,
                sel_spec,
                pl.BlockSpec((rows, depth), lambda s, _: (s, 0)),
                wide_spec,
                sel_spec,
                wide_spec,
            ],
            out_specs=[sel_spec, row_spec, row_spec, whole((2 * PARTS, depth)), whole((4 * width, depth))],
            scratch_shapes=[pltpu.VMEM((4 * width, depth), F32)],
        ),
        out_shape=[
            jax.ShapeDtypeStruct(q_sel.shape, BF),
            jax.ShapeDtypeStruct(k.shape, BF),
            jax.ShapeDtypeStruct(k.shape, BF),
            jax.ShapeDtypeStruct((2 * PARTS, depth), F32),
            jax.ShapeDtypeStruct((4 * width, depth), BF),
        ],
        cost_estimate=SMALL,
        name="attend_backward",
    )(lengths, q_sel, k, v, d_ctx, x, x_sel, ctx_sel, g1)


def erf_gelu(values):
    return 0.5 * (1.0 + lax.erf(values * HALF_ROOT))


def run(body, plain, hbm, outs, hbm_outs, scratch, name):
    return pl.pallas_call(
        body,
        grid=(1,),
        in_specs=[*[shaped(a.shape) for a in plain], *[ANY_SPEC] * len(hbm)],
        out_specs=[*[shaped(a.shape) for a in outs], *[ANY_SPEC] * len(hbm_outs)],
        out_shape=[*outs, *hbm_outs],
        scratch_shapes=scratch,
        cost_estimate=SMALL,
        name=name,
    )(*plain, *hbm)


def struct(dtype, *shape):
    return jax.ShapeDtypeStruct(shape, dtype)


def unit_part(low, wi, bias, act_ref, slope_ref, n):
    pre = nn(low, wi) + bias
    chance = erf_gelu(pre)
    slope_ref[n] = chance + pre * (DENSITY * jnp.exp(-0.5 * pre * pre))
    act = (pre * chance).astype(BF)
    act_ref[n] = act
    return act


def ffn_prep(picked, x, d_out, ctx_sel, wo, wi, wd, small, shared, seqs):
    parts, near = len(wo), len(wi)
    slots = picked.shape[1]
    count, depth, units, width = seqs * slots, x.shape[1], wi[0][0][0].shape[1], ctx_sel[0].shape[1]
    plain = [picked, x, d_out, shared, *ctx_sel, *small]
    hbm = arrays(wo) + arrays(wi) + arrays(wd)

    def body(*refs):
        it = iter(refs)
        pick_ref, x_ref, d_out_ref, shared_ref = (next(it) for _ in range(4))
        ctx_refs = [next(it) for _ in range(parts)]
        small_refs = [next(it) for _ in range(near)]
        wo_refs, wi_refs, wd_refs = take(it, wo), take(it, wi), take(it, wd)
        act_ref, slope_ref, x_sel_ref, cot_ref, low_ref, sum_ref, normed1_ref, inv1_ref = (next(it) for _ in range(8))
        wo_v, wi_v, wd_v, sems = (next(it) for _ in range(4))
        out_copies = stacked_copies(wo_refs, wo_v, sems, 0, 1)
        first = len(flat(wo))
        in_copies = stacked_copies(wi_refs, wi_v, sems, first, 1)
        down_copies = stacked_copies(wd_refs, wd_v, sems, first + len(flat(wi)), 2)
        start_all(flat(out_copies) + flat(in_copies) + flat(down_copies))
        rows = x_ref.shape[0] // seqs
        for seq in range(seqs):
            at = lax.axis_index("tp") * seqs + seq
            spread = spread_of(pick_ref[pl.ds(at, 1), :], rows)
            x_sel_ref[seq * slots : (seq + 1) * slots, :] = tn(spread, x_ref[seq * rows : (seq + 1) * rows, :]).astype(BF)
            cot_ref[seq * slots : (seq + 1) * slots, :] = tn(spread, d_out_ref[seq * rows : (seq + 1) * rows, :]).astype(BF)
        attn_sum = x_sel_ref[...].astype(F32) + shared_ref[0:1, :]
        wait_all(flat(out_copies))
        for part in range(parts):
            attn_sum = attn_sum + nn(ctx_refs[part][...], wo_v[part])
        hidden, normed1, inv1 = norm_forward(attn_sum, shared_ref[2:3, :], shared_ref[4:5, :])
        low = hidden.astype(BF)
        low_ref[...] = low
        normed1_ref[...] = normed1
        inv1_ref[...] = inv1
        total = hidden + shared_ref[1:2, :]
        wait_all(flat(in_copies) + flat(down_copies))
        for n in range(near):
            act = unit_part(low, wi_v[n], small_refs[n][0:1, :], act_ref, slope_ref, n)
            total = total + nn(act, wd_v[n])
        sum_ref[...] = total

    outs = [
        struct(BF, near, count, units),
        struct(F32, near, count, units),
        struct(BF, count, depth),
        struct(BF, count, depth),
        struct(BF, count, depth),
        struct(F32, count, depth),
        struct(F32, count, depth),
        struct(F32, count, 1),
    ]
    scratch = [
        pltpu.VMEM((parts, width, depth), BF),
        pltpu.VMEM((near, depth, units), BF),
        pltpu.VMEM((near, units, depth), BF),
        pltpu.SemaphoreType.DMA((len(hbm),)),
    ]
    return run(body, plain, hbm, outs, [], scratch, "ffn_prep")


def ffn_front(low, total, cot, act, wi, wd, small, shared):
    far, near = len(wi), act.shape[0]
    parts = near + far
    count, depth = low.shape
    units = act.shape[2]
    plain = [low, total, cot, shared, act, *small]
    hbm = arrays(wi) + arrays(wd)

    def body(*refs):
        it = iter(refs)
        low_ref, sum_ref, cot_ref, shared_ref, act_ref = (next(it) for _ in range(5))
        small_refs = [next(it) for _ in range(far)]
        wi_refs, wd_refs = take(it, wi), take(it, wd)
        slope_ref, grad2_ref, g2_ref, vec_ref = (next(it) for _ in range(4))
        gd_refs = [next(it) for _ in range(parts)]
        wi_v, wd_v, far_act, gd_v, sems, out_sems = (next(it) for _ in range(6))
        in_copies = stacked_copies(wi_refs, wi_v, sems, 0, 1)
        down_copies = stacked_copies(wd_refs, wd_v, sems, len(flat(wi)), 2)
        for n in range(far):
            start_all(in_copies[n] + down_copies[n])
        low = low_ref[...]
        total = sum_ref[...]
        for n in range(far):
            wait_all(in_copies[n])
            act = unit_part(low, wi_v[n], small_refs[n][0:1, :], far_act, slope_ref, n)
            wait_all(down_copies[n])
            total = total + nn(act, wd_v[n])
        _, normed2, inv2 = norm_forward(total, shared_ref[3:4, :], shared_ref[5:6, :])
        cotangent = cot_ref[...].astype(F32)
        grad2 = norm_backward(cotangent, normed2, inv2, shared_ref[3:4, :])
        g2 = grad2.astype(BF)
        copies = []
        for part in reversed(range(parts)):
            rows = act_ref[part] if part < near else far_act[part - near]
            gd_v[part] = tn(rows, g2).astype(BF)
            copies.append(pltpu.make_async_copy(gd_v.at[part], gd_refs[part], out_sems.at[part]))
            copies[-1].start()
        vec_ref[...] = jnp.zeros(vec_ref.shape, F32)
        vec_ref[0:1, :] = col_sum(grad2)
        vec_ref[1:2, :] = col_sum(cotangent * normed2)
        vec_ref[2:3, :] = col_sum(cotangent)
        grad2_ref[...] = grad2
        g2_ref[...] = g2
        wait_all(copies)

    outs = [struct(F32, far, count, units), struct(F32, count, depth), struct(BF, count, depth), struct(F32, 16, depth)]
    scratch = [
        pltpu.VMEM((far, depth, units), BF),
        pltpu.VMEM((far, units, depth), BF),
        pltpu.VMEM((far, count, units), BF),
        pltpu.VMEM((parts, units, depth), BF),
        pltpu.SemaphoreType.DMA((len(hbm),)),
        pltpu.SemaphoreType.DMA((parts,)),
    ]
    return run(body, plain, hbm, outs, [struct(BF, units, depth)] * parts, scratch, "ffn_front")


def ffn_mid(g2, low, slopes, wd):
    parts = len(wd)
    count, depth = g2.shape
    units = slopes[0].shape[2]
    hbm = [*slopes, *arrays(wd)]

    def body(*refs):
        it = iter(refs)
        g2_ref, low_ref = next(it), next(it)
        slope_hbm = [next(it) for _ in slopes]
        wd_refs = take(it, wd)
        d_pre_ref, vec_ref = next(it), next(it)
        gi_refs = [next(it) for _ in range(parts)]
        wd_v, slope_v, gi_v, sems, slope_sems, out_sems = (next(it) for _ in range(6))
        down_copies = stacked_copies(wd_refs, wd_v, sems, 0, 2)
        sources = [ref.at[n] for ref in slope_hbm for n in range(ref.shape[0])]
        slope_copies = [pltpu.make_async_copy(sources[part], slope_v.at[part], slope_sems.at[part]) for part in range(parts)]
        order = list(reversed(range(parts)))
        for part in order:
            start_all(down_copies[part] + [slope_copies[part]])
        vec_ref[...] = jnp.zeros(vec_ref.shape, F32)
        g2, low = g2_ref[...], low_ref[...]
        copies = []
        for part in order:
            wait_all(down_copies[part] + [slope_copies[part]])
            d_pre = (nt(g2, wd_v[part]) * slope_v[part]).astype(BF)
            d_pre_ref[part] = d_pre
            gi_v[part] = tn(low, d_pre).astype(BF)
            copies.append(pltpu.make_async_copy(gi_v.at[part], gi_refs[part], out_sems.at[part]))
            copies[-1].start()
            at = 8 + (lax.axis_index("tp") ^ part)
            vec_ref[pl.ds(at, 1), :] = col_sum(d_pre.astype(F32))
        wait_all(copies)

    outs = [struct(BF, parts, count, units), struct(F32, 16, depth)]
    scratch = [
        pltpu.VMEM((parts, units, depth), BF),
        pltpu.VMEM((parts, count, units), F32),
        pltpu.VMEM((parts, depth, units), BF),
        pltpu.SemaphoreType.DMA((len(flat(wd)),)),
        pltpu.SemaphoreType.DMA((parts,)),
        pltpu.SemaphoreType.DMA((parts,)),
    ]
    return run(body, [g2, low], hbm, outs, [struct(BF, depth, units)] * parts, scratch, "ffn_mid")


def ffn_back(grad2, d_pre, normed1, inv1, shared, wi, wo, width):
    parts = len(wi)
    count, depth = grad2.shape
    units = d_pre.shape[2]
    hbm = arrays(wi) + arrays(wo)

    def body(*refs):
        it = iter(refs)
        grad2_ref, d_pre_ref, normed1_ref, inv1_ref, shared_ref = (next(it) for _ in range(5))
        wi_refs, wo_refs = take(it, wi), take(it, wo)
        g1_ref, grad1_ref, vec_ref = next(it), next(it), next(it)
        d_ctx_refs = [next(it) for _ in range(parts)]
        wi_v, wo_v, sems = (next(it) for _ in range(3))
        in_copies = stacked_copies(wi_refs, wi_v, sems, 0, 1)
        out_copies = stacked_copies(wo_refs, wo_v, sems, len(flat(wi)), 1)
        start_all(flat(in_copies) + flat(out_copies))
        d_hidden = grad2_ref[...]
        for part in range(parts):
            wait_all(in_copies[part])
            d_hidden = d_hidden + nt(d_pre_ref[part], wi_v[part])
        normed1 = normed1_ref[...]
        grad1 = norm_backward(d_hidden, normed1, inv1_ref[...], shared_ref[2:3, :])
        vec_ref[...] = jnp.zeros(vec_ref.shape, F32)
        vec_ref[3:4, :] = col_sum(grad1)
        vec_ref[4:5, :] = col_sum(d_hidden * normed1)
        vec_ref[5:6, :] = col_sum(d_hidden)
        grad1_ref[...] = grad1
        g1 = grad1.astype(BF)
        g1_ref[...] = g1
        wait_all(flat(out_copies))
        for part in range(parts):
            d_ctx_refs[part][...] = nt(g1, wo_v[part]).astype(BF)

    outs = [struct(BF, count, depth), struct(F32, count, depth), struct(F32, 16, depth), *[struct(BF, count, width)] * parts]
    scratch = [
        pltpu.VMEM((parts, depth, units), BF),
        pltpu.VMEM((parts, width, depth), BF),
        pltpu.SemaphoreType.DMA((len(hbm),)),
    ]
    return run(body, [grad2, d_pre, normed1, inv1, shared], hbm, outs, [], scratch, "ffn_back")


def ffn_rows(x, ctx, wo, wi, wd, small, shared, first, count):
    parts = len(wo)
    depth = x.shape[1]
    units, width = wi[0][0][0].shape[1], ctx[0].shape[1]
    tile = min(256, count)
    start = first // tile
    hbm = arrays(wo) + arrays(wi) + arrays(wd)

    def body(*refs):
        it = iter(refs)
        x_ref = next(it)
        ctx_refs = [next(it) for _ in range(parts)]
        small_refs = [next(it) for _ in range(parts)]
        shared_ref = next(it)
        wo_refs, wi_refs, wd_refs = take(it, wo), take(it, wi), take(it, wd)
        out_ref, wo_v, wi_v, wd_v, sems = (next(it) for _ in range(5))
        out_copies = flat(stacked_copies(wo_refs, wo_v, sems, 0, 1))
        near = len(flat(wo))
        in_copies = stacked_copies(wi_refs, wi_v, sems, near, 1)
        down_copies = stacked_copies(wd_refs, wd_v, sems, near + len(flat(wi)), 2)
        opening = pl.program_id(0) == 0

        @pl.when(opening)
        def _():
            start_all(out_copies)
            for part in range(parts):
                start_all(in_copies[part] + down_copies[part])
            wait_all(out_copies)

        attn_sum = x_ref[...].astype(F32) + shared_ref[0:1, :]
        for part in range(parts):
            attn_sum = attn_sum + nn(ctx_refs[part][...], wo_v[part])
        hidden, _, _ = norm_forward(attn_sum, shared_ref[2:3, :], shared_ref[4:5, :])
        low = hidden.astype(BF)
        total = hidden + shared_ref[1:2, :]
        for part in range(parts):

            @pl.when(opening)
            def _():
                wait_all(in_copies[part] + down_copies[part])

            pre = nn(low, wi_v[part]) + small_refs[part][0:1, :]
            act = (pre * erf_gelu(pre)).astype(BF)
            total = total + nn(act, wd_v[part])
        out_ref[...] = norm_forward(total, shared_ref[3:4, :], shared_ref[5:6, :])[0].astype(BF)

    return pl.pallas_call(
        body,
        grid=(count // tile,),
        in_specs=[
            pl.BlockSpec((tile, depth), lambda i: (i + start, 0)),
            *[pl.BlockSpec((tile, width), lambda i: (i + start, 0))] * parts,
            *[shaped(a.shape) for a in small],
            shaped(shared.shape),
            *[ANY_SPEC] * len(hbm),
        ],
        out_specs=pl.BlockSpec((tile, depth), lambda i: (i, 0)),
        out_shape=jax.ShapeDtypeStruct((count, depth), BF),
        scratch_shapes=[
            pltpu.VMEM((parts, width, depth), BF),
            pltpu.VMEM((parts, depth, units), BF),
            pltpu.VMEM((parts, units, depth), BF),
            pltpu.SemaphoreType.DMA((len(hbm),)),
        ],
        cost_estimate=SMALL,
        name="ffn_rows",
    )(x, *ctx, *small, shared, *hbm)


def input_gradient(picked, grad1, dq, dk, dv, wq, seqs):
    parts = len(dq)
    slots = picked.shape[1]
    depth = grad1.shape[1]
    rows, width = dk[0].shape[0] // seqs, dk[0].shape[1]
    hbm = arrays(wq)

    def body(*refs):
        it = iter(refs)
        pick_ref, grad1_ref = next(it), next(it)
        dq_refs = [next(it) for _ in range(parts)]
        dk_refs = [next(it) for _ in range(parts)]
        dv_refs = [next(it) for _ in range(parts)]
        wq_refs = take(it, wq)
        out_ref, wq_v, sems = next(it), next(it), next(it)
        copies = flat(stacked_copies(wq_refs, wq_v, sems, 0, 1))
        seq = pl.program_id(0)

        @pl.when(seq == 0)
        def _():
            start_all(copies)
            wait_all(copies)

        chosen = grad1_ref[...]
        for part in range(parts):
            chosen = chosen + nn(dq_refs[part][...], wq_v[part, 0:width, :])
        high = chosen.astype(BF)
        rest = (chosen - high.astype(F32)).astype(BF)
        spread = spread_of(pick_ref[pl.ds(lax.axis_index("tp") * seqs + seq, 1), :], rows)
        total = nn(spread, high) + nn(spread, rest)
        for part in range(parts):
            total = total + nn(dk_refs[part][...], wq_v[part, width : 2 * width, :])
            total = total + nn(dv_refs[part][...], wq_v[part, 2 * width : 3 * width, :])
        out_ref[...] = total.astype(BF)

    row_spec = pl.BlockSpec((rows, width), lambda s: (s, 0))
    return pl.pallas_call(
        body,
        grid=(seqs,),
        in_specs=[
            whole(picked.shape),
            pl.BlockSpec((slots, depth), lambda s: (s, 0)),
            *[pl.BlockSpec((slots, width), lambda s: (s, 0))] * parts,
            *[row_spec] * (2 * parts),
            *[ANY_SPEC] * len(hbm),
        ],
        out_specs=pl.BlockSpec((rows, depth), lambda s: (s, 0)),
        out_shape=jax.ShapeDtypeStruct((seqs * rows, depth), BF),
        scratch_shapes=[pltpu.VMEM((parts, 3 * width, depth), BF), pltpu.SemaphoreType.DMA((len(hbm),))],
        cost_estimate=SMALL,
        name="input_gradient",
    )(picked, grad1, *dq, *dk, *dv, *hbm)


def bits_of(count):
    return [1 << b for b in range(count.bit_length() - 1)]


def swap(value, axis, bit):
    count = lax.axis_size(axis)
    return lax.ppermute(value, axis, [(i, i ^ bit) for i in range(count)])


def half_of(value, bit, own):
    half = value.shape[0] // 2
    side = (lax.axis_index("dp") // bit) % 2
    return lax.dynamic_slice_in_dim(value, jnp.where(side == 0, 0, half) if own else jnp.where(side == 0, half, 0), half, 0)


def joined(own, got, bit):
    side = (lax.axis_index("dp") // bit) % 2
    return jnp.concatenate([jnp.where(side == 0, own, got), jnp.where(side == 0, got, own)], axis=0)


def add(*values):
    total = values[0].astype(F32)
    for value in values[1:]:
        total = total + value.astype(F32)
    return total.astype(BF)


def scatter(value, bit, *after):
    sent, kept = half_of(value, bit, False), half_of(value, bit, True)
    return add(tie(kept, *after), swap(sent, "dp", bit))


def gather(value, bit):
    return joined(value, swap(value, "dp", bit), bit)


def on_device(
    tokens, w_qkv, qv_bias, w_out, out_bias, w_in, in_bias, w_down, down_bias, norm_gain, norm_shift, valid_len, picked, d_out
):
    parts = lax.axis_size("tp")
    rank = lax.axis_index("tp")
    seqs = valid_len.shape[0] // parts
    depth = tokens.shape[1]
    width = w_qkv.shape[2]
    core, far = 1, 2
    dp_bits = bits_of(lax.axis_size("dp"))

    shared = jnp.concatenate([out_bias[None], down_bias[None], norm_gain, norm_shift, jnp.zeros((2, depth), F32)], axis=0)
    small = [jnp.concatenate([in_bias[None], jnp.pad(qv_bias, ((0, 5), (0, depth - width)))], axis=0)]
    small += [swap(small[0], "tp", core)]
    wq = w_qkv.transpose(0, 2, 1).reshape(3 * width, depth)
    qo_far = swap(jnp.concatenate([half_of(wq, 1, True), half_of(w_out, 1, True)], axis=0), "tp", far)
    wq_near = swap(wq, "tp", core)
    ready = small[1]
    small_far = swap(jnp.concatenate(small, axis=0), "tp", far)
    ff_far = swap(tie(jnp.concatenate([half_of(w_in, 1, True), half_of(w_down, 2, True)], axis=0), small_far), "tp", far)
    small += [small_far[:8], small_far[8:]]

    def forward(j, x, pieces):
        return attend_forward(valid_len, x, pieces, width, small[j], picked, seqs)

    out0 = forward(0, tie(tokens, ready), [wq])
    qo_far = tie(qo_far, out0[0])
    qo_rest, qo_far_core = swap(qo_far, "dp", 1), swap(qo_far, "tp", core)
    out1 = forward(1, tie(tokens, qo_far), [wq_near])
    qo_rest = tie(qo_rest, out1[0])
    qo_rest_core = swap(qo_rest, "tp", core)
    wo_near = swap(tie(w_out, qo_rest), "tp", core)
    out2 = forward(2, tie(tokens, qo_rest), [qo_far, qo_rest])
    wi_near, wd_near = swap(tie(w_in, out2[0]), "tp", core), swap(tie(w_down, out2[0]), "tp", core)
    out3 = forward(3, tie(tokens, out2[0]), [qo_far_core, qo_rest_core])
    ff_far = tie(ff_far, out3[0])
    rows_in = ff_far.shape[0] // 2
    wi_rest, wd_rest = swap(ff_far[:rows_in], "dp", 1), swap(ff_far[rows_in:], "dp", 2)
    ff_far_core = swap(ff_far, "tp", core)
    q_sel, k, v, ctx, ctx_sel = zip(out0, out1, out2, out3)
    rows_q = 3 * width // 2

    def pieces(own, near, far_pieces, core_pieces):
        return [[(own, 0)], [(near, 0)], far_pieces, core_pieces]

    wq = pieces(wq, wq_near, [(qo_far, 0), (qo_rest, 0)], [(qo_far_core, 0), (qo_rest_core, 0)])
    wo = pieces(w_out, wo_near, [(qo_far, rows_q), (qo_rest, rows_q)], [(qo_far_core, rows_q), (qo_rest_core, rows_q)])
    near_in, near_down = [[(w_in, 0)], [(wi_near, 0)]], [[(w_down, 0)], [(wd_near, 0)]]
    prep = ffn_prep(picked, tie(tokens, ff_far), d_out, ctx_sel, wo, near_in, near_down, small[:2], shared, seqs)
    act, slope_near, x_sel, cot, low, ffn_sum, normed1, inv1 = prep
    wi_rest, wd_rest = tie((wi_rest, wd_rest), low)
    wi_rest_core, wd_rest_core = swap(wi_rest, "tp", core), swap(wd_rest, "tp", core)
    wi = near_in + [[(ff_far, 0), (wi_rest, 0)], [(ff_far_core, 0), (wi_rest_core, 0)]]
    wd = near_down + [[(ff_far, rows_in), (wd_rest, 0)], [(ff_far_core, rows_in), (wd_rest_core, 0)]]

    slope_far, grad2, g2, vec, *g_down = ffn_front(low, ffn_sum, cot, act, wi[2:], wd[2:], small[2:], shared)

    def near_sums(grads):
        far_sum = add(grads[2], swap(grads[3], "tp", core))
        return far_sum, (grads[0], swap(grads[1], "tp", core))

    def far_step(grads_sum, after):
        far_sum, near = grads_sum
        return add(*tie(near, after), swap(far_sum, "tp", far))

    def backward(j, x):
        return attend_backward(j, valid_len, q_sel[j], k[j], v[j], d_ctx[j], x, x_sel, ctx_sel[j], g1, seqs)

    d_pre, vec_mid, *g_in = ffn_mid(g2, low, [slope_near, slope_far], wd)
    sum_a = near_sums((*g_down[:3], tie(g_down[3], g2)))
    far_a = sum_a[0]
    g1, grad1, vec_back, *d_ctx = ffn_back(tie(grad2, far_a), d_pre, normed1, inv1, shared, wi, wo, width)
    sum_b = near_sums(g_in)
    sum_b = tie(sum_b[0], g1), sum_b[1]
    out3 = backward(3, tie(tokens, sum_b[0]))
    out2 = backward(2, tie(tokens, out3[0]))
    out1 = backward(1, tie(tokens, out2[0]))
    total_a = far_step(sum_a, out1[0])
    sent_a = half_of(total_a, dp_bits[0], False)
    out0 = backward(0, tie(tokens, out1[0], sent_a))
    dq, dk, dv, sums, g_heads = zip(out0, out1, out2, out3)
    far_c = add(tie(out2[4], out0[0]), swap(tie(out3[4], out1[0]), "tp", core))
    sum_c = far_c, (g_heads[0], swap(tie(g_heads[1], out0[0]), "tp", core))
    cut = far_c.shape[0] // 2
    line = jnp.concatenate([vec + vec_mid + vec_back, sums[0] + sums[1] + sums[2] + sums[3]], axis=0)
    half_rows = tokens.shape[0] // 2

    def rows_of(first, *after):
        return ffn_rows(tie(tokens, *after), ctx, wo, wi, wd, small, shared, first, half_rows)

    last = dp_bits[-1]
    out_first = rows_of(0, line, far_c)
    line = tie(line, out_first) + swap(line, "dp", dp_bits[0])
    total_a = add(tie(half_of(total_a, dp_bits[0], True), out_first), swap(sent_a, "dp", dp_bits[0]))
    total_b = far_step(sum_b, out_first)
    sent_a, sent_b = half_of(total_a, dp_bits[1], False), half_of(total_b, dp_bits[0], False)
    d_tokens = input_gradient(tie(picked, sent_a, sent_b, line), grad1, dq, dk, dv, wq, seqs)
    line = tie(line, d_tokens) + swap(line, "dp", dp_bits[1])
    total_a = add(tie(half_of(total_a, dp_bits[1], True), d_tokens), swap(sent_a, "dp", dp_bits[1]))
    for bit in dp_bits[2:-1]:
        total_a, line = scatter(total_a, bit), line + swap(line, "dp", bit)
    out_second = rows_of(half_rows, total_a, line)
    total_a, line = add(tie(total_a, out_second), swap(total_a, "dp", last)), tie(line, out_second) + swap(line, "dp", last)
    total_b = add(tie(half_of(total_b, dp_bits[0], True), out_second), swap(sent_b, "dp", dp_bits[0]))

    def finish(value, bits):
        for bit in bits:
            value = scatter(value, bit) if bit != last else add(value, swap(value, "dp", bit))
        return value

    def spread_out(value, bits):
        for bit in reversed(bits):
            value = gather(value, bit)
        return value

    total_c = far_step(sum_c, out_second)
    total_c, rest_c = total_c[:cut], total_c[cut:]
    total_a = spread_out(total_a, dp_bits[:-1])
    total_c = spread_out(finish(total_c, dp_bits), dp_bits[:-1])
    other = [dp_bits[1], dp_bits[0], *dp_bits[2:]]
    rest_c = spread_out(finish(rest_c, other), other[:-1])
    total_b = spread_out(finish(total_b, dp_bits[1:]), dp_bits[:-1])
    line = line + swap(line, "tp", core)
    line = line + swap(line, "tp", far)
    total_c = jnp.concatenate([total_c.astype(F32), rest_c.astype(F32)], axis=0)
    own = lax.dynamic_slice_in_dim(line, 8 + rank, 1, 0)[0]
    own_q = lax.dynamic_slice(line, (16 + rank, 0), (1, width))
    own_v = lax.dynamic_slice(line, (16 + PARTS + rank, 0), (1, width))
    return (
        jnp.concatenate([out_first, out_second], axis=0),
        d_tokens,
        total_c[: 3 * width].reshape(3, width, depth).transpose(0, 2, 1),
        jnp.concatenate([own_q, own_v], axis=0),
        total_c[3 * width :],
        line[3],
        total_b.astype(F32),
        own,
        total_a.astype(F32),
        line[0],
        jnp.stack([line[4], line[1]]),
        jnp.stack([line[5], line[2]]),
    )


def solution(mesh):
    placed = (
        P(("dp", "tp"), None),
        P(None, None, "tp"),
        P(None, "tp"),
        P("tp", None),
        P(),
        P(None, "tp"),
        P("tp"),
        P("tp", None),
        P(),
        P(),
        P(),
        P("dp"),
        P("dp", None),
        P(("dp", "tp"), None),
    )
    return jax.shard_map(
        on_device,
        mesh=mesh,
        in_specs=placed,
        out_specs=(
            P(("dp", "tp"), None),
            P(("dp", "tp"), None),
            P(None, None, "tp"),
            P(None, "tp"),
            P("tp", None),
            P(),
            P(None, "tp"),
            P("tp"),
            P("tp", None),
            P(),
            P(),
            P(),
        ),
        check_vma=False,
    )
```

```python
import jax
import jax.numpy as jnp
from jax import lax
from jax.experimental import pallas as pl
from jax.experimental.pallas import tpu as pltpu
from jax.sharding import PartitionSpec as P

HD = 64
SCALE = HD ** (-0.5)
NORM_EPS = 1e-06
MASKED = -1e30
HALF_ROOT = 0.5 ** 0.5
DENSITY = 0.3989422804014327
PARTS = 4
BF = jnp.bfloat16
F32 = jnp.float32


def nn(left, right):
    return lax.dot_general(left, right, (((1,), (0,)), ((), ())), preferred_element_type=F32)


def nt(left, right):
    return lax.dot_general(left, right, (((1,), (1,)), ((), ())), preferred_element_type=F32)


def tn(left, right):
    return lax.dot_general(left, right, (((0,), (0,)), ((), ())), preferred_element_type=F32)


def head_masks(width, dtype=BF):
    lane = lax.broadcasted_iota(jnp.int32, (1, width), 1) // HD
    return [(lane == head).astype(dtype) for head in range(width // HD)]


def spread_of(picks, length):
    slots = picks.shape[1]
    return (lax.broadcasted_iota(jnp.int32, (length, slots), 0) == picks).astype(F32).astype(BF)


def whole(shape):
    zeros = (0,) * len(shape)
    return pl.BlockSpec(shape, lambda *_: zeros)


def norm_forward(values, gain, shift):
    average = jnp.mean(values, axis=1, keepdims=True)
    centered = values - average
    inv_std = lax.rsqrt(jnp.mean(centered * centered, axis=1, keepdims=True) + NORM_EPS)
    normed = centered * inv_std
    return normed * gain + shift, normed, inv_std


def norm_backward(grad, normed, inv_std, gain):
    scaled = grad * gain
    first = jnp.mean(scaled, axis=1, keepdims=True)
    second = jnp.mean(scaled * normed, axis=1, keepdims=True)
    return inv_std * (scaled - first - normed * second)


def tie(value, *others):
    return lax.optimization_barrier((value, others))[0]


SMALL = pl.CostEstimate(flops=1024, transcendentals=0, bytes_accessed=1024)


def col_sum(values):
    return jnp.sum(values, axis=0, keepdims=True)


def piece_copies(pieces, target, sems, first, bit):
    rows = target.shape[0]
    if len(pieces) == 1:
        return [pltpu.make_async_copy(pieces[0][0], target, sems.at[first])]
    half, step = rows // 2, rows // len(pieces)
    own = ((lax.axis_index("dp") // bit) % 2) * half
    copies = []
    for n, (ref, skip) in enumerate(pieces):
        base = own if n * step < half else half - own
        start = pl.multiple_of(base + (n * step) % half, step)
        copies.append(pltpu.make_async_copy(ref.at[pl.ds(skip, step), :], target.at[pl.ds(start, step), :], sems.at[first + n]))
    return copies


def stacked_copies(pieces, target, sems, first, bit):
    copies = []
    for part, refs in enumerate(pieces):
        copies.append(piece_copies(refs, target.at[part], sems, first, bit))
        first += len(refs)
    return copies


def take(it, pieces):
    return [[(next(it), skip) for _, skip in piece] for piece in pieces]


def flat(pieces):
    return [p for piece in pieces for p in piece]


def arrays(pieces):
    return [array for array, _ in flat(pieces)]


def start_all(copies):
    for copy in copies:
        copy.start()


def wait_all(copies):
    for copy in copies:
        copy.wait()


ANY_SPEC = pl.BlockSpec(memory_space=pl.ANY)


def shaped(shape):
    return pl.BlockSpec(shape, lambda *_: (0,) * len(shape))


def attend_body(len_ref, x_ref, small_ref, pick_ref, *rest, count):
    w_refs = [(ref, 0) for ref in rest[:count]]
    q_sel_ref, k_ref, v_ref, ctx_ref, ctx_sel_ref, ext_ref, w_ref, sems = rest[count:]
    rows, width = k_ref.shape
    seq = pl.program_id(0)
    row = lax.axis_index("tp") * pl.num_programs(0) + seq
    length = len_ref[row]
    copies = piece_copies(w_refs, w_ref, sems, 0, 1)

    @pl.when(seq == 0)
    def _():
        start_all(copies)
        wait_all(copies)

    x = x_ref[...]
    queries = (nt(x, w_ref[0:width, :]) + small_ref[1:2, :width]).astype(BF)
    key_rows = nt(x, w_ref[width : 2 * width, :]).astype(BF)
    values = (nt(x, w_ref[2 * width : 3 * width, :]) + small_ref[2:3, :width]).astype(BF)
    k_ref[...] = key_rows
    v_ref[...] = values
    ext_ref[:, :width] = values
    ext_ref[:, width:] = jnp.ones((rows, ext_ref.shape[1] - width), BF)
    spread = spread_of(pick_ref[pl.ds(row, 1), :], rows)
    q_sel_ref[...] = tn(spread, queries).astype(BF)
    scaled = queries * jnp.asarray(SCALE, BF)
    masks = head_masks(width)
    tile = min(256, rows)
    keep = lax.broadcasted_iota(jnp.int32, (tile, rows), 1) < length
    for start in range(0, rows, tile):
        total = jnp.zeros((tile, width), F32)
        for mask in masks:
            logits = nt(scaled[start : start + tile] * mask, key_rows)
            logits = jnp.where(keep, logits, MASKED)
            peak = jnp.max(logits, axis=1, keepdims=True)
            probs = jnp.exp(logits - peak).astype(BF)
            mixed = nn(probs, ext_ref[...])
            share = mixed[:, :width] / mixed[:, width : width + 1]
            total = jnp.where(mask.astype(F32) > 0.5, share, total)
        ctx_ref[start : start + tile, :] = total.astype(BF)
    ctx_sel_ref[...] = tn(spread, ctx_ref[...]).astype(BF)


def attend_forward(lengths, x, pieces, width, small, picked, seqs):
    slots = picked.shape[1]
    rows = x.shape[0] // seqs
    depth = x.shape[1]
    ext = -(-(width + 1) // 128) * 128
    row_spec = pl.BlockSpec((rows, width), lambda s, _: (s, 0))
    sel_spec = pl.BlockSpec((slots, width), lambda s, _: (s, 0))
    return pl.pallas_call(
        lambda *refs: attend_body(*refs, count=len(pieces)),
        grid_spec=pltpu.PrefetchScalarGridSpec(
            num_scalar_prefetch=1,
            grid=(seqs,),
            in_specs=[
                pl.BlockSpec((rows, depth), lambda s, _: (s, 0)),
                whole(small.shape),
                whole(picked.shape),
                *[ANY_SPEC] * len(pieces),
            ],
            out_specs=[sel_spec, row_spec, row_spec, row_spec, sel_spec],
            scratch_shapes=[
                pltpu.VMEM((rows, ext), BF),
                pltpu.VMEM((3 * width, depth), BF),
                pltpu.SemaphoreType.DMA((len(pieces),)),
            ],
        ),
        out_shape=[
            jax.ShapeDtypeStruct((seqs * slots, width), BF),
            jax.ShapeDtypeStruct((seqs * rows, width), BF),
            jax.ShapeDtypeStruct((seqs * rows, width), BF),
            jax.ShapeDtypeStruct((seqs * rows, width), BF),
            jax.ShapeDtypeStruct((seqs * slots, width), BF),
        ],
        cost_estimate=SMALL,
        name="attend_forward",
    )(lengths, x, small, picked, *pieces)


def attend_back_body(
    len_ref, q_ref, k_ref, v_ref, d_ctx_ref, x_ref, x_sel_ref, ctx_sel_ref, g1_ref, dq_ref, dk_ref, dv_ref, sums_ref, grad_ref, acc_ref, *, part
):
    rows, width = k_ref.shape
    slots = q_ref.shape[0]
    seq = pl.program_id(0)
    rank = lax.axis_index("tp")
    length = len_ref[rank * pl.num_programs(0) + seq]
    masks = head_masks(width)
    queries, d_ctx = q_ref[...], d_ctx_ref[...]
    key_rows, values = k_ref[...], v_ref[...]
    q_stack = jnp.concatenate([queries * mask for mask in masks], axis=0)
    d_stack = jnp.concatenate([d_ctx * mask for mask in masks], axis=0)
    logits = nt(key_rows, q_stack * jnp.asarray(SCALE, BF))
    keep = lax.broadcasted_iota(jnp.int32, logits.shape, 0) < length
    logits = jnp.where(keep, logits, MASKED)
    grown = jnp.exp(logits - jnp.max(logits, axis=0, keepdims=True))
    probs = grown * (1.0 / jnp.sum(grown, axis=0, keepdims=True))
    d_probs = nt(values, d_stack)
    inner = jnp.sum(probs * d_probs, axis=0, keepdims=True)
    d_raw = (probs * (d_probs - inner) * SCALE).astype(BF)
    d_keys = nn(d_raw, q_stack).astype(BF)
    dk_ref[...] = d_keys
    d_values = nn(probs.astype(BF), d_stack).astype(BF)
    dv_ref[...] = d_values
    dq_stack = tn(d_raw, key_rows)
    dq = jnp.zeros((slots, width), F32)
    for head, mask in enumerate(masks):
        dq = jnp.where(mask.astype(F32) > 0.5, dq_stack[head * slots : (head + 1) * slots], dq)
    dq = dq.astype(BF)
    dq_ref[...] = dq

    @pl.when(seq == 0)
    def _():
        acc_ref[...] = jnp.zeros(acc_ref.shape, F32)
        sums_ref[...] = jnp.zeros(sums_ref.shape, F32)

    at = rank ^ part
    sums_ref[pl.ds(at, 1), 0:width] += col_sum(dq.astype(F32))
    sums_ref[pl.ds(PARTS + at, 1), 0:width] += col_sum(d_values.astype(F32))
    acc_ref[0:width, :] += tn(dq, x_sel_ref[...])
    acc_ref[width : 2 * width, :] += tn(d_keys, x_ref[...])
    acc_ref[2 * width : 3 * width, :] += tn(d_values, x_ref[...])
    acc_ref[3 * width : 4 * width, :] += tn(ctx_sel_ref[...], g1_ref[...])

    @pl.when(seq == pl.num_programs(0) - 1)
    def _():
        grad_ref[...] = acc_ref[...].astype(BF)


def attend_backward(part, lengths, q_sel, k, v, d_ctx, x, x_sel, ctx_sel, g1, seqs):
    rows, slots, width = k.shape[0] // seqs, q_sel.shape[0] // seqs, k.shape[1]
    depth = x.shape[1]
    row_spec = pl.BlockSpec((rows, width), lambda s, _: (s, 0))
    sel_spec = pl.BlockSpec((slots, width), lambda s, _: (s, 0))
    wide_spec = pl.BlockSpec((slots, depth), lambda s, _: (s, 0))
    return pl.pallas_call(
        lambda *refs: attend_back_body(*refs, part=part),
        grid_spec=pltpu.PrefetchScalarGridSpec(
            num_scalar_prefetch=1,
            grid=(seqs,),
            in_specs=[
                sel_spec,
                row_spec,
                row_spec,
                sel_spec,
                pl.BlockSpec((rows, depth), lambda s, _: (s, 0)),
                wide_spec,
                sel_spec,
                wide_spec,
            ],
            out_specs=[sel_spec, row_spec, row_spec, whole((2 * PARTS, depth)), whole((4 * width, depth))],
            scratch_shapes=[pltpu.VMEM((4 * width, depth), F32)],
        ),
        out_shape=[
            jax.ShapeDtypeStruct(q_sel.shape, BF),
            jax.ShapeDtypeStruct(k.shape, BF),
            jax.ShapeDtypeStruct(k.shape, BF),
            jax.ShapeDtypeStruct((2 * PARTS, depth), F32),
            jax.ShapeDtypeStruct((4 * width, depth), BF),
        ],
        cost_estimate=SMALL,
        name="attend_backward",
    )(lengths, q_sel, k, v, d_ctx, x, x_sel, ctx_sel, g1)


def erf_gelu(values):
    return 0.5 * (1.0 + lax.erf(values * HALF_ROOT))


def run(body, plain, hbm, outs, hbm_outs, scratch, name):
    return pl.pallas_call(
        body,
        grid=(1,),
        in_specs=[*[shaped(a.shape) for a in plain], *[ANY_SPEC] * len(hbm)],
        out_specs=[*[shaped(a.shape) for a in outs], *[ANY_SPEC] * len(hbm_outs)],
        out_shape=[*outs, *hbm_outs],
        scratch_shapes=scratch,
        cost_estimate=SMALL,
        name=name,
    )(*plain, *hbm)


def struct(dtype, *shape):
    return jax.ShapeDtypeStruct(shape, dtype)


def unit_part(low, wi, bias, slope_ref, n):
    pre = nn(low, wi) + bias
    chance = erf_gelu(pre)
    slope_ref[n] = chance + pre * (DENSITY * jnp.exp(-0.5 * pre * pre))
    return (pre * chance).astype(BF)


def ffn_prep(picked, x, d_out, ctx_sel, wo, wi, wd, small, shared, seqs):
    parts, near = len(wo), len(wi)
    slots = picked.shape[1]
    count, depth, units, width = seqs * slots, x.shape[1], wi[0][0][0].shape[1], ctx_sel[0].shape[1]
    plain = [picked, x, d_out, shared, *ctx_sel, *small]
    hbm = arrays(wo) + arrays(wi) + arrays(wd)

    def body(*refs):
        it = iter(refs)
        pick_ref, x_ref, d_out_ref, shared_ref = (next(it) for _ in range(4))
        ctx_refs = [next(it) for _ in range(parts)]
        small_refs = [next(it) for _ in range(near)]
        wo_refs, wi_refs, wd_refs = take(it, wo), take(it, wi), take(it, wd)
        act_refs = [next(it) for _ in range(near)]
        slope_ref, x_sel_ref, cot_ref, low_ref, sum_ref, normed1_ref, inv1_ref = (next(it) for _ in range(7))
        wo_v, wi_v, wd_v, sems = (next(it) for _ in range(4))
        out_copies = stacked_copies(wo_refs, wo_v, sems, 0, 1)
        first = len(flat(wo))
        in_copies = stacked_copies(wi_refs, wi_v, sems, first, 1)
        down_copies = stacked_copies(wd_refs, wd_v, sems, first + len(flat(wi)), 2)
        start_all(flat(out_copies) + flat(in_copies) + flat(down_copies))
        rows = x_ref.shape[0] // seqs
        for seq in range(seqs):
            at = lax.axis_index("tp") * seqs + seq
            spread = spread_of(pick_ref[pl.ds(at, 1), :], rows)
            x_sel_ref[seq * slots : (seq + 1) * slots, :] = tn(spread, x_ref[seq * rows : (seq + 1) * rows, :]).astype(BF)
            cot_ref[seq * slots : (seq + 1) * slots, :] = tn(spread, d_out_ref[seq * rows : (seq + 1) * rows, :]).astype(BF)
        attn_sum = x_sel_ref[...].astype(F32) + shared_ref[0:1, :]
        wait_all(flat(out_copies))
        for part in range(parts):
            attn_sum = attn_sum + nn(ctx_refs[part][...], wo_v[part])
        hidden, normed1, inv1 = norm_forward(attn_sum, shared_ref[2:3, :], shared_ref[4:5, :])
        low = hidden.astype(BF)
        low_ref[...] = low
        normed1_ref[...] = normed1
        inv1_ref[...] = inv1
        total = hidden + shared_ref[1:2, :]
        wait_all(flat(in_copies) + flat(down_copies))
        for n in range(near):
            act = unit_part(low, wi_v[n], small_refs[n][0:1, :], slope_ref, n)
            act_refs[n][...] = act
            total = total + nn(act, wd_v[n])
        sum_ref[...] = total

    outs = [
        *[struct(BF, count, units)] * near,
        struct(F32, near, count, units),
        struct(BF, count, depth),
        struct(BF, count, depth),
        struct(BF, count, depth),
        struct(F32, count, depth),
        struct(F32, count, depth),
        struct(F32, count, 1),
    ]
    scratch = [
        pltpu.VMEM((parts, width, depth), BF),
        pltpu.VMEM((near, depth, units), BF),
        pltpu.VMEM((near, units, depth), BF),
        pltpu.SemaphoreType.DMA((len(hbm),)),
    ]
    return run(body, plain, hbm, outs, [], scratch, "ffn_prep")


def ffn_front(low, total, cot, wi, wd, small, shared):
    far = len(wi)
    count, depth = low.shape
    units = wi[0][0][0].shape[1]
    plain = [low, total, cot, shared, *small]
    hbm = arrays(wi) + arrays(wd)

    def body(*refs):
        it = iter(refs)
        low_ref, sum_ref, cot_ref, shared_ref = (next(it) for _ in range(4))
        small_refs = [next(it) for _ in range(far)]
        wi_refs, wd_refs = take(it, wi), take(it, wd)
        sent_ref, g2_ref, slope_ref, grad2_ref, vec_ref = (next(it) for _ in range(5))
        wi_v, wd_v, sems = (next(it) for _ in range(3))
        in_copies = stacked_copies(wi_refs, wi_v, sems, 0, 1)
        down_copies = stacked_copies(wd_refs, wd_v, sems, len(flat(wi)), 2)
        for n in range(far):
            start_all(in_copies[n] + down_copies[n])
        low = low_ref[...]
        total = sum_ref[...]
        for n in range(far):
            wait_all(in_copies[n])
            act = unit_part(low, wi_v[n], small_refs[n][0:1, :], slope_ref, n)
            sent_ref[n * count : (n + 1) * count, :] = act
            wait_all(down_copies[n])
            total = total + nn(act, wd_v[n])
        _, normed2, inv2 = norm_forward(total, shared_ref[3:4, :], shared_ref[5:6, :])
        cotangent = cot_ref[...].astype(F32)
        grad2 = norm_backward(cotangent, normed2, inv2, shared_ref[3:4, :])
        vec_ref[...] = jnp.zeros(vec_ref.shape, F32)
        vec_ref[0:1, :] = col_sum(grad2)
        vec_ref[1:2, :] = col_sum(cotangent * normed2)
        vec_ref[2:3, :] = col_sum(cotangent)
        grad2_ref[...] = grad2
        g2 = grad2.astype(BF)
        g2_ref[...] = g2
        sent_ref[far * count :, :] = g2

    outs = [
        struct(BF, (far + 1) * count, units),
        struct(BF, count, depth),
        struct(F32, far, count, units),
        struct(F32, count, depth),
        struct(F32, 16, depth),
    ]
    scratch = [
        pltpu.VMEM((far, depth, units), BF),
        pltpu.VMEM((far, units, depth), BF),
        pltpu.SemaphoreType.DMA((len(hbm),)),
    ]
    return run(body, plain, hbm, outs, [], scratch, "ffn_front")


def ffn_mid(g2, slopes, wd):
    parts = len(wd)
    near = slopes[0].shape[0]
    count, depth = g2.shape
    units = slopes[0].shape[2]
    hbm = [*slopes, *arrays(wd)]

    def body(*refs):
        it = iter(refs)
        g2_ref = next(it)
        slope_hbm = [next(it) for _ in slopes]
        wd_refs = take(it, wd)
        d_refs = [next(it) for _ in range(near)]
        sent_ref, vec_ref = next(it), next(it)
        wd_v, slope_v, sems, slope_sems = (next(it) for _ in range(4))
        down_copies = stacked_copies(wd_refs, wd_v, sems, 0, 2)
        sources = [ref.at[n] for ref in slope_hbm for n in range(ref.shape[0])]
        slope_copies = [pltpu.make_async_copy(sources[part], slope_v.at[part], slope_sems.at[part]) for part in range(parts)]
        for part in range(parts):
            start_all(down_copies[part] + [slope_copies[part]])
        vec_ref[...] = jnp.zeros(vec_ref.shape, F32)
        g2 = g2_ref[...]
        for part in range(parts):
            wait_all(down_copies[part] + [slope_copies[part]])
            d_pre = (nt(g2, wd_v[part]) * slope_v[part]).astype(BF)
            if part < near:
                d_refs[part][...] = d_pre
            else:
                sent_ref[(part - near) * count : (part - near + 1) * count, :] = d_pre
            at = 8 + (lax.axis_index("tp") ^ part)
            vec_ref[pl.ds(at, 1), :] = col_sum(d_pre.astype(F32))

    outs = [*[struct(BF, count, units)] * near, struct(BF, (parts - near) * count, units), struct(F32, 16, depth)]
    scratch = [
        pltpu.VMEM((parts, units, depth), BF),
        pltpu.VMEM((parts, count, units), F32),
        pltpu.SemaphoreType.DMA((len(arrays(wd)),)),
        pltpu.SemaphoreType.DMA((parts,)),
    ]
    return run(body, [g2], hbm, outs, [], scratch, "ffn_mid")


def pair_sums(pairs):
    count = min(array.shape[0] for array, _ in pairs[0])
    width, depth = pairs[0][0][0].shape[1], pairs[0][1][0].shape[1]
    tile = min(256, width)

    def body(*refs):
        total = tn(refs[0][...], refs[1][...])
        for n in range(1, len(pairs)):
            total = total + tn(refs[2 * n][...], refs[2 * n + 1][...])
        refs[-1][...] = total.astype(BF)

    def left(block):
        return pl.BlockSpec((count, tile), lambda i: (block, i))

    def right(block):
        return pl.BlockSpec((count, depth), lambda i: (block, 0))

    return pl.pallas_call(
        body,
        grid=(width // tile,),
        in_specs=[spec for (_, a), (_, b) in pairs for spec in (left(a), right(b))],
        out_specs=pl.BlockSpec((tile, depth), lambda i: (i, 0)),
        out_shape=jax.ShapeDtypeStruct((width, depth), BF),
        cost_estimate=SMALL,
        name="pair_sums",
    )(*[array for (a, _), (b, _) in pairs for array in (a, b)])


def ffn_back(grad2, d_near, d_far, normed1, inv1, shared, wi, wo, width):
    parts, near = len(wi), len(d_near)
    count, depth = grad2.shape
    units = d_far.shape[1]
    hbm = arrays(wi) + arrays(wo)

    def body(*refs):
        it = iter(refs)
        grad2_ref, normed1_ref, inv1_ref, shared_ref = (next(it) for _ in range(4))
        near_refs = [next(it) for _ in range(near)]
        far_ref = next(it)
        wi_refs, wo_refs = take(it, wi), take(it, wo)
        g1_ref, grad1_ref, vec_ref = next(it), next(it), next(it)
        d_ctx_refs = [next(it) for _ in range(parts)]
        wi_v, wo_v, sems = (next(it) for _ in range(3))
        in_copies = stacked_copies(wi_refs, wi_v, sems, 0, 1)
        out_copies = stacked_copies(wo_refs, wo_v, sems, len(flat(wi)), 1)
        start_all(flat(in_copies) + flat(out_copies))
        d_hidden = grad2_ref[...]
        for part in range(parts):
            wait_all(in_copies[part])
            d_pre = near_refs[part][...] if part < near else far_ref[(part - near) * count : (part - near + 1) * count, :]
            d_hidden = d_hidden + nt(d_pre, wi_v[part])
        normed1 = normed1_ref[...]
        grad1 = norm_backward(d_hidden, normed1, inv1_ref[...], shared_ref[2:3, :])
        vec_ref[...] = jnp.zeros(vec_ref.shape, F32)
        vec_ref[3:4, :] = col_sum(grad1)
        vec_ref[4:5, :] = col_sum(d_hidden * normed1)
        vec_ref[5:6, :] = col_sum(d_hidden)
        grad1_ref[...] = grad1
        g1 = grad1.astype(BF)
        g1_ref[...] = g1
        wait_all(flat(out_copies))
        for part in range(parts):
            d_ctx_refs[part][...] = nt(g1, wo_v[part]).astype(BF)

    outs = [struct(BF, count, depth), struct(F32, count, depth), struct(F32, 16, depth), *[struct(BF, count, width)] * parts]
    scratch = [
        pltpu.VMEM((parts, depth, units), BF),
        pltpu.VMEM((parts, width, depth), BF),
        pltpu.SemaphoreType.DMA((len(hbm),)),
    ]
    return run(body, [grad2, normed1, inv1, shared, *d_near, d_far], hbm, outs, [], scratch, "ffn_back")


def ffn_rows(x, ctx, wo, wi, wd, small, shared, first, count):
    parts = len(wo)
    depth = x.shape[1]
    units, width = wi[0][0][0].shape[1], ctx[0].shape[1]
    tile = min(256, count)
    start = first // tile
    hbm = arrays(wo) + arrays(wi) + arrays(wd)

    def body(*refs):
        it = iter(refs)
        x_ref = next(it)
        ctx_refs = [next(it) for _ in range(parts)]
        small_refs = [next(it) for _ in range(parts)]
        shared_ref = next(it)
        wo_refs, wi_refs, wd_refs = take(it, wo), take(it, wi), take(it, wd)
        out_ref, wo_v, wi_v, wd_v, sems = (next(it) for _ in range(5))
        out_copies = flat(stacked_copies(wo_refs, wo_v, sems, 0, 1))
        near = len(flat(wo))
        in_copies = stacked_copies(wi_refs, wi_v, sems, near, 1)
        down_copies = stacked_copies(wd_refs, wd_v, sems, near + len(flat(wi)), 2)
        opening = pl.program_id(0) == 0

        @pl.when(opening)
        def _():
            start_all(out_copies)
            for part in range(parts):
                start_all(in_copies[part] + down_copies[part])
            wait_all(out_copies)

        attn_sum = x_ref[...].astype(F32) + shared_ref[0:1, :]
        for part in range(parts):
            attn_sum = attn_sum + nn(ctx_refs[part][...], wo_v[part])
        hidden, _, _ = norm_forward(attn_sum, shared_ref[2:3, :], shared_ref[4:5, :])
        low = hidden.astype(BF)
        total = hidden + shared_ref[1:2, :]
        for part in range(parts):

            @pl.when(opening)
            def _():
                wait_all(in_copies[part] + down_copies[part])

            pre = nn(low, wi_v[part]) + small_refs[part][0:1, :]
            act = (pre * erf_gelu(pre)).astype(BF)
            total = total + nn(act, wd_v[part])
        out_ref[...] = norm_forward(total, shared_ref[3:4, :], shared_ref[5:6, :])[0].astype(BF)

    return pl.pallas_call(
        body,
        grid=(count // tile,),
        in_specs=[
            pl.BlockSpec((tile, depth), lambda i: (i + start, 0)),
            *[pl.BlockSpec((tile, width), lambda i: (i + start, 0))] * parts,
            *[shaped(a.shape) for a in small],
            shaped(shared.shape),
            *[ANY_SPEC] * len(hbm),
        ],
        out_specs=pl.BlockSpec((tile, depth), lambda i: (i, 0)),
        out_shape=jax.ShapeDtypeStruct((count, depth), BF),
        scratch_shapes=[
            pltpu.VMEM((parts, width, depth), BF),
            pltpu.VMEM((parts, depth, units), BF),
            pltpu.VMEM((parts, units, depth), BF),
            pltpu.SemaphoreType.DMA((len(hbm),)),
        ],
        cost_estimate=SMALL,
        name="ffn_rows",
    )(x, *ctx, *small, shared, *hbm)


def input_gradient(picked, grad1, dq, dk, dv, wq, seqs):
    parts = len(dq)
    slots = picked.shape[1]
    depth = grad1.shape[1]
    rows, width = dk[0].shape[0] // seqs, dk[0].shape[1]
    hbm = arrays(wq)

    def body(*refs):
        it = iter(refs)
        pick_ref, grad1_ref = next(it), next(it)
        dq_refs = [next(it) for _ in range(parts)]
        dk_refs = [next(it) for _ in range(parts)]
        dv_refs = [next(it) for _ in range(parts)]
        wq_refs = take(it, wq)
        out_ref, wq_v, sems = next(it), next(it), next(it)
        copies = flat(stacked_copies(wq_refs, wq_v, sems, 0, 1))
        seq = pl.program_id(0)

        @pl.when(seq == 0)
        def _():
            start_all(copies)
            wait_all(copies)

        chosen = grad1_ref[...]
        for part in range(parts):
            chosen = chosen + nn(dq_refs[part][...], wq_v[part, 0:width, :])
        high = chosen.astype(BF)
        rest = (chosen - high.astype(F32)).astype(BF)
        spread = spread_of(pick_ref[pl.ds(lax.axis_index("tp") * seqs + seq, 1), :], rows)
        total = nn(spread, high) + nn(spread, rest)
        for part in range(parts):
            total = total + nn(dk_refs[part][...], wq_v[part, width : 2 * width, :])
            total = total + nn(dv_refs[part][...], wq_v[part, 2 * width : 3 * width, :])
        out_ref[...] = total.astype(BF)

    row_spec = pl.BlockSpec((rows, width), lambda s: (s, 0))
    return pl.pallas_call(
        body,
        grid=(seqs,),
        in_specs=[
            whole(picked.shape),
            pl.BlockSpec((slots, depth), lambda s: (s, 0)),
            *[pl.BlockSpec((slots, width), lambda s: (s, 0))] * parts,
            *[row_spec] * (2 * parts),
            *[ANY_SPEC] * len(hbm),
        ],
        out_specs=pl.BlockSpec((rows, depth), lambda s: (s, 0)),
        out_shape=jax.ShapeDtypeStruct((seqs * rows, depth), BF),
        scratch_shapes=[pltpu.VMEM((parts, 3 * width, depth), BF), pltpu.SemaphoreType.DMA((len(hbm),))],
        cost_estimate=SMALL,
        name="input_gradient",
    )(picked, grad1, *dq, *dk, *dv, *hbm)


def bits_of(count):
    return [1 << b for b in range(count.bit_length() - 1)]


def swap(value, axis, bit):
    count = lax.axis_size(axis)
    return lax.ppermute(value, axis, [(i, i ^ bit) for i in range(count)])


def half_of(value, bit, own):
    half = value.shape[0] // 2
    side = (lax.axis_index("dp") // bit) % 2
    return lax.dynamic_slice_in_dim(value, jnp.where(side == 0, 0, half) if own else jnp.where(side == 0, half, 0), half, 0)


def joined(own, got, bit):
    side = (lax.axis_index("dp") // bit) % 2
    return jnp.concatenate([jnp.where(side == 0, own, got), jnp.where(side == 0, got, own)], axis=0)


def add(*values):
    total = values[0].astype(F32)
    for value in values[1:]:
        total = total + value.astype(F32)
    return total.astype(BF)


def scatter(value, bit, *after):
    sent, kept = half_of(value, bit, False), half_of(value, bit, True)
    return add(tie(kept, *after), swap(sent, "dp", bit))


def gather(value, bit):
    return joined(value, swap(value, "dp", bit), bit)


def on_device(
    tokens, w_qkv, qv_bias, w_out, out_bias, w_in, in_bias, w_down, down_bias, norm_gain, norm_shift, valid_len, picked, d_out
):
    parts = lax.axis_size("tp")
    rank = lax.axis_index("tp")
    seqs = valid_len.shape[0] // parts
    depth = tokens.shape[1]
    width = w_qkv.shape[2]
    core, far = 1, 2
    dp_bits = bits_of(lax.axis_size("dp"))

    shared = jnp.concatenate([out_bias[None], down_bias[None], norm_gain, norm_shift, jnp.zeros((2, depth), F32)], axis=0)
    small = [jnp.concatenate([in_bias[None], jnp.pad(qv_bias, ((0, 5), (0, depth - width)))], axis=0)]
    small += [swap(small[0], "tp", core)]
    wq = w_qkv.transpose(0, 2, 1).reshape(3 * width, depth)
    qo_far = swap(jnp.concatenate([half_of(wq, 1, True), half_of(w_out, 1, True)], axis=0), "tp", far)
    wq_near = swap(wq, "tp", core)
    ready = small[1]
    small_far = swap(jnp.concatenate(small, axis=0), "tp", far)
    ff_far = swap(tie(jnp.concatenate([half_of(w_in, 1, True), half_of(w_down, 2, True)], axis=0), small_far), "tp", far)
    small += [small_far[:8], small_far[8:]]

    def forward(j, x, pieces):
        return attend_forward(valid_len, x, pieces, width, small[j], picked, seqs)

    out0 = forward(0, tie(tokens, ready), [wq])
    qo_far = tie(qo_far, out0[0])
    qo_rest, qo_far_core = swap(qo_far, "dp", 1), swap(qo_far, "tp", core)
    out1 = forward(1, tie(tokens, qo_far), [wq_near])
    qo_rest = tie(qo_rest, out1[0])
    qo_rest_core = swap(qo_rest, "tp", core)
    wo_near = swap(tie(w_out, qo_rest), "tp", core)
    out2 = forward(2, tie(tokens, qo_rest), [qo_far, qo_rest])
    wi_near, wd_near = swap(tie(w_in, out2[0]), "tp", core), swap(tie(w_down, out2[0]), "tp", core)
    out3 = forward(3, tie(tokens, out2[0]), [qo_far_core, qo_rest_core])
    ff_far = tie(ff_far, out3[0])
    rows_in = ff_far.shape[0] // 2
    wi_rest, wd_rest = swap(ff_far[:rows_in], "dp", 1), swap(ff_far[rows_in:], "dp", 2)
    ff_far_core = swap(ff_far, "tp", core)
    q_sel, k, v, ctx, ctx_sel = zip(out0, out1, out2, out3)
    rows_q = 3 * width // 2

    def pieces(own, near, far_pieces, core_pieces):
        return [[(own, 0)], [(near, 0)], far_pieces, core_pieces]

    wq = pieces(wq, wq_near, [(qo_far, 0), (qo_rest, 0)], [(qo_far_core, 0), (qo_rest_core, 0)])
    wo = pieces(w_out, wo_near, [(qo_far, rows_q), (qo_rest, rows_q)], [(qo_far_core, rows_q), (qo_rest_core, rows_q)])
    near_in, near_down = [[(w_in, 0)], [(wi_near, 0)]], [[(w_down, 0)], [(wd_near, 0)]]
    prep = ffn_prep(picked, tie(tokens, ff_far), d_out, ctx_sel, wo, near_in, near_down, small[:2], shared, seqs)
    *act, slope_near, x_sel, cot, low, ffn_sum, normed1, inv1 = prep
    low_far, low_near, act_near = swap(low, "tp", far), swap(low, "tp", core), swap(act[1], "tp", core)
    wi_rest, wd_rest = tie((wi_rest, wd_rest), low)
    wi_rest_core, wd_rest_core = swap(wi_rest, "tp", core), swap(wd_rest, "tp", core)
    wi = near_in + [[(ff_far, 0), (wi_rest, 0)], [(ff_far_core, 0), (wi_rest_core, 0)]]
    wd = near_down + [[(ff_far, rows_in), (wd_rest, 0)], [(ff_far_core, rows_in), (wd_rest_core, 0)]]

    sent, g2, slope_far, grad2, vec = ffn_front(tie(low, low_far), ffn_sum, cot, wi[2:], wd[2:], small[2:], shared)
    act_got = swap(sent, "tp", far)
    g2_near, low_diag = swap(g2, "tp", core), swap(tie(low_far, g2), "tp", core)
    *d_near, d_far, vec_mid = ffn_mid(g2, [slope_near, slope_far], wd)
    d_got, d_got_near = swap(d_far, "tp", far), swap(d_near[1], "tp", core)
    g1, grad1, vec_back, *d_ctx = ffn_back(tie(grad2, act_near, low_near, g2_near), d_near, d_far, normed1, inv1, shared, wi, wo, width)
    count = low.shape[0]

    def backward(j, x):
        return attend_backward(j, valid_len, q_sel[j], k[j], v[j], d_ctx[j], x, x_sel, ctx_sel[j], g1, seqs)

    def rows_of(first, *after):
        return ffn_rows(tie(tokens, *after), ctx, wo, wi, wd, small, shared, first, half_rows)

    def finish(value, bits):
        for bit in bits:
            value = scatter(value, bit) if bit != last else add(value, swap(value, "dp", bit))
        return value

    def spread_out(value, bits):
        for bit in reversed(bits):
            value = gather(value, bit)
        return value

    half_rows, last = tokens.shape[0] // 2, dp_bits[-1]
    out3 = backward(3, tie(tokens, d_got_near, low_diag))
    out2 = backward(2, tie(tokens, out3[0]))
    act_got = tie(act_got, out2[0])
    act_diag = swap(act_got[count:], "tp", core)
    out1 = backward(1, tie(tokens, out2[0], act_got))
    total_a = pair_sums(
        [
            ((tie(act[0], out1[0]), 0), (g2, 0)),
            ((act_near, 0), (g2_near, 0)),
            ((act_got, 0), (act_got, 2)),
            ((act_diag, 0), (act_diag, 1)),
        ]
    )
    sent_a = half_of(total_a, dp_bits[0], False)
    out0 = backward(0, tie(tokens, out1[0], sent_a))
    dq, dk, dv, sums, g_heads = zip(out0, out1, out2, out3)
    d_got = tie(d_got, out0[0])
    d_diag = swap(d_got[count:], "tp", core)
    far_c = add(tie(out2[4], out0[0]), swap(tie(out3[4], out1[0]), "tp", core))
    near_c = g_heads[0], swap(tie(g_heads[1], out0[0]), "tp", core)
    line = jnp.concatenate([vec + vec_mid + vec_back, sums[0] + sums[1] + sums[2] + sums[3]], axis=0)
    out_first = rows_of(0, line, far_c, d_got)
    line = tie(line, out_first) + swap(line, "tp", core)
    total_a = add(tie(half_of(total_a, dp_bits[0], True), out_first), swap(sent_a, "dp", dp_bits[0]))
    total_b = pair_sums(
        [
            ((tie(low, out_first), 0), (d_near[0], 0)),
            ((low_near, 0), (d_got_near, 0)),
            ((low_far, 0), (d_got, 0)),
            ((low_diag, 0), (d_diag, 0)),
        ]
    )
    sent_a, sent_b = half_of(total_a, dp_bits[1], False), half_of(total_b, dp_bits[0], False)
    d_tokens = input_gradient(tie(picked, sent_a, sent_b, line), grad1, dq, dk, dv, wq, seqs)
    line = tie(line, d_tokens) + swap(line, "dp", dp_bits[0])
    total_a = add(tie(half_of(total_a, dp_bits[1], True), d_tokens), swap(sent_a, "dp", dp_bits[1]))
    for bit in dp_bits[2:-1]:
        total_a = scatter(total_a, bit)
    out_second = rows_of(half_rows, total_a, line)
    cut = far_c.shape[0] // 2
    total_c = add(*tie(near_c, out_second), swap(far_c, "tp", far))
    other = [dp_bits[1], dp_bits[0], *dp_bits[2:]]
    total_c, rest_c = total_c[:cut], total_c[cut:]
    line = tie(line, out_second) + swap(line, "dp", dp_bits[1])
    total_a = add(tie(total_a, out_second), swap(total_a, "dp", last))
    total_b = add(tie(half_of(total_b, dp_bits[0], True), out_second), swap(sent_b, "dp", dp_bits[0]))
    total_c = scatter(total_c, dp_bits[0])
    line = tie(line, total_c)
    for bit in dp_bits[2:]:
        line = line + swap(line, "dp", bit)
    total_c = scatter(total_c, dp_bits[1])
    line = tie(line, total_c)
    line = line + swap(line, "tp", far)
    total_c = spread_out(finish(total_c, dp_bits[2:]), dp_bits[:-1])
    rest_c = spread_out(finish(rest_c, other), other[:-1])
    total_a = spread_out(total_a, dp_bits[:-1])
    total_b = spread_out(finish(total_b, dp_bits[1:]), dp_bits[:-1])
    total_c = jnp.concatenate([total_c.astype(F32), rest_c.astype(F32)], axis=0)
    own = lax.dynamic_slice_in_dim(line, 8 + rank, 1, 0)[0]
    own_q = lax.dynamic_slice(line, (16 + rank, 0), (1, width))
    own_v = lax.dynamic_slice(line, (16 + PARTS + rank, 0), (1, width))
    return (
        jnp.concatenate([out_first, out_second], axis=0),
        d_tokens,
        total_c[: 3 * width].reshape(3, width, depth).transpose(0, 2, 1),
        jnp.concatenate([own_q, own_v], axis=0),
        total_c[3 * width :],
        line[3],
        total_b.astype(F32),
        own,
        total_a.astype(F32),
        line[0],
        jnp.stack([line[4], line[1]]),
        jnp.stack([line[5], line[2]]),
    )


def solution(mesh):
    placed = (
        P(("dp", "tp"), None),
        P(None, None, "tp"),
        P(None, "tp"),
        P("tp", None),
        P(),
        P(None, "tp"),
        P("tp"),
        P("tp", None),
        P(),
        P(),
        P(),
        P("dp"),
        P("dp", None),
        P(("dp", "tp"), None),
    )
    return jax.shard_map(
        on_device,
        mesh=mesh,
        in_specs=placed,
        out_specs=(
            P(("dp", "tp"), None),
            P(("dp", "tp"), None),
            P(None, None, "tp"),
            P(None, "tp"),
            P("tp", None),
            P(),
            P(None, "tp"),
            P("tp"),
            P("tp", None),
            P(),
            P(),
            P(),
        ),
        check_vma=False,
    )
```

```python
import jax
import jax.numpy as jnp
from jax import lax
from jax.experimental import pallas as pl
from jax.experimental.pallas import tpu as pltpu
from jax.sharding import PartitionSpec as P

HD = 64
SCALE = HD ** (-0.5)
NORM_EPS = 1e-06
MASKED = -1e30
HALF_ROOT = 0.5 ** 0.5
DENSITY = 0.3989422804014327
PARTS = 4
BF = jnp.bfloat16
F32 = jnp.float32


def nn(left, right):
    return lax.dot_general(left, right, (((1,), (0,)), ((), ())), preferred_element_type=F32)


def nt(left, right):
    return lax.dot_general(left, right, (((1,), (1,)), ((), ())), preferred_element_type=F32)


def tn(left, right):
    return lax.dot_general(left, right, (((0,), (0,)), ((), ())), preferred_element_type=F32)


def head_masks(width, dtype=BF):
    lane = lax.broadcasted_iota(jnp.int32, (1, width), 1) // HD
    return [(lane == head).astype(dtype) for head in range(width // HD)]


def spread_of(picks, length):
    slots = picks.shape[1]
    return (lax.broadcasted_iota(jnp.int32, (length, slots), 0) == picks).astype(F32).astype(BF)


def whole(shape):
    zeros = (0,) * len(shape)
    return pl.BlockSpec(shape, lambda *_: zeros)


def norm_forward(values, gain, shift):
    average = jnp.mean(values, axis=1, keepdims=True)
    centered = values - average
    inv_std = lax.rsqrt(jnp.mean(centered * centered, axis=1, keepdims=True) + NORM_EPS)
    normed = centered * inv_std
    return normed * gain + shift, normed, inv_std


def norm_backward(grad, normed, inv_std, gain):
    scaled = grad * gain
    first = jnp.mean(scaled, axis=1, keepdims=True)
    second = jnp.mean(scaled * normed, axis=1, keepdims=True)
    return inv_std * (scaled - first - normed * second)


def tie(value, *others):
    return lax.optimization_barrier((value, others))[0]


SMALL = pl.CostEstimate(flops=1024, transcendentals=0, bytes_accessed=1024)


def col_sum(values):
    return jnp.sum(values, axis=0, keepdims=True)


def piece_copies(pieces, target, sems, first, bit):
    rows = target.shape[0]
    if len(pieces) == 1:
        return [pltpu.make_async_copy(pieces[0][0], target, sems.at[first])]
    half, step = rows // 2, rows // len(pieces)
    own = ((lax.axis_index("dp") // bit) % 2) * half
    copies = []
    for n, (ref, skip) in enumerate(pieces):
        base = own if n * step < half else half - own
        start = pl.multiple_of(base + (n * step) % half, step)
        copies.append(pltpu.make_async_copy(ref.at[pl.ds(skip, step), :], target.at[pl.ds(start, step), :], sems.at[first + n]))
    return copies


def stacked_copies(pieces, target, sems, first, bit):
    copies = []
    for part, refs in enumerate(pieces):
        copies.append(piece_copies(refs, target.at[part], sems, first, bit))
        first += len(refs)
    return copies


def take(it, pieces):
    return [[(next(it), skip) for _, skip in piece] for piece in pieces]


def flat(pieces):
    return [p for piece in pieces for p in piece]


def arrays(pieces):
    return [array for array, _ in flat(pieces)]


def start_all(copies):
    for copy in copies:
        copy.start()


def wait_all(copies):
    for copy in copies:
        copy.wait()


ANY_SPEC = pl.BlockSpec(memory_space=pl.ANY)


def shaped(shape):
    return pl.BlockSpec(shape, lambda *_: (0,) * len(shape))


def attend_body(len_ref, x_ref, small_ref, pick_ref, *rest, count):
    w_refs = [(ref, 0) for ref in rest[:count]]
    q_sel_ref, k_ref, v_ref, ctx_ref, ctx_sel_ref, ext_ref, w_ref, sems = rest[count:]
    rows, width = k_ref.shape
    seq = pl.program_id(0)
    row = lax.axis_index("tp") * pl.num_programs(0) + seq
    length = len_ref[row]
    copies = piece_copies(w_refs, w_ref, sems, 0, 1)

    @pl.when(seq == 0)
    def _():
        start_all(copies)
        wait_all(copies)

    x = x_ref[...]
    queries = (nt(x, w_ref[0:width, :]) + small_ref[1:2, :width]).astype(BF)
    key_rows = nt(x, w_ref[width : 2 * width, :]).astype(BF)
    values = (nt(x, w_ref[2 * width : 3 * width, :]) + small_ref[2:3, :width]).astype(BF)
    k_ref[...] = key_rows
    v_ref[...] = values
    ext_ref[:, :width] = values
    ext_ref[:, width:] = jnp.ones((rows, ext_ref.shape[1] - width), BF)
    spread = spread_of(pick_ref[pl.ds(row, 1), :], rows)
    q_sel_ref[...] = tn(spread, queries).astype(BF)
    scaled = queries * jnp.asarray(SCALE, BF)
    masks = head_masks(width)
    tile = min(256, rows)
    keep = lax.broadcasted_iota(jnp.int32, (tile, rows), 1) < length
    for start in range(0, rows, tile):
        total = jnp.zeros((tile, width), F32)
        for mask in masks:
            logits = nt(scaled[start : start + tile] * mask, key_rows)
            logits = jnp.where(keep, logits, MASKED)
            peak = jnp.max(logits, axis=1, keepdims=True)
            probs = jnp.exp(logits - peak).astype(BF)
            mixed = nn(probs, ext_ref[...])
            share = mixed[:, :width] / mixed[:, width : width + 1]
            total = jnp.where(mask.astype(F32) > 0.5, share, total)
        ctx_ref[start : start + tile, :] = total.astype(BF)
    ctx_sel_ref[...] = tn(spread, ctx_ref[...]).astype(BF)


def attend_forward(lengths, x, pieces, width, small, picked, seqs):
    slots = picked.shape[1]
    rows = x.shape[0] // seqs
    depth = x.shape[1]
    ext = -(-(width + 1) // 128) * 128
    row_spec = pl.BlockSpec((rows, width), lambda s, _: (s, 0))
    sel_spec = pl.BlockSpec((slots, width), lambda s, _: (s, 0))
    return pl.pallas_call(
        lambda *refs: attend_body(*refs, count=len(pieces)),
        grid_spec=pltpu.PrefetchScalarGridSpec(
            num_scalar_prefetch=1,
            grid=(seqs,),
            in_specs=[
                pl.BlockSpec((rows, depth), lambda s, _: (s, 0)),
                whole(small.shape),
                whole(picked.shape),
                *[ANY_SPEC] * len(pieces),
            ],
            out_specs=[sel_spec, row_spec, row_spec, row_spec, sel_spec],
            scratch_shapes=[
                pltpu.VMEM((rows, ext), BF),
                pltpu.VMEM((3 * width, depth), BF),
                pltpu.SemaphoreType.DMA((len(pieces),)),
            ],
        ),
        out_shape=[
            jax.ShapeDtypeStruct((seqs * slots, width), BF),
            jax.ShapeDtypeStruct((seqs * rows, width), BF),
            jax.ShapeDtypeStruct((seqs * rows, width), BF),
            jax.ShapeDtypeStruct((seqs * rows, width), BF),
            jax.ShapeDtypeStruct((seqs * slots, width), BF),
        ],
        cost_estimate=SMALL,
        name="attend_forward",
    )(lengths, x, small, picked, *pieces)


def attend_back_body(
    len_ref, q_ref, k_ref, v_ref, d_ctx_ref, x_ref, x_sel_ref, ctx_sel_ref, g1_ref, dq_ref, dk_ref, dv_ref, sums_ref, grad_ref, acc_ref, *, part
):
    rows, width = k_ref.shape
    slots = q_ref.shape[0]
    seq = pl.program_id(0)
    rank = lax.axis_index("tp")
    length = len_ref[rank * pl.num_programs(0) + seq]
    masks = head_masks(width)
    queries, d_ctx = q_ref[...], d_ctx_ref[...]
    key_rows, values = k_ref[...], v_ref[...]
    q_stack = jnp.concatenate([queries * mask for mask in masks], axis=0)
    d_stack = jnp.concatenate([d_ctx * mask for mask in masks], axis=0)
    logits = nt(key_rows, q_stack * jnp.asarray(SCALE, BF))
    keep = lax.broadcasted_iota(jnp.int32, logits.shape, 0) < length
    logits = jnp.where(keep, logits, MASKED)
    grown = jnp.exp(logits - jnp.max(logits, axis=0, keepdims=True))
    probs = grown * (1.0 / jnp.sum(grown, axis=0, keepdims=True))
    d_probs = nt(values, d_stack)
    inner = jnp.sum(probs * d_probs, axis=0, keepdims=True)
    d_raw = (probs * (d_probs - inner) * SCALE).astype(BF)
    d_keys = nn(d_raw, q_stack).astype(BF)
    dk_ref[...] = d_keys
    d_values = nn(probs.astype(BF), d_stack).astype(BF)
    dv_ref[...] = d_values
    dq_stack = tn(d_raw, key_rows)
    dq = jnp.zeros((slots, width), F32)
    for head, mask in enumerate(masks):
        dq = jnp.where(mask.astype(F32) > 0.5, dq_stack[head * slots : (head + 1) * slots], dq)
    dq = dq.astype(BF)
    dq_ref[...] = dq

    @pl.when(seq == 0)
    def _():
        acc_ref[...] = jnp.zeros(acc_ref.shape, F32)
        sums_ref[...] = jnp.zeros(sums_ref.shape, F32)

    at = rank ^ part
    sums_ref[pl.ds(at, 1), 0:width] += col_sum(dq.astype(F32))
    sums_ref[pl.ds(PARTS + at, 1), 0:width] += col_sum(d_values.astype(F32))
    acc_ref[0:width, :] += tn(dq, x_sel_ref[...])
    acc_ref[width : 2 * width, :] += tn(d_keys, x_ref[...])
    acc_ref[2 * width : 3 * width, :] += tn(d_values, x_ref[...])
    acc_ref[3 * width : 4 * width, :] += tn(ctx_sel_ref[...], g1_ref[...])

    @pl.when(seq == pl.num_programs(0) - 1)
    def _():
        grad_ref[...] = acc_ref[...].astype(BF)


def attend_backward(part, lengths, q_sel, k, v, d_ctx, x, x_sel, ctx_sel, g1, seqs):
    rows, slots, width = k.shape[0] // seqs, q_sel.shape[0] // seqs, k.shape[1]
    depth = x.shape[1]
    row_spec = pl.BlockSpec((rows, width), lambda s, _: (s, 0))
    sel_spec = pl.BlockSpec((slots, width), lambda s, _: (s, 0))
    wide_spec = pl.BlockSpec((slots, depth), lambda s, _: (s, 0))
    return pl.pallas_call(
        lambda *refs: attend_back_body(*refs, part=part),
        grid_spec=pltpu.PrefetchScalarGridSpec(
            num_scalar_prefetch=1,
            grid=(seqs,),
            in_specs=[
                sel_spec,
                row_spec,
                row_spec,
                sel_spec,
                pl.BlockSpec((rows, depth), lambda s, _: (s, 0)),
                wide_spec,
                sel_spec,
                wide_spec,
            ],
            out_specs=[sel_spec, row_spec, row_spec, whole((2 * PARTS, depth)), whole((4 * width, depth))],
            scratch_shapes=[pltpu.VMEM((4 * width, depth), F32)],
        ),
        out_shape=[
            jax.ShapeDtypeStruct(q_sel.shape, BF),
            jax.ShapeDtypeStruct(k.shape, BF),
            jax.ShapeDtypeStruct(k.shape, BF),
            jax.ShapeDtypeStruct((2 * PARTS, depth), F32),
            jax.ShapeDtypeStruct((4 * width, depth), BF),
        ],
        cost_estimate=SMALL,
        name="attend_backward",
    )(lengths, q_sel, k, v, d_ctx, x, x_sel, ctx_sel, g1)


def erf_gelu(values):
    return 0.5 * (1.0 + lax.erf(values * HALF_ROOT))


def run(body, plain, hbm, outs, hbm_outs, scratch, name):
    return pl.pallas_call(
        body,
        grid=(1,),
        in_specs=[*[shaped(a.shape) for a in plain], *[ANY_SPEC] * len(hbm)],
        out_specs=[*[shaped(a.shape) for a in outs], *[ANY_SPEC] * len(hbm_outs)],
        out_shape=[*outs, *hbm_outs],
        scratch_shapes=scratch,
        cost_estimate=SMALL,
        name=name,
    )(*plain, *hbm)


def struct(dtype, *shape):
    return jax.ShapeDtypeStruct(shape, dtype)


def unit_part(low, wi, bias, slope_ref, n):
    pre = nn(low, wi) + bias
    chance = erf_gelu(pre)
    slope_ref[n] = chance + pre * (DENSITY * jnp.exp(-0.5 * pre * pre))
    return (pre * chance).astype(BF)


def ffn_prep(picked, x, d_out, ctx_sel, wo, wi, wd, small, shared, seqs):
    parts, near = len(wo), len(wi)
    slots = picked.shape[1]
    count, depth, units, width = seqs * slots, x.shape[1], wi[0][0][0].shape[1], ctx_sel[0].shape[1]
    plain = [picked, x, d_out, shared, *ctx_sel, *small]
    hbm = arrays(wo) + arrays(wi) + arrays(wd)

    def body(*refs):
        it = iter(refs)
        pick_ref, x_ref, d_out_ref, shared_ref = (next(it) for _ in range(4))
        ctx_refs = [next(it) for _ in range(parts)]
        small_refs = [next(it) for _ in range(near)]
        wo_refs, wi_refs, wd_refs = take(it, wo), take(it, wi), take(it, wd)
        act_refs = [next(it) for _ in range(near)]
        slope_ref, x_sel_ref, cot_ref, low_ref, sum_ref, normed1_ref, inv1_ref = (next(it) for _ in range(7))
        wo_v, wi_v, wd_v, sems = (next(it) for _ in range(4))
        out_copies = stacked_copies(wo_refs, wo_v, sems, 0, 1)
        first = len(flat(wo))
        in_copies = stacked_copies(wi_refs, wi_v, sems, first, 1)
        down_copies = stacked_copies(wd_refs, wd_v, sems, first + len(flat(wi)), 2)
        start_all(flat(out_copies) + flat(in_copies) + flat(down_copies))
        rows = x_ref.shape[0] // seqs
        for seq in range(seqs):
            at = lax.axis_index("tp") * seqs + seq
            spread = spread_of(pick_ref[pl.ds(at, 1), :], rows)
            x_sel_ref[seq * slots : (seq + 1) * slots, :] = tn(spread, x_ref[seq * rows : (seq + 1) * rows, :]).astype(BF)
            cot_ref[seq * slots : (seq + 1) * slots, :] = tn(spread, d_out_ref[seq * rows : (seq + 1) * rows, :]).astype(BF)
        attn_sum = x_sel_ref[...].astype(F32) + shared_ref[0:1, :]
        wait_all(flat(out_copies))
        for part in range(parts):
            attn_sum = attn_sum + nn(ctx_refs[part][...], wo_v[part])
        hidden, normed1, inv1 = norm_forward(attn_sum, shared_ref[2:3, :], shared_ref[4:5, :])
        low = hidden.astype(BF)
        low_ref[...] = low
        normed1_ref[...] = normed1
        inv1_ref[...] = inv1
        total = hidden + shared_ref[1:2, :]
        wait_all(flat(in_copies) + flat(down_copies))
        for n in range(near):
            act = unit_part(low, wi_v[n], small_refs[n][0:1, :], slope_ref, n)
            act_refs[n][...] = act
            total = total + nn(act, wd_v[n])
        sum_ref[...] = total

    outs = [
        *[struct(BF, count, units)] * near,
        struct(F32, near, count, units),
        struct(BF, count, depth),
        struct(BF, count, depth),
        struct(BF, count, depth),
        struct(F32, count, depth),
        struct(F32, count, depth),
        struct(F32, count, 1),
    ]
    scratch = [
        pltpu.VMEM((parts, width, depth), BF),
        pltpu.VMEM((near, depth, units), BF),
        pltpu.VMEM((near, units, depth), BF),
        pltpu.SemaphoreType.DMA((len(hbm),)),
    ]
    return run(body, plain, hbm, outs, [], scratch, "ffn_prep")


def ffn_front(low, total, cot, wi, wd, small, shared):
    far = len(wi)
    count, depth = low.shape
    units = wi[0][0][0].shape[1]
    plain = [low, total, cot, shared, *small]
    hbm = arrays(wi) + arrays(wd)

    def body(*refs):
        it = iter(refs)
        low_ref, sum_ref, cot_ref, shared_ref = (next(it) for _ in range(4))
        small_refs = [next(it) for _ in range(far)]
        wi_refs, wd_refs = take(it, wi), take(it, wd)
        sent_ref, g2_ref, slope_ref, grad2_ref, vec_ref = (next(it) for _ in range(5))
        wi_v, wd_v, sems = (next(it) for _ in range(3))
        in_copies = stacked_copies(wi_refs, wi_v, sems, 0, 1)
        down_copies = stacked_copies(wd_refs, wd_v, sems, len(flat(wi)), 2)
        for n in range(far):
            start_all(in_copies[n] + down_copies[n])
        low = low_ref[...]
        total = sum_ref[...]
        for n in range(far):
            wait_all(in_copies[n])
            act = unit_part(low, wi_v[n], small_refs[n][0:1, :], slope_ref, n)
            sent_ref[n * count : (n + 1) * count, :] = act
            wait_all(down_copies[n])
            total = total + nn(act, wd_v[n])
        _, normed2, inv2 = norm_forward(total, shared_ref[3:4, :], shared_ref[5:6, :])
        cotangent = cot_ref[...].astype(F32)
        grad2 = norm_backward(cotangent, normed2, inv2, shared_ref[3:4, :])
        vec_ref[...] = jnp.zeros(vec_ref.shape, F32)
        vec_ref[0:1, :] = col_sum(grad2)
        vec_ref[1:2, :] = col_sum(cotangent * normed2)
        vec_ref[2:3, :] = col_sum(cotangent)
        grad2_ref[...] = grad2
        g2 = grad2.astype(BF)
        g2_ref[...] = g2
        sent_ref[far * count :, :] = g2

    outs = [
        struct(BF, (far + 1) * count, units),
        struct(BF, count, depth),
        struct(F32, far, count, units),
        struct(F32, count, depth),
        struct(F32, 16, depth),
    ]
    scratch = [
        pltpu.VMEM((far, depth, units), BF),
        pltpu.VMEM((far, units, depth), BF),
        pltpu.SemaphoreType.DMA((len(hbm),)),
    ]
    return run(body, plain, hbm, outs, [], scratch, "ffn_front")


def ffn_mid(g2, low, slopes, wd):
    parts = len(wd)
    near = slopes[0].shape[0]
    count, depth = g2.shape
    units = slopes[0].shape[2]
    hbm = [*slopes, *arrays(wd)]

    def body(*refs):
        it = iter(refs)
        g2_ref, low_ref = next(it), next(it)
        slope_hbm = [next(it) for _ in slopes]
        wd_refs = take(it, wd)
        d_refs = [next(it) for _ in range(near)]
        sent_ref, vec_ref = next(it), next(it)
        wd_v, slope_v, sems, slope_sems = (next(it) for _ in range(4))
        down_copies = stacked_copies(wd_refs, wd_v, sems, 0, 2)
        sources = [ref.at[n] for ref in slope_hbm for n in range(ref.shape[0])]
        slope_copies = [pltpu.make_async_copy(sources[part], slope_v.at[part], slope_sems.at[part]) for part in range(parts)]
        for part in range(parts):
            start_all(down_copies[part] + [slope_copies[part]])
        vec_ref[...] = jnp.zeros(vec_ref.shape, F32)
        g2 = g2_ref[...]
        for part in range(parts):
            wait_all(down_copies[part] + [slope_copies[part]])
            d_pre = (nt(g2, wd_v[part]) * slope_v[part]).astype(BF)
            if part < near:
                d_refs[part][...] = d_pre
            else:
                sent_ref[(part - near) * count : (part - near + 1) * count, :] = d_pre
            at = 8 + (lax.axis_index("tp") ^ part)
            vec_ref[pl.ds(at, 1), :] = col_sum(d_pre.astype(F32))
        sent_ref[(parts - near) * count :, :] = low_ref[...]

    outs = [*[struct(BF, count, units)] * near, struct(BF, (parts - near + 1) * count, units), struct(F32, 16, depth)]
    scratch = [
        pltpu.VMEM((parts, units, depth), BF),
        pltpu.VMEM((parts, count, units), F32),
        pltpu.SemaphoreType.DMA((len(arrays(wd)),)),
        pltpu.SemaphoreType.DMA((parts,)),
    ]
    return run(body, [g2, low], hbm, outs, [], scratch, "ffn_mid")


def pair_sums(pairs):
    count = min(array.shape[0] for array, _ in pairs[0])
    width, depth = pairs[0][0][0].shape[1], pairs[0][1][0].shape[1]
    tile = min(256, width)

    def body(*refs):
        total = tn(refs[0][...], refs[1][...])
        for n in range(1, len(pairs)):
            total = total + tn(refs[2 * n][...], refs[2 * n + 1][...])
        refs[-1][...] = total.astype(BF)

    def left(block):
        return pl.BlockSpec((count, tile), lambda i: (block, i))

    def right(block):
        return pl.BlockSpec((count, depth), lambda i: (block, 0))

    return pl.pallas_call(
        body,
        grid=(width // tile,),
        in_specs=[spec for (_, a), (_, b) in pairs for spec in (left(a), right(b))],
        out_specs=pl.BlockSpec((tile, depth), lambda i: (i, 0)),
        out_shape=jax.ShapeDtypeStruct((width, depth), BF),
        cost_estimate=SMALL,
        name="pair_sums",
    )(*[array for (a, _), (b, _) in pairs for array in (a, b)])


def ffn_back(grad2, d_near, d_far, normed1, inv1, shared, wi, wo, width):
    parts, near = len(wi), len(d_near)
    count, depth = grad2.shape
    units = d_far.shape[1]
    hbm = arrays(wi) + arrays(wo)

    def body(*refs):
        it = iter(refs)
        grad2_ref, normed1_ref, inv1_ref, shared_ref = (next(it) for _ in range(4))
        near_refs = [next(it) for _ in range(near)]
        far_ref = next(it)
        wi_refs, wo_refs = take(it, wi), take(it, wo)
        g1_ref, grad1_ref, vec_ref = next(it), next(it), next(it)
        d_ctx_refs = [next(it) for _ in range(parts)]
        wi_v, wo_v, sems = (next(it) for _ in range(3))
        in_copies = stacked_copies(wi_refs, wi_v, sems, 0, 1)
        out_copies = stacked_copies(wo_refs, wo_v, sems, len(flat(wi)), 1)
        start_all(flat(in_copies) + flat(out_copies))
        d_hidden = grad2_ref[...]
        for part in range(parts):
            wait_all(in_copies[part])
            d_pre = near_refs[part][...] if part < near else far_ref[(part - near) * count : (part - near + 1) * count, :]
            d_hidden = d_hidden + nt(d_pre, wi_v[part])
        normed1 = normed1_ref[...]
        grad1 = norm_backward(d_hidden, normed1, inv1_ref[...], shared_ref[2:3, :])
        vec_ref[...] = jnp.zeros(vec_ref.shape, F32)
        vec_ref[3:4, :] = col_sum(grad1)
        vec_ref[4:5, :] = col_sum(d_hidden * normed1)
        vec_ref[5:6, :] = col_sum(d_hidden)
        grad1_ref[...] = grad1
        g1 = grad1.astype(BF)
        g1_ref[...] = g1
        wait_all(flat(out_copies))
        for part in range(parts):
            d_ctx_refs[part][...] = nt(g1, wo_v[part]).astype(BF)

    outs = [struct(BF, count, depth), struct(F32, count, depth), struct(F32, 16, depth), *[struct(BF, count, width)] * parts]
    scratch = [
        pltpu.VMEM((parts, depth, units), BF),
        pltpu.VMEM((parts, width, depth), BF),
        pltpu.SemaphoreType.DMA((len(hbm),)),
    ]
    return run(body, [grad2, normed1, inv1, shared, *d_near, d_far], hbm, outs, [], scratch, "ffn_back")


def ffn_rows(x, ctx, wo, wi, wd, small, shared, first, count):
    parts = len(wo)
    depth = x.shape[1]
    units, width = wi[0][0][0].shape[1], ctx[0].shape[1]
    tile = min(256, count)
    start = first // tile
    hbm = arrays(wo) + arrays(wi) + arrays(wd)

    def body(*refs):
        it = iter(refs)
        x_ref = next(it)
        ctx_refs = [next(it) for _ in range(parts)]
        small_refs = [next(it) for _ in range(parts)]
        shared_ref = next(it)
        wo_refs, wi_refs, wd_refs = take(it, wo), take(it, wi), take(it, wd)
        out_ref, wo_v, wi_v, wd_v, sems = (next(it) for _ in range(5))
        out_copies = flat(stacked_copies(wo_refs, wo_v, sems, 0, 1))
        near = len(flat(wo))
        in_copies = stacked_copies(wi_refs, wi_v, sems, near, 1)
        down_copies = stacked_copies(wd_refs, wd_v, sems, near + len(flat(wi)), 2)
        opening = pl.program_id(0) == 0

        @pl.when(opening)
        def _():
            start_all(out_copies)
            for part in range(parts):
                start_all(in_copies[part] + down_copies[part])
            wait_all(out_copies)

        attn_sum = x_ref[...].astype(F32) + shared_ref[0:1, :]
        for part in range(parts):
            attn_sum = attn_sum + nn(ctx_refs[part][...], wo_v[part])
        hidden, _, _ = norm_forward(attn_sum, shared_ref[2:3, :], shared_ref[4:5, :])
        low = hidden.astype(BF)
        total = hidden + shared_ref[1:2, :]
        for part in range(parts):

            @pl.when(opening)
            def _():
                wait_all(in_copies[part] + down_copies[part])

            pre = nn(low, wi_v[part]) + small_refs[part][0:1, :]
            act = (pre * erf_gelu(pre)).astype(BF)
            total = total + nn(act, wd_v[part])
        out_ref[...] = norm_forward(total, shared_ref[3:4, :], shared_ref[5:6, :])[0].astype(BF)

    return pl.pallas_call(
        body,
        grid=(count // tile,),
        in_specs=[
            pl.BlockSpec((tile, depth), lambda i: (i + start, 0)),
            *[pl.BlockSpec((tile, width), lambda i: (i + start, 0))] * parts,
            *[shaped(a.shape) for a in small],
            shaped(shared.shape),
            *[ANY_SPEC] * len(hbm),
        ],
        out_specs=pl.BlockSpec((tile, depth), lambda i: (i, 0)),
        out_shape=jax.ShapeDtypeStruct((count, depth), BF),
        scratch_shapes=[
            pltpu.VMEM((parts, width, depth), BF),
            pltpu.VMEM((parts, depth, units), BF),
            pltpu.VMEM((parts, units, depth), BF),
            pltpu.SemaphoreType.DMA((len(hbm),)),
        ],
        cost_estimate=SMALL,
        name="ffn_rows",
    )(x, *ctx, *small, shared, *hbm)


def input_gradient(picked, grad1, dq, dk, dv, wq, seqs):
    parts = len(dq)
    slots = picked.shape[1]
    depth = grad1.shape[1]
    rows, width = dk[0].shape[0] // seqs, dk[0].shape[1]
    hbm = arrays(wq)

    def body(*refs):
        it = iter(refs)
        pick_ref, grad1_ref = next(it), next(it)
        dq_refs = [next(it) for _ in range(parts)]
        dk_refs = [next(it) for _ in range(parts)]
        dv_refs = [next(it) for _ in range(parts)]
        wq_refs = take(it, wq)
        out_ref, wq_v, sems = next(it), next(it), next(it)
        copies = flat(stacked_copies(wq_refs, wq_v, sems, 0, 1))
        seq = pl.program_id(0)

        @pl.when(seq == 0)
        def _():
            start_all(copies)
            wait_all(copies)

        chosen = grad1_ref[...]
        for part in range(parts):
            chosen = chosen + nn(dq_refs[part][...], wq_v[part, 0:width, :])
        high = chosen.astype(BF)
        rest = (chosen - high.astype(F32)).astype(BF)
        spread = spread_of(pick_ref[pl.ds(lax.axis_index("tp") * seqs + seq, 1), :], rows)
        total = nn(spread, high) + nn(spread, rest)
        for part in range(parts):
            total = total + nn(dk_refs[part][...], wq_v[part, width : 2 * width, :])
            total = total + nn(dv_refs[part][...], wq_v[part, 2 * width : 3 * width, :])
        out_ref[...] = total.astype(BF)

    row_spec = pl.BlockSpec((rows, width), lambda s: (s, 0))
    return pl.pallas_call(
        body,
        grid=(seqs,),
        in_specs=[
            whole(picked.shape),
            pl.BlockSpec((slots, depth), lambda s: (s, 0)),
            *[pl.BlockSpec((slots, width), lambda s: (s, 0))] * parts,
            *[row_spec] * (2 * parts),
            *[ANY_SPEC] * len(hbm),
        ],
        out_specs=pl.BlockSpec((rows, depth), lambda s: (s, 0)),
        out_shape=jax.ShapeDtypeStruct((seqs * rows, depth), BF),
        scratch_shapes=[pltpu.VMEM((parts, 3 * width, depth), BF), pltpu.SemaphoreType.DMA((len(hbm),))],
        cost_estimate=SMALL,
        name="input_gradient",
    )(picked, grad1, *dq, *dk, *dv, *hbm)


def bits_of(count):
    return [1 << b for b in range(count.bit_length() - 1)]


def swap(value, axis, bit):
    count = lax.axis_size(axis)
    return lax.ppermute(value, axis, [(i, i ^ bit) for i in range(count)])


def half_of(value, bit, own):
    half = value.shape[0] // 2
    side = (lax.axis_index("dp") // bit) % 2
    return lax.dynamic_slice_in_dim(value, jnp.where(side == 0, 0, half) if own else jnp.where(side == 0, half, 0), half, 0)


def joined(own, got, bit):
    side = (lax.axis_index("dp") // bit) % 2
    return jnp.concatenate([jnp.where(side == 0, own, got), jnp.where(side == 0, got, own)], axis=0)


def add(*values):
    total = values[0].astype(F32)
    for value in values[1:]:
        total = total + value.astype(F32)
    return total.astype(BF)


def scatter(value, bit, *after):
    sent, kept = half_of(value, bit, False), half_of(value, bit, True)
    return add(tie(kept, *after), swap(sent, "dp", bit))


def gather(value, bit):
    return joined(value, swap(value, "dp", bit), bit)


def on_device(
    tokens, w_qkv, qv_bias, w_out, out_bias, w_in, in_bias, w_down, down_bias, norm_gain, norm_shift, valid_len, picked, d_out
):
    parts = lax.axis_size("tp")
    rank = lax.axis_index("tp")
    seqs = valid_len.shape[0] // parts
    depth = tokens.shape[1]
    width = w_qkv.shape[2]
    core, far = 1, 2
    dp_bits = bits_of(lax.axis_size("dp"))

    shared = jnp.concatenate([out_bias[None], down_bias[None], norm_gain, norm_shift, jnp.zeros((2, depth), F32)], axis=0)
    small = [jnp.concatenate([in_bias[None], jnp.pad(qv_bias, ((0, 5), (0, depth - width)))], axis=0)]
    small += [swap(small[0], "tp", core)]
    wq = w_qkv.transpose(0, 2, 1).reshape(3 * width, depth)
    qo_far = swap(jnp.concatenate([half_of(wq, 1, True), half_of(w_out, 1, True)], axis=0), "tp", far)
    wq_near = swap(wq, "tp", core)
    ready = small[1]
    small_far = swap(jnp.concatenate(small, axis=0), "tp", far)
    ff_far = swap(tie(jnp.concatenate([half_of(w_in, 1, True), half_of(w_down, 2, True)], axis=0), small_far), "tp", far)
    small += [small_far[:8], small_far[8:]]

    def forward(j, x, pieces):
        return attend_forward(valid_len, x, pieces, width, small[j], picked, seqs)

    out0 = forward(0, tie(tokens, ready), [wq])
    qo_far = tie(qo_far, out0[0])
    qo_rest, qo_far_core = swap(qo_far, "dp", 1), swap(qo_far, "tp", core)
    out1 = forward(1, tie(tokens, qo_far), [wq_near])
    qo_rest = tie(qo_rest, out1[0])
    qo_rest_core = swap(qo_rest, "tp", core)
    wo_near = swap(tie(w_out, qo_rest), "tp", core)
    out2 = forward(2, tie(tokens, qo_rest), [qo_far, qo_rest])
    wi_near, wd_near = swap(tie(w_in, out2[0]), "tp", core), swap(tie(w_down, out2[0]), "tp", core)
    out3 = forward(3, tie(tokens, out2[0]), [qo_far_core, qo_rest_core])
    ff_far = tie(ff_far, out3[0])
    rows_in = ff_far.shape[0] // 2
    wi_rest, wd_rest = swap(ff_far[:rows_in], "dp", 1), swap(ff_far[rows_in:], "dp", 2)
    ff_far_core = swap(ff_far, "tp", core)
    q_sel, k, v, ctx, ctx_sel = zip(out0, out1, out2, out3)
    rows_q = 3 * width // 2

    def pieces(own, near, far_pieces, core_pieces):
        return [[(own, 0)], [(near, 0)], far_pieces, core_pieces]

    wq = pieces(wq, wq_near, [(qo_far, 0), (qo_rest, 0)], [(qo_far_core, 0), (qo_rest_core, 0)])
    wo = pieces(w_out, wo_near, [(qo_far, rows_q), (qo_rest, rows_q)], [(qo_far_core, rows_q), (qo_rest_core, rows_q)])
    near_in, near_down = [[(w_in, 0)], [(wi_near, 0)]], [[(w_down, 0)], [(wd_near, 0)]]
    prep = ffn_prep(picked, tie(tokens, ff_far), d_out, ctx_sel, wo, near_in, near_down, small[:2], shared, seqs)
    *act, slope_near, x_sel, cot, low, ffn_sum, normed1, inv1 = prep
    low_near, act_near = swap(low, "tp", core), swap(act[1], "tp", core)
    wi_rest, wd_rest = tie((wi_rest, wd_rest), low)
    wi_rest_core, wd_rest_core = swap(wi_rest, "tp", core), swap(wd_rest, "tp", core)
    wi = near_in + [[(ff_far, 0), (wi_rest, 0)], [(ff_far_core, 0), (wi_rest_core, 0)]]
    wd = near_down + [[(ff_far, rows_in), (wd_rest, 0)], [(ff_far_core, rows_in), (wd_rest_core, 0)]]

    sent, g2, slope_far, grad2, vec = ffn_front(low, ffn_sum, cot, wi[2:], wd[2:], small[2:], shared)
    act_got = swap(sent, "tp", far)
    g2_near = swap(g2, "tp", core)
    *d_near, d_far, vec_mid = ffn_mid(g2, low, [slope_near, slope_far], wd)
    d_got, d_got_near = swap(d_far, "tp", far), swap(d_near[1], "tp", core)
    g1, grad1, vec_back, *d_ctx = ffn_back(tie(grad2, act_near, low_near, g2_near), d_near, d_far, normed1, inv1, shared, wi, wo, width)
    count = low.shape[0]

    def backward(j, x):
        return attend_backward(j, valid_len, q_sel[j], k[j], v[j], d_ctx[j], x, x_sel, ctx_sel[j], g1, seqs)

    def rows_of(first, *after):
        return ffn_rows(tie(tokens, *after), ctx, wo, wi, wd, small, shared, first, half_rows)

    def finish(value, bits):
        for bit in bits:
            value = scatter(value, bit) if bit != last else add(value, swap(value, "dp", bit))
        return value

    def spread_out(value, bits):
        for bit in reversed(bits):
            value = gather(value, bit)
        return value

    half_rows, last = tokens.shape[0] // 2, dp_bits[-1]
    out3 = backward(3, tie(tokens, d_got_near))
    out2 = backward(2, tie(tokens, out3[0]))
    act_got = tie(act_got, out2[0])
    act_diag = swap(act_got[count:], "tp", core)
    out1 = backward(1, tie(tokens, out2[0], act_got))
    total_a = pair_sums(
        [
            ((tie(act[0], out1[0]), 0), (g2, 0)),
            ((act_near, 0), (g2_near, 0)),
            ((act_got, 0), (act_got, 2)),
            ((act_diag, 0), (act_diag, 1)),
        ]
    )
    sent_a = half_of(total_a, dp_bits[0], False)
    out0 = backward(0, tie(tokens, out1[0], sent_a))
    dq, dk, dv, sums, g_heads = zip(out0, out1, out2, out3)
    d_got = tie(d_got, out0[0])
    d_diag = swap(d_got[count:], "tp", core)
    far_c = add(tie(out2[4], out0[0]), swap(tie(out3[4], out1[0]), "tp", core))
    near_c = g_heads[0], swap(tie(g_heads[1], out0[0]), "tp", core)
    line = jnp.concatenate([vec + vec_mid + vec_back, sums[0] + sums[1] + sums[2] + sums[3]], axis=0)
    out_first = rows_of(0, line, far_c, d_got)
    total_a = add(tie(half_of(total_a, dp_bits[0], True), out_first), swap(sent_a, "dp", dp_bits[0]))
    sent_a = half_of(total_a, dp_bits[1], False)
    total_b = pair_sums(
        [
            ((tie(low, out_first), 0), (d_near[0], 0)),
            ((low_near, 0), (d_got_near, 0)),
            ((d_got, 2), (d_got, 0)),
            ((d_diag, 1), (d_diag, 0)),
        ]
    )
    sent_b = half_of(total_b, dp_bits[0], False)
    d_tokens = input_gradient(tie(picked, sent_a, sent_b), grad1, dq, dk, dv, wq, seqs)
    total_b = add(tie(half_of(total_b, dp_bits[0], True), d_tokens), swap(sent_b, "dp", dp_bits[0]))
    total_a = add(tie(half_of(total_a, dp_bits[1], True), d_tokens), swap(sent_a, "dp", dp_bits[1]))
    for bit in dp_bits[2:-1]:
        total_a = scatter(total_a, bit)
    total_c = add(*tie(near_c, d_tokens), swap(far_c, "tp", far))
    cut = far_c.shape[0] // 2
    other = [dp_bits[1], dp_bits[0], *dp_bits[2:]]
    total_c, rest_c = total_c[:cut], total_c[cut:]
    sent_c, sent_d = half_of(total_c, dp_bits[0], False), half_of(rest_c, other[0], False)
    sent_b = half_of(total_b, dp_bits[1], False)
    out_second = rows_of(half_rows, total_a, sent_b, sent_c, sent_d)
    total_a = add(tie(total_a, out_second), swap(total_a, "dp", last))
    total_b = add(tie(half_of(total_b, dp_bits[1], True), out_second), swap(sent_b, "dp", dp_bits[1]))
    total_c = add(tie(half_of(total_c, dp_bits[0], True), out_second), swap(sent_c, "dp", dp_bits[0]))
    rest_c = add(tie(half_of(rest_c, other[0], True), out_second), swap(sent_d, "dp", other[0]))
    line = tie(line, total_c)
    line = line + swap(line, "dp", dp_bits[0])
    total_c, rest_c = scatter(total_c, dp_bits[1]), scatter(rest_c, other[1])
    line = tie(line, total_c)
    line = line + swap(line, "dp", dp_bits[1])
    total_c, rest_c = finish(total_c, dp_bits[2:]), finish(rest_c, other[2:])
    line = tie(line, total_c)
    for bit in dp_bits[2:]:
        line = line + swap(line, "dp", bit)
    total_c, rest_c = spread_out(total_c, dp_bits[1:-1]), spread_out(rest_c, other[1:-1])
    line = tie(line, total_c)
    for bit in (core, far):
        line = line + swap(line, "tp", bit)
    total_a = spread_out(total_a, dp_bits[:-1])
    total_b = spread_out(finish(total_b, dp_bits[2:]), dp_bits[:-1])
    total_c, rest_c = gather(total_c, dp_bits[0]), gather(rest_c, other[0])
    total_c = jnp.concatenate([total_c.astype(F32), rest_c.astype(F32)], axis=0)
    own = lax.dynamic_slice_in_dim(line, 8 + rank, 1, 0)[0]
    own_q = lax.dynamic_slice(line, (16 + rank, 0), (1, width))
    own_v = lax.dynamic_slice(line, (16 + PARTS + rank, 0), (1, width))
    return (
        jnp.concatenate([out_first, out_second], axis=0),
        d_tokens,
        total_c[: 3 * width].reshape(3, width, depth).transpose(0, 2, 1),
        jnp.concatenate([own_q, own_v], axis=0),
        total_c[3 * width :],
        line[3],
        total_b.astype(F32),
        own,
        total_a.astype(F32),
        line[0],
        jnp.stack([line[4], line[1]]),
        jnp.stack([line[5], line[2]]),
    )


def solution(mesh):
    placed = (
        P(("dp", "tp"), None),
        P(None, None, "tp"),
        P(None, "tp"),
        P("tp", None),
        P(),
        P(None, "tp"),
        P("tp"),
        P("tp", None),
        P(),
        P(),
        P(),
        P("dp"),
        P("dp", None),
        P(("dp", "tp"), None),
    )
    return jax.shard_map(
        on_device,
        mesh=mesh,
        in_specs=placed,
        out_specs=(
            P(("dp", "tp"), None),
            P(("dp", "tp"), None),
            P(None, None, "tp"),
            P(None, "tp"),
            P("tp", None),
            P(),
            P(None, "tp"),
            P("tp"),
            P("tp", None),
            P(),
            P(),
            P(),
        ),
        check_vma=False,
    )
```

```python
import jax
import jax.numpy as jnp
from jax import lax
from jax.experimental import pallas as pl
from jax.experimental.pallas import tpu as pltpu
from jax.sharding import PartitionSpec as P

HD = 64
SCALE = HD ** (-0.5)
NORM_EPS = 1e-06
MASKED = -1e30
HALF_ROOT = 0.5 ** 0.5
DENSITY = 0.3989422804014327
PARTS = 4
BF = jnp.bfloat16
F32 = jnp.float32


def nn(left, right):
    return lax.dot_general(left, right, (((1,), (0,)), ((), ())), preferred_element_type=F32)


def nt(left, right):
    return lax.dot_general(left, right, (((1,), (1,)), ((), ())), preferred_element_type=F32)


def tn(left, right):
    return lax.dot_general(left, right, (((0,), (0,)), ((), ())), preferred_element_type=F32)


def head_masks(width, dtype=BF):
    lane = lax.broadcasted_iota(jnp.int32, (1, width), 1) // HD
    return [(lane == head).astype(dtype) for head in range(width // HD)]


def spread_of(picks, length):
    slots = picks.shape[1]
    return (lax.broadcasted_iota(jnp.int32, (length, slots), 0) == picks).astype(F32).astype(BF)


def whole(shape):
    zeros = (0,) * len(shape)
    return pl.BlockSpec(shape, lambda *_: zeros)


def norm_forward(values, gain, shift):
    average = jnp.mean(values, axis=1, keepdims=True)
    centered = values - average
    inv_std = lax.rsqrt(jnp.mean(centered * centered, axis=1, keepdims=True) + NORM_EPS)
    normed = centered * inv_std
    return normed * gain + shift, normed, inv_std


def norm_backward(grad, normed, inv_std, gain):
    scaled = grad * gain
    first = jnp.mean(scaled, axis=1, keepdims=True)
    second = jnp.mean(scaled * normed, axis=1, keepdims=True)
    return inv_std * (scaled - first - normed * second)


def tie(value, *others):
    return lax.optimization_barrier((value, others))[0]


SMALL = pl.CostEstimate(flops=1024, transcendentals=0, bytes_accessed=1024)


def col_sum(values):
    return jnp.sum(values, axis=0, keepdims=True)


def piece_copies(pieces, target, sems, first, bit):
    rows = target.shape[0]
    if len(pieces) == 1:
        return [pltpu.make_async_copy(pieces[0][0], target, sems.at[first])]
    half, step = rows // 2, rows // len(pieces)
    if len(pieces) == 4:
        upper = piece_copies(pieces[:2], target.at[pl.ds(0, half), :], sems, first, bit)
        return upper + piece_copies(pieces[2:], target.at[pl.ds(half, half), :], sems, first + 2, 2 * bit)
    own = ((lax.axis_index("dp") // bit) % 2) * half
    copies = []
    for n, (ref, skip) in enumerate(pieces):
        base = own if n * step < half else half - own
        start = pl.multiple_of(base + (n * step) % half, step)
        copies.append(pltpu.make_async_copy(ref.at[pl.ds(skip, step), :], target.at[pl.ds(start, step), :], sems.at[first + n]))
    return copies


def stacked_copies(pieces, target, sems, first, bit):
    copies = []
    for part, refs in enumerate(pieces):
        copies.append(piece_copies(refs, target.at[part], sems, first, bit))
        first += len(refs)
    return copies


def take(it, pieces):
    return [[(next(it), skip) for _, skip in piece] for piece in pieces]


def flat(pieces):
    return [p for piece in pieces for p in piece]


def arrays(pieces):
    return [array for array, _ in flat(pieces)]


def start_all(copies):
    for copy in copies:
        copy.start()


def wait_all(copies):
    for copy in copies:
        copy.wait()


ANY_SPEC = pl.BlockSpec(memory_space=pl.ANY)


def shaped(shape):
    return pl.BlockSpec(shape, lambda *_: (0,) * len(shape))


def attend_body(len_ref, x_ref, small_ref, pick_ref, *rest, count):
    w_refs = [(ref, 0) for ref in rest[:count]]
    q_sel_ref, k_ref, v_ref, ctx_ref, ctx_sel_ref, ext_ref, w_ref, sems = rest[count:]
    rows, width = k_ref.shape
    seq = pl.program_id(0)
    row = lax.axis_index("tp") * pl.num_programs(0) + seq
    length = len_ref[row]
    copies = piece_copies(w_refs, w_ref, sems, 0, 1)

    @pl.when(seq == 0)
    def _():
        start_all(copies)
        wait_all(copies)

    x = x_ref[...]
    queries = (nt(x, w_ref[0:width, :]) + small_ref[1:2, :width]).astype(BF)
    key_rows = nt(x, w_ref[width : 2 * width, :]).astype(BF)
    values = (nt(x, w_ref[2 * width : 3 * width, :]) + small_ref[2:3, :width]).astype(BF)
    k_ref[...] = key_rows
    v_ref[...] = values
    ext_ref[:, :width] = values
    ext_ref[:, width:] = jnp.ones((rows, ext_ref.shape[1] - width), BF)
    spread = spread_of(pick_ref[pl.ds(row, 1), :], rows)
    q_sel_ref[...] = tn(spread, queries).astype(BF)
    scaled = queries * jnp.asarray(SCALE, BF)
    masks = head_masks(width)
    tile = min(256, rows)
    keep = lax.broadcasted_iota(jnp.int32, (tile, rows), 1) < length
    for start in range(0, rows, tile):
        total = jnp.zeros((tile, width), F32)
        for mask in masks:
            logits = nt(scaled[start : start + tile] * mask, key_rows)
            logits = jnp.where(keep, logits, MASKED)
            peak = jnp.max(logits, axis=1, keepdims=True)
            probs = jnp.exp(logits - peak).astype(BF)
            mixed = nn(probs, ext_ref[...])
            share = mixed[:, :width] / mixed[:, width : width + 1]
            total = jnp.where(mask.astype(F32) > 0.5, share, total)
        ctx_ref[start : start + tile, :] = total.astype(BF)
    ctx_sel_ref[...] = tn(spread, ctx_ref[...]).astype(BF)


def attend_forward(lengths, x, pieces, width, small, picked, seqs):
    slots = picked.shape[1]
    rows = x.shape[0] // seqs
    depth = x.shape[1]
    ext = -(-(width + 1) // 128) * 128
    row_spec = pl.BlockSpec((rows, width), lambda s, _: (s, 0))
    sel_spec = pl.BlockSpec((slots, width), lambda s, _: (s, 0))
    return pl.pallas_call(
        lambda *refs: attend_body(*refs, count=len(pieces)),
        grid_spec=pltpu.PrefetchScalarGridSpec(
            num_scalar_prefetch=1,
            grid=(seqs,),
            in_specs=[
                pl.BlockSpec((rows, depth), lambda s, _: (s, 0)),
                whole(small.shape),
                whole(picked.shape),
                *[ANY_SPEC] * len(pieces),
            ],
            out_specs=[sel_spec, row_spec, row_spec, row_spec, sel_spec],
            scratch_shapes=[
                pltpu.VMEM((rows, ext), BF),
                pltpu.VMEM((3 * width, depth), BF),
                pltpu.SemaphoreType.DMA((len(pieces),)),
            ],
        ),
        out_shape=[
            jax.ShapeDtypeStruct((seqs * slots, width), BF),
            jax.ShapeDtypeStruct((seqs * rows, width), BF),
            jax.ShapeDtypeStruct((seqs * rows, width), BF),
            jax.ShapeDtypeStruct((seqs * rows, width), BF),
            jax.ShapeDtypeStruct((seqs * slots, width), BF),
        ],
        cost_estimate=SMALL,
        name="attend_forward",
    )(lengths, x, small, picked, *pieces)


def attend_back_body(
    len_ref, q_ref, k_ref, v_ref, d_ctx_ref, x_ref, x_sel_ref, ctx_sel_ref, g1_ref, dq_ref, dk_ref, dv_ref, sums_ref, grad_ref, acc_ref, *, part
):
    rows, width = k_ref.shape
    slots = q_ref.shape[0]
    seq = pl.program_id(0)
    rank = lax.axis_index("tp")
    length = len_ref[rank * pl.num_programs(0) + seq]
    masks = head_masks(width)
    queries, d_ctx = q_ref[...], d_ctx_ref[...]
    key_rows, values = k_ref[...], v_ref[...]
    q_stack = jnp.concatenate([queries * mask for mask in masks], axis=0)
    d_stack = jnp.concatenate([d_ctx * mask for mask in masks], axis=0)
    logits = nt(key_rows, q_stack * jnp.asarray(SCALE, BF))
    keep = lax.broadcasted_iota(jnp.int32, logits.shape, 0) < length
    logits = jnp.where(keep, logits, MASKED)
    grown = jnp.exp(logits - jnp.max(logits, axis=0, keepdims=True))
    probs = grown * (1.0 / jnp.sum(grown, axis=0, keepdims=True))
    d_probs = nt(values, d_stack)
    inner = jnp.sum(probs * d_probs, axis=0, keepdims=True)
    d_raw = (probs * (d_probs - inner) * SCALE).astype(BF)
    d_keys = nn(d_raw, q_stack).astype(BF)
    dk_ref[...] = d_keys
    d_values = nn(probs.astype(BF), d_stack).astype(BF)
    dv_ref[...] = d_values
    dq_stack = tn(d_raw, key_rows)
    dq = jnp.zeros((slots, width), F32)
    for head, mask in enumerate(masks):
        dq = jnp.where(mask.astype(F32) > 0.5, dq_stack[head * slots : (head + 1) * slots], dq)
    dq = dq.astype(BF)
    dq_ref[...] = dq

    @pl.when(seq == 0)
    def _():
        acc_ref[...] = jnp.zeros(acc_ref.shape, F32)
        sums_ref[...] = jnp.zeros(sums_ref.shape, F32)

    at = rank ^ part
    sums_ref[pl.ds(at, 1), 0:width] += col_sum(dq.astype(F32))
    sums_ref[pl.ds(PARTS + at, 1), 0:width] += col_sum(d_values.astype(F32))
    acc_ref[0:width, :] += tn(dq, x_sel_ref[...])
    acc_ref[width : 2 * width, :] += tn(d_keys, x_ref[...])
    acc_ref[2 * width : 3 * width, :] += tn(d_values, x_ref[...])
    acc_ref[3 * width : 4 * width, :] += tn(ctx_sel_ref[...], g1_ref[...])

    @pl.when(seq == pl.num_programs(0) - 1)
    def _():
        grad_ref[...] = acc_ref[...].astype(BF)


def attend_backward(part, lengths, q_sel, k, v, d_ctx, x, x_sel, ctx_sel, g1, seqs):
    rows, slots, width = k.shape[0] // seqs, q_sel.shape[0] // seqs, k.shape[1]
    depth = x.shape[1]
    row_spec = pl.BlockSpec((rows, width), lambda s, _: (s, 0))
    sel_spec = pl.BlockSpec((slots, width), lambda s, _: (s, 0))
    wide_spec = pl.BlockSpec((slots, depth), lambda s, _: (s, 0))
    return pl.pallas_call(
        lambda *refs: attend_back_body(*refs, part=part),
        grid_spec=pltpu.PrefetchScalarGridSpec(
            num_scalar_prefetch=1,
            grid=(seqs,),
            in_specs=[
                sel_spec,
                row_spec,
                row_spec,
                sel_spec,
                pl.BlockSpec((rows, depth), lambda s, _: (s, 0)),
                wide_spec,
                sel_spec,
                wide_spec,
            ],
            out_specs=[sel_spec, row_spec, row_spec, whole((2 * PARTS, depth)), whole((4 * width, depth))],
            scratch_shapes=[pltpu.VMEM((4 * width, depth), F32)],
        ),
        out_shape=[
            jax.ShapeDtypeStruct(q_sel.shape, BF),
            jax.ShapeDtypeStruct(k.shape, BF),
            jax.ShapeDtypeStruct(k.shape, BF),
            jax.ShapeDtypeStruct((2 * PARTS, depth), F32),
            jax.ShapeDtypeStruct((4 * width, depth), BF),
        ],
        cost_estimate=SMALL,
        name="attend_backward",
    )(lengths, q_sel, k, v, d_ctx, x, x_sel, ctx_sel, g1)


def erf_gelu(values):
    return 0.5 * (1.0 + lax.erf(values * HALF_ROOT))


def run(body, plain, hbm, outs, hbm_outs, scratch, name):
    return pl.pallas_call(
        body,
        grid=(1,),
        in_specs=[*[shaped(a.shape) for a in plain], *[ANY_SPEC] * len(hbm)],
        out_specs=[*[shaped(a.shape) for a in outs], *[ANY_SPEC] * len(hbm_outs)],
        out_shape=[*outs, *hbm_outs],
        scratch_shapes=scratch,
        cost_estimate=SMALL,
        name=name,
    )(*plain, *hbm)


def struct(dtype, *shape):
    return jax.ShapeDtypeStruct(shape, dtype)


def unit_part(low, wi, bias, slope_ref, n):
    pre = nn(low, wi) + bias
    chance = erf_gelu(pre)
    slope_ref[n] = chance + pre * (DENSITY * jnp.exp(-0.5 * pre * pre))
    return (pre * chance).astype(BF)


def ffn_prep(picked, x, d_out, ctx_sel, wo, wi, wd, small, shared, seqs):
    parts, near = len(wo), len(wi)
    slots = picked.shape[1]
    count, depth, units, width = seqs * slots, x.shape[1], wi[0][0][0].shape[1], ctx_sel[0].shape[1]
    plain = [picked, x, d_out, shared, *ctx_sel, *small]
    hbm = arrays(wo) + arrays(wi) + arrays(wd)

    def body(*refs):
        it = iter(refs)
        pick_ref, x_ref, d_out_ref, shared_ref = (next(it) for _ in range(4))
        ctx_refs = [next(it) for _ in range(parts)]
        small_refs = [next(it) for _ in range(near)]
        wo_refs, wi_refs, wd_refs = take(it, wo), take(it, wi), take(it, wd)
        act_refs = [next(it) for _ in range(near)]
        slope_ref, x_sel_ref, cot_ref, low_ref, sum_ref, normed1_ref, inv1_ref = (next(it) for _ in range(7))
        wo_v, wi_v, wd_v, sems = (next(it) for _ in range(4))
        out_copies = stacked_copies(wo_refs, wo_v, sems, 0, 1)
        first = len(flat(wo))
        in_copies = stacked_copies(wi_refs, wi_v, sems, first, 1)
        down_copies = stacked_copies(wd_refs, wd_v, sems, first + len(flat(wi)), 1)
        start_all(flat(out_copies) + flat(in_copies) + flat(down_copies))
        rows = x_ref.shape[0] // seqs
        for seq in range(seqs):
            at = lax.axis_index("tp") * seqs + seq
            spread = spread_of(pick_ref[pl.ds(at, 1), :], rows)
            x_sel_ref[seq * slots : (seq + 1) * slots, :] = tn(spread, x_ref[seq * rows : (seq + 1) * rows, :]).astype(BF)
            cot_ref[seq * slots : (seq + 1) * slots, :] = tn(spread, d_out_ref[seq * rows : (seq + 1) * rows, :]).astype(BF)
        attn_sum = x_sel_ref[...].astype(F32) + shared_ref[0:1, :]
        wait_all(flat(out_copies))
        for part in range(parts):
            attn_sum = attn_sum + nn(ctx_refs[part][...], wo_v[part])
        hidden, normed1, inv1 = norm_forward(attn_sum, shared_ref[2:3, :], shared_ref[4:5, :])
        low = hidden.astype(BF)
        low_ref[...] = low
        normed1_ref[...] = normed1
        inv1_ref[...] = inv1
        total = hidden + shared_ref[1:2, :]
        wait_all(flat(in_copies) + flat(down_copies))
        for n in range(near):
            act = unit_part(low, wi_v[n], small_refs[n][0:1, :], slope_ref, n)
            act_refs[n][...] = act
            total = total + nn(act, wd_v[n])
        sum_ref[...] = total

    outs = [
        *[struct(BF, count, units)] * near,
        struct(F32, near, count, units),
        struct(BF, count, depth),
        struct(BF, count, depth),
        struct(BF, count, depth),
        struct(F32, count, depth),
        struct(F32, count, depth),
        struct(F32, count, 1),
    ]
    scratch = [
        pltpu.VMEM((parts, width, depth), BF),
        pltpu.VMEM((near, depth, units), BF),
        pltpu.VMEM((near, units, depth), BF),
        pltpu.SemaphoreType.DMA((len(hbm),)),
    ]
    return run(body, plain, hbm, outs, [], scratch, "ffn_prep")


def ffn_front(low, total, cot, wi, wd, small, shared):
    far = len(wi)
    count, depth = low.shape
    units = wi[0][0][0].shape[1]
    plain = [low, total, cot, shared, *small]
    hbm = arrays(wi) + arrays(wd)

    def body(*refs):
        it = iter(refs)
        low_ref, sum_ref, cot_ref, shared_ref = (next(it) for _ in range(4))
        small_refs = [next(it) for _ in range(far)]
        wi_refs, wd_refs = take(it, wi), take(it, wd)
        sent_ref, g2_ref, slope_ref, grad2_ref, vec_ref = (next(it) for _ in range(5))
        wi_v, wd_v, sems = (next(it) for _ in range(3))
        in_copies = stacked_copies(wi_refs, wi_v, sems, 0, 1)
        down_copies = stacked_copies(wd_refs, wd_v, sems, len(flat(wi)), 1)
        for n in range(far):
            start_all(in_copies[n] + down_copies[n])
        low = low_ref[...]
        total = sum_ref[...]
        for n in range(far):
            wait_all(in_copies[n])
            act = unit_part(low, wi_v[n], small_refs[n][0:1, :], slope_ref, n)
            sent_ref[n * count : (n + 1) * count, :] = act
            wait_all(down_copies[n])
            total = total + nn(act, wd_v[n])
        _, normed2, inv2 = norm_forward(total, shared_ref[3:4, :], shared_ref[5:6, :])
        cotangent = cot_ref[...].astype(F32)
        grad2 = norm_backward(cotangent, normed2, inv2, shared_ref[3:4, :])
        vec_ref[...] = jnp.zeros(vec_ref.shape, F32)
        vec_ref[0:1, :] = col_sum(grad2)
        vec_ref[1:2, :] = col_sum(cotangent * normed2)
        vec_ref[2:3, :] = col_sum(cotangent)
        grad2_ref[...] = grad2
        g2 = grad2.astype(BF)
        g2_ref[...] = g2
        sent_ref[far * count :, :] = g2

    outs = [
        struct(BF, (far + 1) * count, units),
        struct(BF, count, depth),
        struct(F32, far, count, units),
        struct(F32, count, depth),
        struct(F32, 16, depth),
    ]
    scratch = [
        pltpu.VMEM((far, depth, units), BF),
        pltpu.VMEM((far, units, depth), BF),
        pltpu.SemaphoreType.DMA((len(hbm),)),
    ]
    return run(body, plain, hbm, outs, [], scratch, "ffn_front")


def ffn_mid(g2, low, slopes, wd):
    parts = len(wd)
    near = slopes[0].shape[0]
    count, depth = g2.shape
    units = slopes[0].shape[2]
    hbm = [*slopes, *arrays(wd)]

    def body(*refs):
        it = iter(refs)
        g2_ref, low_ref = next(it), next(it)
        slope_hbm = [next(it) for _ in slopes]
        wd_refs = take(it, wd)
        d_refs = [next(it) for _ in range(near)]
        sent_ref, vec_ref = next(it), next(it)
        wd_v, slope_v, sems, slope_sems = (next(it) for _ in range(4))
        down_copies = stacked_copies(wd_refs, wd_v, sems, 0, 1)
        sources = [ref.at[n] for ref in slope_hbm for n in range(ref.shape[0])]
        slope_copies = [pltpu.make_async_copy(sources[part], slope_v.at[part], slope_sems.at[part]) for part in range(parts)]
        for part in range(parts):
            start_all(down_copies[part] + [slope_copies[part]])
        vec_ref[...] = jnp.zeros(vec_ref.shape, F32)
        g2 = g2_ref[...]
        for part in range(parts):
            wait_all(down_copies[part] + [slope_copies[part]])
            d_pre = (nt(g2, wd_v[part]) * slope_v[part]).astype(BF)
            if part < near:
                d_refs[part][...] = d_pre
            else:
                sent_ref[(part - near) * count : (part - near + 1) * count, :] = d_pre
            at = 8 + (lax.axis_index("tp") ^ part)
            vec_ref[pl.ds(at, 1), :] = col_sum(d_pre.astype(F32))
        sent_ref[(parts - near) * count :, :] = low_ref[...]

    outs = [*[struct(BF, count, units)] * near, struct(BF, (parts - near + 1) * count, units), struct(F32, 16, depth)]
    scratch = [
        pltpu.VMEM((parts, units, depth), BF),
        pltpu.VMEM((parts, count, units), F32),
        pltpu.SemaphoreType.DMA((len(arrays(wd)),)),
        pltpu.SemaphoreType.DMA((parts,)),
    ]
    return run(body, [g2, low], hbm, outs, [], scratch, "ffn_mid")


def pair_sums(pairs):
    count = min(array.shape[0] for array, _ in pairs[0])
    width, depth = pairs[0][0][0].shape[1], pairs[0][1][0].shape[1]
    tile = min(256, width)

    def body(*refs):
        total = tn(refs[0][...], refs[1][...])
        for n in range(1, len(pairs)):
            total = total + tn(refs[2 * n][...], refs[2 * n + 1][...])
        refs[-1][...] = total.astype(BF)

    def left(block):
        return pl.BlockSpec((count, tile), lambda i: (block, i))

    def right(block):
        return pl.BlockSpec((count, depth), lambda i: (block, 0))

    return pl.pallas_call(
        body,
        grid=(width // tile,),
        in_specs=[spec for (_, a), (_, b) in pairs for spec in (left(a), right(b))],
        out_specs=pl.BlockSpec((tile, depth), lambda i: (i, 0)),
        out_shape=jax.ShapeDtypeStruct((width, depth), BF),
        cost_estimate=SMALL,
        name="pair_sums",
    )(*[array for (a, _), (b, _) in pairs for array in (a, b)])


def ffn_back(grad2, d_near, d_far, normed1, inv1, shared, wi, wo, width):
    parts, near = len(wi), len(d_near)
    count, depth = grad2.shape
    units = d_far.shape[1]
    hbm = arrays(wi) + arrays(wo)

    def body(*refs):
        it = iter(refs)
        grad2_ref, normed1_ref, inv1_ref, shared_ref = (next(it) for _ in range(4))
        near_refs = [next(it) for _ in range(near)]
        far_ref = next(it)
        wi_refs, wo_refs = take(it, wi), take(it, wo)
        g1_ref, grad1_ref, vec_ref = next(it), next(it), next(it)
        d_ctx_refs = [next(it) for _ in range(parts)]
        wi_v, wo_v, sems = (next(it) for _ in range(3))
        in_copies = stacked_copies(wi_refs, wi_v, sems, 0, 1)
        out_copies = stacked_copies(wo_refs, wo_v, sems, len(flat(wi)), 1)
        start_all(flat(in_copies) + flat(out_copies))
        d_hidden = grad2_ref[...]
        for part in range(parts):
            wait_all(in_copies[part])
            d_pre = near_refs[part][...] if part < near else far_ref[(part - near) * count : (part - near + 1) * count, :]
            d_hidden = d_hidden + nt(d_pre, wi_v[part])
        normed1 = normed1_ref[...]
        grad1 = norm_backward(d_hidden, normed1, inv1_ref[...], shared_ref[2:3, :])
        vec_ref[...] = jnp.zeros(vec_ref.shape, F32)
        vec_ref[3:4, :] = col_sum(grad1)
        vec_ref[4:5, :] = col_sum(d_hidden * normed1)
        vec_ref[5:6, :] = col_sum(d_hidden)
        grad1_ref[...] = grad1
        g1 = grad1.astype(BF)
        g1_ref[...] = g1
        wait_all(flat(out_copies))
        for part in range(parts):
            d_ctx_refs[part][...] = nt(g1, wo_v[part]).astype(BF)

    outs = [struct(BF, count, depth), struct(F32, count, depth), struct(F32, 16, depth), *[struct(BF, count, width)] * parts]
    scratch = [
        pltpu.VMEM((parts, depth, units), BF),
        pltpu.VMEM((parts, width, depth), BF),
        pltpu.SemaphoreType.DMA((len(hbm),)),
    ]
    return run(body, [grad2, normed1, inv1, shared, *d_near, d_far], hbm, outs, [], scratch, "ffn_back")


def ffn_rows(x, ctx, wo, wi, wd, small, shared, first, count, before):
    parts = len(wo)
    depth = x.shape[1]
    units, width = wi[0][0][0].shape[1], ctx[0].shape[1]
    tile = min(256, count)
    start = first // tile
    hbm = arrays(wo) + arrays(wi) + arrays(wd)
    last_inputs = [] if before is None else [before]

    def body(*refs):
        it = iter(refs)
        x_ref = next(it)
        ctx_refs = [next(it) for _ in range(parts)]
        small_refs = [next(it) for _ in range(parts)]
        shared_ref = next(it)
        wo_refs, wi_refs, wd_refs = take(it, wo), take(it, wi), take(it, wd)
        for _ in last_inputs:
            next(it)
        out_ref, wo_v, wi_v, wd_v, sems = (next(it) for _ in range(5))
        out_copies = flat(stacked_copies(wo_refs, wo_v, sems, 0, 1))
        near = len(flat(wo))
        in_copies = stacked_copies(wi_refs, wi_v, sems, near, 1)
        down_copies = stacked_copies(wd_refs, wd_v, sems, near + len(flat(wi)), 1)
        opening = pl.program_id(0) == 0

        @pl.when(opening)
        def _():
            start_all(out_copies)
            for part in range(parts):
                start_all(in_copies[part] + down_copies[part])
            wait_all(out_copies)

        attn_sum = x_ref[...].astype(F32) + shared_ref[0:1, :]
        for part in range(parts):
            attn_sum = attn_sum + nn(ctx_refs[part][...], wo_v[part])
        hidden, _, _ = norm_forward(attn_sum, shared_ref[2:3, :], shared_ref[4:5, :])
        low = hidden.astype(BF)
        total = hidden + shared_ref[1:2, :]
        for part in range(parts):

            @pl.when(opening)
            def _():
                wait_all(in_copies[part] + down_copies[part])

            pre = nn(low, wi_v[part]) + small_refs[part][0:1, :]
            act = (pre * erf_gelu(pre)).astype(BF)
            total = total + nn(act, wd_v[part])
        out_ref[...] = norm_forward(total, shared_ref[3:4, :], shared_ref[5:6, :])[0].astype(BF)

    return pl.pallas_call(
        body,
        grid=(count // tile,),
        in_specs=[
            pl.BlockSpec((tile, depth), lambda i: (i + start, 0)),
            *[pl.BlockSpec((tile, width), lambda i: (i + start, 0))] * parts,
            *[shaped(a.shape) for a in small],
            shaped(shared.shape),
            *[ANY_SPEC] * (len(hbm) + len(last_inputs)),
        ],
        out_specs=pl.BlockSpec((tile, depth), lambda i: (i + start, 0)),
        out_shape=jax.ShapeDtypeStruct(x.shape, BF),
        input_output_aliases={} if before is None else {2 + 2 * parts + len(hbm): 0},
        scratch_shapes=[
            pltpu.VMEM((parts, width, depth), BF),
            pltpu.VMEM((parts, depth, units), BF),
            pltpu.VMEM((parts, units, depth), BF),
            pltpu.SemaphoreType.DMA((len(hbm),)),
        ],
        cost_estimate=SMALL,
        name="ffn_rows",
    )(x, *ctx, *small, shared, *hbm, *last_inputs)


def input_gradient(picked, grad1, dq, dk, dv, wq, seqs):
    parts = len(dq)
    slots = picked.shape[1]
    depth = grad1.shape[1]
    rows, width = dk[0].shape[0] // seqs, dk[0].shape[1]
    hbm = arrays(wq)

    def body(*refs):
        it = iter(refs)
        pick_ref, grad1_ref = next(it), next(it)
        dq_refs = [next(it) for _ in range(parts)]
        dk_refs = [next(it) for _ in range(parts)]
        dv_refs = [next(it) for _ in range(parts)]
        wq_refs = take(it, wq)
        out_ref, wq_v, sems = next(it), next(it), next(it)
        copies = flat(stacked_copies(wq_refs, wq_v, sems, 0, 1))
        seq = pl.program_id(0)

        @pl.when(seq == 0)
        def _():
            start_all(copies)
            wait_all(copies)

        chosen = grad1_ref[...]
        for part in range(parts):
            chosen = chosen + nn(dq_refs[part][...], wq_v[part, 0:width, :])
        high = chosen.astype(BF)
        rest = (chosen - high.astype(F32)).astype(BF)
        spread = spread_of(pick_ref[pl.ds(lax.axis_index("tp") * seqs + seq, 1), :], rows)
        total = nn(spread, high) + nn(spread, rest)
        for part in range(parts):
            total = total + nn(dk_refs[part][...], wq_v[part, width : 2 * width, :])
            total = total + nn(dv_refs[part][...], wq_v[part, 2 * width : 3 * width, :])
        out_ref[...] = total.astype(BF)

    row_spec = pl.BlockSpec((rows, width), lambda s: (s, 0))
    return pl.pallas_call(
        body,
        grid=(seqs,),
        in_specs=[
            whole(picked.shape),
            pl.BlockSpec((slots, depth), lambda s: (s, 0)),
            *[pl.BlockSpec((slots, width), lambda s: (s, 0))] * parts,
            *[row_spec] * (2 * parts),
            *[ANY_SPEC] * len(hbm),
        ],
        out_specs=pl.BlockSpec((rows, depth), lambda s: (s, 0)),
        out_shape=jax.ShapeDtypeStruct((seqs * rows, depth), BF),
        scratch_shapes=[pltpu.VMEM((parts, 3 * width, depth), BF), pltpu.SemaphoreType.DMA((len(hbm),))],
        cost_estimate=SMALL,
        name="input_gradient",
    )(picked, grad1, *dq, *dk, *dv, *hbm)


def bits_of(count):
    return [1 << b for b in range(count.bit_length() - 1)]


def swap(value, axis, bit):
    count = lax.axis_size(axis)
    return lax.ppermute(value, axis, [(i, i ^ bit) for i in range(count)])


def half_of(value, bit, own):
    half = value.shape[0] // 2
    side = (lax.axis_index("dp") // bit) % 2
    return lax.dynamic_slice_in_dim(value, jnp.where(side == 0, 0, half) if own else jnp.where(side == 0, half, 0), half, 0)


def joined(own, got, bit):
    side = (lax.axis_index("dp") // bit) % 2
    return jnp.concatenate([jnp.where(side == 0, own, got), jnp.where(side == 0, got, own)], axis=0)


def add(*values):
    total = values[0].astype(F32)
    for value in values[1:]:
        total = total + value.astype(F32)
    return total.astype(BF)


def scatter(value, bit, *after):
    sent, kept = half_of(value, bit, False), half_of(value, bit, True)
    return add(tie(kept, *after), swap(sent, "dp", bit))


def gather(value, bit):
    return joined(value, swap(value, "dp", bit), bit)


def on_device(
    tokens, w_qkv, qv_bias, w_out, out_bias, w_in, in_bias, w_down, down_bias, norm_gain, norm_shift, valid_len, picked, d_out
):
    parts = lax.axis_size("tp")
    rank = lax.axis_index("tp")
    seqs = valid_len.shape[0] // parts
    depth = tokens.shape[1]
    width = w_qkv.shape[2]
    core, far = 1, 2
    dp_bits = bits_of(lax.axis_size("dp"))

    shared = jnp.concatenate([out_bias[None], down_bias[None], norm_gain, norm_shift, jnp.zeros((2, depth), F32)], axis=0)
    small = [jnp.concatenate([in_bias[None], jnp.pad(qv_bias, ((0, 5), (0, depth - width)))], axis=0)]
    small += [swap(small[0], "tp", core)]
    wq = w_qkv.transpose(0, 2, 1).reshape(3 * width, depth)
    qo_far = swap(jnp.concatenate([half_of(wq, 1, True), half_of(w_out, 1, True)], axis=0), "tp", far)
    wq_near = swap(wq, "tp", core)
    ready = small[1]
    small_far = swap(jnp.concatenate(small, axis=0), "tp", far)
    cut = w_down.shape[0] // 2
    ff_far = swap(tie(jnp.concatenate([half_of(w_in, 1, True), half_of(w_down[:cut], 1, True)], axis=0), small_far), "tp", far)
    fd_far = swap(tie(half_of(w_down[cut:], 2, True), small_far), "tp", far)
    small += [small_far[:8], small_far[8:]]

    def forward(j, x, pieces):
        return attend_forward(valid_len, x, pieces, width, small[j], picked, seqs)

    out0 = forward(0, tie(tokens, ready), [wq])
    qo_far = tie(qo_far, out0[0])
    qo_rest, qo_far_core = swap(qo_far, "dp", 1), swap(qo_far, "tp", core)
    out1 = forward(1, tie(tokens, qo_far), [wq_near])
    qo_rest = tie(qo_rest, out1[0])
    qo_rest_core = swap(qo_rest, "tp", core)
    wo_near = swap(tie(w_out, qo_rest), "tp", core)
    out2 = forward(2, tie(tokens, qo_rest), [qo_far, qo_rest])
    wi_near, wd_near = swap(tie(w_in, out2[0]), "tp", core), swap(tie(w_down, out2[0]), "tp", core)
    ff_far = tie(ff_far, out2[0])
    rows_in = w_in.shape[0] // 2
    ff_rest = swap(ff_far, "dp", 1)
    ff_far_core = swap(ff_far, "tp", core)
    out3 = forward(3, tie(tokens, ff_far), [qo_far_core, qo_rest_core])
    fd_far = tie(fd_far, out3[0])
    fd_rest, fd_far_core = swap(fd_far, "dp", 2), swap(fd_far, "tp", core)
    q_sel, k, v, ctx, ctx_sel = zip(out0, out1, out2, out3)
    rows_q = 3 * width // 2

    def pieces(own, near, far_pieces, core_pieces):
        return [[(own, 0)], [(near, 0)], far_pieces, core_pieces]

    wq = pieces(wq, wq_near, [(qo_far, 0), (qo_rest, 0)], [(qo_far_core, 0), (qo_rest_core, 0)])
    wo = pieces(w_out, wo_near, [(qo_far, rows_q), (qo_rest, rows_q)], [(qo_far_core, rows_q), (qo_rest_core, rows_q)])
    near_in, near_down = [[(w_in, 0)], [(wi_near, 0)]], [[(w_down, 0)], [(wd_near, 0)]]
    prep = ffn_prep(picked, tie(tokens, fd_far), d_out, ctx_sel, wo, near_in, near_down, small[:2], shared, seqs)
    *act, slope_near, x_sel, cot, low, ffn_sum, normed1, inv1 = prep
    low_near, act_near = swap(low, "tp", core), swap(act[1], "tp", core)
    ff_rest, fd_rest = tie((ff_rest, fd_rest), low)
    ff_rest_core, fd_rest_core = swap(ff_rest, "tp", core), swap(fd_rest, "tp", core)
    wi = near_in + [[(ff_far, 0), (ff_rest, 0)], [(ff_far_core, 0), (ff_rest_core, 0)]]
    wd = near_down + [
        [(ff_far, rows_in), (ff_rest, rows_in), (fd_far, 0), (fd_rest, 0)],
        [(ff_far_core, rows_in), (ff_rest_core, rows_in), (fd_far_core, 0), (fd_rest_core, 0)],
    ]

    sent, g2, slope_far, grad2, vec = ffn_front(low, ffn_sum, cot, wi[2:], wd[2:], small[2:], shared)
    act_got = swap(sent, "tp", far)
    g2_near = swap(g2, "tp", core)
    *d_near, d_far, vec_mid = ffn_mid(g2, low, [slope_near, slope_far], wd)
    d_got, d_got_near = swap(d_far, "tp", far), swap(d_near[1], "tp", core)
    g1, grad1, vec_back, *d_ctx = ffn_back(tie(grad2, act_near, low_near, g2_near), d_near, d_far, normed1, inv1, shared, wi, wo, width)
    count = low.shape[0]

    def backward(j, x):
        return attend_backward(j, valid_len, q_sel[j], k[j], v[j], d_ctx[j], x, x_sel, ctx_sel[j], g1, seqs)

    def rows_of(first, count, before, *after):
        return ffn_rows(tie(tokens, *after), ctx, wo, wi, wd, small, shared, first, count, before)

    def finish(value, bits):
        for bit in bits:
            value = scatter(value, bit) if bit != last else add(value, swap(value, "dp", bit))
        return value

    def spread_out(value, bits):
        for bit in reversed(bits):
            value = gather(value, bit)
        return value

    half_rows, last = tokens.shape[0] // 2, dp_bits[-1]
    out3 = backward(3, tie(tokens, d_got_near))
    out2 = backward(2, tie(tokens, out3[0]))
    act_got = tie(act_got, out2[0])
    act_diag = swap(act_got[count:], "tp", core)
    out1 = backward(1, tie(tokens, out2[0], act_got))
    total_a = pair_sums(
        [
            ((tie(act[0], out1[0]), 0), (g2, 0)),
            ((act_near, 0), (g2_near, 0)),
            ((act_got, 0), (act_got, 2)),
            ((act_diag, 0), (act_diag, 1)),
        ]
    )
    sent_a = half_of(total_a, dp_bits[0], False)
    out0 = backward(0, tie(tokens, out1[0], sent_a))
    dq, dk, dv, sums, g_heads = zip(out0, out1, out2, out3)
    d_got = tie(d_got, out0[0])
    d_diag = swap(d_got[count:], "tp", core)
    far_c = add(tie(out2[4], out0[0]), swap(tie(out3[4], out1[0]), "tp", core))
    near_c = g_heads[0], swap(tie(g_heads[1], out0[0]), "tp", core)
    line = jnp.concatenate([vec + vec_mid + vec_back, sums[0] + sums[1] + sums[2] + sums[3]], axis=0)
    out_first = rows_of(0, half_rows, None, line, far_c, d_got)
    total_a = add(tie(half_of(total_a, dp_bits[0], True), out_first), swap(sent_a, "dp", dp_bits[0]))
    sent_a = half_of(total_a, dp_bits[1], False)
    total_b = pair_sums(
        [
            ((tie(low, out_first), 0), (d_near[0], 0)),
            ((low_near, 0), (d_got_near, 0)),
            ((d_got, 2), (d_got, 0)),
            ((d_diag, 1), (d_diag, 0)),
        ]
    )
    sent_b = half_of(total_b, dp_bits[0], False)
    d_tokens = input_gradient(tie(picked, sent_a, sent_b), grad1, dq, dk, dv, wq, seqs)
    total_a = add(tie(half_of(total_a, dp_bits[1], True), d_tokens), swap(sent_a, "dp", dp_bits[1]))
    for bit in dp_bits[2:-1]:
        total_a = scatter(total_a, bit)
    total_b = add(tie(half_of(total_b, dp_bits[0], True), d_tokens), swap(sent_b, "dp", dp_bits[0]))
    total_c = add(*tie(near_c, d_tokens), swap(far_c, "tp", far))
    cut = far_c.shape[0] // 2
    other = [dp_bits[1], dp_bits[0], *dp_bits[2:]]
    total_c, rest_c = total_c[:cut], total_c[cut:]
    sent_b = half_of(total_b, dp_bits[1], False)
    sent_c, sent_d = half_of(total_c, dp_bits[0], False), half_of(rest_c, other[0], False)
    line = tie(line, d_tokens)
    out_second = rows_of(half_rows, half_rows // 2, out_first, total_a, sent_b, sent_c, sent_d, line)
    total_a = add(tie(total_a, out_second), swap(total_a, "dp", last))
    total_b = add(tie(half_of(total_b, dp_bits[1], True), out_second), swap(sent_b, "dp", dp_bits[1]))
    for bit in dp_bits[2:-1]:
        total_b = scatter(total_b, bit)
    total_c = add(tie(half_of(total_c, dp_bits[0], True), out_second), swap(sent_c, "dp", dp_bits[0]))
    rest_c = add(tie(half_of(rest_c, other[0], True), out_second), swap(sent_d, "dp", other[0]))
    line = tie(line, out_second) + swap(line, "tp", core)
    sent_c, sent_d = half_of(total_c, dp_bits[1], False), half_of(rest_c, other[1], False)
    out_third = rows_of(half_rows + half_rows // 2, half_rows // 2, out_second, total_a, total_b, sent_c, sent_d, line)
    for bit in reversed(dp_bits[2:-1]):
        total_a = gather(total_a, bit)
    total_a = joined(tie(total_a, out_third), swap(total_a, "dp", dp_bits[1]), dp_bits[1])
    total_b = add(tie(total_b, out_third), swap(total_b, "dp", last))
    total_c = add(tie(half_of(total_c, dp_bits[1], True), out_third), swap(sent_c, "dp", dp_bits[1]))
    rest_c = add(tie(half_of(rest_c, other[1], True), out_third), swap(sent_d, "dp", other[1]))
    line = tie(line, total_c, rest_c) + swap(line, "dp", dp_bits[0])
    for bit in dp_bits[1:2]:
        line = line + swap(line, "dp", bit)
    total_c, rest_c = finish(total_c, dp_bits[2:]), finish(rest_c, other[2:])
    line = tie(line, total_c)
    for bit in dp_bits[2:]:
        line = line + swap(line, "dp", bit)
    total_b = spread_out(total_b, dp_bits[1:-1])
    total_c, rest_c = spread_out(total_c, dp_bits[1:-1]), spread_out(rest_c, other[1:-1])
    line = tie(line, total_c)
    line = line + swap(line, "tp", far)
    total_a, total_b = gather(total_a, dp_bits[0]), gather(total_b, dp_bits[0])
    total_c, rest_c = gather(total_c, dp_bits[0]), gather(rest_c, other[0])
    total_c = jnp.concatenate([total_c.astype(F32), rest_c.astype(F32)], axis=0)
    own = lax.dynamic_slice_in_dim(line, 8 + rank, 1, 0)[0]
    own_q = lax.dynamic_slice(line, (16 + rank, 0), (1, width))
    own_v = lax.dynamic_slice(line, (16 + PARTS + rank, 0), (1, width))
    return (
        out_third,
        d_tokens,
        total_c[: 3 * width].reshape(3, width, depth).transpose(0, 2, 1),
        jnp.concatenate([own_q, own_v], axis=0),
        total_c[3 * width :],
        line[3],
        total_b.astype(F32),
        own,
        total_a.astype(F32),
        line[0],
        jnp.stack([line[4], line[1]]),
        jnp.stack([line[5], line[2]]),
    )


def solution(mesh):
    placed = (
        P(("dp", "tp"), None),
        P(None, None, "tp"),
        P(None, "tp"),
        P("tp", None),
        P(),
        P(None, "tp"),
        P("tp"),
        P("tp", None),
        P(),
        P(),
        P(),
        P("dp"),
        P("dp", None),
        P(("dp", "tp"), None),
    )
    return jax.shard_map(
        on_device,
        mesh=mesh,
        in_specs=placed,
        out_specs=(
            P(("dp", "tp"), None),
            P(("dp", "tp"), None),
            P(None, None, "tp"),
            P(None, "tp"),
            P("tp", None),
            P(),
            P(None, "tp"),
            P("tp"),
            P("tp", None),
            P(),
            P(),
            P(),
        ),
        check_vma=False,
    )
```

```python
import jax
import jax.numpy as jnp
from jax import lax
from jax.experimental import pallas as pl
from jax.experimental.pallas import tpu as pltpu
from jax.sharding import PartitionSpec as P

HD = 64
SCALE = HD ** (-0.5)
NORM_EPS = 1e-06
MASKED = -1e30
HALF_ROOT = 0.5 ** 0.5
DENSITY = 0.3989422804014327
PARTS = 4
BF = jnp.bfloat16
F32 = jnp.float32


def nn(left, right):
    return lax.dot_general(left, right, (((1,), (0,)), ((), ())), preferred_element_type=F32)


def nt(left, right):
    return lax.dot_general(left, right, (((1,), (1,)), ((), ())), preferred_element_type=F32)


def tn(left, right):
    return lax.dot_general(left, right, (((0,), (0,)), ((), ())), preferred_element_type=F32)


def head_masks(width, dtype=BF):
    lane = lax.broadcasted_iota(jnp.int32, (1, width), 1) // HD
    return [(lane == head).astype(dtype) for head in range(width // HD)]


def spread_of(picks, length):
    slots = picks.shape[1]
    return (lax.broadcasted_iota(jnp.int32, (length, slots), 0) == picks).astype(F32).astype(BF)


def whole(shape):
    zeros = (0,) * len(shape)
    return pl.BlockSpec(shape, lambda *_: zeros)


def norm_forward(values, gain, shift):
    average = jnp.mean(values, axis=1, keepdims=True)
    centered = values - average
    inv_std = lax.rsqrt(jnp.mean(centered * centered, axis=1, keepdims=True) + NORM_EPS)
    normed = centered * inv_std
    return normed * gain + shift, normed, inv_std


def norm_backward(grad, normed, inv_std, gain):
    scaled = grad * gain
    first = jnp.mean(scaled, axis=1, keepdims=True)
    second = jnp.mean(scaled * normed, axis=1, keepdims=True)
    return inv_std * (scaled - first - normed * second)


def tie(value, *others):
    return lax.optimization_barrier((value, others))[0]


SMALL = pl.CostEstimate(flops=1024, transcendentals=0, bytes_accessed=1024)


def col_sum(values):
    return jnp.sum(values, axis=0, keepdims=True)


def piece_copies(pieces, target, sems, first, bit):
    rows = target.shape[0]
    if len(pieces) == 1:
        return [pltpu.make_async_copy(pieces[0][0], target, sems.at[first])]
    half, step = rows // 2, rows // len(pieces)
    if len(pieces) == 4:
        upper = piece_copies(pieces[:2], target.at[pl.ds(0, half), :], sems, first, bit)
        return upper + piece_copies(pieces[2:], target.at[pl.ds(half, half), :], sems, first + 2, 2 * bit)
    own = ((lax.axis_index("dp") // bit) % 2) * half
    copies = []
    for n, (ref, skip) in enumerate(pieces):
        base = own if n * step < half else half - own
        start = pl.multiple_of(base + (n * step) % half, step)
        copies.append(pltpu.make_async_copy(ref.at[pl.ds(skip, step), :], target.at[pl.ds(start, step), :], sems.at[first + n]))
    return copies


def stacked_copies(pieces, target, sems, first, bit):
    copies = []
    for part, refs in enumerate(pieces):
        copies.append(piece_copies(refs, target.at[part], sems, first, bit))
        first += len(refs)
    return copies


def take(it, pieces):
    return [[(next(it), skip) for _, skip in piece] for piece in pieces]


def flat(pieces):
    return [p for piece in pieces for p in piece]


def arrays(pieces):
    return [array for array, _ in flat(pieces)]


def start_all(copies):
    for copy in copies:
        copy.start()


def wait_all(copies):
    for copy in copies:
        copy.wait()


ANY_SPEC = pl.BlockSpec(memory_space=pl.ANY)


def shaped(shape):
    return pl.BlockSpec(shape, lambda *_: (0,) * len(shape))


def attend_body(len_ref, x_ref, small_ref, pick_ref, *rest, count):
    w_refs = [(ref, 0) for ref in rest[:count]]
    q_sel_ref, k_ref, v_ref, ctx_ref, ctx_sel_ref, ext_ref, w_ref, sems = rest[count:]
    rows, width = k_ref.shape
    seq = pl.program_id(0)
    row = lax.axis_index("tp") * pl.num_programs(0) + seq
    length = len_ref[row]
    copies = piece_copies(w_refs, w_ref, sems, 0, 1)

    @pl.when(seq == 0)
    def _():
        start_all(copies)
        wait_all(copies)

    x = x_ref[...]
    queries = (nt(x, w_ref[0:width, :]) + small_ref[1:2, :width]).astype(BF)
    key_rows = nt(x, w_ref[width : 2 * width, :]).astype(BF)
    values = (nt(x, w_ref[2 * width : 3 * width, :]) + small_ref[2:3, :width]).astype(BF)
    k_ref[...] = key_rows
    v_ref[...] = values
    ext_ref[:, :width] = values
    ext_ref[:, width:] = jnp.ones((rows, ext_ref.shape[1] - width), BF)
    spread = spread_of(pick_ref[pl.ds(row, 1), :], rows)
    q_sel_ref[...] = tn(spread, queries).astype(BF)
    scaled = queries * jnp.asarray(SCALE, BF)
    masks = head_masks(width)
    tile = min(256, rows)
    keep = lax.broadcasted_iota(jnp.int32, (tile, rows), 1) < length
    for start in range(0, rows, tile):
        total = jnp.zeros((tile, width), F32)
        for mask in masks:
            logits = nt(scaled[start : start + tile] * mask, key_rows)
            logits = jnp.where(keep, logits, MASKED)
            peak = jnp.max(logits, axis=1, keepdims=True)
            probs = jnp.exp(logits - peak).astype(BF)
            mixed = nn(probs, ext_ref[...])
            share = mixed[:, :width] / mixed[:, width : width + 1]
            total = jnp.where(mask.astype(F32) > 0.5, share, total)
        ctx_ref[start : start + tile, :] = total.astype(BF)
    ctx_sel_ref[...] = tn(spread, ctx_ref[...]).astype(BF)


def attend_forward(lengths, x, pieces, width, small, picked, seqs):
    slots = picked.shape[1]
    rows = x.shape[0] // seqs
    depth = x.shape[1]
    ext = -(-(width + 1) // 128) * 128
    row_spec = pl.BlockSpec((rows, width), lambda s, _: (s, 0))
    sel_spec = pl.BlockSpec((slots, width), lambda s, _: (s, 0))
    return pl.pallas_call(
        lambda *refs: attend_body(*refs, count=len(pieces)),
        grid_spec=pltpu.PrefetchScalarGridSpec(
            num_scalar_prefetch=1,
            grid=(seqs,),
            in_specs=[
                pl.BlockSpec((rows, depth), lambda s, _: (s, 0)),
                whole(small.shape),
                whole(picked.shape),
                *[ANY_SPEC] * len(pieces),
            ],
            out_specs=[sel_spec, row_spec, row_spec, row_spec, sel_spec],
            scratch_shapes=[
                pltpu.VMEM((rows, ext), BF),
                pltpu.VMEM((3 * width, depth), BF),
                pltpu.SemaphoreType.DMA((len(pieces),)),
            ],
        ),
        out_shape=[
            jax.ShapeDtypeStruct((seqs * slots, width), BF),
            jax.ShapeDtypeStruct((seqs * rows, width), BF),
            jax.ShapeDtypeStruct((seqs * rows, width), BF),
            jax.ShapeDtypeStruct((seqs * rows, width), BF),
            jax.ShapeDtypeStruct((seqs * slots, width), BF),
        ],
        cost_estimate=SMALL,
        name="attend_forward",
    )(lengths, x, small, picked, *pieces)


def attend_back_body(
    len_ref, q_ref, k_ref, v_ref, d_ctx_ref, x_ref, x_sel_ref, ctx_sel_ref, g1_ref, dq_ref, dk_ref, dv_ref, sums_ref, grad_ref, acc_ref, *, part
):
    rows, width = k_ref.shape
    slots = q_ref.shape[0]
    seq = pl.program_id(0)
    rank = lax.axis_index("tp")
    length = len_ref[rank * pl.num_programs(0) + seq]
    masks = head_masks(width)
    queries, d_ctx = q_ref[...], d_ctx_ref[...]
    key_rows, values = k_ref[...], v_ref[...]
    q_stack = jnp.concatenate([queries * mask for mask in masks], axis=0)
    d_stack = jnp.concatenate([d_ctx * mask for mask in masks], axis=0)
    logits = nt(key_rows, q_stack * jnp.asarray(SCALE, BF))
    keep = lax.broadcasted_iota(jnp.int32, logits.shape, 0) < length
    logits = jnp.where(keep, logits, MASKED)
    grown = jnp.exp(logits - jnp.max(logits, axis=0, keepdims=True))
    probs = grown * (1.0 / jnp.sum(grown, axis=0, keepdims=True))
    d_probs = nt(values, d_stack)
    inner = jnp.sum(probs * d_probs, axis=0, keepdims=True)
    d_raw = (probs * (d_probs - inner) * SCALE).astype(BF)
    d_keys = nn(d_raw, q_stack).astype(BF)
    dk_ref[...] = d_keys
    d_values = nn(probs.astype(BF), d_stack).astype(BF)
    dv_ref[...] = d_values
    dq_stack = tn(d_raw, key_rows)
    dq = jnp.zeros((slots, width), F32)
    for head, mask in enumerate(masks):
        dq = jnp.where(mask.astype(F32) > 0.5, dq_stack[head * slots : (head + 1) * slots], dq)
    dq = dq.astype(BF)
    dq_ref[...] = dq

    @pl.when(seq == 0)
    def _():
        acc_ref[...] = jnp.zeros(acc_ref.shape, F32)
        sums_ref[...] = jnp.zeros(sums_ref.shape, F32)

    at = rank ^ part
    sums_ref[pl.ds(at, 1), 0:width] += col_sum(dq.astype(F32))
    sums_ref[pl.ds(PARTS + at, 1), 0:width] += col_sum(d_values.astype(F32))
    acc_ref[0:width, :] += tn(dq, x_sel_ref[...])
    acc_ref[width : 2 * width, :] += tn(d_keys, x_ref[...])
    acc_ref[2 * width : 3 * width, :] += tn(d_values, x_ref[...])
    acc_ref[3 * width : 4 * width, :] += tn(ctx_sel_ref[...], g1_ref[...])

    @pl.when(seq == pl.num_programs(0) - 1)
    def _():
        grad_ref[...] = acc_ref[...].astype(BF)


def attend_backward(part, lengths, q_sel, k, v, d_ctx, x, x_sel, ctx_sel, g1, seqs):
    rows, slots, width = k.shape[0] // seqs, q_sel.shape[0] // seqs, k.shape[1]
    depth = x.shape[1]
    row_spec = pl.BlockSpec((rows, width), lambda s, _: (s, 0))
    sel_spec = pl.BlockSpec((slots, width), lambda s, _: (s, 0))
    wide_spec = pl.BlockSpec((slots, depth), lambda s, _: (s, 0))
    return pl.pallas_call(
        lambda *refs: attend_back_body(*refs, part=part),
        grid_spec=pltpu.PrefetchScalarGridSpec(
            num_scalar_prefetch=1,
            grid=(seqs,),
            in_specs=[
                sel_spec,
                row_spec,
                row_spec,
                sel_spec,
                pl.BlockSpec((rows, depth), lambda s, _: (s, 0)),
                wide_spec,
                sel_spec,
                wide_spec,
            ],
            out_specs=[sel_spec, row_spec, row_spec, whole((2 * PARTS, depth)), whole((4 * width, depth))],
            scratch_shapes=[pltpu.VMEM((4 * width, depth), F32)],
        ),
        out_shape=[
            jax.ShapeDtypeStruct(q_sel.shape, BF),
            jax.ShapeDtypeStruct(k.shape, BF),
            jax.ShapeDtypeStruct(k.shape, BF),
            jax.ShapeDtypeStruct((2 * PARTS, depth), F32),
            jax.ShapeDtypeStruct((4 * width, depth), BF),
        ],
        cost_estimate=SMALL,
        name="attend_backward",
    )(lengths, q_sel, k, v, d_ctx, x, x_sel, ctx_sel, g1)


def erf_gelu(values):
    return 0.5 * (1.0 + lax.erf(values * HALF_ROOT))


def run(body, plain, hbm, outs, hbm_outs, scratch, name):
    return pl.pallas_call(
        body,
        grid=(1,),
        in_specs=[*[shaped(a.shape) for a in plain], *[ANY_SPEC] * len(hbm)],
        out_specs=[*[shaped(a.shape) for a in outs], *[ANY_SPEC] * len(hbm_outs)],
        out_shape=[*outs, *hbm_outs],
        scratch_shapes=scratch,
        cost_estimate=SMALL,
        name=name,
    )(*plain, *hbm)


def struct(dtype, *shape):
    return jax.ShapeDtypeStruct(shape, dtype)


def unit_part(low, wi, bias, slope_ref, n):
    pre = nn(low, wi) + bias
    chance = erf_gelu(pre)
    slope_ref[n] = chance + pre * (DENSITY * jnp.exp(-0.5 * pre * pre))
    return (pre * chance).astype(BF)


def ffn_prep(picked, x, d_out, ctx_sel, wo, wi, wd, small, shared, seqs):
    parts, near = len(wo), len(wi)
    slots = picked.shape[1]
    count, depth, units, width = seqs * slots, x.shape[1], wi[0][0][0].shape[1], ctx_sel[0].shape[1]
    plain = [picked, x, d_out, shared, *ctx_sel, *small]
    hbm = arrays(wo) + arrays(wi) + arrays(wd)

    def body(*refs):
        it = iter(refs)
        pick_ref, x_ref, d_out_ref, shared_ref = (next(it) for _ in range(4))
        ctx_refs = [next(it) for _ in range(parts)]
        small_refs = [next(it) for _ in range(near)]
        wo_refs, wi_refs, wd_refs = take(it, wo), take(it, wi), take(it, wd)
        act_refs = [next(it) for _ in range(near)]
        slope_ref, x_sel_ref, cot_ref, low_ref, sum_ref, normed1_ref, inv1_ref = (next(it) for _ in range(7))
        wo_v, wi_v, wd_v, sems = (next(it) for _ in range(4))
        out_copies = stacked_copies(wo_refs, wo_v, sems, 0, 1)
        first = len(flat(wo))
        in_copies = stacked_copies(wi_refs, wi_v, sems, first, 1)
        down_copies = stacked_copies(wd_refs, wd_v, sems, first + len(flat(wi)), 1)
        start_all(flat(out_copies) + flat(in_copies) + flat(down_copies))
        rows = x_ref.shape[0] // seqs
        for seq in range(seqs):
            at = lax.axis_index("tp") * seqs + seq
            spread = spread_of(pick_ref[pl.ds(at, 1), :], rows)
            x_sel_ref[seq * slots : (seq + 1) * slots, :] = tn(spread, x_ref[seq * rows : (seq + 1) * rows, :]).astype(BF)
            cot_ref[seq * slots : (seq + 1) * slots, :] = tn(spread, d_out_ref[seq * rows : (seq + 1) * rows, :]).astype(BF)
        attn_sum = x_sel_ref[...].astype(F32) + shared_ref[0:1, :]
        wait_all(flat(out_copies))
        for part in range(parts):
            attn_sum = attn_sum + nn(ctx_refs[part][...], wo_v[part])
        hidden, normed1, inv1 = norm_forward(attn_sum, shared_ref[2:3, :], shared_ref[4:5, :])
        low = hidden.astype(BF)
        low_ref[...] = low
        normed1_ref[...] = normed1
        inv1_ref[...] = inv1
        total = hidden + shared_ref[1:2, :]
        wait_all(flat(in_copies) + flat(down_copies))
        for n in range(near):
            act = unit_part(low, wi_v[n], small_refs[n][0:1, :], slope_ref, n)
            act_refs[n][...] = act
            total = total + nn(act, wd_v[n])
        sum_ref[...] = total

    outs = [
        *[struct(BF, count, units)] * near,
        struct(F32, near, count, units),
        struct(BF, count, depth),
        struct(BF, count, depth),
        struct(BF, count, depth),
        struct(F32, count, depth),
        struct(F32, count, depth),
        struct(F32, count, 1),
    ]
    scratch = [
        pltpu.VMEM((parts, width, depth), BF),
        pltpu.VMEM((near, depth, units), BF),
        pltpu.VMEM((near, units, depth), BF),
        pltpu.SemaphoreType.DMA((len(hbm),)),
    ]
    return run(body, plain, hbm, outs, [], scratch, "ffn_prep")


def ffn_front(low, total, cot, wi, wd, small, shared):
    far = len(wi)
    count, depth = low.shape
    units = wi[0][0][0].shape[1]
    plain = [low, total, cot, shared, *small]
    hbm = arrays(wi) + arrays(wd)

    def body(*refs):
        it = iter(refs)
        low_ref, sum_ref, cot_ref, shared_ref = (next(it) for _ in range(4))
        small_refs = [next(it) for _ in range(far)]
        wi_refs, wd_refs = take(it, wi), take(it, wd)
        sent_ref, g2_ref, slope_ref, grad2_ref, vec_ref = (next(it) for _ in range(5))
        wi_v, wd_v, sems = (next(it) for _ in range(3))
        in_copies = stacked_copies(wi_refs, wi_v, sems, 0, 1)
        down_copies = stacked_copies(wd_refs, wd_v, sems, len(flat(wi)), 1)
        for n in range(far):
            start_all(in_copies[n] + down_copies[n])
        low = low_ref[...]
        total = sum_ref[...]
        for n in range(far):
            wait_all(in_copies[n])
            act = unit_part(low, wi_v[n], small_refs[n][0:1, :], slope_ref, n)
            sent_ref[n * count : (n + 1) * count, :] = act
            wait_all(down_copies[n])
            total = total + nn(act, wd_v[n])
        _, normed2, inv2 = norm_forward(total, shared_ref[3:4, :], shared_ref[5:6, :])
        cotangent = cot_ref[...].astype(F32)
        grad2 = norm_backward(cotangent, normed2, inv2, shared_ref[3:4, :])
        vec_ref[...] = jnp.zeros(vec_ref.shape, F32)
        vec_ref[0:1, :] = col_sum(grad2)
        vec_ref[1:2, :] = col_sum(cotangent * normed2)
        vec_ref[2:3, :] = col_sum(cotangent)
        grad2_ref[...] = grad2
        g2 = grad2.astype(BF)
        g2_ref[...] = g2
        sent_ref[far * count :, :] = g2

    outs = [
        struct(BF, (far + 1) * count, units),
        struct(BF, count, depth),
        struct(F32, far, count, units),
        struct(F32, count, depth),
        struct(F32, 16, depth),
    ]
    scratch = [
        pltpu.VMEM((far, depth, units), BF),
        pltpu.VMEM((far, units, depth), BF),
        pltpu.SemaphoreType.DMA((len(hbm),)),
    ]
    return run(body, plain, hbm, outs, [], scratch, "ffn_front")


def ffn_mid(g2, low, slopes, wd):
    parts = len(wd)
    near = slopes[0].shape[0]
    count, depth = g2.shape
    units = slopes[0].shape[2]
    hbm = [*slopes, *arrays(wd)]

    def body(*refs):
        it = iter(refs)
        g2_ref, low_ref = next(it), next(it)
        slope_hbm = [next(it) for _ in slopes]
        wd_refs = take(it, wd)
        d_refs = [next(it) for _ in range(near)]
        sent_ref, vec_ref = next(it), next(it)
        wd_v, slope_v, sems, slope_sems = (next(it) for _ in range(4))
        down_copies = stacked_copies(wd_refs, wd_v, sems, 0, 1)
        sources = [ref.at[n] for ref in slope_hbm for n in range(ref.shape[0])]
        slope_copies = [pltpu.make_async_copy(sources[part], slope_v.at[part], slope_sems.at[part]) for part in range(parts)]
        for part in range(parts):
            start_all(down_copies[part] + [slope_copies[part]])
        vec_ref[...] = jnp.zeros(vec_ref.shape, F32)
        g2 = g2_ref[...]
        for part in range(parts):
            wait_all(down_copies[part] + [slope_copies[part]])
            d_pre = (nt(g2, wd_v[part]) * slope_v[part]).astype(BF)
            if part < near:
                d_refs[part][...] = d_pre
            else:
                sent_ref[(part - near) * count : (part - near + 1) * count, :] = d_pre
            at = 8 + (lax.axis_index("tp") ^ part)
            vec_ref[pl.ds(at, 1), :] = col_sum(d_pre.astype(F32))
        sent_ref[(parts - near) * count :, :] = low_ref[...]

    outs = [*[struct(BF, count, units)] * near, struct(BF, (parts - near + 1) * count, units), struct(F32, 16, depth)]
    scratch = [
        pltpu.VMEM((parts, units, depth), BF),
        pltpu.VMEM((parts, count, units), F32),
        pltpu.SemaphoreType.DMA((len(arrays(wd)),)),
        pltpu.SemaphoreType.DMA((parts,)),
    ]
    return run(body, [g2, low], hbm, outs, [], scratch, "ffn_mid")


def pair_sums(pairs):
    count = min(array.shape[0] for array, _ in pairs[0])
    width, depth = pairs[0][0][0].shape[1], pairs[0][1][0].shape[1]
    tile = min(256, width)

    def body(*refs):
        total = tn(refs[0][...], refs[1][...])
        for n in range(1, len(pairs)):
            total = total + tn(refs[2 * n][...], refs[2 * n + 1][...])
        refs[-1][...] = total.astype(BF)

    def left(block):
        return pl.BlockSpec((count, tile), lambda i: (block, i))

    def right(block):
        return pl.BlockSpec((count, depth), lambda i: (block, 0))

    return pl.pallas_call(
        body,
        grid=(width // tile,),
        in_specs=[spec for (_, a), (_, b) in pairs for spec in (left(a), right(b))],
        out_specs=pl.BlockSpec((tile, depth), lambda i: (i, 0)),
        out_shape=jax.ShapeDtypeStruct((width, depth), BF),
        cost_estimate=SMALL,
        name="pair_sums",
    )(*[array for (a, _), (b, _) in pairs for array in (a, b)])


def ffn_back(grad2, d_near, d_far, normed1, inv1, shared, wi, wo, width):
    parts, near = len(wi), len(d_near)
    count, depth = grad2.shape
    units = d_far.shape[1]
    hbm = arrays(wi) + arrays(wo)

    def body(*refs):
        it = iter(refs)
        grad2_ref, normed1_ref, inv1_ref, shared_ref = (next(it) for _ in range(4))
        near_refs = [next(it) for _ in range(near)]
        far_ref = next(it)
        wi_refs, wo_refs = take(it, wi), take(it, wo)
        g1_ref, grad1_ref, vec_ref = next(it), next(it), next(it)
        d_ctx_refs = [next(it) for _ in range(parts)]
        wi_v, wo_v, sems = (next(it) for _ in range(3))
        in_copies = stacked_copies(wi_refs, wi_v, sems, 0, 1)
        out_copies = stacked_copies(wo_refs, wo_v, sems, len(flat(wi)), 1)
        start_all(flat(in_copies) + flat(out_copies))
        d_hidden = grad2_ref[...]
        for part in range(parts):
            wait_all(in_copies[part])
            d_pre = near_refs[part][...] if part < near else far_ref[(part - near) * count : (part - near + 1) * count, :]
            d_hidden = d_hidden + nt(d_pre, wi_v[part])
        normed1 = normed1_ref[...]
        grad1 = norm_backward(d_hidden, normed1, inv1_ref[...], shared_ref[2:3, :])
        vec_ref[...] = jnp.zeros(vec_ref.shape, F32)
        vec_ref[3:4, :] = col_sum(grad1)
        vec_ref[4:5, :] = col_sum(d_hidden * normed1)
        vec_ref[5:6, :] = col_sum(d_hidden)
        grad1_ref[...] = grad1
        g1 = grad1.astype(BF)
        g1_ref[...] = g1
        wait_all(flat(out_copies))
        for part in range(parts):
            d_ctx_refs[part][...] = nt(g1, wo_v[part]).astype(BF)

    outs = [struct(BF, count, depth), struct(F32, count, depth), struct(F32, 16, depth), *[struct(BF, count, width)] * parts]
    scratch = [
        pltpu.VMEM((parts, depth, units), BF),
        pltpu.VMEM((parts, width, depth), BF),
        pltpu.SemaphoreType.DMA((len(hbm),)),
    ]
    return run(body, [grad2, normed1, inv1, shared, *d_near, d_far], hbm, outs, [], scratch, "ffn_back")


def ffn_rows(x, ctx, wo, wi, wd, small, shared, first, count, before):
    parts = len(wo)
    depth = x.shape[1]
    units, width = wi[0][0][0].shape[1], ctx[0].shape[1]
    tile = min(256, count)
    start = first // tile
    hbm = arrays(wo) + arrays(wi) + arrays(wd)
    last_inputs = [] if before is None else [before]

    def body(*refs):
        it = iter(refs)
        x_ref = next(it)
        ctx_refs = [next(it) for _ in range(parts)]
        small_refs = [next(it) for _ in range(parts)]
        shared_ref = next(it)
        wo_refs, wi_refs, wd_refs = take(it, wo), take(it, wi), take(it, wd)
        for _ in last_inputs:
            next(it)
        out_ref, wo_v, wi_v, wd_v, sems = (next(it) for _ in range(5))
        out_copies = flat(stacked_copies(wo_refs, wo_v, sems, 0, 1))
        near = len(flat(wo))
        in_copies = stacked_copies(wi_refs, wi_v, sems, near, 1)
        down_copies = stacked_copies(wd_refs, wd_v, sems, near + len(flat(wi)), 1)
        opening = pl.program_id(0) == 0

        @pl.when(opening)
        def _():
            start_all(out_copies)
            for part in range(parts):
                start_all(in_copies[part] + down_copies[part])
            wait_all(out_copies)

        attn_sum = x_ref[...].astype(F32) + shared_ref[0:1, :]
        for part in range(parts):
            attn_sum = attn_sum + nn(ctx_refs[part][...], wo_v[part])
        hidden, _, _ = norm_forward(attn_sum, shared_ref[2:3, :], shared_ref[4:5, :])
        low = hidden.astype(BF)
        total = hidden + shared_ref[1:2, :]
        for part in range(parts):

            @pl.when(opening)
            def _():
                wait_all(in_copies[part] + down_copies[part])

            pre = nn(low, wi_v[part]) + small_refs[part][0:1, :]
            act = (pre * erf_gelu(pre)).astype(BF)
            total = total + nn(act, wd_v[part])
        out_ref[...] = norm_forward(total, shared_ref[3:4, :], shared_ref[5:6, :])[0].astype(BF)

    return pl.pallas_call(
        body,
        grid=(count // tile,),
        in_specs=[
            pl.BlockSpec((tile, depth), lambda i: (i + start, 0)),
            *[pl.BlockSpec((tile, width), lambda i: (i + start, 0))] * parts,
            *[shaped(a.shape) for a in small],
            shaped(shared.shape),
            *[ANY_SPEC] * (len(hbm) + len(last_inputs)),
        ],
        out_specs=pl.BlockSpec((tile, depth), lambda i: (i + start, 0)),
        out_shape=jax.ShapeDtypeStruct(x.shape, BF),
        input_output_aliases={} if before is None else {2 + 2 * parts + len(hbm): 0},
        scratch_shapes=[
            pltpu.VMEM((parts, width, depth), BF),
            pltpu.VMEM((parts, depth, units), BF),
            pltpu.VMEM((parts, units, depth), BF),
            pltpu.SemaphoreType.DMA((len(hbm),)),
        ],
        cost_estimate=SMALL,
        name="ffn_rows",
    )(x, *ctx, *small, shared, *hbm, *last_inputs)


def input_gradient(picked, grad1, dq, dk, dv, wq, seqs):
    parts = len(dq)
    slots = picked.shape[1]
    depth = grad1.shape[1]
    rows, width = dk[0].shape[0] // seqs, dk[0].shape[1]
    hbm = arrays(wq)

    def body(*refs):
        it = iter(refs)
        pick_ref, grad1_ref = next(it), next(it)
        dq_refs = [next(it) for _ in range(parts)]
        dk_refs = [next(it) for _ in range(parts)]
        dv_refs = [next(it) for _ in range(parts)]
        wq_refs = take(it, wq)
        out_ref, wq_v, sems = next(it), next(it), next(it)
        copies = flat(stacked_copies(wq_refs, wq_v, sems, 0, 1))
        seq = pl.program_id(0)

        @pl.when(seq == 0)
        def _():
            start_all(copies)
            wait_all(copies)

        chosen = grad1_ref[...]
        for part in range(parts):
            chosen = chosen + nn(dq_refs[part][...], wq_v[part, 0:width, :])
        high = chosen.astype(BF)
        rest = (chosen - high.astype(F32)).astype(BF)
        spread = spread_of(pick_ref[pl.ds(lax.axis_index("tp") * seqs + seq, 1), :], rows)
        total = nn(spread, high) + nn(spread, rest)
        for part in range(parts):
            total = total + nn(dk_refs[part][...], wq_v[part, width : 2 * width, :])
            total = total + nn(dv_refs[part][...], wq_v[part, 2 * width : 3 * width, :])
        out_ref[...] = total.astype(BF)

    row_spec = pl.BlockSpec((rows, width), lambda s: (s, 0))
    return pl.pallas_call(
        body,
        grid=(seqs,),
        in_specs=[
            whole(picked.shape),
            pl.BlockSpec((slots, depth), lambda s: (s, 0)),
            *[pl.BlockSpec((slots, width), lambda s: (s, 0))] * parts,
            *[row_spec] * (2 * parts),
            *[ANY_SPEC] * len(hbm),
        ],
        out_specs=pl.BlockSpec((rows, depth), lambda s: (s, 0)),
        out_shape=jax.ShapeDtypeStruct((seqs * rows, depth), BF),
        scratch_shapes=[pltpu.VMEM((parts, 3 * width, depth), BF), pltpu.SemaphoreType.DMA((len(hbm),))],
        cost_estimate=SMALL,
        name="input_gradient",
    )(picked, grad1, *dq, *dk, *dv, *hbm)


def bits_of(count):
    return [1 << b for b in range(count.bit_length() - 1)]


def swap(value, axis, bit):
    count = lax.axis_size(axis)
    return lax.ppermute(value, axis, [(i, i ^ bit) for i in range(count)])


def half_of(value, bit, own):
    half = value.shape[0] // 2
    side = (lax.axis_index("dp") // bit) % 2
    return lax.dynamic_slice_in_dim(value, jnp.where(side == 0, 0, half) if own else jnp.where(side == 0, half, 0), half, 0)


def joined(own, got, bit):
    side = (lax.axis_index("dp") // bit) % 2
    return jnp.concatenate([jnp.where(side == 0, own, got), jnp.where(side == 0, got, own)], axis=0)


def add(*values):
    total = values[0].astype(F32)
    for value in values[1:]:
        total = total + value.astype(F32)
    return total.astype(BF)


def scatter(value, bit, *after):
    sent, kept = half_of(value, bit, False), half_of(value, bit, True)
    return add(tie(kept, *after), swap(sent, "dp", bit))


def gather(value, bit):
    return joined(value, swap(value, "dp", bit), bit)


def on_device(
    tokens, w_qkv, qv_bias, w_out, out_bias, w_in, in_bias, w_down, down_bias, norm_gain, norm_shift, valid_len, picked, d_out
):
    parts = lax.axis_size("tp")
    rank = lax.axis_index("tp")
    seqs = valid_len.shape[0] // parts
    depth = tokens.shape[1]
    width = w_qkv.shape[2]
    core, far = 1, 2
    dp_bits = bits_of(lax.axis_size("dp"))

    shared = jnp.concatenate([out_bias[None], down_bias[None], norm_gain, norm_shift, jnp.zeros((2, depth), F32)], axis=0)
    small = [jnp.concatenate([in_bias[None], jnp.pad(qv_bias, ((0, 5), (0, depth - width)))], axis=0)]
    small += [swap(small[0], "tp", core)]
    wq = w_qkv.transpose(0, 2, 1).reshape(3 * width, depth)
    qo_far = swap(jnp.concatenate([half_of(wq, 1, True), half_of(w_out, 1, True)], axis=0), "tp", far)
    wq_near = swap(wq, "tp", core)
    ready = small[1]
    small_far = swap(jnp.concatenate(small, axis=0), "tp", far)
    small += [small_far[:8], small_far[8:]]

    def forward(j, x, pieces):
        return attend_forward(valid_len, x, pieces, width, small[j], picked, seqs)

    out0 = forward(0, tie(tokens, ready), [wq])
    cut = w_down.shape[0] // 2
    ff_far = swap(tie(jnp.concatenate([half_of(w_in, 1, True), half_of(w_down[:cut], 1, True)], axis=0), small_far, out0[0]), "tp", far)
    fd_far = swap(tie(half_of(w_down[cut:], 2, True), small_far, out0[0]), "tp", far)
    qo_far = tie(qo_far, out0[0])
    qo_rest, qo_far_core = swap(qo_far, "dp", 1), swap(qo_far, "tp", core)
    out1 = forward(1, tie(tokens, qo_far), [wq_near])
    qo_rest = tie(qo_rest, out1[0])
    qo_rest_core = swap(qo_rest, "tp", core)
    wo_near = swap(tie(w_out, qo_rest), "tp", core)
    wi_near, wd_near = swap(tie(w_in, ready), "tp", core), swap(tie(w_down, ready), "tp", core)
    out2 = forward(2, tie(tokens, qo_rest, qo_far_core, wi_near, wd_near), [qo_far, qo_rest])
    ff_far = tie(ff_far, out2[0])
    rows_in = w_in.shape[0] // 2
    ff_rest = swap(ff_far, "dp", 1)
    ff_far_core = swap(ff_far, "tp", core)
    out3 = forward(3, tie(tokens, ff_far), [qo_far_core, qo_rest_core])
    fd_far = tie(fd_far, out3[0])
    fd_rest, fd_far_core = swap(fd_far, "dp", 2), swap(fd_far, "tp", core)
    q_sel, k, v, ctx, ctx_sel = zip(out0, out1, out2, out3)
    rows_q = 3 * width // 2

    def pieces(own, near, far_pieces, core_pieces):
        return [[(own, 0)], [(near, 0)], far_pieces, core_pieces]

    wq = pieces(wq, wq_near, [(qo_far, 0), (qo_rest, 0)], [(qo_far_core, 0), (qo_rest_core, 0)])
    wo = pieces(w_out, wo_near, [(qo_far, rows_q), (qo_rest, rows_q)], [(qo_far_core, rows_q), (qo_rest_core, rows_q)])
    near_in, near_down = [[(w_in, 0)], [(wi_near, 0)]], [[(w_down, 0)], [(wd_near, 0)]]
    prep = ffn_prep(picked, tie(tokens, fd_far), d_out, ctx_sel, wo, near_in, near_down, small[:2], shared, seqs)
    *act, slope_near, x_sel, cot, low, ffn_sum, normed1, inv1 = prep
    low_near, act_near = swap(low, "tp", core), swap(act[1], "tp", core)
    ff_rest, fd_rest = tie((ff_rest, fd_rest), low)
    ff_rest_core, fd_rest_core = swap(ff_rest, "tp", core), swap(fd_rest, "tp", core)
    wi = near_in + [[(ff_far, 0), (ff_rest, 0)], [(ff_far_core, 0), (ff_rest_core, 0)]]
    wd = near_down + [
        [(ff_far, rows_in), (ff_rest, rows_in), (fd_far, 0), (fd_rest, 0)],
        [(ff_far_core, rows_in), (ff_rest_core, rows_in), (fd_far_core, 0), (fd_rest_core, 0)],
    ]

    sent, g2, slope_far, grad2, vec = ffn_front(low, ffn_sum, cot, wi[2:], wd[2:], small[2:], shared)
    act_got = swap(sent, "tp", far)
    g2_near = swap(g2, "tp", core)
    *d_near, d_far, vec_mid = ffn_mid(g2, low, [slope_near, slope_far], wd)
    d_got, d_got_near = swap(d_far, "tp", far), swap(d_near[1], "tp", core)
    g1, grad1, vec_back, *d_ctx = ffn_back(tie(grad2, act_near, low_near, g2_near), d_near, d_far, normed1, inv1, shared, wi, wo, width)
    count = low.shape[0]

    def backward(j, x):
        return attend_backward(j, valid_len, q_sel[j], k[j], v[j], d_ctx[j], x, x_sel, ctx_sel[j], g1, seqs)

    def rows_of(first, count, before, *after):
        return ffn_rows(tie(tokens, *after), ctx, wo, wi, wd, small, shared, first, count, before)

    def finish(value, bits):
        for bit in bits:
            value = scatter(value, bit) if bit != last else add(value, swap(value, "dp", bit))
        return value

    def spread_out(value, bits):
        for bit in reversed(bits):
            value = gather(value, bit)
        return value

    half_rows, last = tokens.shape[0] // 2, dp_bits[-1]
    out3 = backward(3, tie(tokens, d_got_near))
    out2 = backward(2, tie(tokens, out3[0]))
    act_got = tie(act_got, out2[0])
    act_diag = swap(act_got[count:], "tp", core)
    out1 = backward(1, tie(tokens, out2[0], act_got))
    total_a = pair_sums(
        [
            ((tie(act[0], out1[0]), 0), (g2, 0)),
            ((act_near, 0), (g2_near, 0)),
            ((act_got, 0), (act_got, 2)),
            ((act_diag, 0), (act_diag, 1)),
        ]
    )
    sent_a = half_of(total_a, dp_bits[0], False)
    out0 = backward(0, tie(tokens, out1[0], sent_a))
    dq, dk, dv, sums, g_heads = zip(out0, out1, out2, out3)
    d_got = tie(d_got, out0[0])
    d_diag = swap(d_got[count:], "tp", core)
    far_c = add(tie(out2[4], out0[0]), swap(tie(out3[4], out1[0]), "tp", core))
    near_c = g_heads[0], swap(tie(g_heads[1], out0[0]), "tp", core)
    line = jnp.concatenate([vec + vec_mid + vec_back, sums[0] + sums[1] + sums[2] + sums[3]], axis=0)
    total_a = add(tie(half_of(total_a, dp_bits[0], True), far_c), swap(sent_a, "dp", dp_bits[0]))
    sent_a = half_of(total_a, dp_bits[1], False)
    out_first = rows_of(0, half_rows, None, line, far_c, d_got, sent_a)
    total_a = add(tie(half_of(total_a, dp_bits[1], True), out_first), swap(sent_a, "dp", dp_bits[1]))
    for bit in dp_bits[2:-1]:
        total_a = scatter(total_a, bit)
    total_b = pair_sums(
        [
            ((tie(low, out_first), 0), (d_near[0], 0)),
            ((low_near, 0), (d_got_near, 0)),
            ((d_got, 2), (d_got, 0)),
            ((d_diag, 1), (d_diag, 0)),
        ]
    )
    sent_b = half_of(total_b, dp_bits[0], False)
    d_tokens = input_gradient(tie(picked, total_a, sent_b), grad1, dq, dk, dv, wq, seqs)
    total_a = add(tie(total_a, d_tokens), swap(total_a, "dp", last))
    total_b = add(tie(half_of(total_b, dp_bits[0], True), d_tokens), swap(sent_b, "dp", dp_bits[0]))
    total_c = add(*tie(near_c, d_tokens), swap(far_c, "tp", far))
    cut = far_c.shape[0] // 2
    other = [dp_bits[1], dp_bits[0], *dp_bits[2:]]
    total_c, rest_c = total_c[:cut], total_c[cut:]
    sent_b = half_of(total_b, dp_bits[1], False)
    sent_c, sent_d = half_of(total_c, dp_bits[0], False), half_of(rest_c, other[0], False)
    line = tie(line, d_tokens)
    out_second = rows_of(half_rows, half_rows // 2, out_first, total_a, sent_b, sent_c, sent_d, line)
    for bit in reversed(dp_bits[2:-1]):
        total_a = gather(total_a, bit)
    total_a = joined(tie(total_a, out_second), swap(total_a, "dp", dp_bits[1]), dp_bits[1])
    total_b = add(tie(half_of(total_b, dp_bits[1], True), out_second), swap(sent_b, "dp", dp_bits[1]))
    for bit in dp_bits[2:-1]:
        total_b = scatter(total_b, bit)
    total_c = add(tie(half_of(total_c, dp_bits[0], True), out_second), swap(sent_c, "dp", dp_bits[0]))
    rest_c = add(tie(half_of(rest_c, other[0], True), out_second), swap(sent_d, "dp", other[0]))
    line = tie(line, out_second) + swap(line, "tp", core)
    sent_c, sent_d = half_of(total_c, dp_bits[1], False), half_of(rest_c, other[1], False)
    out_third = rows_of(half_rows + half_rows // 2, half_rows // 2, out_second, total_a, total_b, sent_c, sent_d, line)
    total_a = joined(tie(total_a, out_third), swap(total_a, "dp", dp_bits[0]), dp_bits[0])
    total_b = add(tie(total_b, out_third), swap(total_b, "dp", last))
    total_c = add(tie(half_of(total_c, dp_bits[1], True), out_third), swap(sent_c, "dp", dp_bits[1]))
    rest_c = add(tie(half_of(rest_c, other[1], True), out_third), swap(sent_d, "dp", other[1]))
    line = tie(line, total_c, rest_c) + swap(line, "dp", dp_bits[0])
    for bit in dp_bits[1:2]:
        line = line + swap(line, "dp", bit)
    total_c, rest_c = finish(total_c, dp_bits[2:]), finish(rest_c, other[2:])
    line = tie(line, total_c)
    for bit in dp_bits[2:]:
        line = line + swap(line, "dp", bit)
    total_b = spread_out(total_b, dp_bits[1:-1])
    total_c, rest_c = spread_out(total_c, dp_bits[1:-1]), spread_out(rest_c, other[1:-1])
    line = tie(line, total_c)
    line = line + swap(line, "tp", far)
    total_b = gather(total_b, dp_bits[0])
    total_c, rest_c = gather(total_c, dp_bits[0]), gather(rest_c, other[0])
    total_c = jnp.concatenate([total_c.astype(F32), rest_c.astype(F32)], axis=0)
    own = lax.dynamic_slice_in_dim(line, 8 + rank, 1, 0)[0]
    own_q = lax.dynamic_slice(line, (16 + rank, 0), (1, width))
    own_v = lax.dynamic_slice(line, (16 + PARTS + rank, 0), (1, width))
    return (
        out_third,
        d_tokens,
        total_c[: 3 * width].reshape(3, width, depth).transpose(0, 2, 1),
        jnp.concatenate([own_q, own_v], axis=0),
        total_c[3 * width :],
        line[3],
        total_b.astype(F32),
        own,
        total_a.astype(F32),
        line[0],
        jnp.stack([line[4], line[1]]),
        jnp.stack([line[5], line[2]]),
    )


def solution(mesh):
    placed = (
        P(("dp", "tp"), None),
        P(None, None, "tp"),
        P(None, "tp"),
        P("tp", None),
        P(),
        P(None, "tp"),
        P("tp"),
        P("tp", None),
        P(),
        P(),
        P(),
        P("dp"),
        P("dp", None),
        P(("dp", "tp"), None),
    )
    return jax.shard_map(
        on_device,
        mesh=mesh,
        in_specs=placed,
        out_specs=(
            P(("dp", "tp"), None),
            P(("dp", "tp"), None),
            P(None, None, "tp"),
            P(None, "tp"),
            P("tp", None),
            P(),
            P(None, "tp"),
            P("tp"),
            P("tp", None),
            P(),
            P(),
            P(),
        ),
        check_vma=False,
    )
```

```python
import jax
import jax.numpy as jnp
from jax import lax
from jax.experimental import pallas as pl
from jax.experimental.pallas import tpu as pltpu
from jax.sharding import PartitionSpec as P

HD = 64
SCALE = HD ** (-0.5)
NORM_EPS = 1e-06
MASKED = -1e30
HALF_ROOT = 0.5 ** 0.5
DENSITY = 0.3989422804014327
PARTS = 4
BF = jnp.bfloat16
F32 = jnp.float32


def nn(left, right):
    return lax.dot_general(left, right, (((1,), (0,)), ((), ())), preferred_element_type=F32)


def nt(left, right):
    return lax.dot_general(left, right, (((1,), (1,)), ((), ())), preferred_element_type=F32)


def tn(left, right):
    return lax.dot_general(left, right, (((0,), (0,)), ((), ())), preferred_element_type=F32)


def head_masks(width, dtype=BF):
    lane = lax.broadcasted_iota(jnp.int32, (1, width), 1) // HD
    return [(lane == head).astype(dtype) for head in range(width // HD)]


def spread_of(picks, length):
    slots = picks.shape[1]
    return (lax.broadcasted_iota(jnp.int32, (length, slots), 0) == picks).astype(F32).astype(BF)


def whole(shape):
    zeros = (0,) * len(shape)
    return pl.BlockSpec(shape, lambda *_: zeros)


def norm_forward(values, gain, shift):
    average = jnp.mean(values, axis=1, keepdims=True)
    centered = values - average
    inv_std = lax.rsqrt(jnp.mean(centered * centered, axis=1, keepdims=True) + NORM_EPS)
    normed = centered * inv_std
    return normed * gain + shift, normed, inv_std


def norm_backward(grad, normed, inv_std, gain):
    scaled = grad * gain
    first = jnp.mean(scaled, axis=1, keepdims=True)
    second = jnp.mean(scaled * normed, axis=1, keepdims=True)
    return inv_std * (scaled - first - normed * second)


def tie(value, *others):
    return lax.optimization_barrier((value, others))[0]


SMALL = pl.CostEstimate(flops=1024, transcendentals=0, bytes_accessed=1024)


def col_sum(values):
    return jnp.sum(values, axis=0, keepdims=True)


def piece_copies(pieces, target, sems, first, bit, each=1):
    rows = target.shape[0]
    if len(pieces) == 1:
        return [pltpu.make_async_copy(pieces[0][0], target, sems.at[first])]
    half, step = rows // 2, rows // len(pieces)
    if len(pieces) == 4:
        upper = piece_copies(pieces[:2], target.at[pl.ds(0, half), :], sems, first, bit, each)
        return upper + piece_copies(pieces[2:], target.at[pl.ds(half, half), :], sems, first + 2 * each, 2 * bit, each)
    own = ((lax.axis_index("dp") // bit) % 2) * half
    copies = []
    for n, (ref, skip) in enumerate(pieces):
        base = own if n * step < half else half - own
        start = pl.multiple_of(base + (n * step) % half, step)
        copies.append(pltpu.make_async_copy(ref.at[pl.ds(skip, step), :], target.at[pl.ds(start, step), :], sems.at[first + n * each]))
    return copies


def stacked_copies(pieces, target, sems, first, bit):
    copies = []
    for part, refs in enumerate(pieces):
        copies.append(piece_copies(refs, target.at[part], sems, first, bit))
        first += len(refs)
    return copies


def part_copies(pieces, target, sems):
    return flat([piece_copies(refs, target.at[part], sems, part, 1, 0) for part, refs in enumerate(pieces)])


def wait_part(target, sems, part):
    pltpu.make_async_copy(target.at[part], target.at[part], sems.at[part]).wait()


def take(it, pieces):
    return [[(next(it), skip) for _, skip in piece] for piece in pieces]


def flat(pieces):
    return [p for piece in pieces for p in piece]


def arrays(pieces):
    return [array for array, _ in flat(pieces)]


def start_all(copies):
    for copy in copies:
        copy.start()


def wait_all(copies):
    for copy in copies:
        copy.wait()


ANY_SPEC = pl.BlockSpec(memory_space=pl.ANY)


def shaped(shape):
    return pl.BlockSpec(shape, lambda *_: (0,) * len(shape))


def attend_body(len_ref, x_ref, small_ref, pick_ref, *rest, count):
    w_refs = [(ref, 0) for ref in rest[:count]]
    q_sel_ref, k_ref, v_ref, ctx_ref, ctx_sel_ref, ext_ref, scaled_ref, w_ref, sems = rest[count:]
    rows, width = k_ref.shape
    seq = pl.program_id(0)
    row = lax.axis_index("tp") * pl.num_programs(0) + seq
    length = len_ref[row]
    copies = piece_copies(w_refs, w_ref, sems, 0, 1)

    @pl.when(seq == 0)
    def _():
        start_all(copies)
        wait_all(copies)

    x = x_ref[...]
    queries = (nt(x, w_ref[0:width, :]) + small_ref[1:2, :width]).astype(BF)
    key_rows = nt(x, w_ref[width : 2 * width, :]).astype(BF)
    values = (nt(x, w_ref[2 * width : 3 * width, :]) + small_ref[2:3, :width]).astype(BF)
    k_ref[...] = key_rows
    v_ref[...] = values
    ext_ref[:, :width] = values
    ext_ref[:, width:] = jnp.ones((rows, ext_ref.shape[1] - width), BF)
    spread = spread_of(pick_ref[pl.ds(row, 1), :], rows)
    q_sel_ref[...] = tn(spread, queries).astype(BF)
    scaled_ref[...] = queries * jnp.asarray(SCALE, BF)
    masks = head_masks(width)
    tile = min(256, rows)
    keep = lax.broadcasted_iota(jnp.int32, (tile, rows), 1) < length

    def one_tile(n, carry):
        at = pl.ds(pl.multiple_of(n * tile, tile), tile)
        scaled = scaled_ref[at, :]
        total = jnp.zeros((tile, width), F32)
        for mask in masks:
            logits = nt(scaled * mask, k_ref[...])
            logits = jnp.where(keep, logits, MASKED)
            peak = jnp.max(logits, axis=1, keepdims=True)
            probs = jnp.exp(logits - peak).astype(BF)
            mixed = nn(probs, ext_ref[...])
            share = mixed[:, :width] / mixed[:, width : width + 1]
            total = jnp.where(mask.astype(F32) > 0.5, share, total)
        ctx_ref[at, :] = total.astype(BF)
        return carry

    lax.fori_loop(0, rows // tile, one_tile, 0)
    ctx_sel_ref[...] = tn(spread, ctx_ref[...]).astype(BF)


def attend_forward(lengths, x, pieces, width, small, picked, seqs):
    slots = picked.shape[1]
    rows = x.shape[0] // seqs
    depth = x.shape[1]
    ext = -(-(width + 1) // 128) * 128
    row_spec = pl.BlockSpec((rows, width), lambda s, _: (s, 0))
    sel_spec = pl.BlockSpec((slots, width), lambda s, _: (s, 0))
    return pl.pallas_call(
        lambda *refs: attend_body(*refs, count=len(pieces)),
        grid_spec=pltpu.PrefetchScalarGridSpec(
            num_scalar_prefetch=1,
            grid=(seqs,),
            in_specs=[
                pl.BlockSpec((rows, depth), lambda s, _: (s, 0)),
                whole(small.shape),
                whole(picked.shape),
                *[ANY_SPEC] * len(pieces),
            ],
            out_specs=[sel_spec, row_spec, row_spec, row_spec, sel_spec],
            scratch_shapes=[
                pltpu.VMEM((rows, ext), BF),
                pltpu.VMEM((rows, width), BF),
                pltpu.VMEM((3 * width, depth), BF),
                pltpu.SemaphoreType.DMA((len(pieces),)),
            ],
        ),
        out_shape=[
            jax.ShapeDtypeStruct((seqs * slots, width), BF),
            jax.ShapeDtypeStruct((seqs * rows, width), BF),
            jax.ShapeDtypeStruct((seqs * rows, width), BF),
            jax.ShapeDtypeStruct((seqs * rows, width), BF),
            jax.ShapeDtypeStruct((seqs * slots, width), BF),
        ],
        cost_estimate=SMALL,
        name="attend_forward",
    )(lengths, x, small, picked, *pieces)


def attend_back_body(
    len_ref, q_ref, k_ref, v_ref, d_ctx_ref, x_ref, x_sel_ref, ctx_sel_ref, g1_ref, dq_ref, dk_ref, dv_ref, sums_ref, grad_ref, acc_ref, *, part
):
    rows, width = k_ref.shape
    slots = q_ref.shape[0]
    seq = pl.program_id(0)
    rank = lax.axis_index("tp")
    length = len_ref[rank * pl.num_programs(0) + seq]
    masks = head_masks(width)
    queries, d_ctx = q_ref[...], d_ctx_ref[...]
    key_rows, values = k_ref[...], v_ref[...]
    q_stack = jnp.concatenate([queries * mask for mask in masks], axis=0)
    d_stack = jnp.concatenate([d_ctx * mask for mask in masks], axis=0)
    logits = nt(key_rows, q_stack * jnp.asarray(SCALE, BF))
    keep = lax.broadcasted_iota(jnp.int32, logits.shape, 0) < length
    logits = jnp.where(keep, logits, MASKED)
    grown = jnp.exp(logits - jnp.max(logits, axis=0, keepdims=True))
    probs = grown * (1.0 / jnp.sum(grown, axis=0, keepdims=True))
    d_probs = nt(values, d_stack)
    inner = jnp.sum(probs * d_probs, axis=0, keepdims=True)
    d_raw = (probs * (d_probs - inner) * SCALE).astype(BF)
    d_keys = nn(d_raw, q_stack).astype(BF)
    dk_ref[...] = d_keys
    d_values = nn(probs.astype(BF), d_stack).astype(BF)
    dv_ref[...] = d_values
    dq_stack = tn(d_raw, key_rows)
    dq = jnp.zeros((slots, width), F32)
    for head, mask in enumerate(masks):
        dq = jnp.where(mask.astype(F32) > 0.5, dq_stack[head * slots : (head + 1) * slots], dq)
    dq = dq.astype(BF)
    dq_ref[...] = dq

    @pl.when(seq == 0)
    def _():
        acc_ref[...] = jnp.zeros(acc_ref.shape, F32)
        sums_ref[...] = jnp.zeros(sums_ref.shape, F32)

    at = rank ^ part
    sums_ref[pl.ds(at, 1), 0:width] += col_sum(dq.astype(F32))
    sums_ref[pl.ds(PARTS + at, 1), 0:width] += col_sum(d_values.astype(F32))
    acc_ref[0:width, :] += tn(dq, x_sel_ref[...])
    acc_ref[width : 2 * width, :] += tn(d_keys, x_ref[...])
    acc_ref[2 * width : 3 * width, :] += tn(d_values, x_ref[...])
    acc_ref[3 * width : 4 * width, :] += tn(ctx_sel_ref[...], g1_ref[...])

    @pl.when(seq == pl.num_programs(0) - 1)
    def _():
        grad_ref[...] = acc_ref[...].astype(BF)


def attend_backward(part, lengths, q_sel, k, v, d_ctx, x, x_sel, ctx_sel, g1, seqs):
    rows, slots, width = k.shape[0] // seqs, q_sel.shape[0] // seqs, k.shape[1]
    depth = x.shape[1]
    row_spec = pl.BlockSpec((rows, width), lambda s, _: (s, 0))
    sel_spec = pl.BlockSpec((slots, width), lambda s, _: (s, 0))
    wide_spec = pl.BlockSpec((slots, depth), lambda s, _: (s, 0))
    return pl.pallas_call(
        lambda *refs: attend_back_body(*refs, part=part),
        grid_spec=pltpu.PrefetchScalarGridSpec(
            num_scalar_prefetch=1,
            grid=(seqs,),
            in_specs=[
                sel_spec,
                row_spec,
                row_spec,
                sel_spec,
                pl.BlockSpec((rows, depth), lambda s, _: (s, 0)),
                wide_spec,
                sel_spec,
                wide_spec,
            ],
            out_specs=[sel_spec, row_spec, row_spec, whole((2 * PARTS, depth)), whole((4 * width, depth))],
            scratch_shapes=[pltpu.VMEM((4 * width, depth), F32)],
        ),
        out_shape=[
            jax.ShapeDtypeStruct(q_sel.shape, BF),
            jax.ShapeDtypeStruct(k.shape, BF),
            jax.ShapeDtypeStruct(k.shape, BF),
            jax.ShapeDtypeStruct((2 * PARTS, depth), F32),
            jax.ShapeDtypeStruct((4 * width, depth), BF),
        ],
        cost_estimate=SMALL,
        name="attend_backward",
    )(lengths, q_sel, k, v, d_ctx, x, x_sel, ctx_sel, g1)


def erf_gelu(values):
    return 0.5 * (1.0 + lax.erf(values * HALF_ROOT))


def run(body, plain, hbm, outs, hbm_outs, scratch, name):
    return pl.pallas_call(
        body,
        grid=(1,),
        in_specs=[*[shaped(a.shape) for a in plain], *[ANY_SPEC] * len(hbm)],
        out_specs=[*[shaped(a.shape) for a in outs], *[ANY_SPEC] * len(hbm_outs)],
        out_shape=[*outs, *hbm_outs],
        scratch_shapes=scratch,
        cost_estimate=SMALL,
        name=name,
    )(*plain, *hbm)


def struct(dtype, *shape):
    return jax.ShapeDtypeStruct(shape, dtype)


def unit_part(low, wi, bias, slope_ref, n):
    pre = nn(low, wi) + bias
    chance = erf_gelu(pre)
    slope_ref[n] = chance + pre * (DENSITY * jnp.exp(-0.5 * pre * pre))
    return (pre * chance).astype(BF)


def ffn_prep(picked, x, d_out, ctx_sel, wo, wi, wd, small, shared, seqs):
    parts, near = len(wo), len(wi)
    slots = picked.shape[1]
    count, depth, units, width = seqs * slots, x.shape[1], wi[0][0][0].shape[1], ctx_sel[0].shape[1]
    plain = [picked, x, d_out, shared, *ctx_sel, *small]
    hbm = arrays(wo) + arrays(wi) + arrays(wd)

    def body(*refs):
        it = iter(refs)
        pick_ref, x_ref, d_out_ref, shared_ref = (next(it) for _ in range(4))
        ctx_refs = [next(it) for _ in range(parts)]
        small_refs = [next(it) for _ in range(near)]
        wo_refs, wi_refs, wd_refs = take(it, wo), take(it, wi), take(it, wd)
        act_refs = [next(it) for _ in range(near)]
        slope_ref, x_sel_ref, cot_ref, low_ref, sum_ref, normed1_ref, inv1_ref = (next(it) for _ in range(7))
        wo_v, wi_v, wd_v, sems = (next(it) for _ in range(4))
        out_copies = stacked_copies(wo_refs, wo_v, sems, 0, 1)
        first = len(flat(wo))
        in_copies = stacked_copies(wi_refs, wi_v, sems, first, 1)
        down_copies = stacked_copies(wd_refs, wd_v, sems, first + len(flat(wi)), 1)
        start_all(flat(out_copies) + flat(in_copies) + flat(down_copies))
        rows = x_ref.shape[0] // seqs
        for seq in range(seqs):
            at = lax.axis_index("tp") * seqs + seq
            spread = spread_of(pick_ref[pl.ds(at, 1), :], rows)
            x_sel_ref[seq * slots : (seq + 1) * slots, :] = tn(spread, x_ref[seq * rows : (seq + 1) * rows, :]).astype(BF)
            cot_ref[seq * slots : (seq + 1) * slots, :] = tn(spread, d_out_ref[seq * rows : (seq + 1) * rows, :]).astype(BF)
        attn_sum = x_sel_ref[...].astype(F32) + shared_ref[0:1, :]
        wait_all(flat(out_copies))
        for part in range(parts):
            attn_sum = attn_sum + nn(ctx_refs[part][...], wo_v[part])
        hidden, normed1, inv1 = norm_forward(attn_sum, shared_ref[2:3, :], shared_ref[4:5, :])
        low = hidden.astype(BF)
        low_ref[...] = low
        normed1_ref[...] = normed1
        inv1_ref[...] = inv1
        total = hidden + shared_ref[1:2, :]
        wait_all(flat(in_copies) + flat(down_copies))
        for n in range(near):
            act = unit_part(low, wi_v[n], small_refs[n][0:1, :], slope_ref, n)
            act_refs[n][...] = act
            total = total + nn(act, wd_v[n])
        sum_ref[...] = total

    outs = [
        *[struct(BF, count, units)] * near,
        struct(F32, near, count, units),
        struct(BF, count, depth),
        struct(BF, count, depth),
        struct(BF, count, depth),
        struct(F32, count, depth),
        struct(F32, count, depth),
        struct(F32, count, 1),
    ]
    scratch = [
        pltpu.VMEM((parts, width, depth), BF),
        pltpu.VMEM((near, depth, units), BF),
        pltpu.VMEM((near, units, depth), BF),
        pltpu.SemaphoreType.DMA((len(hbm),)),
    ]
    return run(body, plain, hbm, outs, [], scratch, "ffn_prep")


def ffn_front(low, total, cot, wi, wd, small, shared):
    far = len(wi)
    count, depth = low.shape
    units = wi[0][0][0].shape[1]
    plain = [low, total, cot, shared, *small]
    hbm = arrays(wi) + arrays(wd)

    def body(*refs):
        it = iter(refs)
        low_ref, sum_ref, cot_ref, shared_ref = (next(it) for _ in range(4))
        small_refs = [next(it) for _ in range(far)]
        wi_refs, wd_refs = take(it, wi), take(it, wd)
        sent_ref, g2_ref, slope_ref, grad2_ref, vec_ref = (next(it) for _ in range(5))
        wi_v, wd_v, sems = (next(it) for _ in range(3))
        in_copies = stacked_copies(wi_refs, wi_v, sems, 0, 1)
        down_copies = stacked_copies(wd_refs, wd_v, sems, len(flat(wi)), 1)
        for n in range(far):
            start_all(in_copies[n] + down_copies[n])
        low = low_ref[...]
        total = sum_ref[...]
        for n in range(far):
            wait_all(in_copies[n])
            act = unit_part(low, wi_v[n], small_refs[n][0:1, :], slope_ref, n)
            sent_ref[n * count : (n + 1) * count, :] = act
            wait_all(down_copies[n])
            total = total + nn(act, wd_v[n])
        _, normed2, inv2 = norm_forward(total, shared_ref[3:4, :], shared_ref[5:6, :])
        cotangent = cot_ref[...].astype(F32)
        grad2 = norm_backward(cotangent, normed2, inv2, shared_ref[3:4, :])
        vec_ref[...] = jnp.zeros(vec_ref.shape, F32)
        vec_ref[0:1, :] = col_sum(grad2)
        vec_ref[1:2, :] = col_sum(cotangent * normed2)
        vec_ref[2:3, :] = col_sum(cotangent)
        grad2_ref[...] = grad2
        g2 = grad2.astype(BF)
        g2_ref[...] = g2
        sent_ref[far * count :, :] = g2

    outs = [
        struct(BF, (far + 1) * count, units),
        struct(BF, count, depth),
        struct(F32, far, count, units),
        struct(F32, count, depth),
        struct(F32, 16, depth),
    ]
    scratch = [
        pltpu.VMEM((far, depth, units), BF),
        pltpu.VMEM((far, units, depth), BF),
        pltpu.SemaphoreType.DMA((len(hbm),)),
    ]
    return run(body, plain, hbm, outs, [], scratch, "ffn_front")


def ffn_mid(g2, low, slopes, wd):
    parts = len(wd)
    near = slopes[0].shape[0]
    count, depth = g2.shape
    units = slopes[0].shape[2]
    hbm = [*slopes, *arrays(wd)]

    def body(*refs):
        it = iter(refs)
        g2_ref, low_ref = next(it), next(it)
        slope_hbm = [next(it) for _ in slopes]
        wd_refs = take(it, wd)
        d_refs = [next(it) for _ in range(near)]
        sent_ref, vec_ref = next(it), next(it)
        wd_v, slope_v, sems, slope_sems = (next(it) for _ in range(4))
        down_copies = stacked_copies(wd_refs, wd_v, sems, 0, 1)
        sources = [ref.at[n] for ref in slope_hbm for n in range(ref.shape[0])]
        slope_copies = [pltpu.make_async_copy(sources[part], slope_v.at[part], slope_sems.at[part]) for part in range(parts)]
        for part in range(parts):
            start_all(down_copies[part] + [slope_copies[part]])
        vec_ref[...] = jnp.zeros(vec_ref.shape, F32)
        g2 = g2_ref[...]
        for part in range(parts):
            wait_all(down_copies[part] + [slope_copies[part]])
            d_pre = (nt(g2, wd_v[part]) * slope_v[part]).astype(BF)
            if part < near:
                d_refs[part][...] = d_pre
            else:
                sent_ref[(part - near) * count : (part - near + 1) * count, :] = d_pre
            at = 8 + (lax.axis_index("tp") ^ part)
            vec_ref[pl.ds(at, 1), :] = col_sum(d_pre.astype(F32))
        sent_ref[(parts - near) * count :, :] = low_ref[...]

    outs = [*[struct(BF, count, units)] * near, struct(BF, (parts - near + 1) * count, units), struct(F32, 16, depth)]
    scratch = [
        pltpu.VMEM((parts, units, depth), BF),
        pltpu.VMEM((parts, count, units), F32),
        pltpu.SemaphoreType.DMA((len(arrays(wd)),)),
        pltpu.SemaphoreType.DMA((parts,)),
    ]
    return run(body, [g2, low], hbm, outs, [], scratch, "ffn_mid")


def pair_sums(pairs):
    count = min(array.shape[0] for array, _ in pairs[0])
    width, depth = pairs[0][0][0].shape[1], pairs[0][1][0].shape[1]
    tile = min(256, width)

    def body(*refs):
        total = tn(refs[0][...], refs[1][...])
        for n in range(1, len(pairs)):
            total = total + tn(refs[2 * n][...], refs[2 * n + 1][...])
        refs[-1][...] = total.astype(BF)

    def left(block):
        return pl.BlockSpec((count, tile), lambda i: (block, i))

    def right(block):
        return pl.BlockSpec((count, depth), lambda i: (block, 0))

    return pl.pallas_call(
        body,
        grid=(width // tile,),
        in_specs=[spec for (_, a), (_, b) in pairs for spec in (left(a), right(b))],
        out_specs=pl.BlockSpec((tile, depth), lambda i: (i, 0)),
        out_shape=jax.ShapeDtypeStruct((width, depth), BF),
        cost_estimate=SMALL,
        name="pair_sums",
    )(*[array for (a, _), (b, _) in pairs for array in (a, b)])


def ffn_back(grad2, d_near, d_far, normed1, inv1, shared, wi, wo, width):
    parts, near = len(wi), len(d_near)
    count, depth = grad2.shape
    units = d_far.shape[1]
    hbm = arrays(wi) + arrays(wo)

    def body(*refs):
        it = iter(refs)
        grad2_ref, normed1_ref, inv1_ref, shared_ref = (next(it) for _ in range(4))
        near_refs = [next(it) for _ in range(near)]
        far_ref = next(it)
        wi_refs, wo_refs = take(it, wi), take(it, wo)
        g1_ref, grad1_ref, vec_ref = next(it), next(it), next(it)
        d_ctx_refs = [next(it) for _ in range(parts)]
        wi_v, wo_v, sems = (next(it) for _ in range(3))
        in_copies = stacked_copies(wi_refs, wi_v, sems, 0, 1)
        out_copies = stacked_copies(wo_refs, wo_v, sems, len(flat(wi)), 1)
        start_all(flat(in_copies) + flat(out_copies))
        d_hidden = grad2_ref[...]
        for part in range(parts):
            wait_all(in_copies[part])
            d_pre = near_refs[part][...] if part < near else far_ref[(part - near) * count : (part - near + 1) * count, :]
            d_hidden = d_hidden + nt(d_pre, wi_v[part])
        normed1 = normed1_ref[...]
        grad1 = norm_backward(d_hidden, normed1, inv1_ref[...], shared_ref[2:3, :])
        vec_ref[...] = jnp.zeros(vec_ref.shape, F32)
        vec_ref[3:4, :] = col_sum(grad1)
        vec_ref[4:5, :] = col_sum(d_hidden * normed1)
        vec_ref[5:6, :] = col_sum(d_hidden)
        grad1_ref[...] = grad1
        g1 = grad1.astype(BF)
        g1_ref[...] = g1
        wait_all(flat(out_copies))
        for part in range(parts):
            d_ctx_refs[part][...] = nt(g1, wo_v[part]).astype(BF)

    outs = [struct(BF, count, depth), struct(F32, count, depth), struct(F32, 16, depth), *[struct(BF, count, width)] * parts]
    scratch = [
        pltpu.VMEM((parts, depth, units), BF),
        pltpu.VMEM((parts, width, depth), BF),
        pltpu.SemaphoreType.DMA((len(hbm),)),
    ]
    return run(body, [grad2, normed1, inv1, shared, *d_near, d_far], hbm, outs, [], scratch, "ffn_back")


def ffn_rows(x, ctx, wo, wi, wd, small, shared, first, count, before):
    parts = len(wo)
    depth = x.shape[1]
    units, width = wi[0][0][0].shape[1], ctx[0].shape[1]
    tile = min(256, count)
    start = first // tile
    hbm = arrays(wo) + arrays(wi) + arrays(wd)
    last_inputs = [] if before is None else [before]

    def body(*refs):
        it = iter(refs)
        x_ref = next(it)
        ctx_refs = [next(it) for _ in range(parts)]
        bias_ref, shared_ref = next(it), next(it)
        wo_refs, wi_refs, wd_refs = take(it, wo), take(it, wi), take(it, wd)
        for _ in last_inputs:
            next(it)
        out_ref, wo_v, wi_v, wd_v, low_ref, sum_ref, sems, in_sems, down_sems = (next(it) for _ in range(9))
        opening = pl.program_id(0) == 0

        @pl.when(opening)
        def _():
            out_copies = flat(stacked_copies(wo_refs, wo_v, sems, 0, 1))
            start_all(out_copies + part_copies(wi_refs, wi_v, in_sems) + part_copies(wd_refs, wd_v, down_sems))
            wait_all(out_copies)

        attn_sum = x_ref[...].astype(F32) + shared_ref[0:1, :]
        for part in range(parts):
            attn_sum = attn_sum + nn(ctx_refs[part][...], wo_v[part])
        hidden, _, _ = norm_forward(attn_sum, shared_ref[2:3, :], shared_ref[4:5, :])
        low_ref[...] = hidden.astype(BF)
        sum_ref[...] = hidden + shared_ref[1:2, :]

        def one_part(part, carry):
            @pl.when(opening)
            def _():
                wait_part(wi_v, in_sems, part)
                wait_part(wd_v, down_sems, part)

            pre = nn(low_ref[...], wi_v[part]) + bias_ref[pl.ds(part * 8, 1), :]
            act = (pre * erf_gelu(pre)).astype(BF)
            sum_ref[...] += nn(act, wd_v[part])
            return carry

        lax.fori_loop(0, parts, one_part, 0)
        out_ref[...] = norm_forward(sum_ref[...], shared_ref[3:4, :], shared_ref[5:6, :])[0].astype(BF)

    return pl.pallas_call(
        body,
        grid=(count // tile,),
        in_specs=[
            pl.BlockSpec((tile, depth), lambda i: (i + start, 0)),
            *[pl.BlockSpec((tile, width), lambda i: (i + start, 0))] * parts,
            shaped(small.shape),
            shaped(shared.shape),
            *[ANY_SPEC] * (len(hbm) + len(last_inputs)),
        ],
        out_specs=pl.BlockSpec((tile, depth), lambda i: (i + start, 0)),
        out_shape=jax.ShapeDtypeStruct(x.shape, BF),
        input_output_aliases={} if before is None else {3 + parts + len(hbm): 0},
        scratch_shapes=[
            pltpu.VMEM((parts, width, depth), BF),
            pltpu.VMEM((parts, depth, units), BF),
            pltpu.VMEM((parts, units, depth), BF),
            pltpu.VMEM((tile, depth), BF),
            pltpu.VMEM((tile, depth), F32),
            pltpu.SemaphoreType.DMA((len(arrays(wo)),)),
            pltpu.SemaphoreType.DMA((parts,)),
            pltpu.SemaphoreType.DMA((parts,)),
        ],
        cost_estimate=SMALL,
        name="ffn_rows",
    )(x, *ctx, small, shared, *hbm, *last_inputs)


def input_gradient(picked, grad1, dq, dk, dv, wq, seqs):
    parts = len(dq)
    slots = picked.shape[1]
    depth = grad1.shape[1]
    rows, width = dk[0].shape[0] // seqs, dk[0].shape[1]
    hbm = arrays(wq)

    def body(*refs):
        it = iter(refs)
        pick_ref, grad1_ref = next(it), next(it)
        dq_refs = [next(it) for _ in range(parts)]
        dk_refs = [next(it) for _ in range(parts)]
        dv_refs = [next(it) for _ in range(parts)]
        wq_refs = take(it, wq)
        out_ref, wq_v, sems = next(it), next(it), next(it)
        copies = flat(stacked_copies(wq_refs, wq_v, sems, 0, 1))
        seq = pl.program_id(0)

        @pl.when(seq == 0)
        def _():
            start_all(copies)
            wait_all(copies)

        chosen = grad1_ref[...]
        for part in range(parts):
            chosen = chosen + nn(dq_refs[part][...], wq_v[part, 0:width, :])
        high = chosen.astype(BF)
        rest = (chosen - high.astype(F32)).astype(BF)
        spread = spread_of(pick_ref[pl.ds(lax.axis_index("tp") * seqs + seq, 1), :], rows)
        total = nn(spread, high) + nn(spread, rest)
        for part in range(parts):
            total = total + nn(dk_refs[part][...], wq_v[part, width : 2 * width, :])
            total = total + nn(dv_refs[part][...], wq_v[part, 2 * width : 3 * width, :])
        out_ref[...] = total.astype(BF)

    row_spec = pl.BlockSpec((rows, width), lambda s: (s, 0))
    return pl.pallas_call(
        body,
        grid=(seqs,),
        in_specs=[
            whole(picked.shape),
            pl.BlockSpec((slots, depth), lambda s: (s, 0)),
            *[pl.BlockSpec((slots, width), lambda s: (s, 0))] * parts,
            *[row_spec] * (2 * parts),
            *[ANY_SPEC] * len(hbm),
        ],
        out_specs=pl.BlockSpec((rows, depth), lambda s: (s, 0)),
        out_shape=jax.ShapeDtypeStruct((seqs * rows, depth), BF),
        scratch_shapes=[pltpu.VMEM((parts, 3 * width, depth), BF), pltpu.SemaphoreType.DMA((len(hbm),))],
        cost_estimate=SMALL,
        name="input_gradient",
    )(picked, grad1, *dq, *dk, *dv, *hbm)


def bits_of(count):
    return [1 << b for b in range(count.bit_length() - 1)]


def swap(value, axis, bit):
    count = lax.axis_size(axis)
    return lax.ppermute(value, axis, [(i, i ^ bit) for i in range(count)])


def half_of(value, bit, own):
    half = value.shape[0] // 2
    side = (lax.axis_index("dp") // bit) % 2
    return lax.dynamic_slice_in_dim(value, jnp.where(side == 0, 0, half) if own else jnp.where(side == 0, half, 0), half, 0)


def joined(own, got, bit):
    side = (lax.axis_index("dp") // bit) % 2
    return jnp.concatenate([jnp.where(side == 0, own, got), jnp.where(side == 0, got, own)], axis=0)


def add(*values):
    total = values[0].astype(F32)
    for value in values[1:]:
        total = total + value.astype(F32)
    return total.astype(BF)


def scatter(value, bit, *after):
    sent, kept = half_of(value, bit, False), half_of(value, bit, True)
    return add(tie(kept, *after), swap(sent, "dp", bit))


def gather(value, bit):
    return joined(value, swap(value, "dp", bit), bit)


def on_device(
    tokens, w_qkv, qv_bias, w_out, out_bias, w_in, in_bias, w_down, down_bias, norm_gain, norm_shift, valid_len, picked, d_out
):
    parts = lax.axis_size("tp")
    rank = lax.axis_index("tp")
    seqs = valid_len.shape[0] // parts
    depth = tokens.shape[1]
    width = w_qkv.shape[2]
    core, far = 1, 2
    dp_bits = bits_of(lax.axis_size("dp"))

    shared = jnp.concatenate([out_bias[None], down_bias[None], norm_gain, norm_shift, jnp.zeros((2, depth), F32)], axis=0)
    small = [jnp.concatenate([in_bias[None], jnp.pad(qv_bias, ((0, 5), (0, depth - width)))], axis=0)]
    small += [swap(small[0], "tp", core)]
    wq = w_qkv.transpose(0, 2, 1).reshape(3 * width, depth)
    qo_far = swap(jnp.concatenate([half_of(wq, 1, True), half_of(w_out, 1, True)], axis=0), "tp", far)
    wq_near = swap(wq, "tp", core)
    ready = small[1]
    small_far = swap(jnp.concatenate(small, axis=0), "tp", far)
    small += [small_far[:8], small_far[8:]]

    def forward(j, x, pieces):
        return attend_forward(valid_len, x, pieces, width, small[j], picked, seqs)

    out0 = forward(0, tie(tokens, ready), [wq])
    cut = w_down.shape[0] // 2
    ff_far = swap(tie(jnp.concatenate([half_of(w_in, 1, True), half_of(w_down[:cut], 1, True)], axis=0), small_far, out0[0]), "tp", far)
    fd_far = swap(tie(half_of(w_down[cut:], 2, True), small_far, out0[0]), "tp", far)
    qo_far = tie(qo_far, out0[0])
    qo_rest, qo_far_core = swap(qo_far, "dp", 1), swap(qo_far, "tp", core)
    out1 = forward(1, tie(tokens, qo_far), [wq_near])
    qo_rest = tie(qo_rest, out1[0])
    qo_rest_core = swap(qo_rest, "tp", core)
    wo_near = swap(tie(w_out, qo_rest), "tp", core)
    wi_near, wd_near = swap(tie(w_in, ready), "tp", core), swap(tie(w_down, ready), "tp", core)
    out2 = forward(2, tie(tokens, qo_rest, qo_far_core, wi_near, wd_near), [qo_far, qo_rest])
    ff_far = tie(ff_far, out2[0])
    rows_in = w_in.shape[0] // 2
    ff_rest = swap(ff_far, "dp", 1)
    ff_far_core = swap(ff_far, "tp", core)
    out3 = forward(3, tie(tokens, ff_far), [qo_far_core, qo_rest_core])
    fd_far = tie(fd_far, out3[0])
    fd_rest, fd_far_core = swap(fd_far, "dp", 2), swap(fd_far, "tp", core)
    q_sel, k, v, ctx, ctx_sel = zip(out0, out1, out2, out3)
    rows_q = 3 * width // 2

    def pieces(own, near, far_pieces, core_pieces):
        return [[(own, 0)], [(near, 0)], far_pieces, core_pieces]

    wq = pieces(wq, wq_near, [(qo_far, 0), (qo_rest, 0)], [(qo_far_core, 0), (qo_rest_core, 0)])
    wo = pieces(w_out, wo_near, [(qo_far, rows_q), (qo_rest, rows_q)], [(qo_far_core, rows_q), (qo_rest_core, rows_q)])
    near_in, near_down = [[(w_in, 0)], [(wi_near, 0)]], [[(w_down, 0)], [(wd_near, 0)]]
    prep = ffn_prep(picked, tie(tokens, fd_far), d_out, ctx_sel, wo, near_in, near_down, small[:2], shared, seqs)
    *act, slope_near, x_sel, cot, low, ffn_sum, normed1, inv1 = prep
    low_near, act_near = swap(low, "tp", core), swap(act[1], "tp", core)
    ff_rest, fd_rest = tie((ff_rest, fd_rest), low)
    ff_rest_core, fd_rest_core = swap(ff_rest, "tp", core), swap(fd_rest, "tp", core)
    wi = near_in + [[(ff_far, 0), (ff_rest, 0)], [(ff_far_core, 0), (ff_rest_core, 0)]]
    wd = near_down + [
        [(ff_far, rows_in), (ff_rest, rows_in), (fd_far, 0), (fd_rest, 0)],
        [(ff_far_core, rows_in), (ff_rest_core, rows_in), (fd_far_core, 0), (fd_rest_core, 0)],
    ]

    sent, g2, slope_far, grad2, vec = ffn_front(low, ffn_sum, cot, wi[2:], wd[2:], small[2:], shared)
    act_got = swap(sent, "tp", far)
    g2_near = swap(g2, "tp", core)
    *d_near, d_far, vec_mid = ffn_mid(g2, low, [slope_near, slope_far], wd)
    d_got, d_got_near = swap(d_far, "tp", far), swap(d_near[1], "tp", core)
    g1, grad1, vec_back, *d_ctx = ffn_back(tie(grad2, act_near, low_near, g2_near), d_near, d_far, normed1, inv1, shared, wi, wo, width)
    count = low.shape[0]

    def backward(j, x):
        return attend_backward(j, valid_len, q_sel[j], k[j], v[j], d_ctx[j], x, x_sel, ctx_sel[j], g1, seqs)

    def rows_of(first, count, before, *after):
        return ffn_rows(tie(tokens, *after), ctx, wo, wi, wd, small_all, shared, first, count, before)

    def finish(value, bits):
        for bit in bits:
            value = scatter(value, bit) if bit != last else add(value, swap(value, "dp", bit))
        return value

    def spread_out(value, bits):
        for bit in reversed(bits):
            value = gather(value, bit)
        return value

    small_all = jnp.concatenate(small, axis=0)
    half_rows, last = tokens.shape[0] // 2, dp_bits[-1]
    out3 = backward(3, tie(tokens, d_got_near))
    out2 = backward(2, tie(tokens, out3[0]))
    act_got = tie(act_got, out2[0])
    act_diag = swap(act_got[count:], "tp", core)
    out1 = backward(1, tie(tokens, out2[0], act_got))
    total_a = pair_sums(
        [
            ((tie(act[0], out1[0]), 0), (g2, 0)),
            ((act_near, 0), (g2_near, 0)),
            ((act_got, 0), (act_got, 2)),
            ((act_diag, 0), (act_diag, 1)),
        ]
    )
    sent_a = half_of(total_a, dp_bits[0], False)
    out0 = backward(0, tie(tokens, out1[0], sent_a))
    dq, dk, dv, sums, g_heads = zip(out0, out1, out2, out3)
    d_got = tie(d_got, out0[0])
    d_diag = swap(d_got[count:], "tp", core)
    far_c = add(tie(out2[4], out1[0]), swap(tie(out3[4], out2[0]), "tp", core))
    near_c = g_heads[0], swap(tie(g_heads[1], out0[0]), "tp", core)
    line = jnp.concatenate([vec + vec_mid + vec_back, sums[0] + sums[1] + sums[2] + sums[3]], axis=0)
    total_a = add(tie(half_of(total_a, dp_bits[0], True), far_c), swap(sent_a, "dp", dp_bits[0]))
    sent_a = half_of(total_a, dp_bits[1], False)
    out_first = rows_of(0, half_rows, None, line, far_c, d_got, sent_a)
    total_a = add(tie(half_of(total_a, dp_bits[1], True), out_first), swap(sent_a, "dp", dp_bits[1]))
    for bit in dp_bits[2:-1]:
        total_a = scatter(total_a, bit)
    total_b = pair_sums(
        [
            ((tie(low, out_first), 0), (d_near[0], 0)),
            ((low_near, 0), (d_got_near, 0)),
            ((d_got, 2), (d_got, 0)),
            ((d_diag, 1), (d_diag, 0)),
        ]
    )
    sent_b = half_of(total_b, dp_bits[0], False)
    total_c = add(*tie(near_c, sent_b), swap(far_c, "tp", far))
    cut = far_c.shape[0] // 2
    other = [dp_bits[1], dp_bits[0], *dp_bits[2:]]
    total_c, rest_c = total_c[:cut], total_c[cut:]
    sent_c, sent_d = half_of(total_c, dp_bits[0], False), half_of(rest_c, other[0], False)
    d_tokens = input_gradient(tie(picked, total_a, sent_b, sent_c, sent_d), grad1, dq, dk, dv, wq, seqs)
    total_a = add(tie(total_a, d_tokens), swap(total_a, "dp", last))
    total_b = add(tie(half_of(total_b, dp_bits[0], True), d_tokens), swap(sent_b, "dp", dp_bits[0]))
    total_c = add(tie(half_of(total_c, dp_bits[0], True), d_tokens), swap(sent_c, "dp", dp_bits[0]))
    rest_c = add(tie(half_of(rest_c, other[0], True), d_tokens), swap(sent_d, "dp", other[0]))
    sent_b = half_of(total_b, dp_bits[1], False)
    sent_c, sent_d = half_of(total_c, dp_bits[1], False), half_of(rest_c, other[1], False)
    line = tie(line, d_tokens)
    out_second = rows_of(half_rows, half_rows // 2, out_first, total_a, sent_b, sent_c, sent_d, line)
    for bit in reversed(dp_bits[2:-1]):
        total_a = gather(total_a, bit)
    total_a = joined(tie(total_a, out_second), swap(total_a, "dp", dp_bits[1]), dp_bits[1])
    total_b = add(tie(half_of(total_b, dp_bits[1], True), out_second), swap(sent_b, "dp", dp_bits[1]))
    total_c = add(tie(half_of(total_c, dp_bits[1], True), out_second), swap(sent_c, "dp", dp_bits[1]))
    rest_c = add(tie(half_of(rest_c, other[1], True), out_second), swap(sent_d, "dp", other[1]))
    for bit in dp_bits[2:-1]:
        total_b, total_c, rest_c = scatter(total_b, bit), scatter(total_c, bit), scatter(rest_c, bit)
    line = tie(line, out_second) + swap(line, "tp", core)
    out_third = rows_of(half_rows + half_rows // 2, half_rows // 2, out_second, total_a, total_b, total_c, rest_c, line)
    total_a = joined(tie(total_a, out_third), swap(total_a, "dp", dp_bits[0]), dp_bits[0])
    total_b = add(tie(total_b, out_third), swap(total_b, "dp", last))
    total_c = add(tie(total_c, out_third), swap(total_c, "dp", last))
    rest_c = add(tie(rest_c, out_third), swap(rest_c, "dp", last))
    line = tie(line, total_c, rest_c) + swap(line, "dp", dp_bits[0])
    for bit in dp_bits[1:2]:
        line = line + swap(line, "dp", bit)
    for bit in dp_bits[2:]:
        line = line + swap(line, "dp", bit)
    total_b = spread_out(total_b, dp_bits[1:-1])
    total_c, rest_c = spread_out(total_c, dp_bits[1:-1]), spread_out(rest_c, other[1:-1])
    line = tie(line, total_c)
    line = line + swap(line, "tp", far)
    total_b = gather(total_b, dp_bits[0])
    total_c, rest_c = gather(total_c, dp_bits[0]), gather(rest_c, other[0])
    total_c = jnp.concatenate([total_c.astype(F32), rest_c.astype(F32)], axis=0)
    own = lax.dynamic_slice_in_dim(line, 8 + rank, 1, 0)[0]
    own_q = lax.dynamic_slice(line, (16 + rank, 0), (1, width))
    own_v = lax.dynamic_slice(line, (16 + PARTS + rank, 0), (1, width))
    return (
        out_third,
        d_tokens,
        total_c[: 3 * width].reshape(3, width, depth).transpose(0, 2, 1),
        jnp.concatenate([own_q, own_v], axis=0),
        total_c[3 * width :],
        line[3],
        total_b.astype(F32),
        own,
        total_a.astype(F32),
        line[0],
        jnp.stack([line[4], line[1]]),
        jnp.stack([line[5], line[2]]),
    )


def solution(mesh):
    placed = (
        P(("dp", "tp"), None),
        P(None, None, "tp"),
        P(None, "tp"),
        P("tp", None),
        P(),
        P(None, "tp"),
        P("tp"),
        P("tp", None),
        P(),
        P(),
        P(),
        P("dp"),
        P("dp", None),
        P(("dp", "tp"), None),
    )
    return jax.shard_map(
        on_device,
        mesh=mesh,
        in_specs=placed,
        out_specs=(
            P(("dp", "tp"), None),
            P(("dp", "tp"), None),
            P(None, None, "tp"),
            P(None, "tp"),
            P("tp", None),
            P(),
            P(None, "tp"),
            P("tp"),
            P("tp", None),
            P(),
            P(),
            P(),
        ),
        check_vma=False,
    )
```

```python
import jax
import jax.numpy as jnp
from jax import lax
from jax.experimental import pallas as pl
from jax.experimental.pallas import tpu as pltpu
from jax.sharding import PartitionSpec as P

HD = 64
SCALE = HD ** (-0.5)
NORM_EPS = 1e-06
MASKED = -1e30
HALF_ROOT = 0.5 ** 0.5
DENSITY = 0.3989422804014327
PARTS = 4
BF = jnp.bfloat16
F32 = jnp.float32


def nn(left, right):
    return lax.dot_general(left, right, (((1,), (0,)), ((), ())), preferred_element_type=F32)


def nt(left, right):
    return lax.dot_general(left, right, (((1,), (1,)), ((), ())), preferred_element_type=F32)


def tn(left, right):
    return lax.dot_general(left, right, (((0,), (0,)), ((), ())), preferred_element_type=F32)


def head_masks(width, dtype=BF):
    lane = lax.broadcasted_iota(jnp.int32, (1, width), 1) // HD
    return [(lane == head).astype(dtype) for head in range(width // HD)]


def spread_of(picks, length):
    slots = picks.shape[1]
    return (lax.broadcasted_iota(jnp.int32, (length, slots), 0) == picks).astype(F32).astype(BF)


def whole(shape):
    zeros = (0,) * len(shape)
    return pl.BlockSpec(shape, lambda *_: zeros)


def norm_forward(values, gain, shift):
    average = jnp.mean(values, axis=1, keepdims=True)
    centered = values - average
    inv_std = lax.rsqrt(jnp.mean(centered * centered, axis=1, keepdims=True) + NORM_EPS)
    normed = centered * inv_std
    return normed * gain + shift, normed, inv_std


def norm_backward(grad, normed, inv_std, gain):
    scaled = grad * gain
    first = jnp.mean(scaled, axis=1, keepdims=True)
    second = jnp.mean(scaled * normed, axis=1, keepdims=True)
    return inv_std * (scaled - first - normed * second)


def tie(value, *others):
    return lax.optimization_barrier((value, others))[0]


SMALL = pl.CostEstimate(flops=1024, transcendentals=0, bytes_accessed=1024)


def col_sum(values):
    return jnp.sum(values, axis=0, keepdims=True)


def piece_copies(pieces, target, sems, first, bit):
    rows = target.shape[0]
    if len(pieces) == 1:
        return [pltpu.make_async_copy(pieces[0][0], target, sems.at[first])]
    half, step = rows // 2, rows // len(pieces)
    if len(pieces) == 4:
        upper = piece_copies(pieces[:2], target.at[pl.ds(0, half), :], sems, first, bit)
        return upper + piece_copies(pieces[2:], target.at[pl.ds(half, half), :], sems, first + 2, 2 * bit)
    own = ((lax.axis_index("dp") // bit) % 2) * half
    copies = []
    for n, (ref, skip) in enumerate(pieces):
        base = own if n * step < half else half - own
        start = pl.multiple_of(base + (n * step) % half, step)
        copies.append(pltpu.make_async_copy(ref.at[pl.ds(skip, step), :], target.at[pl.ds(start, step), :], sems.at[first + n]))
    return copies


def stacked_copies(pieces, target, sems, first, bit):
    copies = []
    for part, refs in enumerate(pieces):
        copies.append(piece_copies(refs, target.at[part], sems, first, bit))
        first += len(refs)
    return copies


def take(it, pieces):
    return [[(next(it), skip) for _, skip in piece] for piece in pieces]


def flat(pieces):
    return [p for piece in pieces for p in piece]


def arrays(pieces):
    return [array for array, _ in flat(pieces)]


def start_all(copies):
    for copy in copies:
        copy.start()


def wait_all(copies):
    for copy in copies:
        copy.wait()


ANY_SPEC = pl.BlockSpec(memory_space=pl.ANY)


def shaped(shape):
    return pl.BlockSpec(shape, lambda *_: (0,) * len(shape))


def attend_body(len_ref, x_ref, small_ref, pick_ref, *rest, count):
    w_refs = [(ref, 0) for ref in rest[:count]]
    q_sel_ref, k_ref, v_ref, ctx_ref, ctx_sel_ref, ext_ref, w_ref, sems = rest[count:]
    rows, width = k_ref.shape
    seq = pl.program_id(0)
    row = lax.axis_index("tp") * pl.num_programs(0) + seq
    length = len_ref[row]
    copies = piece_copies(w_refs, w_ref, sems, 0, 1)

    @pl.when(seq == 0)
    def _():
        start_all(copies)
        wait_all(copies)

    x = x_ref[...]
    queries = (nt(x, w_ref[0:width, :]) + small_ref[1:2, :width]).astype(BF)
    key_rows = nt(x, w_ref[width : 2 * width, :]).astype(BF)
    values = (nt(x, w_ref[2 * width : 3 * width, :]) + small_ref[2:3, :width]).astype(BF)
    k_ref[...] = key_rows
    v_ref[...] = values
    ext_ref[:, :width] = values
    ext_ref[:, width:] = jnp.ones((rows, ext_ref.shape[1] - width), BF)
    spread = spread_of(pick_ref[pl.ds(row, 1), :], rows)
    q_sel_ref[...] = tn(spread, queries).astype(BF)
    scaled = queries * jnp.asarray(SCALE, BF)
    masks = head_masks(width)
    tile = min(256, rows)
    keep = lax.broadcasted_iota(jnp.int32, (tile, rows), 1) < length
    for start in range(0, rows, tile):
        total = jnp.zeros((tile, width), F32)
        for mask in masks:
            logits = nt(scaled[start : start + tile] * mask, key_rows)
            logits = jnp.where(keep, logits, MASKED)
            peak = jnp.max(logits, axis=1, keepdims=True)
            probs = jnp.exp(logits - peak).astype(BF)
            mixed = nn(probs, ext_ref[...])
            share = mixed[:, :width] / mixed[:, width : width + 1]
            total = jnp.where(mask.astype(F32) > 0.5, share, total)
        ctx_ref[start : start + tile, :] = total.astype(BF)
    ctx_sel_ref[...] = tn(spread, ctx_ref[...]).astype(BF)


def attend_forward(lengths, x, pieces, width, small, picked, seqs):
    slots = picked.shape[1]
    rows = x.shape[0] // seqs
    depth = x.shape[1]
    ext = -(-(width + 1) // 128) * 128
    row_spec = pl.BlockSpec((rows, width), lambda s, _: (s, 0))
    sel_spec = pl.BlockSpec((slots, width), lambda s, _: (s, 0))
    return pl.pallas_call(
        lambda *refs: attend_body(*refs, count=len(pieces)),
        grid_spec=pltpu.PrefetchScalarGridSpec(
            num_scalar_prefetch=1,
            grid=(seqs,),
            in_specs=[
                pl.BlockSpec((rows, depth), lambda s, _: (s, 0)),
                whole(small.shape),
                whole(picked.shape),
                *[ANY_SPEC] * len(pieces),
            ],
            out_specs=[sel_spec, row_spec, row_spec, row_spec, sel_spec],
            scratch_shapes=[
                pltpu.VMEM((rows, ext), BF),
                pltpu.VMEM((3 * width, depth), BF),
                pltpu.SemaphoreType.DMA((len(pieces),)),
            ],
        ),
        out_shape=[
            jax.ShapeDtypeStruct((seqs * slots, width), BF),
            jax.ShapeDtypeStruct((seqs * rows, width), BF),
            jax.ShapeDtypeStruct((seqs * rows, width), BF),
            jax.ShapeDtypeStruct((seqs * rows, width), BF),
            jax.ShapeDtypeStruct((seqs * slots, width), BF),
        ],
        cost_estimate=SMALL,
        name="attend_forward",
    )(lengths, x, small, picked, *pieces)


def attend_back_body(
    len_ref, q_ref, k_ref, v_ref, d_ctx_ref, x_ref, x_sel_ref, ctx_sel_ref, g1_ref, dq_ref, dk_ref, dv_ref, sums_ref, grad_ref, acc_ref, *, part
):
    rows, width = k_ref.shape
    slots = q_ref.shape[0]
    seq = pl.program_id(0)
    rank = lax.axis_index("tp")
    length = len_ref[rank * pl.num_programs(0) + seq]
    masks = head_masks(width)
    queries, d_ctx = q_ref[...], d_ctx_ref[...]
    key_rows, values = k_ref[...], v_ref[...]
    q_stack = jnp.concatenate([queries * mask for mask in masks], axis=0)
    d_stack = jnp.concatenate([d_ctx * mask for mask in masks], axis=0)
    logits = nt(key_rows, q_stack * jnp.asarray(SCALE, BF))
    keep = lax.broadcasted_iota(jnp.int32, logits.shape, 0) < length
    logits = jnp.where(keep, logits, MASKED)
    grown = jnp.exp(logits - jnp.max(logits, axis=0, keepdims=True))
    probs = grown * (1.0 / jnp.sum(grown, axis=0, keepdims=True))
    d_probs = nt(values, d_stack)
    inner = jnp.sum(probs * d_probs, axis=0, keepdims=True)
    d_raw = (probs * (d_probs - inner) * SCALE).astype(BF)
    d_keys = nn(d_raw, q_stack).astype(BF)
    dk_ref[...] = d_keys
    d_values = nn(probs.astype(BF), d_stack).astype(BF)
    dv_ref[...] = d_values
    dq_stack = tn(d_raw, key_rows)
    dq = jnp.zeros((slots, width), F32)
    for head, mask in enumerate(masks):
        dq = jnp.where(mask.astype(F32) > 0.5, dq_stack[head * slots : (head + 1) * slots], dq)
    dq = dq.astype(BF)
    dq_ref[...] = dq

    @pl.when(seq == 0)
    def _():
        acc_ref[...] = jnp.zeros(acc_ref.shape, F32)
        sums_ref[...] = jnp.zeros(sums_ref.shape, F32)

    at = rank ^ part
    sums_ref[pl.ds(at, 1), 0:width] += col_sum(dq.astype(F32))
    sums_ref[pl.ds(PARTS + at, 1), 0:width] += col_sum(d_values.astype(F32))
    acc_ref[0:width, :] += tn(dq, x_sel_ref[...])
    acc_ref[width : 2 * width, :] += tn(d_keys, x_ref[...])
    acc_ref[2 * width : 3 * width, :] += tn(d_values, x_ref[...])
    acc_ref[3 * width : 4 * width, :] += tn(ctx_sel_ref[...], g1_ref[...])

    @pl.when(seq == pl.num_programs(0) - 1)
    def _():
        grad_ref[...] = acc_ref[...].astype(BF)


def attend_backward(part, lengths, q_sel, k, v, d_ctx, x, x_sel, ctx_sel, g1, seqs):
    rows, slots, width = k.shape[0] // seqs, q_sel.shape[0] // seqs, k.shape[1]
    depth = x.shape[1]
    row_spec = pl.BlockSpec((rows, width), lambda s, _: (s, 0))
    sel_spec = pl.BlockSpec((slots, width), lambda s, _: (s, 0))
    wide_spec = pl.BlockSpec((slots, depth), lambda s, _: (s, 0))
    return pl.pallas_call(
        lambda *refs: attend_back_body(*refs, part=part),
        grid_spec=pltpu.PrefetchScalarGridSpec(
            num_scalar_prefetch=1,
            grid=(seqs,),
            in_specs=[
                sel_spec,
                row_spec,
                row_spec,
                sel_spec,
                pl.BlockSpec((rows, depth), lambda s, _: (s, 0)),
                wide_spec,
                sel_spec,
                wide_spec,
            ],
            out_specs=[sel_spec, row_spec, row_spec, whole((2 * PARTS, depth)), whole((4 * width, depth))],
            scratch_shapes=[pltpu.VMEM((4 * width, depth), F32)],
        ),
        out_shape=[
            jax.ShapeDtypeStruct(q_sel.shape, BF),
            jax.ShapeDtypeStruct(k.shape, BF),
            jax.ShapeDtypeStruct(k.shape, BF),
            jax.ShapeDtypeStruct((2 * PARTS, depth), F32),
            jax.ShapeDtypeStruct((4 * width, depth), BF),
        ],
        cost_estimate=SMALL,
        name="attend_backward",
    )(lengths, q_sel, k, v, d_ctx, x, x_sel, ctx_sel, g1)


def erf_gelu(values):
    return 0.5 * (1.0 + lax.erf(values * HALF_ROOT))


def run(body, plain, hbm, outs, hbm_outs, scratch, name):
    return pl.pallas_call(
        body,
        grid=(1,),
        in_specs=[*[shaped(a.shape) for a in plain], *[ANY_SPEC] * len(hbm)],
        out_specs=[*[shaped(a.shape) for a in outs], *[ANY_SPEC] * len(hbm_outs)],
        out_shape=[*outs, *hbm_outs],
        scratch_shapes=scratch,
        cost_estimate=SMALL,
        name=name,
    )(*plain, *hbm)


def struct(dtype, *shape):
    return jax.ShapeDtypeStruct(shape, dtype)


def unit_part(low, wi, bias, slope_ref, n):
    pre = nn(low, wi) + bias
    chance = erf_gelu(pre)
    slope_ref[n] = chance + pre * (DENSITY * jnp.exp(-0.5 * pre * pre))
    return (pre * chance).astype(BF)


def ffn_prep(picked, x, d_out, ctx_sel, wo, wi, wd, small, shared, seqs):
    parts, near = len(wo), len(wi)
    slots = picked.shape[1]
    count, depth, units, width = seqs * slots, x.shape[1], wi[0][0][0].shape[1], ctx_sel[0].shape[1]
    plain = [picked, x, d_out, shared, *ctx_sel, *small]
    hbm = arrays(wo) + arrays(wi) + arrays(wd)

    def body(*refs):
        it = iter(refs)
        pick_ref, x_ref, d_out_ref, shared_ref = (next(it) for _ in range(4))
        ctx_refs = [next(it) for _ in range(parts)]
        small_refs = [next(it) for _ in range(near)]
        wo_refs, wi_refs, wd_refs = take(it, wo), take(it, wi), take(it, wd)
        act_refs = [next(it) for _ in range(near)]
        slope_ref, x_sel_ref, cot_ref, low_ref, sum_ref, normed1_ref, inv1_ref = (next(it) for _ in range(7))
        wo_v, wi_v, wd_v, sems = (next(it) for _ in range(4))
        out_copies = stacked_copies(wo_refs, wo_v, sems, 0, 1)
        first = len(flat(wo))
        in_copies = stacked_copies(wi_refs, wi_v, sems, first, 1)
        down_copies = stacked_copies(wd_refs, wd_v, sems, first + len(flat(wi)), 1)
        start_all(flat(out_copies) + flat(in_copies) + flat(down_copies))
        rows = x_ref.shape[0] // seqs
        for seq in range(seqs):
            at = lax.axis_index("tp") * seqs + seq
            spread = spread_of(pick_ref[pl.ds(at, 1), :], rows)
            x_sel_ref[seq * slots : (seq + 1) * slots, :] = tn(spread, x_ref[seq * rows : (seq + 1) * rows, :]).astype(BF)
            cot_ref[seq * slots : (seq + 1) * slots, :] = tn(spread, d_out_ref[seq * rows : (seq + 1) * rows, :]).astype(BF)
        attn_sum = x_sel_ref[...].astype(F32) + shared_ref[0:1, :]
        wait_all(flat(out_copies))
        for part in range(parts):
            attn_sum = attn_sum + nn(ctx_refs[part][...], wo_v[part])
        hidden, normed1, inv1 = norm_forward(attn_sum, shared_ref[2:3, :], shared_ref[4:5, :])
        low = hidden.astype(BF)
        low_ref[...] = low
        normed1_ref[...] = normed1
        inv1_ref[...] = inv1
        total = hidden + shared_ref[1:2, :]
        wait_all(flat(in_copies) + flat(down_copies))
        for n in range(near):
            act = unit_part(low, wi_v[n], small_refs[n][0:1, :], slope_ref, n)
            act_refs[n][...] = act
            total = total + nn(act, wd_v[n])
        sum_ref[...] = total

    outs = [
        *[struct(BF, count, units)] * near,
        struct(F32, near, count, units),
        struct(BF, count, depth),
        struct(BF, count, depth),
        struct(BF, count, depth),
        struct(F32, count, depth),
        struct(F32, count, depth),
        struct(F32, count, 1),
    ]
    scratch = [
        pltpu.VMEM((parts, width, depth), BF),
        pltpu.VMEM((near, depth, units), BF),
        pltpu.VMEM((near, units, depth), BF),
        pltpu.SemaphoreType.DMA((len(hbm),)),
    ]
    return run(body, plain, hbm, outs, [], scratch, "ffn_prep")


def ffn_front(low, total, cot, wi, wd, small, shared):
    far = len(wi)
    count, depth = low.shape
    units = wi[0][0][0].shape[1]
    plain = [low, total, cot, shared, *small]
    hbm = arrays(wi) + arrays(wd)

    def body(*refs):
        it = iter(refs)
        low_ref, sum_ref, cot_ref, shared_ref = (next(it) for _ in range(4))
        small_refs = [next(it) for _ in range(far)]
        wi_refs, wd_refs = take(it, wi), take(it, wd)
        sent_ref, g2_ref, slope_ref, grad2_ref, vec_ref = (next(it) for _ in range(5))
        wi_v, wd_v, sems = (next(it) for _ in range(3))
        in_copies = stacked_copies(wi_refs, wi_v, sems, 0, 1)
        down_copies = stacked_copies(wd_refs, wd_v, sems, len(flat(wi)), 1)
        for n in range(far):
            start_all(in_copies[n] + down_copies[n])
        low = low_ref[...]
        total = sum_ref[...]
        for n in range(far):
            wait_all(in_copies[n])
            act = unit_part(low, wi_v[n], small_refs[n][0:1, :], slope_ref, n)
            sent_ref[n * count : (n + 1) * count, :] = act
            wait_all(down_copies[n])
            total = total + nn(act, wd_v[n])
        _, normed2, inv2 = norm_forward(total, shared_ref[3:4, :], shared_ref[5:6, :])
        cotangent = cot_ref[...].astype(F32)
        grad2 = norm_backward(cotangent, normed2, inv2, shared_ref[3:4, :])
        vec_ref[...] = jnp.zeros(vec_ref.shape, F32)
        vec_ref[0:1, :] = col_sum(grad2)
        vec_ref[1:2, :] = col_sum(cotangent * normed2)
        vec_ref[2:3, :] = col_sum(cotangent)
        grad2_ref[...] = grad2
        g2 = grad2.astype(BF)
        g2_ref[...] = g2
        sent_ref[far * count :, :] = g2

    outs = [
        struct(BF, (far + 1) * count, units),
        struct(BF, count, depth),
        struct(F32, far, count, units),
        struct(F32, count, depth),
        struct(F32, 16, depth),
    ]
    scratch = [
        pltpu.VMEM((far, depth, units), BF),
        pltpu.VMEM((far, units, depth), BF),
        pltpu.SemaphoreType.DMA((len(hbm),)),
    ]
    return run(body, plain, hbm, outs, [], scratch, "ffn_front")


def ffn_mid(g2, low, slopes, wd):
    parts = len(wd)
    near = slopes[0].shape[0]
    count, depth = g2.shape
    units = slopes[0].shape[2]
    hbm = [*slopes, *arrays(wd)]

    def body(*refs):
        it = iter(refs)
        g2_ref, low_ref = next(it), next(it)
        slope_hbm = [next(it) for _ in slopes]
        wd_refs = take(it, wd)
        d_refs = [next(it) for _ in range(near)]
        sent_ref, vec_ref = next(it), next(it)
        wd_v, slope_v, sems, slope_sems = (next(it) for _ in range(4))
        down_copies = stacked_copies(wd_refs, wd_v, sems, 0, 1)
        sources = [ref.at[n] for ref in slope_hbm for n in range(ref.shape[0])]
        slope_copies = [pltpu.make_async_copy(sources[part], slope_v.at[part], slope_sems.at[part]) for part in range(parts)]
        for part in range(parts):
            start_all(down_copies[part] + [slope_copies[part]])
        vec_ref[...] = jnp.zeros(vec_ref.shape, F32)
        g2 = g2_ref[...]
        for part in range(parts):
            wait_all(down_copies[part] + [slope_copies[part]])
            d_pre = (nt(g2, wd_v[part]) * slope_v[part]).astype(BF)
            if part < near:
                d_refs[part][...] = d_pre
            else:
                sent_ref[(part - near) * count : (part - near + 1) * count, :] = d_pre
            at = 8 + (lax.axis_index("tp") ^ part)
            vec_ref[pl.ds(at, 1), :] = col_sum(d_pre.astype(F32))
        sent_ref[(parts - near) * count :, :] = low_ref[...]

    outs = [*[struct(BF, count, units)] * near, struct(BF, (parts - near + 1) * count, units), struct(F32, 16, depth)]
    scratch = [
        pltpu.VMEM((parts, units, depth), BF),
        pltpu.VMEM((parts, count, units), F32),
        pltpu.SemaphoreType.DMA((len(arrays(wd)),)),
        pltpu.SemaphoreType.DMA((parts,)),
    ]
    return run(body, [g2, low], hbm, outs, [], scratch, "ffn_mid")


def pair_sums(pairs):
    count = min(array.shape[0] for array, _ in pairs[0])
    width, depth = pairs[0][0][0].shape[1], pairs[0][1][0].shape[1]
    tile = min(256, width)

    def body(*refs):
        total = tn(refs[0][...], refs[1][...])
        for n in range(1, len(pairs)):
            total = total + tn(refs[2 * n][...], refs[2 * n + 1][...])
        refs[-1][...] = total.astype(BF)

    def left(block):
        return pl.BlockSpec((count, tile), lambda i: (block, i))

    def right(block):
        return pl.BlockSpec((count, depth), lambda i: (block, 0))

    return pl.pallas_call(
        body,
        grid=(width // tile,),
        in_specs=[spec for (_, a), (_, b) in pairs for spec in (left(a), right(b))],
        out_specs=pl.BlockSpec((tile, depth), lambda i: (i, 0)),
        out_shape=jax.ShapeDtypeStruct((width, depth), BF),
        cost_estimate=SMALL,
        name="pair_sums",
    )(*[array for (a, _), (b, _) in pairs for array in (a, b)])


def ffn_back(grad2, d_near, d_far, normed1, inv1, shared, wi, wo, width):
    parts, near = len(wi), len(d_near)
    count, depth = grad2.shape
    units = d_far.shape[1]
    hbm = arrays(wi) + arrays(wo)

    def body(*refs):
        it = iter(refs)
        grad2_ref, normed1_ref, inv1_ref, shared_ref = (next(it) for _ in range(4))
        near_refs = [next(it) for _ in range(near)]
        far_ref = next(it)
        wi_refs, wo_refs = take(it, wi), take(it, wo)
        g1_ref, grad1_ref, vec_ref = next(it), next(it), next(it)
        d_ctx_refs = [next(it) for _ in range(parts)]
        wi_v, wo_v, sems = (next(it) for _ in range(3))
        in_copies = stacked_copies(wi_refs, wi_v, sems, 0, 1)
        out_copies = stacked_copies(wo_refs, wo_v, sems, len(flat(wi)), 1)
        start_all(flat(in_copies) + flat(out_copies))
        d_hidden = grad2_ref[...]
        for part in range(parts):
            wait_all(in_copies[part])
            d_pre = near_refs[part][...] if part < near else far_ref[(part - near) * count : (part - near + 1) * count, :]
            d_hidden = d_hidden + nt(d_pre, wi_v[part])
        normed1 = normed1_ref[...]
        grad1 = norm_backward(d_hidden, normed1, inv1_ref[...], shared_ref[2:3, :])
        vec_ref[...] = jnp.zeros(vec_ref.shape, F32)
        vec_ref[3:4, :] = col_sum(grad1)
        vec_ref[4:5, :] = col_sum(d_hidden * normed1)
        vec_ref[5:6, :] = col_sum(d_hidden)
        grad1_ref[...] = grad1
        g1 = grad1.astype(BF)
        g1_ref[...] = g1
        wait_all(flat(out_copies))
        for part in range(parts):
            d_ctx_refs[part][...] = nt(g1, wo_v[part]).astype(BF)

    outs = [struct(BF, count, depth), struct(F32, count, depth), struct(F32, 16, depth), *[struct(BF, count, width)] * parts]
    scratch = [
        pltpu.VMEM((parts, depth, units), BF),
        pltpu.VMEM((parts, width, depth), BF),
        pltpu.SemaphoreType.DMA((len(hbm),)),
    ]
    return run(body, [grad2, normed1, inv1, shared, *d_near, d_far], hbm, outs, [], scratch, "ffn_back")


def ffn_rows(x, ctx, wo, wi, wd, small, shared, first, count, before):
    parts = len(wo)
    depth = x.shape[1]
    units, width = wi[0][0][0].shape[1], ctx[0].shape[1]
    tile = min(256, count)
    start = first // tile
    hbm = arrays(wo) + arrays(wi) + arrays(wd)
    last_inputs = [] if before is None else [before]

    def body(*refs):
        it = iter(refs)
        x_ref = next(it)
        ctx_refs = [next(it) for _ in range(parts)]
        small_refs = [next(it) for _ in range(parts)]
        shared_ref = next(it)
        wo_refs, wi_refs, wd_refs = take(it, wo), take(it, wi), take(it, wd)
        for _ in last_inputs:
            next(it)
        out_ref, wo_v, wi_v, wd_v, sems = (next(it) for _ in range(5))
        out_copies = flat(stacked_copies(wo_refs, wo_v, sems, 0, 1))
        near = len(flat(wo))
        in_copies = stacked_copies(wi_refs, wi_v, sems, near, 1)
        down_copies = stacked_copies(wd_refs, wd_v, sems, near + len(flat(wi)), 1)
        opening = pl.program_id(0) == 0

        @pl.when(opening)
        def _():
            start_all(out_copies)
            for part in range(parts):
                start_all(in_copies[part] + down_copies[part])
            wait_all(out_copies)

        attn_sum = x_ref[...].astype(F32) + shared_ref[0:1, :]
        for part in range(parts):
            attn_sum = attn_sum + nn(ctx_refs[part][...], wo_v[part])
        hidden, _, _ = norm_forward(attn_sum, shared_ref[2:3, :], shared_ref[4:5, :])
        low = hidden.astype(BF)
        total = hidden + shared_ref[1:2, :]
        for part in range(parts):

            @pl.when(opening)
            def _():
                wait_all(in_copies[part] + down_copies[part])

            pre = nn(low, wi_v[part]) + small_refs[part][0:1, :]
            act = (pre * erf_gelu(pre)).astype(BF)
            total = total + nn(act, wd_v[part])
        out_ref[...] = norm_forward(total, shared_ref[3:4, :], shared_ref[5:6, :])[0].astype(BF)

    return pl.pallas_call(
        body,
        grid=(count // tile,),
        in_specs=[
            pl.BlockSpec((tile, depth), lambda i: (i + start, 0)),
            *[pl.BlockSpec((tile, width), lambda i: (i + start, 0))] * parts,
            *[shaped(a.shape) for a in small],
            shaped(shared.shape),
            *[ANY_SPEC] * (len(hbm) + len(last_inputs)),
        ],
        out_specs=pl.BlockSpec((tile, depth), lambda i: (i + start, 0)),
        out_shape=jax.ShapeDtypeStruct(x.shape, BF),
        input_output_aliases={} if before is None else {2 + 2 * parts + len(hbm): 0},
        scratch_shapes=[
            pltpu.VMEM((parts, width, depth), BF),
            pltpu.VMEM((parts, depth, units), BF),
            pltpu.VMEM((parts, units, depth), BF),
            pltpu.SemaphoreType.DMA((len(hbm),)),
        ],
        cost_estimate=SMALL,
        name="ffn_rows",
    )(x, *ctx, *small, shared, *hbm, *last_inputs)


def input_gradient(picked, grad1, dq, dk, dv, wq, seqs):
    parts = len(dq)
    slots = picked.shape[1]
    depth = grad1.shape[1]
    rows, width = dk[0].shape[0] // seqs, dk[0].shape[1]
    hbm = arrays(wq)

    def body(*refs):
        it = iter(refs)
        pick_ref, grad1_ref = next(it), next(it)
        dq_refs = [next(it) for _ in range(parts)]
        dk_refs = [next(it) for _ in range(parts)]
        dv_refs = [next(it) for _ in range(parts)]
        wq_refs = take(it, wq)
        out_ref, wq_v, sems = next(it), next(it), next(it)
        copies = flat(stacked_copies(wq_refs, wq_v, sems, 0, 1))
        seq = pl.program_id(0)

        @pl.when(seq == 0)
        def _():
            start_all(copies)
            wait_all(copies)

        chosen = grad1_ref[...]
        for part in range(parts):
            chosen = chosen + nn(dq_refs[part][...], wq_v[part, 0:width, :])
        high = chosen.astype(BF)
        rest = (chosen - high.astype(F32)).astype(BF)
        spread = spread_of(pick_ref[pl.ds(lax.axis_index("tp") * seqs + seq, 1), :], rows)
        total = nn(spread, high) + nn(spread, rest)
        for part in range(parts):
            total = total + nn(dk_refs[part][...], wq_v[part, width : 2 * width, :])
            total = total + nn(dv_refs[part][...], wq_v[part, 2 * width : 3 * width, :])
        out_ref[...] = total.astype(BF)

    row_spec = pl.BlockSpec((rows, width), lambda s: (s, 0))
    return pl.pallas_call(
        body,
        grid=(seqs,),
        in_specs=[
            whole(picked.shape),
            pl.BlockSpec((slots, depth), lambda s: (s, 0)),
            *[pl.BlockSpec((slots, width), lambda s: (s, 0))] * parts,
            *[row_spec] * (2 * parts),
            *[ANY_SPEC] * len(hbm),
        ],
        out_specs=pl.BlockSpec((rows, depth), lambda s: (s, 0)),
        out_shape=jax.ShapeDtypeStruct((seqs * rows, depth), BF),
        scratch_shapes=[pltpu.VMEM((parts, 3 * width, depth), BF), pltpu.SemaphoreType.DMA((len(hbm),))],
        cost_estimate=SMALL,
        name="input_gradient",
    )(picked, grad1, *dq, *dk, *dv, *hbm)


def bits_of(count):
    return [1 << b for b in range(count.bit_length() - 1)]


def swap(value, axis, bit):
    count = lax.axis_size(axis)
    return lax.ppermute(value, axis, [(i, i ^ bit) for i in range(count)])


def half_of(value, bit, own):
    half = value.shape[0] // 2
    side = (lax.axis_index("dp") // bit) % 2
    return lax.dynamic_slice_in_dim(value, jnp.where(side == 0, 0, half) if own else jnp.where(side == 0, half, 0), half, 0)


def joined(own, got, bit):
    side = (lax.axis_index("dp") // bit) % 2
    return jnp.concatenate([jnp.where(side == 0, own, got), jnp.where(side == 0, got, own)], axis=0)


def add(*values):
    total = values[0].astype(F32)
    for value in values[1:]:
        total = total + value.astype(F32)
    return total.astype(BF)


def scatter(value, bit, *after):
    sent, kept = half_of(value, bit, False), half_of(value, bit, True)
    return add(tie(kept, *after), swap(sent, "dp", bit))


def gather(value, bit):
    return joined(value, swap(value, "dp", bit), bit)


def on_device(
    tokens, w_qkv, qv_bias, w_out, out_bias, w_in, in_bias, w_down, down_bias, norm_gain, norm_shift, valid_len, picked, d_out
):
    parts = lax.axis_size("tp")
    rank = lax.axis_index("tp")
    seqs = valid_len.shape[0] // parts
    depth = tokens.shape[1]
    width = w_qkv.shape[2]
    core, far = 1, 2
    dp_bits = bits_of(lax.axis_size("dp"))

    shared = jnp.concatenate([out_bias[None], down_bias[None], norm_gain, norm_shift, jnp.zeros((2, depth), F32)], axis=0)
    small = [jnp.concatenate([in_bias[None], jnp.pad(qv_bias, ((0, 5), (0, depth - width)))], axis=0)]
    small += [swap(small[0], "tp", core)]
    wq = w_qkv.transpose(0, 2, 1).reshape(3 * width, depth)
    qo_far = swap(jnp.concatenate([half_of(wq, 1, True), half_of(w_out, 1, True)], axis=0), "tp", far)
    wq_near = swap(wq, "tp", core)
    ready = small[1]
    small_far = swap(jnp.concatenate(small, axis=0), "tp", far)
    small += [small_far[:8], small_far[8:]]

    def forward(j, x, pieces):
        return attend_forward(valid_len, x, pieces, width, small[j], picked, seqs)

    out0 = forward(0, tie(tokens, ready), [wq])
    cut = w_down.shape[0] // 2
    ff_far = swap(tie(jnp.concatenate([half_of(w_in, 1, True), half_of(w_down[:cut], 1, True)], axis=0), small_far, out0[0]), "tp", far)
    fd_far = swap(tie(half_of(w_down[cut:], 2, True), small_far, out0[0]), "tp", far)
    qo_far = tie(qo_far, out0[0])
    qo_rest, qo_far_core = swap(qo_far, "dp", 1), swap(qo_far, "tp", core)
    out1 = forward(1, tie(tokens, qo_far), [wq_near])
    qo_rest = tie(qo_rest, out1[0])
    qo_rest_core = swap(qo_rest, "tp", core)
    wo_near = swap(tie(w_out, qo_rest), "tp", core)
    wi_near, wd_near = swap(tie(w_in, ready), "tp", core), swap(tie(w_down, ready), "tp", core)
    out2 = forward(2, tie(tokens, qo_rest, qo_far_core, wi_near, wd_near), [qo_far, qo_rest])
    ff_far = tie(ff_far, out2[0])
    rows_in = w_in.shape[0] // 2
    ff_rest = swap(ff_far, "dp", 1)
    ff_far_core = swap(ff_far, "tp", core)
    out3 = forward(3, tie(tokens, ff_far), [qo_far_core, qo_rest_core])
    fd_far = tie(fd_far, out3[0])
    fd_rest, fd_far_core = swap(fd_far, "dp", 2), swap(fd_far, "tp", core)
    q_sel, k, v, ctx, ctx_sel = zip(out0, out1, out2, out3)
    rows_q = 3 * width // 2

    def pieces(own, near, far_pieces, core_pieces):
        return [[(own, 0)], [(near, 0)], far_pieces, core_pieces]

    wq = pieces(wq, wq_near, [(qo_far, 0), (qo_rest, 0)], [(qo_far_core, 0), (qo_rest_core, 0)])
    wo = pieces(w_out, wo_near, [(qo_far, rows_q), (qo_rest, rows_q)], [(qo_far_core, rows_q), (qo_rest_core, rows_q)])
    near_in, near_down = [[(w_in, 0)], [(wi_near, 0)]], [[(w_down, 0)], [(wd_near, 0)]]
    prep = ffn_prep(picked, tie(tokens, fd_far), d_out, ctx_sel, wo, near_in, near_down, small[:2], shared, seqs)
    *act, slope_near, x_sel, cot, low, ffn_sum, normed1, inv1 = prep
    low_near, act_near = swap(low, "tp", core), swap(act[1], "tp", core)
    ff_rest, fd_rest = tie((ff_rest, fd_rest), low)
    ff_rest_core, fd_rest_core = swap(ff_rest, "tp", core), swap(fd_rest, "tp", core)
    wi = near_in + [[(ff_far, 0), (ff_rest, 0)], [(ff_far_core, 0), (ff_rest_core, 0)]]
    wd = near_down + [
        [(ff_far, rows_in), (ff_rest, rows_in), (fd_far, 0), (fd_rest, 0)],
        [(ff_far_core, rows_in), (ff_rest_core, rows_in), (fd_far_core, 0), (fd_rest_core, 0)],
    ]

    sent, g2, slope_far, grad2, vec = ffn_front(low, ffn_sum, cot, wi[2:], wd[2:], small[2:], shared)
    act_got = swap(sent, "tp", far)
    g2_near = swap(g2, "tp", core)
    *d_near, d_far, vec_mid = ffn_mid(g2, low, [slope_near, slope_far], wd)
    d_got, d_got_near = swap(d_far, "tp", far), swap(d_near[1], "tp", core)
    g1, grad1, vec_back, *d_ctx = ffn_back(tie(grad2, act_near, low_near, g2_near), d_near, d_far, normed1, inv1, shared, wi, wo, width)
    count = low.shape[0]

    def backward(j, x):
        return attend_backward(j, valid_len, q_sel[j], k[j], v[j], d_ctx[j], x, x_sel, ctx_sel[j], g1, seqs)

    def rows_of(first, count, before, *after):
        return ffn_rows(tie(tokens, *after), ctx, wo, wi, wd, small, shared, first, count, before)

    def finish(value, bits):
        for bit in bits:
            value = scatter(value, bit) if bit != last else add(value, swap(value, "dp", bit))
        return value

    def spread_out(value, bits):
        for bit in reversed(bits):
            value = gather(value, bit)
        return value

    half_rows, last = tokens.shape[0] // 2, dp_bits[-1]
    out3 = backward(3, tie(tokens, d_got_near))
    out2 = backward(2, tie(tokens, out3[0]))
    act_got = tie(act_got, out2[0])
    act_diag = swap(act_got[count:], "tp", core)
    out1 = backward(1, tie(tokens, out2[0], act_got))
    total_a = pair_sums(
        [
            ((tie(act[0], out1[0]), 0), (g2, 0)),
            ((act_near, 0), (g2_near, 0)),
            ((act_got, 0), (act_got, 2)),
            ((act_diag, 0), (act_diag, 1)),
        ]
    )
    sent_a = half_of(total_a, dp_bits[0], False)
    out0 = backward(0, tie(tokens, out1[0], sent_a))
    dq, dk, dv, sums, g_heads = zip(out0, out1, out2, out3)
    d_got = tie(d_got, out0[0])
    d_diag = swap(d_got[count:], "tp", core)
    far_c = add(tie(out2[4], out1[0]), swap(tie(out3[4], out2[0]), "tp", core))
    near_c = g_heads[0], swap(tie(g_heads[1], out0[0]), "tp", core)
    line = jnp.concatenate([vec + vec_mid + vec_back, sums[0] + sums[1] + sums[2] + sums[3]], axis=0)
    total_a = add(tie(half_of(total_a, dp_bits[0], True), far_c), swap(sent_a, "dp", dp_bits[0]))
    sent_a = half_of(total_a, dp_bits[1], False)
    total_b = pair_sums(
        [
            ((tie(low, sent_a), 0), (d_near[0], 0)),
            ((low_near, 0), (d_got_near, 0)),
            ((d_got, 2), (d_got, 0)),
            ((d_diag, 1), (d_diag, 0)),
        ]
    )
    sent_b = half_of(total_b, dp_bits[0], False)
    out_first = rows_of(0, half_rows, None, line, sent_b)
    total_a = add(tie(half_of(total_a, dp_bits[1], True), out_first), swap(sent_a, "dp", dp_bits[1]))
    for bit in dp_bits[2:-1]:
        total_a = scatter(total_a, bit)
    total_b = add(tie(half_of(total_b, dp_bits[0], True), out_first), swap(sent_b, "dp", dp_bits[0]))
    sent_b = half_of(total_b, dp_bits[1], False)
    total_c = add(*tie(near_c, out_first), swap(far_c, "tp", far))
    cut = far_c.shape[0] // 2
    other = [dp_bits[1], dp_bits[0], *dp_bits[2:]]
    total_c, rest_c = total_c[:cut], total_c[cut:]
    sent_c, sent_d = half_of(total_c, dp_bits[0], False), half_of(rest_c, other[0], False)
    d_tokens = input_gradient(tie(picked, total_a, sent_b, sent_c, sent_d), grad1, dq, dk, dv, wq, seqs)
    total_a = add(tie(total_a, d_tokens), swap(total_a, "dp", last))
    total_b = add(tie(half_of(total_b, dp_bits[1], True), d_tokens), swap(sent_b, "dp", dp_bits[1]))
    for bit in dp_bits[2:-1]:
        total_b = scatter(total_b, bit)
    total_c = add(tie(half_of(total_c, dp_bits[0], True), d_tokens), swap(sent_c, "dp", dp_bits[0]))
    rest_c = add(tie(half_of(rest_c, other[0], True), d_tokens), swap(sent_d, "dp", other[0]))
    sent_c, sent_d = half_of(total_c, dp_bits[1], False), half_of(rest_c, other[1], False)
    line = tie(line, d_tokens)
    out_second = rows_of(half_rows, half_rows // 2, out_first, total_a, total_b, sent_c, sent_d, line)
    for bit in reversed(dp_bits[2:-1]):
        total_a = gather(total_a, bit)
    total_a = joined(tie(total_a, out_second), swap(total_a, "dp", dp_bits[1]), dp_bits[1])
    total_b = add(tie(total_b, out_second), swap(total_b, "dp", last))
    for bit in reversed(dp_bits[2:-1]):
        total_b = gather(total_b, bit)
    total_c = add(tie(half_of(total_c, dp_bits[1], True), out_second), swap(sent_c, "dp", dp_bits[1]))
    rest_c = add(tie(half_of(rest_c, other[1], True), out_second), swap(sent_d, "dp", other[1]))
    for bit in dp_bits[2:-1]:
        total_c, rest_c = scatter(total_c, bit), scatter(rest_c, bit)
    line = tie(line, out_second) + swap(line, "tp", core)
    out_third = rows_of(half_rows + half_rows // 2, half_rows // 2, out_second, total_a, total_b, total_c, rest_c, line)
    total_a = joined(tie(total_a, out_third), swap(total_a, "dp", dp_bits[0]), dp_bits[0])
    total_b = joined(tie(total_b, out_third), swap(total_b, "dp", dp_bits[1]), dp_bits[1])
    total_c = add(tie(total_c, out_third), swap(total_c, "dp", last))
    rest_c = add(tie(rest_c, out_third), swap(rest_c, "dp", last))
    line = tie(line, total_c, rest_c) + swap(line, "dp", dp_bits[0])
    for bit in dp_bits[1:2]:
        line = line + swap(line, "dp", bit)
    for bit in dp_bits[2:]:
        line = line + swap(line, "dp", bit)
    total_c, rest_c = spread_out(total_c, dp_bits[1:-1]), spread_out(rest_c, other[1:-1])
    line = tie(line, total_c)
    line = line + swap(line, "tp", far)
    total_b = gather(total_b, dp_bits[0])
    total_c, rest_c = gather(total_c, dp_bits[0]), gather(rest_c, other[0])
    total_c = jnp.concatenate([total_c.astype(F32), rest_c.astype(F32)], axis=0)
    own = lax.dynamic_slice_in_dim(line, 8 + rank, 1, 0)[0]
    own_q = lax.dynamic_slice(line, (16 + rank, 0), (1, width))
    own_v = lax.dynamic_slice(line, (16 + PARTS + rank, 0), (1, width))
    return (
        out_third,
        d_tokens,
        total_c[: 3 * width].reshape(3, width, depth).transpose(0, 2, 1),
        jnp.concatenate([own_q, own_v], axis=0),
        total_c[3 * width :],
        line[3],
        total_b.astype(F32),
        own,
        total_a.astype(F32),
        line[0],
        jnp.stack([line[4], line[1]]),
        jnp.stack([line[5], line[2]]),
    )


def solution(mesh):
    placed = (
        P(("dp", "tp"), None),
        P(None, None, "tp"),
        P(None, "tp"),
        P("tp", None),
        P(),
        P(None, "tp"),
        P("tp"),
        P("tp", None),
        P(),
        P(),
        P(),
        P("dp"),
        P("dp", None),
        P(("dp", "tp"), None),
    )
    return jax.shard_map(
        on_device,
        mesh=mesh,
        in_specs=placed,
        out_specs=(
            P(("dp", "tp"), None),
            P(("dp", "tp"), None),
            P(None, None, "tp"),
            P(None, "tp"),
            P("tp", None),
            P(),
            P(None, "tp"),
            P("tp"),
            P("tp", None),
            P(),
            P(),
            P(),
        ),
        check_vma=False,
    )
```

```python
import jax
import jax.numpy as jnp
from jax import lax
from jax.experimental import pallas as pl
from jax.experimental.pallas import tpu as pltpu
from jax.sharding import PartitionSpec as P

HD = 64
SCALE = HD ** (-0.5)
NORM_EPS = 1e-06
MASKED = -1e30
HALF_ROOT = 0.5 ** 0.5
DENSITY = 0.3989422804014327
PARTS = 4
BF = jnp.bfloat16
F32 = jnp.float32


def nn(left, right):
    return lax.dot_general(left, right, (((1,), (0,)), ((), ())), preferred_element_type=F32)


def nt(left, right):
    return lax.dot_general(left, right, (((1,), (1,)), ((), ())), preferred_element_type=F32)


def tn(left, right):
    return lax.dot_general(left, right, (((0,), (0,)), ((), ())), preferred_element_type=F32)


def head_masks(width, dtype=BF):
    lane = lax.broadcasted_iota(jnp.int32, (1, width), 1) // HD
    return [(lane == head).astype(dtype) for head in range(width // HD)]


def spread_of(picks, length):
    slots = picks.shape[1]
    return (lax.broadcasted_iota(jnp.int32, (length, slots), 0) == picks).astype(F32).astype(BF)


def whole(shape):
    zeros = (0,) * len(shape)
    return pl.BlockSpec(shape, lambda *_: zeros)


def norm_forward(values, gain, shift):
    average = jnp.mean(values, axis=1, keepdims=True)
    centered = values - average
    inv_std = lax.rsqrt(jnp.mean(centered * centered, axis=1, keepdims=True) + NORM_EPS)
    normed = centered * inv_std
    return normed * gain + shift, normed, inv_std


def norm_backward(grad, normed, inv_std, gain):
    scaled = grad * gain
    first = jnp.mean(scaled, axis=1, keepdims=True)
    second = jnp.mean(scaled * normed, axis=1, keepdims=True)
    return inv_std * (scaled - first - normed * second)


def tie(value, *others):
    return lax.optimization_barrier((value, others))[0]


SMALL = pl.CostEstimate(flops=1024, transcendentals=0, bytes_accessed=1024)


def col_sum(values):
    return jnp.sum(values, axis=0, keepdims=True)


def piece_copies(pieces, target, sems, first, bit):
    rows = target.shape[0]
    if len(pieces) == 1:
        return [pltpu.make_async_copy(pieces[0][0], target, sems.at[first])]
    half, step = rows // 2, rows // len(pieces)
    if len(pieces) == 4:
        upper = piece_copies(pieces[:2], target.at[pl.ds(0, half), :], sems, first, bit)
        return upper + piece_copies(pieces[2:], target.at[pl.ds(half, half), :], sems, first + 2, 2 * bit)
    own = ((lax.axis_index("dp") // bit) % 2) * half
    copies = []
    for n, (ref, skip) in enumerate(pieces):
        base = own if n * step < half else half - own
        start = pl.multiple_of(base + (n * step) % half, step)
        copies.append(pltpu.make_async_copy(ref.at[pl.ds(skip, step), :], target.at[pl.ds(start, step), :], sems.at[first + n]))
    return copies


def stacked_copies(pieces, target, sems, first, bit):
    copies = []
    for part, refs in enumerate(pieces):
        copies.append(piece_copies(refs, target.at[part], sems, first, bit))
        first += len(refs)
    return copies


def take(it, pieces):
    return [[(next(it), skip) for _, skip in piece] for piece in pieces]


def flat(pieces):
    return [p for piece in pieces for p in piece]


def arrays(pieces):
    return [array for array, _ in flat(pieces)]


def start_all(copies):
    for copy in copies:
        copy.start()


def wait_all(copies):
    for copy in copies:
        copy.wait()


ANY_SPEC = pl.BlockSpec(memory_space=pl.ANY)


def shaped(shape):
    return pl.BlockSpec(shape, lambda *_: (0,) * len(shape))


def attend_body(len_ref, x_ref, small_ref, pick_ref, *rest, count):
    w_refs = [(ref, 0) for ref in rest[:count]]
    q_sel_ref, k_ref, v_ref, ctx_ref, ctx_sel_ref, ext_ref, w_ref, sems = rest[count:]
    rows, width = k_ref.shape
    seq = pl.program_id(0)
    row = lax.axis_index("tp") * pl.num_programs(0) + seq
    length = len_ref[row]
    copies = piece_copies(w_refs, w_ref, sems, 0, 1)

    @pl.when(seq == 0)
    def _():
        start_all(copies)
        wait_all(copies)

    x = x_ref[...]
    queries = (nt(x, w_ref[0:width, :]) + small_ref[1:2, :width]).astype(BF)
    key_rows = nt(x, w_ref[width : 2 * width, :]).astype(BF)
    values = (nt(x, w_ref[2 * width : 3 * width, :]) + small_ref[2:3, :width]).astype(BF)
    k_ref[...] = key_rows
    v_ref[...] = values
    ext_ref[:, :width] = values
    ext_ref[:, width:] = jnp.ones((rows, ext_ref.shape[1] - width), BF)
    spread = spread_of(pick_ref[pl.ds(row, 1), :], rows)
    q_sel_ref[...] = tn(spread, queries).astype(BF)
    scaled = queries * jnp.asarray(SCALE, BF)
    masks = head_masks(width)
    tile = min(256, rows)
    keep = lax.broadcasted_iota(jnp.int32, (tile, rows), 1) < length
    for start in range(0, rows, tile):
        total = jnp.zeros((tile, width), F32)
        for mask in masks:
            logits = nt(scaled[start : start + tile] * mask, key_rows)
            logits = jnp.where(keep, logits, MASKED)
            peak = jnp.max(logits, axis=1, keepdims=True)
            probs = jnp.exp(logits - peak).astype(BF)
            mixed = nn(probs, ext_ref[...])
            share = mixed[:, :width] / mixed[:, width : width + 1]
            total = jnp.where(mask.astype(F32) > 0.5, share, total)
        ctx_ref[start : start + tile, :] = total.astype(BF)
    ctx_sel_ref[...] = tn(spread, ctx_ref[...]).astype(BF)


def attend_forward(lengths, x, pieces, width, small, picked, seqs):
    slots = picked.shape[1]
    rows = x.shape[0] // seqs
    depth = x.shape[1]
    ext = -(-(width + 1) // 128) * 128
    row_spec = pl.BlockSpec((rows, width), lambda s, _: (s, 0))
    sel_spec = pl.BlockSpec((slots, width), lambda s, _: (s, 0))
    return pl.pallas_call(
        lambda *refs: attend_body(*refs, count=len(pieces)),
        grid_spec=pltpu.PrefetchScalarGridSpec(
            num_scalar_prefetch=1,
            grid=(seqs,),
            in_specs=[
                pl.BlockSpec((rows, depth), lambda s, _: (s, 0)),
                whole(small.shape),
                whole(picked.shape),
                *[ANY_SPEC] * len(pieces),
            ],
            out_specs=[sel_spec, row_spec, row_spec, row_spec, sel_spec],
            scratch_shapes=[
                pltpu.VMEM((rows, ext), BF),
                pltpu.VMEM((3 * width, depth), BF),
                pltpu.SemaphoreType.DMA((len(pieces),)),
            ],
        ),
        out_shape=[
            jax.ShapeDtypeStruct((seqs * slots, width), BF),
            jax.ShapeDtypeStruct((seqs * rows, width), BF),
            jax.ShapeDtypeStruct((seqs * rows, width), BF),
            jax.ShapeDtypeStruct((seqs * rows, width), BF),
            jax.ShapeDtypeStruct((seqs * slots, width), BF),
        ],
        cost_estimate=SMALL,
        name="attend_forward",
    )(lengths, x, small, picked, *pieces)


def attend_back_body(
    len_ref, q_ref, k_ref, v_ref, d_ctx_ref, x_ref, x_sel_ref, ctx_sel_ref, g1_ref, dq_ref, dk_ref, dv_ref, sums_ref, grad_ref, acc_ref, *, part
):
    rows, width = k_ref.shape
    slots = q_ref.shape[0]
    seq = pl.program_id(0)
    rank = lax.axis_index("tp")
    length = len_ref[rank * pl.num_programs(0) + seq]
    masks = head_masks(width)
    queries, d_ctx = q_ref[...], d_ctx_ref[...]
    key_rows, values = k_ref[...], v_ref[...]
    q_stack = jnp.concatenate([queries * mask for mask in masks], axis=0)
    d_stack = jnp.concatenate([d_ctx * mask for mask in masks], axis=0)
    logits = nt(key_rows, q_stack * jnp.asarray(SCALE, BF))
    keep = lax.broadcasted_iota(jnp.int32, logits.shape, 0) < length
    logits = jnp.where(keep, logits, MASKED)
    grown = jnp.exp(logits - jnp.max(logits, axis=0, keepdims=True))
    probs = grown * (1.0 / jnp.sum(grown, axis=0, keepdims=True))
    d_probs = nt(values, d_stack)
    inner = jnp.sum(probs * d_probs, axis=0, keepdims=True)
    d_raw = (probs * (d_probs - inner) * SCALE).astype(BF)
    d_keys = nn(d_raw, q_stack).astype(BF)
    dk_ref[...] = d_keys
    d_values = nn(probs.astype(BF), d_stack).astype(BF)
    dv_ref[...] = d_values
    dq_stack = tn(d_raw, key_rows)
    dq = jnp.zeros((slots, width), F32)
    for head, mask in enumerate(masks):
        dq = jnp.where(mask.astype(F32) > 0.5, dq_stack[head * slots : (head + 1) * slots], dq)
    dq = dq.astype(BF)
    dq_ref[...] = dq

    @pl.when(seq == 0)
    def _():
        acc_ref[...] = jnp.zeros(acc_ref.shape, F32)
        sums_ref[...] = jnp.zeros(sums_ref.shape, F32)

    at = rank ^ part
    sums_ref[pl.ds(at, 1), 0:width] += col_sum(dq.astype(F32))
    sums_ref[pl.ds(PARTS + at, 1), 0:width] += col_sum(d_values.astype(F32))
    acc_ref[0:width, :] += tn(dq, x_sel_ref[...])
    acc_ref[width : 2 * width, :] += tn(d_keys, x_ref[...])
    acc_ref[2 * width : 3 * width, :] += tn(d_values, x_ref[...])
    acc_ref[3 * width : 4 * width, :] += tn(ctx_sel_ref[...], g1_ref[...])

    @pl.when(seq == pl.num_programs(0) - 1)
    def _():
        grad_ref[...] = acc_ref[...].astype(BF)


def attend_backward(part, lengths, q_sel, k, v, d_ctx, x, x_sel, ctx_sel, g1, seqs):
    rows, slots, width = k.shape[0] // seqs, q_sel.shape[0] // seqs, k.shape[1]
    depth = x.shape[1]
    row_spec = pl.BlockSpec((rows, width), lambda s, _: (s, 0))
    sel_spec = pl.BlockSpec((slots, width), lambda s, _: (s, 0))
    wide_spec = pl.BlockSpec((slots, depth), lambda s, _: (s, 0))
    return pl.pallas_call(
        lambda *refs: attend_back_body(*refs, part=part),
        grid_spec=pltpu.PrefetchScalarGridSpec(
            num_scalar_prefetch=1,
            grid=(seqs,),
            in_specs=[
                sel_spec,
                row_spec,
                row_spec,
                sel_spec,
                pl.BlockSpec((rows, depth), lambda s, _: (s, 0)),
                wide_spec,
                sel_spec,
                wide_spec,
            ],
            out_specs=[sel_spec, row_spec, row_spec, whole((2 * PARTS, depth)), whole((4 * width, depth))],
            scratch_shapes=[pltpu.VMEM((4 * width, depth), F32)],
        ),
        out_shape=[
            jax.ShapeDtypeStruct(q_sel.shape, BF),
            jax.ShapeDtypeStruct(k.shape, BF),
            jax.ShapeDtypeStruct(k.shape, BF),
            jax.ShapeDtypeStruct((2 * PARTS, depth), F32),
            jax.ShapeDtypeStruct((4 * width, depth), BF),
        ],
        cost_estimate=SMALL,
        name="attend_backward",
    )(lengths, q_sel, k, v, d_ctx, x, x_sel, ctx_sel, g1)


def erf_gelu(values):
    return 0.5 * (1.0 + lax.erf(values * HALF_ROOT))


def run(body, plain, hbm, outs, hbm_outs, scratch, name):
    return pl.pallas_call(
        body,
        grid=(1,),
        in_specs=[*[shaped(a.shape) for a in plain], *[ANY_SPEC] * len(hbm)],
        out_specs=[*[shaped(a.shape) for a in outs], *[ANY_SPEC] * len(hbm_outs)],
        out_shape=[*outs, *hbm_outs],
        scratch_shapes=scratch,
        cost_estimate=SMALL,
        name=name,
    )(*plain, *hbm)


def struct(dtype, *shape):
    return jax.ShapeDtypeStruct(shape, dtype)


def unit_part(low, wi, bias, slope_ref, n):
    pre = nn(low, wi) + bias
    chance = erf_gelu(pre)
    slope_ref[n] = chance + pre * (DENSITY * jnp.exp(-0.5 * pre * pre))
    return (pre * chance).astype(BF)


def ffn_prep(picked, x, d_out, ctx_sel, wo, wi, wd, small, shared, seqs):
    parts, near = len(wo), len(wi)
    slots = picked.shape[1]
    count, depth, units, width = seqs * slots, x.shape[1], wi[0][0][0].shape[1], ctx_sel[0].shape[1]
    plain = [picked, x, d_out, shared, *ctx_sel, *small]
    hbm = arrays(wo) + arrays(wi) + arrays(wd)

    def body(*refs):
        it = iter(refs)
        pick_ref, x_ref, d_out_ref, shared_ref = (next(it) for _ in range(4))
        ctx_refs = [next(it) for _ in range(parts)]
        small_refs = [next(it) for _ in range(near)]
        wo_refs, wi_refs, wd_refs = take(it, wo), take(it, wi), take(it, wd)
        act_refs = [next(it) for _ in range(near)]
        slope_ref, x_sel_ref, cot_ref, low_ref, sum_ref, normed1_ref, inv1_ref = (next(it) for _ in range(7))
        wo_v, wi_v, wd_v, sems = (next(it) for _ in range(4))
        out_copies = stacked_copies(wo_refs, wo_v, sems, 0, 1)
        first = len(flat(wo))
        in_copies = stacked_copies(wi_refs, wi_v, sems, first, 1)
        down_copies = stacked_copies(wd_refs, wd_v, sems, first + len(flat(wi)), 1)
        start_all(flat(out_copies) + flat(in_copies) + flat(down_copies))
        rows = x_ref.shape[0] // seqs
        for seq in range(seqs):
            at = lax.axis_index("tp") * seqs + seq
            spread = spread_of(pick_ref[pl.ds(at, 1), :], rows)
            x_sel_ref[seq * slots : (seq + 1) * slots, :] = tn(spread, x_ref[seq * rows : (seq + 1) * rows, :]).astype(BF)
            cot_ref[seq * slots : (seq + 1) * slots, :] = tn(spread, d_out_ref[seq * rows : (seq + 1) * rows, :]).astype(BF)
        attn_sum = x_sel_ref[...].astype(F32) + shared_ref[0:1, :]
        wait_all(flat(out_copies))
        for part in range(parts):
            attn_sum = attn_sum + nn(ctx_refs[part][...], wo_v[part])
        hidden, normed1, inv1 = norm_forward(attn_sum, shared_ref[2:3, :], shared_ref[4:5, :])
        low = hidden.astype(BF)
        low_ref[...] = low
        normed1_ref[...] = normed1
        inv1_ref[...] = inv1
        total = hidden + shared_ref[1:2, :]
        wait_all(flat(in_copies) + flat(down_copies))
        for n in range(near):
            act = unit_part(low, wi_v[n], small_refs[n][0:1, :], slope_ref, n)
            act_refs[n][...] = act
            total = total + nn(act, wd_v[n])
        sum_ref[...] = total

    outs = [
        *[struct(BF, count, units)] * near,
        struct(F32, near, count, units),
        struct(BF, count, depth),
        struct(BF, count, depth),
        struct(BF, count, depth),
        struct(F32, count, depth),
        struct(F32, count, depth),
        struct(F32, count, 1),
    ]
    scratch = [
        pltpu.VMEM((parts, width, depth), BF),
        pltpu.VMEM((near, depth, units), BF),
        pltpu.VMEM((near, units, depth), BF),
        pltpu.SemaphoreType.DMA((len(hbm),)),
    ]
    return run(body, plain, hbm, outs, [], scratch, "ffn_prep")


def ffn_front(low, total, cot, wi, wd, small, shared):
    far = len(wi)
    count, depth = low.shape
    units = wi[0][0][0].shape[1]
    plain = [low, total, cot, shared, *small]
    hbm = arrays(wi) + arrays(wd)

    def body(*refs):
        it = iter(refs)
        low_ref, sum_ref, cot_ref, shared_ref = (next(it) for _ in range(4))
        small_refs = [next(it) for _ in range(far)]
        wi_refs, wd_refs = take(it, wi), take(it, wd)
        sent_ref, g2_ref, slope_ref, grad2_ref, vec_ref = (next(it) for _ in range(5))
        wi_v, wd_v, sems = (next(it) for _ in range(3))
        in_copies = stacked_copies(wi_refs, wi_v, sems, 0, 1)
        down_copies = stacked_copies(wd_refs, wd_v, sems, len(flat(wi)), 1)
        for n in range(far):
            start_all(in_copies[n] + down_copies[n])
        low = low_ref[...]
        total = sum_ref[...]
        for n in range(far):
            wait_all(in_copies[n])
            act = unit_part(low, wi_v[n], small_refs[n][0:1, :], slope_ref, n)
            sent_ref[n * count : (n + 1) * count, :] = act
            wait_all(down_copies[n])
            total = total + nn(act, wd_v[n])
        _, normed2, inv2 = norm_forward(total, shared_ref[3:4, :], shared_ref[5:6, :])
        cotangent = cot_ref[...].astype(F32)
        grad2 = norm_backward(cotangent, normed2, inv2, shared_ref[3:4, :])
        vec_ref[...] = jnp.zeros(vec_ref.shape, F32)
        vec_ref[0:1, :] = col_sum(grad2)
        vec_ref[1:2, :] = col_sum(cotangent * normed2)
        vec_ref[2:3, :] = col_sum(cotangent)
        grad2_ref[...] = grad2
        g2 = grad2.astype(BF)
        g2_ref[...] = g2
        sent_ref[far * count :, :] = g2

    outs = [
        struct(BF, (far + 1) * count, units),
        struct(BF, count, depth),
        struct(F32, far, count, units),
        struct(F32, count, depth),
        struct(F32, 16, depth),
    ]
    scratch = [
        pltpu.VMEM((far, depth, units), BF),
        pltpu.VMEM((far, units, depth), BF),
        pltpu.SemaphoreType.DMA((len(hbm),)),
    ]
    return run(body, plain, hbm, outs, [], scratch, "ffn_front")


def ffn_mid(g2, low, slopes, wd):
    parts = len(wd)
    near = slopes[0].shape[0]
    count, depth = g2.shape
    units = slopes[0].shape[2]
    hbm = [*slopes, *arrays(wd)]

    def body(*refs):
        it = iter(refs)
        g2_ref, low_ref = next(it), next(it)
        slope_hbm = [next(it) for _ in slopes]
        wd_refs = take(it, wd)
        d_refs = [next(it) for _ in range(near)]
        sent_ref, vec_ref = next(it), next(it)
        wd_v, slope_v, sems, slope_sems = (next(it) for _ in range(4))
        down_copies = stacked_copies(wd_refs, wd_v, sems, 0, 1)
        sources = [ref.at[n] for ref in slope_hbm for n in range(ref.shape[0])]
        slope_copies = [pltpu.make_async_copy(sources[part], slope_v.at[part], slope_sems.at[part]) for part in range(parts)]
        for part in range(parts):
            start_all(down_copies[part] + [slope_copies[part]])
        vec_ref[...] = jnp.zeros(vec_ref.shape, F32)
        g2 = g2_ref[...]
        for part in range(parts):
            wait_all(down_copies[part] + [slope_copies[part]])
            d_pre = (nt(g2, wd_v[part]) * slope_v[part]).astype(BF)
            if part < near:
                d_refs[part][...] = d_pre
            else:
                sent_ref[(part - near) * count : (part - near + 1) * count, :] = d_pre
            at = 8 + (lax.axis_index("tp") ^ part)
            vec_ref[pl.ds(at, 1), :] = col_sum(d_pre.astype(F32))
        sent_ref[(parts - near) * count :, :] = low_ref[...]

    outs = [*[struct(BF, count, units)] * near, struct(BF, (parts - near + 1) * count, units), struct(F32, 16, depth)]
    scratch = [
        pltpu.VMEM((parts, units, depth), BF),
        pltpu.VMEM((parts, count, units), F32),
        pltpu.SemaphoreType.DMA((len(arrays(wd)),)),
        pltpu.SemaphoreType.DMA((parts,)),
    ]
    return run(body, [g2, low], hbm, outs, [], scratch, "ffn_mid")


def pair_sums(pairs):
    count = min(array.shape[0] for array, _ in pairs[0])
    width, depth = pairs[0][0][0].shape[1], pairs[0][1][0].shape[1]
    tile = min(256, width)

    def body(*refs):
        total = tn(refs[0][...], refs[1][...])
        for n in range(1, len(pairs)):
            total = total + tn(refs[2 * n][...], refs[2 * n + 1][...])
        refs[-1][...] = total.astype(BF)

    def left(block):
        return pl.BlockSpec((count, tile), lambda i: (block, i))

    def right(block):
        return pl.BlockSpec((count, depth), lambda i: (block, 0))

    return pl.pallas_call(
        body,
        grid=(width // tile,),
        in_specs=[spec for (_, a), (_, b) in pairs for spec in (left(a), right(b))],
        out_specs=pl.BlockSpec((tile, depth), lambda i: (i, 0)),
        out_shape=jax.ShapeDtypeStruct((width, depth), BF),
        cost_estimate=SMALL,
        name="pair_sums",
    )(*[array for (a, _), (b, _) in pairs for array in (a, b)])


def ffn_back(grad2, d_near, d_far, normed1, inv1, shared, wi, wo, width):
    parts, near = len(wi), len(d_near)
    count, depth = grad2.shape
    units = d_far.shape[1]
    hbm = arrays(wi) + arrays(wo)

    def body(*refs):
        it = iter(refs)
        grad2_ref, normed1_ref, inv1_ref, shared_ref = (next(it) for _ in range(4))
        near_refs = [next(it) for _ in range(near)]
        far_ref = next(it)
        wi_refs, wo_refs = take(it, wi), take(it, wo)
        g1_ref, grad1_ref, vec_ref = next(it), next(it), next(it)
        d_ctx_refs = [next(it) for _ in range(parts)]
        wi_v, wo_v, sems = (next(it) for _ in range(3))
        in_copies = stacked_copies(wi_refs, wi_v, sems, 0, 1)
        out_copies = stacked_copies(wo_refs, wo_v, sems, len(flat(wi)), 1)
        start_all(flat(in_copies) + flat(out_copies))
        d_hidden = grad2_ref[...]
        for part in range(parts):
            wait_all(in_copies[part])
            d_pre = near_refs[part][...] if part < near else far_ref[(part - near) * count : (part - near + 1) * count, :]
            d_hidden = d_hidden + nt(d_pre, wi_v[part])
        normed1 = normed1_ref[...]
        grad1 = norm_backward(d_hidden, normed1, inv1_ref[...], shared_ref[2:3, :])
        vec_ref[...] = jnp.zeros(vec_ref.shape, F32)
        vec_ref[3:4, :] = col_sum(grad1)
        vec_ref[4:5, :] = col_sum(d_hidden * normed1)
        vec_ref[5:6, :] = col_sum(d_hidden)
        grad1_ref[...] = grad1
        g1 = grad1.astype(BF)
        g1_ref[...] = g1
        wait_all(flat(out_copies))
        for part in range(parts):
            d_ctx_refs[part][...] = nt(g1, wo_v[part]).astype(BF)

    outs = [struct(BF, count, depth), struct(F32, count, depth), struct(F32, 16, depth), *[struct(BF, count, width)] * parts]
    scratch = [
        pltpu.VMEM((parts, depth, units), BF),
        pltpu.VMEM((parts, width, depth), BF),
        pltpu.SemaphoreType.DMA((len(hbm),)),
    ]
    return run(body, [grad2, normed1, inv1, shared, *d_near, d_far], hbm, outs, [], scratch, "ffn_back")


def ffn_rows(x, ctx, wo, wi, wd, small, shared, first, count, before):
    parts = len(wo)
    depth = x.shape[1]
    units, width = wi[0][0][0].shape[1], ctx[0].shape[1]
    tile = min(256, count)
    start = first // tile
    hbm = arrays(wo) + arrays(wi) + arrays(wd)
    last_inputs = [] if before is None else [before]

    def body(*refs):
        it = iter(refs)
        x_ref = next(it)
        ctx_refs = [next(it) for _ in range(parts)]
        small_refs = [next(it) for _ in range(parts)]
        shared_ref = next(it)
        wo_refs, wi_refs, wd_refs = take(it, wo), take(it, wi), take(it, wd)
        for _ in last_inputs:
            next(it)
        out_ref, wo_v, wi_v, wd_v, sems = (next(it) for _ in range(5))
        out_copies = flat(stacked_copies(wo_refs, wo_v, sems, 0, 1))
        near = len(flat(wo))
        in_copies = stacked_copies(wi_refs, wi_v, sems, near, 1)
        down_copies = stacked_copies(wd_refs, wd_v, sems, near + len(flat(wi)), 1)
        opening = pl.program_id(0) == 0

        @pl.when(opening)
        def _():
            start_all(out_copies)
            for part in range(parts):
                start_all(in_copies[part] + down_copies[part])
            wait_all(out_copies)

        attn_sum = x_ref[...].astype(F32) + shared_ref[0:1, :]
        for part in range(parts):
            attn_sum = attn_sum + nn(ctx_refs[part][...], wo_v[part])
        hidden, _, _ = norm_forward(attn_sum, shared_ref[2:3, :], shared_ref[4:5, :])
        low = hidden.astype(BF)
        total = hidden + shared_ref[1:2, :]
        for part in range(parts):

            @pl.when(opening)
            def _():
                wait_all(in_copies[part] + down_copies[part])

            pre = nn(low, wi_v[part]) + small_refs[part][0:1, :]
            act = (pre * erf_gelu(pre)).astype(BF)
            total = total + nn(act, wd_v[part])
        out_ref[...] = norm_forward(total, shared_ref[3:4, :], shared_ref[5:6, :])[0].astype(BF)

    return pl.pallas_call(
        body,
        grid=(count // tile,),
        in_specs=[
            pl.BlockSpec((tile, depth), lambda i: (i + start, 0)),
            *[pl.BlockSpec((tile, width), lambda i: (i + start, 0))] * parts,
            *[shaped(a.shape) for a in small],
            shaped(shared.shape),
            *[ANY_SPEC] * (len(hbm) + len(last_inputs)),
        ],
        out_specs=pl.BlockSpec((tile, depth), lambda i: (i + start, 0)),
        out_shape=jax.ShapeDtypeStruct(x.shape, BF),
        input_output_aliases={} if before is None else {2 + 2 * parts + len(hbm): 0},
        scratch_shapes=[
            pltpu.VMEM((parts, width, depth), BF),
            pltpu.VMEM((parts, depth, units), BF),
            pltpu.VMEM((parts, units, depth), BF),
            pltpu.SemaphoreType.DMA((len(hbm),)),
        ],
        cost_estimate=SMALL,
        name="ffn_rows",
    )(x, *ctx, *small, shared, *hbm, *last_inputs)


def input_gradient(picked, grad1, dq, dk, dv, wq, seqs):
    parts = len(dq)
    slots = picked.shape[1]
    depth = grad1.shape[1]
    rows, width = dk[0].shape[0] // seqs, dk[0].shape[1]
    hbm = arrays(wq)

    def body(*refs):
        it = iter(refs)
        pick_ref, grad1_ref = next(it), next(it)
        dq_refs = [next(it) for _ in range(parts)]
        dk_refs = [next(it) for _ in range(parts)]
        dv_refs = [next(it) for _ in range(parts)]
        wq_refs = take(it, wq)
        out_ref, wq_v, sems = next(it), next(it), next(it)
        copies = flat(stacked_copies(wq_refs, wq_v, sems, 0, 1))
        seq = pl.program_id(0)

        @pl.when(seq == 0)
        def _():
            start_all(copies)
            wait_all(copies)

        chosen = grad1_ref[...]
        for part in range(parts):
            chosen = chosen + nn(dq_refs[part][...], wq_v[part, 0:width, :])
        high = chosen.astype(BF)
        rest = (chosen - high.astype(F32)).astype(BF)
        spread = spread_of(pick_ref[pl.ds(lax.axis_index("tp") * seqs + seq, 1), :], rows)
        total = nn(spread, high) + nn(spread, rest)
        for part in range(parts):
            total = total + nn(dk_refs[part][...], wq_v[part, width : 2 * width, :])
            total = total + nn(dv_refs[part][...], wq_v[part, 2 * width : 3 * width, :])
        out_ref[...] = total.astype(BF)

    row_spec = pl.BlockSpec((rows, width), lambda s: (s, 0))
    return pl.pallas_call(
        body,
        grid=(seqs,),
        in_specs=[
            whole(picked.shape),
            pl.BlockSpec((slots, depth), lambda s: (s, 0)),
            *[pl.BlockSpec((slots, width), lambda s: (s, 0))] * parts,
            *[row_spec] * (2 * parts),
            *[ANY_SPEC] * len(hbm),
        ],
        out_specs=pl.BlockSpec((rows, depth), lambda s: (s, 0)),
        out_shape=jax.ShapeDtypeStruct((seqs * rows, depth), BF),
        scratch_shapes=[pltpu.VMEM((parts, 3 * width, depth), BF), pltpu.SemaphoreType.DMA((len(hbm),))],
        cost_estimate=SMALL,
        name="input_gradient",
    )(picked, grad1, *dq, *dk, *dv, *hbm)


def bits_of(count):
    return [1 << b for b in range(count.bit_length() - 1)]


def swap(value, axis, bit):
    count = lax.axis_size(axis)
    return lax.ppermute(value, axis, [(i, i ^ bit) for i in range(count)])


def half_of(value, bit, own):
    half = value.shape[0] // 2
    side = (lax.axis_index("dp") // bit) % 2
    return lax.dynamic_slice_in_dim(value, jnp.where(side == 0, 0, half) if own else jnp.where(side == 0, half, 0), half, 0)


def joined(own, got, bit):
    side = (lax.axis_index("dp") // bit) % 2
    return jnp.concatenate([jnp.where(side == 0, own, got), jnp.where(side == 0, got, own)], axis=0)


def add(*values):
    total = values[0].astype(F32)
    for value in values[1:]:
        total = total + value.astype(F32)
    return total.astype(BF)


def scatter(value, bit, *after):
    sent, kept = half_of(value, bit, False), half_of(value, bit, True)
    return add(tie(kept, *after), swap(sent, "dp", bit))


def gather(value, bit):
    return joined(value, swap(value, "dp", bit), bit)


def on_device(
    tokens, w_qkv, qv_bias, w_out, out_bias, w_in, in_bias, w_down, down_bias, norm_gain, norm_shift, valid_len, picked, d_out
):
    parts = lax.axis_size("tp")
    rank = lax.axis_index("tp")
    seqs = valid_len.shape[0] // parts
    depth = tokens.shape[1]
    width = w_qkv.shape[2]
    core, far = 1, 2
    dp_bits = bits_of(lax.axis_size("dp"))

    shared = jnp.concatenate([out_bias[None], down_bias[None], norm_gain, norm_shift, jnp.zeros((2, depth), F32)], axis=0)
    small = [jnp.concatenate([in_bias[None], jnp.pad(qv_bias, ((0, 5), (0, depth - width)))], axis=0)]
    small += [swap(small[0], "tp", core)]
    wq = w_qkv.transpose(0, 2, 1).reshape(3 * width, depth)
    qo_far = swap(jnp.concatenate([half_of(wq, 1, True), half_of(w_out, 1, True)], axis=0), "tp", far)
    wq_near = swap(wq, "tp", core)
    ready = small[1]
    small_far = swap(jnp.concatenate(small, axis=0), "tp", far)
    small += [small_far[:8], small_far[8:]]

    def forward(j, x, pieces):
        return attend_forward(valid_len, x, pieces, width, small[j], picked, seqs)

    out0 = forward(0, tie(tokens, ready), [wq])
    cut = w_down.shape[0] // 2
    ff_far = swap(tie(jnp.concatenate([half_of(w_in, 1, True), half_of(w_down[:cut], 1, True)], axis=0), small_far, out0[0]), "tp", far)
    fd_far = swap(tie(half_of(w_down[cut:], 2, True), small_far, out0[0]), "tp", far)
    qo_far = tie(qo_far, out0[0])
    qo_rest, qo_far_core = swap(qo_far, "dp", 1), swap(qo_far, "tp", core)
    out1 = forward(1, tie(tokens, qo_far), [wq_near])
    qo_rest = tie(qo_rest, out1[0])
    qo_rest_core = swap(qo_rest, "tp", core)
    wo_near = swap(tie(w_out, qo_rest), "tp", core)
    wi_near, wd_near = swap(tie(w_in, ready), "tp", core), swap(tie(w_down, ready), "tp", core)
    out2 = forward(2, tie(tokens, qo_rest, qo_far_core, wi_near, wd_near), [qo_far, qo_rest])
    ff_far = tie(ff_far, out2[0])
    rows_in = w_in.shape[0] // 2
    ff_rest = swap(ff_far, "dp", 1)
    ff_far_core = swap(ff_far, "tp", core)
    out3 = forward(3, tie(tokens, ff_far), [qo_far_core, qo_rest_core])
    fd_far = tie(fd_far, out3[0])
    fd_rest, fd_far_core = swap(fd_far, "dp", 2), swap(fd_far, "tp", core)
    q_sel, k, v, ctx, ctx_sel = zip(out0, out1, out2, out3)
    rows_q = 3 * width // 2

    def pieces(own, near, far_pieces, core_pieces):
        return [[(own, 0)], [(near, 0)], far_pieces, core_pieces]

    wq = pieces(wq, wq_near, [(qo_far, 0), (qo_rest, 0)], [(qo_far_core, 0), (qo_rest_core, 0)])
    wo = pieces(w_out, wo_near, [(qo_far, rows_q), (qo_rest, rows_q)], [(qo_far_core, rows_q), (qo_rest_core, rows_q)])
    near_in, near_down = [[(w_in, 0)], [(wi_near, 0)]], [[(w_down, 0)], [(wd_near, 0)]]
    prep = ffn_prep(picked, tie(tokens, fd_far), d_out, ctx_sel, wo, near_in, near_down, small[:2], shared, seqs)
    *act, slope_near, x_sel, cot, low, ffn_sum, normed1, inv1 = prep
    low_near, act_near = swap(low, "tp", core), swap(act[1], "tp", core)
    ff_rest, fd_rest = tie((ff_rest, fd_rest), low)
    ff_rest_core, fd_rest_core = swap(ff_rest, "tp", core), swap(fd_rest, "tp", core)
    wi = near_in + [[(ff_far, 0), (ff_rest, 0)], [(ff_far_core, 0), (ff_rest_core, 0)]]
    wd = near_down + [
        [(ff_far, rows_in), (ff_rest, rows_in), (fd_far, 0), (fd_rest, 0)],
        [(ff_far_core, rows_in), (ff_rest_core, rows_in), (fd_far_core, 0), (fd_rest_core, 0)],
    ]

    sent, g2, slope_far, grad2, vec = ffn_front(low, ffn_sum, cot, wi[2:], wd[2:], small[2:], shared)
    act_got = swap(sent, "tp", far)
    g2_near = swap(g2, "tp", core)
    *d_near, d_far, vec_mid = ffn_mid(g2, low, [slope_near, slope_far], wd)
    d_got, d_got_near = swap(d_far, "tp", far), swap(d_near[1], "tp", core)
    g1, grad1, vec_back, *d_ctx = ffn_back(tie(grad2, act_near, low_near, g2_near), d_near, d_far, normed1, inv1, shared, wi, wo, width)
    count = low.shape[0]

    def backward(j, x):
        return attend_backward(j, valid_len, q_sel[j], k[j], v[j], d_ctx[j], x, x_sel, ctx_sel[j], g1, seqs)

    def rows_of(first, count, before, *after):
        return ffn_rows(tie(tokens, *after), ctx, wo, wi, wd, small, shared, first, count, before)

    def finish(value, bits):
        for bit in bits:
            value = scatter(value, bit) if bit != last else add(value, swap(value, "dp", bit))
        return value

    def spread_out(value, bits):
        for bit in reversed(bits):
            value = gather(value, bit)
        return value

    half_rows, last = tokens.shape[0] // 2, dp_bits[-1]
    out3 = backward(3, tie(tokens, d_got_near))
    out2 = backward(2, tie(tokens, out3[0]))
    act_got = tie(act_got, out2[0])
    act_diag = swap(act_got[count:], "tp", core)
    out1 = backward(1, tie(tokens, out2[0], act_got))
    total_a = pair_sums(
        [
            ((tie(act[0], out1[0]), 0), (g2, 0)),
            ((act_near, 0), (g2_near, 0)),
            ((act_got, 0), (act_got, 2)),
            ((act_diag, 0), (act_diag, 1)),
        ]
    )
    sent_a = half_of(total_a, dp_bits[0], False)
    out0 = backward(0, tie(tokens, out1[0], sent_a))
    dq, dk, dv, sums, g_heads = zip(out0, out1, out2, out3)
    d_got = tie(d_got, out0[0])
    d_diag = swap(d_got[count:], "tp", core)
    far_c = add(tie(out2[4], out1[0]), swap(tie(out3[4], out2[0]), "tp", core))
    near_c = g_heads[0], swap(tie(g_heads[1], out0[0]), "tp", core)
    line = jnp.concatenate([vec + vec_mid + vec_back, sums[0] + sums[1] + sums[2] + sums[3]], axis=0)
    total_a = add(tie(half_of(total_a, dp_bits[0], True), far_c), swap(sent_a, "dp", dp_bits[0]))
    sent_a = half_of(total_a, dp_bits[1], False)
    total_b = pair_sums(
        [
            ((tie(low, sent_a), 0), (d_near[0], 0)),
            ((low_near, 0), (d_got_near, 0)),
            ((d_got, 2), (d_got, 0)),
            ((d_diag, 1), (d_diag, 0)),
        ]
    )
    sent_b = half_of(total_b, dp_bits[0], False)
    out_first = rows_of(0, half_rows, None, line, sent_b)
    total_a = add(tie(half_of(total_a, dp_bits[1], True), out_first), swap(sent_a, "dp", dp_bits[1]))
    for bit in dp_bits[2:-1]:
        total_a = scatter(total_a, bit)
    total_b = add(tie(half_of(total_b, dp_bits[0], True), out_first), swap(sent_b, "dp", dp_bits[0]))
    sent_b = half_of(total_b, dp_bits[1], False)
    total_c = add(*tie(near_c, out_first), swap(far_c, "tp", far))
    cut = far_c.shape[0] // 2
    other = [dp_bits[1], dp_bits[0], *dp_bits[2:]]
    total_c, rest_c = total_c[:cut], total_c[cut:]
    sent_c, sent_d = half_of(total_c, dp_bits[0], False), half_of(rest_c, other[0], False)
    d_tokens = input_gradient(tie(picked, total_a, sent_b, sent_c, sent_d), grad1, dq, dk, dv, wq, seqs)
    total_a = add(tie(total_a, d_tokens), swap(total_a, "dp", last))
    total_b = add(tie(half_of(total_b, dp_bits[1], True), d_tokens), swap(sent_b, "dp", dp_bits[1]))
    for bit in dp_bits[2:-1]:
        total_b = scatter(total_b, bit)
    total_c = add(tie(half_of(total_c, dp_bits[0], True), d_tokens), swap(sent_c, "dp", dp_bits[0]))
    rest_c = add(tie(half_of(rest_c, other[0], True), d_tokens), swap(sent_d, "dp", other[0]))
    sent_c, sent_d = half_of(total_c, dp_bits[1], False), half_of(rest_c, other[1], False)
    line = tie(line, d_tokens)
    out_second = rows_of(half_rows, half_rows // 2, out_first, total_a, total_b, sent_c, sent_d, line)
    for bit in reversed(dp_bits[2:-1]):
        total_a = gather(total_a, bit)
    total_a = joined(tie(total_a, out_second), swap(total_a, "dp", dp_bits[1]), dp_bits[1])
    total_b = add(tie(total_b, out_second), swap(total_b, "dp", last))
    for bit in reversed(dp_bits[2:-1]):
        total_b = gather(total_b, bit)
    total_c = add(tie(half_of(total_c, dp_bits[1], True), out_second), swap(sent_c, "dp", dp_bits[1]))
    rest_c = add(tie(half_of(rest_c, other[1], True), out_second), swap(sent_d, "dp", other[1]))
    for bit in dp_bits[2:-1]:
        total_c, rest_c = scatter(total_c, bit), scatter(rest_c, bit)
    line = tie(line, out_second) + swap(line, "tp", core)
    out_third = rows_of(half_rows + half_rows // 2, half_rows // 2, out_second, total_a, total_b, total_c, rest_c, line)
    total_a = joined(tie(total_a, out_third), swap(total_a, "dp", dp_bits[0]), dp_bits[0])
    total_b = joined(tie(total_b, out_third), swap(total_b, "dp", dp_bits[1]), dp_bits[1])
    total_c = add(tie(total_c, out_third), swap(total_c, "dp", last))
    rest_c = add(tie(rest_c, out_third), swap(rest_c, "dp", last))
    total_c, rest_c = tie((total_c, rest_c), total_b)
    rest_c = tie(rest_c, total_a)
    line = tie(line, total_c, rest_c) + swap(line, "dp", dp_bits[0])
    for bit in dp_bits[1:2]:
        line = line + swap(line, "dp", bit)
    for bit in dp_bits[2:]:
        line = line + swap(line, "dp", bit)
    total_c, rest_c = spread_out(total_c, dp_bits[1:-1]), spread_out(rest_c, other[1:-1])
    line = tie(line, total_c)
    line = line + swap(line, "tp", far)
    total_b = gather(total_b, dp_bits[0])
    total_c, rest_c = gather(total_c, dp_bits[0]), gather(rest_c, other[0])
    total_c = jnp.concatenate([total_c.astype(F32), rest_c.astype(F32)], axis=0)
    own = lax.dynamic_slice_in_dim(line, 8 + rank, 1, 0)[0]
    own_q = lax.dynamic_slice(line, (16 + rank, 0), (1, width))
    own_v = lax.dynamic_slice(line, (16 + PARTS + rank, 0), (1, width))
    return (
        out_third,
        d_tokens,
        total_c[: 3 * width].reshape(3, width, depth).transpose(0, 2, 1),
        jnp.concatenate([own_q, own_v], axis=0),
        total_c[3 * width :],
        line[3],
        total_b.astype(F32),
        own,
        total_a.astype(F32),
        line[0],
        jnp.stack([line[4], line[1]]),
        jnp.stack([line[5], line[2]]),
    )


def solution(mesh):
    placed = (
        P(("dp", "tp"), None),
        P(None, None, "tp"),
        P(None, "tp"),
        P("tp", None),
        P(),
        P(None, "tp"),
        P("tp"),
        P("tp", None),
        P(),
        P(),
        P(),
        P("dp"),
        P("dp", None),
        P(("dp", "tp"), None),
    )
    return jax.shard_map(
        on_device,
        mesh=mesh,
        in_specs=placed,
        out_specs=(
            P(("dp", "tp"), None),
            P(("dp", "tp"), None),
            P(None, None, "tp"),
            P(None, "tp"),
            P("tp", None),
            P(),
            P(None, "tp"),
            P("tp"),
            P("tp", None),
            P(),
            P(),
            P(),
        ),
        check_vma=False,
    )
```

```python
import jax
import jax.numpy as jnp
from jax import lax
from jax.experimental import pallas as pl
from jax.experimental.pallas import tpu as pltpu
from jax.sharding import PartitionSpec as P

HD = 64
SCALE = HD ** (-0.5)
NORM_EPS = 1e-06
MASKED = -1e30
HALF_ROOT = 0.5 ** 0.5
DENSITY = 0.3989422804014327
PARTS = 4
BF = jnp.bfloat16
F32 = jnp.float32


def nn(left, right):
    return lax.dot_general(left, right, (((1,), (0,)), ((), ())), preferred_element_type=F32)


def nt(left, right):
    return lax.dot_general(left, right, (((1,), (1,)), ((), ())), preferred_element_type=F32)


def tn(left, right):
    return lax.dot_general(left, right, (((0,), (0,)), ((), ())), preferred_element_type=F32)


def head_masks(width, dtype=BF):
    lane = lax.broadcasted_iota(jnp.int32, (1, width), 1) // HD
    return [(lane == head).astype(dtype) for head in range(width // HD)]


def spread_of(picks, length):
    slots = picks.shape[1]
    return (lax.broadcasted_iota(jnp.int32, (length, slots), 0) == picks).astype(F32).astype(BF)


def whole(shape):
    zeros = (0,) * len(shape)
    return pl.BlockSpec(shape, lambda *_: zeros)


def norm_forward(values, gain, shift):
    average = jnp.mean(values, axis=1, keepdims=True)
    centered = values - average
    inv_std = lax.rsqrt(jnp.mean(centered * centered, axis=1, keepdims=True) + NORM_EPS)
    normed = centered * inv_std
    return normed * gain + shift, normed, inv_std


def norm_backward(grad, normed, inv_std, gain):
    scaled = grad * gain
    first = jnp.mean(scaled, axis=1, keepdims=True)
    second = jnp.mean(scaled * normed, axis=1, keepdims=True)
    return inv_std * (scaled - first - normed * second)


def tie(value, *others):
    return lax.optimization_barrier((value, others))[0]


SMALL = pl.CostEstimate(flops=1024, transcendentals=0, bytes_accessed=1024)


def col_sum(values):
    return jnp.sum(values, axis=0, keepdims=True)


def piece_copies(pieces, target, sems, first, bit):
    rows = target.shape[0]
    if len(pieces) == 1:
        return [pltpu.make_async_copy(pieces[0][0], target, sems.at[first])]
    half, step = rows // 2, rows // len(pieces)
    if len(pieces) == 4:
        upper = piece_copies(pieces[:2], target.at[pl.ds(0, half), :], sems, first, bit)
        return upper + piece_copies(pieces[2:], target.at[pl.ds(half, half), :], sems, first + 2, 2 * bit)
    own = ((lax.axis_index("dp") // bit) % 2) * half
    copies = []
    for n, (ref, skip) in enumerate(pieces):
        base = own if n * step < half else half - own
        start = pl.multiple_of(base + (n * step) % half, step)
        copies.append(pltpu.make_async_copy(ref.at[pl.ds(skip, step), :], target.at[pl.ds(start, step), :], sems.at[first + n]))
    return copies


def stacked_copies(pieces, target, sems, first, bit):
    copies = []
    for part, refs in enumerate(pieces):
        copies.append(piece_copies(refs, target.at[part], sems, first, bit))
        first += len(refs)
    return copies


def take(it, pieces):
    return [[(next(it), skip) for _, skip in piece] for piece in pieces]


def flat(pieces):
    return [p for piece in pieces for p in piece]


def arrays(pieces):
    return [array for array, _ in flat(pieces)]


def start_all(copies):
    for copy in copies:
        copy.start()


def wait_all(copies):
    for copy in copies:
        copy.wait()


ANY_SPEC = pl.BlockSpec(memory_space=pl.ANY)


def shaped(shape):
    return pl.BlockSpec(shape, lambda *_: (0,) * len(shape))


def attend_body(len_ref, x_ref, small_ref, pick_ref, *rest, count):
    w_refs = [(ref, 0) for ref in rest[:count]]
    q_sel_ref, k_ref, v_ref, ctx_ref, ctx_sel_ref, ext_ref, w_ref, sems = rest[count:]
    rows, width = k_ref.shape
    seq = pl.program_id(0)
    row = lax.axis_index("tp") * pl.num_programs(0) + seq
    length = len_ref[row]
    copies = piece_copies(w_refs, w_ref, sems, 0, 1)

    @pl.when(seq == 0)
    def _():
        start_all(copies)
        wait_all(copies)

    x = x_ref[...]
    queries = (nt(x, w_ref[0:width, :]) + small_ref[1:2, :width]).astype(BF)
    key_rows = nt(x, w_ref[width : 2 * width, :]).astype(BF)
    values = (nt(x, w_ref[2 * width : 3 * width, :]) + small_ref[2:3, :width]).astype(BF)
    k_ref[...] = key_rows
    v_ref[...] = values
    ext_ref[:, :width] = values
    ext_ref[:, width:] = jnp.ones((rows, ext_ref.shape[1] - width), BF)
    spread = spread_of(pick_ref[pl.ds(row, 1), :], rows)
    q_sel_ref[...] = tn(spread, queries).astype(BF)
    scaled = queries * jnp.asarray(SCALE, BF)
    masks = head_masks(width)
    tile = min(256, rows)
    keep = lax.broadcasted_iota(jnp.int32, (tile, rows), 1) < length
    for start in range(0, rows, tile):
        total = jnp.zeros((tile, width), F32)
        for mask in masks:
            logits = nt(scaled[start : start + tile] * mask, key_rows)
            logits = jnp.where(keep, logits, MASKED)
            peak = jnp.max(logits, axis=1, keepdims=True)
            probs = jnp.exp(logits - peak).astype(BF)
            mixed = nn(probs, ext_ref[...])
            share = mixed[:, :width] / mixed[:, width : width + 1]
            total = jnp.where(mask.astype(F32) > 0.5, share, total)
        ctx_ref[start : start + tile, :] = total.astype(BF)
    ctx_sel_ref[...] = tn(spread, ctx_ref[...]).astype(BF)


def attend_forward(lengths, x, pieces, width, small, picked, seqs):
    slots = picked.shape[1]
    rows = x.shape[0] // seqs
    depth = x.shape[1]
    ext = -(-(width + 1) // 128) * 128
    row_spec = pl.BlockSpec((rows, width), lambda s, _: (s, 0))
    sel_spec = pl.BlockSpec((slots, width), lambda s, _: (s, 0))
    return pl.pallas_call(
        lambda *refs: attend_body(*refs, count=len(pieces)),
        grid_spec=pltpu.PrefetchScalarGridSpec(
            num_scalar_prefetch=1,
            grid=(seqs,),
            in_specs=[
                pl.BlockSpec((rows, depth), lambda s, _: (s, 0)),
                whole(small.shape),
                whole(picked.shape),
                *[ANY_SPEC] * len(pieces),
            ],
            out_specs=[sel_spec, row_spec, row_spec, row_spec, sel_spec],
            scratch_shapes=[
                pltpu.VMEM((rows, ext), BF),
                pltpu.VMEM((3 * width, depth), BF),
                pltpu.SemaphoreType.DMA((len(pieces),)),
            ],
        ),
        out_shape=[
            jax.ShapeDtypeStruct((seqs * slots, width), BF),
            jax.ShapeDtypeStruct((seqs * rows, width), BF),
            jax.ShapeDtypeStruct((seqs * rows, width), BF),
            jax.ShapeDtypeStruct((seqs * rows, width), BF),
            jax.ShapeDtypeStruct((seqs * slots, width), BF),
        ],
        cost_estimate=SMALL,
        name="attend_forward",
    )(lengths, x, small, picked, *pieces)


def attend_back_body(
    len_ref, q_ref, k_ref, v_ref, d_ctx_ref, x_ref, x_sel_ref, ctx_sel_ref, g1_ref, dq_ref, dk_ref, dv_ref, sums_ref, grad_ref, acc_ref, *, part
):
    rows, width = k_ref.shape
    slots = q_ref.shape[0]
    seq = pl.program_id(0)
    rank = lax.axis_index("tp")
    length = len_ref[rank * pl.num_programs(0) + seq]
    masks = head_masks(width)
    queries, d_ctx = q_ref[...], d_ctx_ref[...]
    key_rows, values = k_ref[...], v_ref[...]
    q_stack = jnp.concatenate([queries * mask for mask in masks], axis=0)
    d_stack = jnp.concatenate([d_ctx * mask for mask in masks], axis=0)
    logits = nt(key_rows, q_stack * jnp.asarray(SCALE, BF))
    keep = lax.broadcasted_iota(jnp.int32, logits.shape, 0) < length
    logits = jnp.where(keep, logits, MASKED)
    grown = jnp.exp(logits - jnp.max(logits, axis=0, keepdims=True))
    probs = grown * (1.0 / jnp.sum(grown, axis=0, keepdims=True))
    d_probs = nt(values, d_stack)
    inner = jnp.sum(probs * d_probs, axis=0, keepdims=True)
    d_raw = (probs * (d_probs - inner) * SCALE).astype(BF)
    d_keys = nn(d_raw, q_stack).astype(BF)
    dk_ref[...] = d_keys
    d_values = nn(probs.astype(BF), d_stack).astype(BF)
    dv_ref[...] = d_values
    dq_stack = tn(d_raw, key_rows)
    dq = jnp.zeros((slots, width), F32)
    for head, mask in enumerate(masks):
        dq = jnp.where(mask.astype(F32) > 0.5, dq_stack[head * slots : (head + 1) * slots], dq)
    dq = dq.astype(BF)
    dq_ref[...] = dq

    @pl.when(seq == 0)
    def _():
        acc_ref[...] = jnp.zeros(acc_ref.shape, F32)
        sums_ref[...] = jnp.zeros(sums_ref.shape, F32)

    at = rank ^ part
    sums_ref[pl.ds(at, 1), 0:width] += col_sum(dq.astype(F32))
    sums_ref[pl.ds(PARTS + at, 1), 0:width] += col_sum(d_values.astype(F32))
    acc_ref[0:width, :] += tn(dq, x_sel_ref[...])
    acc_ref[width : 2 * width, :] += tn(d_keys, x_ref[...])
    acc_ref[2 * width : 3 * width, :] += tn(d_values, x_ref[...])
    acc_ref[3 * width : 4 * width, :] += tn(ctx_sel_ref[...], g1_ref[...])

    @pl.when(seq == pl.num_programs(0) - 1)
    def _():
        grad_ref[...] = acc_ref[...].astype(BF)


def attend_backward(part, lengths, q_sel, k, v, d_ctx, x, x_sel, ctx_sel, g1, seqs):
    rows, slots, width = k.shape[0] // seqs, q_sel.shape[0] // seqs, k.shape[1]
    depth = x.shape[1]
    row_spec = pl.BlockSpec((rows, width), lambda s, _: (s, 0))
    sel_spec = pl.BlockSpec((slots, width), lambda s, _: (s, 0))
    wide_spec = pl.BlockSpec((slots, depth), lambda s, _: (s, 0))
    return pl.pallas_call(
        lambda *refs: attend_back_body(*refs, part=part),
        grid_spec=pltpu.PrefetchScalarGridSpec(
            num_scalar_prefetch=1,
            grid=(seqs,),
            in_specs=[
                sel_spec,
                row_spec,
                row_spec,
                sel_spec,
                pl.BlockSpec((rows, depth), lambda s, _: (s, 0)),
                wide_spec,
                sel_spec,
                wide_spec,
            ],
            out_specs=[sel_spec, row_spec, row_spec, whole((2 * PARTS, depth)), whole((4 * width, depth))],
            scratch_shapes=[pltpu.VMEM((4 * width, depth), F32)],
        ),
        out_shape=[
            jax.ShapeDtypeStruct(q_sel.shape, BF),
            jax.ShapeDtypeStruct(k.shape, BF),
            jax.ShapeDtypeStruct(k.shape, BF),
            jax.ShapeDtypeStruct((2 * PARTS, depth), F32),
            jax.ShapeDtypeStruct((4 * width, depth), BF),
        ],
        cost_estimate=SMALL,
        name="attend_backward",
    )(lengths, q_sel, k, v, d_ctx, x, x_sel, ctx_sel, g1)


def erf_gelu(values):
    return 0.5 * (1.0 + lax.erf(values * HALF_ROOT))


def run(body, plain, hbm, outs, hbm_outs, scratch, name):
    return pl.pallas_call(
        body,
        grid=(1,),
        in_specs=[*[shaped(a.shape) for a in plain], *[ANY_SPEC] * len(hbm)],
        out_specs=[*[shaped(a.shape) for a in outs], *[ANY_SPEC] * len(hbm_outs)],
        out_shape=[*outs, *hbm_outs],
        scratch_shapes=scratch,
        cost_estimate=SMALL,
        name=name,
    )(*plain, *hbm)


def struct(dtype, *shape):
    return jax.ShapeDtypeStruct(shape, dtype)


def unit_part(low, wi, bias, slope_ref, n):
    pre = nn(low, wi) + bias
    chance = erf_gelu(pre)
    slope_ref[n] = chance + pre * (DENSITY * jnp.exp(-0.5 * pre * pre))
    return (pre * chance).astype(BF)


def ffn_prep(picked, x, d_out, ctx_sel, wo, wi, wd, small, shared, seqs):
    parts, near = len(wo), len(wi)
    slots = picked.shape[1]
    count, depth, units, width = seqs * slots, x.shape[1], wi[0][0][0].shape[1], ctx_sel[0].shape[1]
    plain = [picked, x, d_out, shared, *ctx_sel, *small]
    hbm = arrays(wo) + arrays(wi) + arrays(wd)

    def body(*refs):
        it = iter(refs)
        pick_ref, x_ref, d_out_ref, shared_ref = (next(it) for _ in range(4))
        ctx_refs = [next(it) for _ in range(parts)]
        small_refs = [next(it) for _ in range(near)]
        wo_refs, wi_refs, wd_refs = take(it, wo), take(it, wi), take(it, wd)
        act_refs = [next(it) for _ in range(near)]
        slope_ref, x_sel_ref, cot_ref, low_ref, sum_ref, normed1_ref, inv1_ref = (next(it) for _ in range(7))
        wo_v, wi_v, wd_v, sems = (next(it) for _ in range(4))
        out_copies = stacked_copies(wo_refs, wo_v, sems, 0, 1)
        first = len(flat(wo))
        in_copies = stacked_copies(wi_refs, wi_v, sems, first, 1)
        down_copies = stacked_copies(wd_refs, wd_v, sems, first + len(flat(wi)), 1)
        start_all(flat(out_copies) + flat(in_copies) + flat(down_copies))
        rows = x_ref.shape[0] // seqs
        for seq in range(seqs):
            at = lax.axis_index("tp") * seqs + seq
            spread = spread_of(pick_ref[pl.ds(at, 1), :], rows)
            x_sel_ref[seq * slots : (seq + 1) * slots, :] = tn(spread, x_ref[seq * rows : (seq + 1) * rows, :]).astype(BF)
            cot_ref[seq * slots : (seq + 1) * slots, :] = tn(spread, d_out_ref[seq * rows : (seq + 1) * rows, :]).astype(BF)
        attn_sum = x_sel_ref[...].astype(F32) + shared_ref[0:1, :]
        wait_all(flat(out_copies))
        for part in range(parts):
            attn_sum = attn_sum + nn(ctx_refs[part][...], wo_v[part])
        hidden, normed1, inv1 = norm_forward(attn_sum, shared_ref[2:3, :], shared_ref[4:5, :])
        low = hidden.astype(BF)
        low_ref[...] = low
        normed1_ref[...] = normed1
        inv1_ref[...] = inv1
        total = hidden + shared_ref[1:2, :]
        wait_all(flat(in_copies) + flat(down_copies))
        for n in range(near):
            act = unit_part(low, wi_v[n], small_refs[n][0:1, :], slope_ref, n)
            act_refs[n][...] = act
            total = total + nn(act, wd_v[n])
        sum_ref[...] = total

    outs = [
        *[struct(BF, count, units)] * near,
        struct(F32, near, count, units),
        struct(BF, count, depth),
        struct(BF, count, depth),
        struct(BF, count, depth),
        struct(F32, count, depth),
        struct(F32, count, depth),
        struct(F32, count, 1),
    ]
    scratch = [
        pltpu.VMEM((parts, width, depth), BF),
        pltpu.VMEM((near, depth, units), BF),
        pltpu.VMEM((near, units, depth), BF),
        pltpu.SemaphoreType.DMA((len(hbm),)),
    ]
    return run(body, plain, hbm, outs, [], scratch, "ffn_prep")


def ffn_front(low, total, cot, wi, wd, small, shared):
    far = len(wi)
    count, depth = low.shape
    units = wi[0][0][0].shape[1]
    plain = [low, total, cot, shared, *small]
    hbm = arrays(wi) + arrays(wd)

    def body(*refs):
        it = iter(refs)
        low_ref, sum_ref, cot_ref, shared_ref = (next(it) for _ in range(4))
        small_refs = [next(it) for _ in range(far)]
        wi_refs, wd_refs = take(it, wi), take(it, wd)
        sent_ref, g2_ref, slope_ref, grad2_ref, vec_ref = (next(it) for _ in range(5))
        wi_v, wd_v, sems = (next(it) for _ in range(3))
        in_copies = stacked_copies(wi_refs, wi_v, sems, 0, 1)
        down_copies = stacked_copies(wd_refs, wd_v, sems, len(flat(wi)), 1)
        for n in range(far):
            start_all(in_copies[n] + down_copies[n])
        low = low_ref[...]
        total = sum_ref[...]
        for n in range(far):
            wait_all(in_copies[n])
            act = unit_part(low, wi_v[n], small_refs[n][0:1, :], slope_ref, n)
            sent_ref[n * count : (n + 1) * count, :] = act
            wait_all(down_copies[n])
            total = total + nn(act, wd_v[n])
        _, normed2, inv2 = norm_forward(total, shared_ref[3:4, :], shared_ref[5:6, :])
        cotangent = cot_ref[...].astype(F32)
        grad2 = norm_backward(cotangent, normed2, inv2, shared_ref[3:4, :])
        vec_ref[...] = jnp.zeros(vec_ref.shape, F32)
        vec_ref[0:1, :] = col_sum(grad2)
        vec_ref[1:2, :] = col_sum(cotangent * normed2)
        vec_ref[2:3, :] = col_sum(cotangent)
        grad2_ref[...] = grad2
        g2 = grad2.astype(BF)
        g2_ref[...] = g2
        sent_ref[far * count :, :] = g2

    outs = [
        struct(BF, (far + 1) * count, units),
        struct(BF, count, depth),
        struct(F32, far, count, units),
        struct(F32, count, depth),
        struct(F32, 16, depth),
    ]
    scratch = [
        pltpu.VMEM((far, depth, units), BF),
        pltpu.VMEM((far, units, depth), BF),
        pltpu.SemaphoreType.DMA((len(hbm),)),
    ]
    return run(body, plain, hbm, outs, [], scratch, "ffn_front")


def ffn_mid(g2, low, slopes, wd):
    parts = len(wd)
    near = slopes[0].shape[0]
    count, depth = g2.shape
    units = slopes[0].shape[2]
    hbm = [*slopes, *arrays(wd)]

    def body(*refs):
        it = iter(refs)
        g2_ref, low_ref = next(it), next(it)
        slope_hbm = [next(it) for _ in slopes]
        wd_refs = take(it, wd)
        d_refs = [next(it) for _ in range(near)]
        sent_ref, vec_ref = next(it), next(it)
        wd_v, slope_v, sems, slope_sems = (next(it) for _ in range(4))
        down_copies = stacked_copies(wd_refs, wd_v, sems, 0, 1)
        sources = [ref.at[n] for ref in slope_hbm for n in range(ref.shape[0])]
        slope_copies = [pltpu.make_async_copy(sources[part], slope_v.at[part], slope_sems.at[part]) for part in range(parts)]
        for part in range(parts):
            start_all(down_copies[part] + [slope_copies[part]])
        vec_ref[...] = jnp.zeros(vec_ref.shape, F32)
        g2 = g2_ref[...]
        for part in range(parts):
            wait_all(down_copies[part] + [slope_copies[part]])
            d_pre = (nt(g2, wd_v[part]) * slope_v[part]).astype(BF)
            if part < near:
                d_refs[part][...] = d_pre
            else:
                sent_ref[(part - near) * count : (part - near + 1) * count, :] = d_pre
            at = 8 + (lax.axis_index("tp") ^ part)
            vec_ref[pl.ds(at, 1), :] = col_sum(d_pre.astype(F32))
        sent_ref[(parts - near) * count :, :] = low_ref[...]

    outs = [*[struct(BF, count, units)] * near, struct(BF, (parts - near + 1) * count, units), struct(F32, 16, depth)]
    scratch = [
        pltpu.VMEM((parts, units, depth), BF),
        pltpu.VMEM((parts, count, units), F32),
        pltpu.SemaphoreType.DMA((len(arrays(wd)),)),
        pltpu.SemaphoreType.DMA((parts,)),
    ]
    return run(body, [g2, low], hbm, outs, [], scratch, "ffn_mid")


def pair_sums(pairs):
    count = min(array.shape[0] for array, _ in pairs[0])
    width, depth = pairs[0][0][0].shape[1], pairs[0][1][0].shape[1]
    tile = min(256, width)

    def body(*refs):
        total = tn(refs[0][...], refs[1][...])
        for n in range(1, len(pairs)):
            total = total + tn(refs[2 * n][...], refs[2 * n + 1][...])
        refs[-1][...] = total.astype(BF)

    def left(block):
        return pl.BlockSpec((count, tile), lambda i: (block, i))

    def right(block):
        return pl.BlockSpec((count, depth), lambda i: (block, 0))

    return pl.pallas_call(
        body,
        grid=(width // tile,),
        in_specs=[spec for (_, a), (_, b) in pairs for spec in (left(a), right(b))],
        out_specs=pl.BlockSpec((tile, depth), lambda i: (i, 0)),
        out_shape=jax.ShapeDtypeStruct((width, depth), BF),
        cost_estimate=SMALL,
        name="pair_sums",
    )(*[array for (a, _), (b, _) in pairs for array in (a, b)])


def ffn_back(grad2, d_near, d_far, normed1, inv1, shared, wi, wo, width):
    parts, near = len(wi), len(d_near)
    count, depth = grad2.shape
    units = d_far.shape[1]
    hbm = arrays(wi) + arrays(wo)

    def body(*refs):
        it = iter(refs)
        grad2_ref, normed1_ref, inv1_ref, shared_ref = (next(it) for _ in range(4))
        near_refs = [next(it) for _ in range(near)]
        far_ref = next(it)
        wi_refs, wo_refs = take(it, wi), take(it, wo)
        g1_ref, grad1_ref, vec_ref = next(it), next(it), next(it)
        d_ctx_refs = [next(it) for _ in range(parts)]
        wi_v, wo_v, sems = (next(it) for _ in range(3))
        in_copies = stacked_copies(wi_refs, wi_v, sems, 0, 1)
        out_copies = stacked_copies(wo_refs, wo_v, sems, len(flat(wi)), 1)
        start_all(flat(in_copies) + flat(out_copies))
        d_hidden = grad2_ref[...]
        for part in range(parts):
            wait_all(in_copies[part])
            d_pre = near_refs[part][...] if part < near else far_ref[(part - near) * count : (part - near + 1) * count, :]
            d_hidden = d_hidden + nt(d_pre, wi_v[part])
        normed1 = normed1_ref[...]
        grad1 = norm_backward(d_hidden, normed1, inv1_ref[...], shared_ref[2:3, :])
        vec_ref[...] = jnp.zeros(vec_ref.shape, F32)
        vec_ref[3:4, :] = col_sum(grad1)
        vec_ref[4:5, :] = col_sum(d_hidden * normed1)
        vec_ref[5:6, :] = col_sum(d_hidden)
        grad1_ref[...] = grad1
        g1 = grad1.astype(BF)
        g1_ref[...] = g1
        wait_all(flat(out_copies))
        for part in range(parts):
            d_ctx_refs[part][...] = nt(g1, wo_v[part]).astype(BF)

    outs = [struct(BF, count, depth), struct(F32, count, depth), struct(F32, 16, depth), *[struct(BF, count, width)] * parts]
    scratch = [
        pltpu.VMEM((parts, depth, units), BF),
        pltpu.VMEM((parts, width, depth), BF),
        pltpu.SemaphoreType.DMA((len(hbm),)),
    ]
    return run(body, [grad2, normed1, inv1, shared, *d_near, d_far], hbm, outs, [], scratch, "ffn_back")


def ffn_rows(x, ctx, wo, wi, wd, small, shared, first, count, before):
    parts = len(wo)
    depth = x.shape[1]
    units, width = wi[0][0][0].shape[1], ctx[0].shape[1]
    tile = min(256, count)
    start = first // tile
    hbm = arrays(wo) + arrays(wi) + arrays(wd)
    last_inputs = [] if before is None else [before]

    def body(*refs):
        it = iter(refs)
        x_ref = next(it)
        ctx_refs = [next(it) for _ in range(parts)]
        small_refs = [next(it) for _ in range(parts)]
        shared_ref = next(it)
        wo_refs, wi_refs, wd_refs = take(it, wo), take(it, wi), take(it, wd)
        for _ in last_inputs:
            next(it)
        out_ref, wo_v, wi_v, wd_v, sems = (next(it) for _ in range(5))
        out_copies = flat(stacked_copies(wo_refs, wo_v, sems, 0, 1))
        near = len(flat(wo))
        in_copies = stacked_copies(wi_refs, wi_v, sems, near, 1)
        down_copies = stacked_copies(wd_refs, wd_v, sems, near + len(flat(wi)), 1)
        opening = pl.program_id(0) == 0

        @pl.when(opening)
        def _():
            start_all(out_copies)
            for part in range(parts):
                start_all(in_copies[part] + down_copies[part])
            wait_all(out_copies)

        attn_sum = x_ref[...].astype(F32) + shared_ref[0:1, :]
        for part in range(parts):
            attn_sum = attn_sum + nn(ctx_refs[part][...], wo_v[part])
        hidden, _, _ = norm_forward(attn_sum, shared_ref[2:3, :], shared_ref[4:5, :])
        low = hidden.astype(BF)
        total = hidden + shared_ref[1:2, :]
        for part in range(parts):

            @pl.when(opening)
            def _():
                wait_all(in_copies[part] + down_copies[part])

            pre = nn(low, wi_v[part]) + small_refs[part][0:1, :]
            act = (pre * erf_gelu(pre)).astype(BF)
            total = total + nn(act, wd_v[part])
        out_ref[...] = norm_forward(total, shared_ref[3:4, :], shared_ref[5:6, :])[0].astype(BF)

    return pl.pallas_call(
        body,
        grid=(count // tile,),
        in_specs=[
            pl.BlockSpec((tile, depth), lambda i: (i + start, 0)),
            *[pl.BlockSpec((tile, width), lambda i: (i + start, 0))] * parts,
            *[shaped(a.shape) for a in small],
            shaped(shared.shape),
            *[ANY_SPEC] * (len(hbm) + len(last_inputs)),
        ],
        out_specs=pl.BlockSpec((tile, depth), lambda i: (i + start, 0)),
        out_shape=jax.ShapeDtypeStruct(x.shape, BF),
        input_output_aliases={} if before is None else {2 + 2 * parts + len(hbm): 0},
        scratch_shapes=[
            pltpu.VMEM((parts, width, depth), BF),
            pltpu.VMEM((parts, depth, units), BF),
            pltpu.VMEM((parts, units, depth), BF),
            pltpu.SemaphoreType.DMA((len(hbm),)),
        ],
        cost_estimate=SMALL,
        name="ffn_rows",
    )(x, *ctx, *small, shared, *hbm, *last_inputs)


def input_gradient(picked, grad1, dq, dk, dv, wq, seqs):
    parts = len(dq)
    slots = picked.shape[1]
    depth = grad1.shape[1]
    rows, width = dk[0].shape[0] // seqs, dk[0].shape[1]
    hbm = arrays(wq)

    def body(*refs):
        it = iter(refs)
        pick_ref, grad1_ref = next(it), next(it)
        dq_refs = [next(it) for _ in range(parts)]
        dk_refs = [next(it) for _ in range(parts)]
        dv_refs = [next(it) for _ in range(parts)]
        wq_refs = take(it, wq)
        out_ref, wq_v, sems = next(it), next(it), next(it)
        copies = flat(stacked_copies(wq_refs, wq_v, sems, 0, 1))
        seq = pl.program_id(0)

        @pl.when(seq == 0)
        def _():
            start_all(copies)
            wait_all(copies)

        chosen = grad1_ref[...]
        for part in range(parts):
            chosen = chosen + nn(dq_refs[part][...], wq_v[part, 0:width, :])
        high = chosen.astype(BF)
        rest = (chosen - high.astype(F32)).astype(BF)
        spread = spread_of(pick_ref[pl.ds(lax.axis_index("tp") * seqs + seq, 1), :], rows)
        total = nn(spread, high) + nn(spread, rest)
        for part in range(parts):
            total = total + nn(dk_refs[part][...], wq_v[part, width : 2 * width, :])
            total = total + nn(dv_refs[part][...], wq_v[part, 2 * width : 3 * width, :])
        out_ref[...] = total.astype(BF)

    row_spec = pl.BlockSpec((rows, width), lambda s: (s, 0))
    return pl.pallas_call(
        body,
        grid=(seqs,),
        in_specs=[
            whole(picked.shape),
            pl.BlockSpec((slots, depth), lambda s: (s, 0)),
            *[pl.BlockSpec((slots, width), lambda s: (s, 0))] * parts,
            *[row_spec] * (2 * parts),
            *[ANY_SPEC] * len(hbm),
        ],
        out_specs=pl.BlockSpec((rows, depth), lambda s: (s, 0)),
        out_shape=jax.ShapeDtypeStruct((seqs * rows, depth), BF),
        scratch_shapes=[pltpu.VMEM((parts, 3 * width, depth), BF), pltpu.SemaphoreType.DMA((len(hbm),))],
        cost_estimate=SMALL,
        name="input_gradient",
    )(picked, grad1, *dq, *dk, *dv, *hbm)


def bits_of(count):
    return [1 << b for b in range(count.bit_length() - 1)]


def swap(value, axis, bit):
    count = lax.axis_size(axis)
    return lax.ppermute(value, axis, [(i, i ^ bit) for i in range(count)])


def half_of(value, bit, own):
    half = value.shape[0] // 2
    side = (lax.axis_index("dp") // bit) % 2
    return lax.dynamic_slice_in_dim(value, jnp.where(side == 0, 0, half) if own else jnp.where(side == 0, half, 0), half, 0)


def joined(own, got, bit):
    side = (lax.axis_index("dp") // bit) % 2
    return jnp.concatenate([jnp.where(side == 0, own, got), jnp.where(side == 0, got, own)], axis=0)


def add(*values):
    total = values[0].astype(F32)
    for value in values[1:]:
        total = total + value.astype(F32)
    return total.astype(BF)


def scatter(value, bit, *after):
    sent, kept = half_of(value, bit, False), half_of(value, bit, True)
    return add(tie(kept, *after), swap(sent, "dp", bit))


def gather(value, bit):
    return joined(value, swap(value, "dp", bit), bit)


def on_device(
    tokens, w_qkv, qv_bias, w_out, out_bias, w_in, in_bias, w_down, down_bias, norm_gain, norm_shift, valid_len, picked, d_out
):
    parts = lax.axis_size("tp")
    rank = lax.axis_index("tp")
    seqs = valid_len.shape[0] // parts
    depth = tokens.shape[1]
    width = w_qkv.shape[2]
    core, far = 1, 2
    dp_bits = bits_of(lax.axis_size("dp"))

    shared = jnp.concatenate([out_bias[None], down_bias[None], norm_gain, norm_shift, jnp.zeros((2, depth), F32)], axis=0)
    small = [jnp.concatenate([in_bias[None], jnp.pad(qv_bias, ((0, 5), (0, depth - width)))], axis=0)]
    small += [swap(small[0], "tp", core)]
    wq = w_qkv.transpose(0, 2, 1).reshape(3 * width, depth)
    qo_far = swap(jnp.concatenate([half_of(wq, 1, True), half_of(w_out, 1, True)], axis=0), "tp", far)
    wq_near = swap(wq, "tp", core)
    ready = small[1]
    small_far = swap(jnp.concatenate(small, axis=0), "tp", far)
    small += [small_far[:8], small_far[8:]]

    def forward(j, x, pieces):
        return attend_forward(valid_len, x, pieces, width, small[j], picked, seqs)

    out0 = forward(0, tie(tokens, ready), [wq])
    cut = w_down.shape[0] // 2
    ff_far = swap(tie(jnp.concatenate([half_of(w_in, 1, True), half_of(w_down[:cut], 1, True)], axis=0), small_far, out0[0]), "tp", far)
    fd_far = swap(tie(half_of(w_down[cut:], 2, True), small_far, out0[0]), "tp", far)
    qo_far = tie(qo_far, out0[0])
    qo_rest, qo_far_core = swap(qo_far, "dp", 1), swap(qo_far, "tp", core)
    out1 = forward(1, tie(tokens, qo_far), [wq_near])
    qo_rest = tie(qo_rest, out1[0])
    qo_rest_core = swap(qo_rest, "tp", core)
    wo_near = swap(tie(w_out, qo_rest), "tp", core)
    wi_near, wd_near = swap(tie(w_in, ready), "tp", core), swap(tie(w_down, ready), "tp", core)
    out2 = forward(2, tie(tokens, qo_rest, qo_far_core, wi_near, wd_near), [qo_far, qo_rest])
    ff_far = tie(ff_far, out2[0])
    rows_in = w_in.shape[0] // 2
    ff_rest = swap(ff_far, "dp", 1)
    ff_far_core = swap(ff_far, "tp", core)
    out3 = forward(3, tie(tokens, ff_far), [qo_far_core, qo_rest_core])
    fd_far = tie(fd_far, out3[0])
    fd_rest, fd_far_core = swap(fd_far, "dp", 2), swap(fd_far, "tp", core)
    q_sel, k, v, ctx, ctx_sel = zip(out0, out1, out2, out3)
    rows_q = 3 * width // 2

    def pieces(own, near, far_pieces, core_pieces):
        return [[(own, 0)], [(near, 0)], far_pieces, core_pieces]

    wq = pieces(wq, wq_near, [(qo_far, 0), (qo_rest, 0)], [(qo_far_core, 0), (qo_rest_core, 0)])
    wo = pieces(w_out, wo_near, [(qo_far, rows_q), (qo_rest, rows_q)], [(qo_far_core, rows_q), (qo_rest_core, rows_q)])
    near_in, near_down = [[(w_in, 0)], [(wi_near, 0)]], [[(w_down, 0)], [(wd_near, 0)]]
    prep = ffn_prep(picked, tie(tokens, fd_far), d_out, ctx_sel, wo, near_in, near_down, small[:2], shared, seqs)
    *act, slope_near, x_sel, cot, low, ffn_sum, normed1, inv1 = prep
    low_near, act_near = swap(low, "tp", core), swap(act[1], "tp", core)
    ff_rest, fd_rest = tie((ff_rest, fd_rest), low)
    ff_rest_core, fd_rest_core = swap(ff_rest, "tp", core), swap(fd_rest, "tp", core)
    wi = near_in + [[(ff_far, 0), (ff_rest, 0)], [(ff_far_core, 0), (ff_rest_core, 0)]]
    wd = near_down + [
        [(ff_far, rows_in), (ff_rest, rows_in), (fd_far, 0), (fd_rest, 0)],
        [(ff_far_core, rows_in), (ff_rest_core, rows_in), (fd_far_core, 0), (fd_rest_core, 0)],
    ]

    sent, g2, slope_far, grad2, vec = ffn_front(low, ffn_sum, cot, wi[2:], wd[2:], small[2:], shared)
    act_got = swap(sent, "tp", far)
    g2_near = swap(g2, "tp", core)
    *d_near, d_far, vec_mid = ffn_mid(g2, low, [slope_near, slope_far], wd)
    d_got, d_got_near = swap(d_far, "tp", far), swap(d_near[1], "tp", core)
    g1, grad1, vec_back, *d_ctx = ffn_back(tie(grad2, act_near, low_near, g2_near), d_near, d_far, normed1, inv1, shared, wi, wo, width)
    count = low.shape[0]

    def backward(j, x):
        return attend_backward(j, valid_len, q_sel[j], k[j], v[j], d_ctx[j], x, x_sel, ctx_sel[j], g1, seqs)

    def rows_of(first, count, before, *after):
        return ffn_rows(tie(tokens, *after), ctx, wo, wi, wd, small, shared, first, count, before)

    def finish(value, bits):
        for bit in bits:
            value = scatter(value, bit) if bit != last else add(value, swap(value, "dp", bit))
        return value

    def spread_out(value, bits):
        for bit in reversed(bits):
            value = gather(value, bit)
        return value

    half_rows, last = tokens.shape[0] // 2, dp_bits[-1]
    out3 = backward(3, tie(tokens, d_got_near))
    out2 = backward(2, tie(tokens, out3[0]))
    act_got = tie(act_got, out2[0])
    act_diag = swap(act_got[count:], "tp", core)
    out1 = backward(1, tie(tokens, out2[0], act_got))
    total_a = pair_sums(
        [
            ((tie(act[0], out1[0]), 0), (g2, 0)),
            ((act_near, 0), (g2_near, 0)),
            ((act_got, 0), (act_got, 2)),
            ((act_diag, 0), (act_diag, 1)),
        ]
    )
    sent_a = half_of(total_a, dp_bits[0], False)
    out0 = backward(0, tie(tokens, out1[0], sent_a))
    dq, dk, dv, sums, g_heads = zip(out0, out1, out2, out3)
    d_got = tie(d_got, out0[0])
    d_diag = swap(d_got[count:], "tp", core)
    far_c = add(tie(out2[4], out1[0]), swap(tie(out3[4], out2[0]), "tp", core))
    near_c = g_heads[0], swap(tie(g_heads[1], out0[0]), "tp", core)
    line = jnp.concatenate([vec + vec_mid + vec_back, sums[0] + sums[1] + sums[2] + sums[3]], axis=0)
    total_a = add(tie(half_of(total_a, dp_bits[0], True), far_c), swap(sent_a, "dp", dp_bits[0]))
    sent_a = half_of(total_a, dp_bits[1], False)
    total_b = pair_sums(
        [
            ((tie(low, sent_a), 0), (d_near[0], 0)),
            ((low_near, 0), (d_got_near, 0)),
            ((d_got, 2), (d_got, 0)),
            ((d_diag, 1), (d_diag, 0)),
        ]
    )
    sent_b = half_of(total_b, dp_bits[0], False)
    out_first = rows_of(0, half_rows, None, line, sent_b)
    total_a = add(tie(half_of(total_a, dp_bits[1], True), out_first), swap(sent_a, "dp", dp_bits[1]))
    for bit in dp_bits[2:-1]:
        total_a = scatter(total_a, bit)
    total_b = add(tie(half_of(total_b, dp_bits[0], True), out_first), swap(sent_b, "dp", dp_bits[0]))
    sent_b = half_of(total_b, dp_bits[1], False)
    total_c = add(*tie(near_c, out_first), swap(far_c, "tp", far))
    cut = far_c.shape[0] // 2
    other = [dp_bits[1], dp_bits[0], *dp_bits[2:]]
    total_c, rest_c = total_c[:cut], total_c[cut:]
    sent_c, sent_d = half_of(total_c, dp_bits[0], False), half_of(rest_c, other[0], False)
    d_tokens = input_gradient(tie(picked, total_a, sent_b, sent_c, sent_d), grad1, dq, dk, dv, wq, seqs)
    total_a = add(tie(total_a, d_tokens), swap(total_a, "dp", last))
    total_b = add(tie(half_of(total_b, dp_bits[1], True), d_tokens), swap(sent_b, "dp", dp_bits[1]))
    for bit in dp_bits[2:-1]:
        total_b = scatter(total_b, bit)
    total_c = add(tie(half_of(total_c, dp_bits[0], True), d_tokens), swap(sent_c, "dp", dp_bits[0]))
    rest_c = add(tie(half_of(rest_c, other[0], True), d_tokens), swap(sent_d, "dp", other[0]))
    sent_c, sent_d = half_of(total_c, dp_bits[1], False), half_of(rest_c, other[1], False)
    line = tie(line, d_tokens)
    out_second = rows_of(half_rows, half_rows // 2, out_first, total_a, total_b, sent_c, sent_d, line)
    for bit in reversed(dp_bits[2:-1]):
        total_a = gather(total_a, bit)
    total_a = joined(tie(total_a, out_second), swap(total_a, "dp", dp_bits[1]), dp_bits[1])
    total_b = add(tie(total_b, out_second), swap(total_b, "dp", last))
    for bit in reversed(dp_bits[2:-1]):
        total_b = gather(total_b, bit)
    total_c = add(tie(half_of(total_c, dp_bits[1], True), out_second), swap(sent_c, "dp", dp_bits[1]))
    rest_c = add(tie(half_of(rest_c, other[1], True), out_second), swap(sent_d, "dp", other[1]))
    for bit in dp_bits[2:-1]:
        total_c, rest_c = scatter(total_c, bit), scatter(rest_c, bit)
    line = tie(line, out_second) + swap(line, "tp", core)
    out_third = rows_of(half_rows + half_rows // 2, half_rows // 2, out_second, total_a, total_b, total_c, rest_c, line)
    total_a = joined(tie(total_a, out_third), swap(total_a, "dp", dp_bits[0]), dp_bits[0])
    total_b = joined(tie(total_b, out_third), swap(total_b, "dp", dp_bits[1]), dp_bits[1])
    total_c = add(tie(total_c, out_third), swap(total_c, "dp", last))
    rest_c = add(tie(rest_c, out_third), swap(rest_c, "dp", last))
    total_c, rest_c = tie((total_c, rest_c), total_b)
    rest_c = tie(rest_c, total_a)
    line = tie(line, total_c, rest_c) + swap(line, "dp", dp_bits[0])
    for bit in dp_bits[1:2]:
        line = line + swap(line, "dp", bit)
    for bit in dp_bits[2:]:
        line = line + swap(line, "dp", bit)
    total_c, rest_c = spread_out(total_c, dp_bits[1:-1]), spread_out(rest_c, other[1:-1])
    line = tie(line, total_c)
    line = line + swap(line, "tp", far)
    total_a, total_b = total_a.astype(F32), gather(total_b, dp_bits[0]).astype(F32)
    total_c = joined(tie(total_c, total_b, line), swap(total_c, "dp", dp_bits[0]), dp_bits[0])
    rest_c = gather(rest_c, other[0])
    total_c = jnp.concatenate([total_c.astype(F32), rest_c.astype(F32)], axis=0)
    own = lax.dynamic_slice_in_dim(line, 8 + rank, 1, 0)[0]
    own_q = lax.dynamic_slice(line, (16 + rank, 0), (1, width))
    own_v = lax.dynamic_slice(line, (16 + PARTS + rank, 0), (1, width))
    return (
        out_third,
        d_tokens,
        total_c[: 3 * width].reshape(3, width, depth).transpose(0, 2, 1),
        jnp.concatenate([own_q, own_v], axis=0),
        total_c[3 * width :],
        line[3],
        total_b,
        own,
        total_a,
        line[0],
        jnp.stack([line[4], line[1]]),
        jnp.stack([line[5], line[2]]),
    )


def solution(mesh):
    placed = (
        P(("dp", "tp"), None),
        P(None, None, "tp"),
        P(None, "tp"),
        P("tp", None),
        P(),
        P(None, "tp"),
        P("tp"),
        P("tp", None),
        P(),
        P(),
        P(),
        P("dp"),
        P("dp", None),
        P(("dp", "tp"), None),
    )
    return jax.shard_map(
        on_device,
        mesh=mesh,
        in_specs=placed,
        out_specs=(
            P(("dp", "tp"), None),
            P(("dp", "tp"), None),
            P(None, None, "tp"),
            P(None, "tp"),
            P("tp", None),
            P(),
            P(None, "tp"),
            P("tp"),
            P("tp", None),
            P(),
            P(),
            P(),
        ),
        check_vma=False,
    )
```
